32 devices in a mesh: dp: 16 (over z, x, core), seq: 2 (over y).
Axes of the slice: x: 2, y: 2, z: 4, core: 2. Of those that a mesh axis runs over, the one named last changes fastest.
Arguments:
- tokens: bfloat16 [16, 256, 1024], P('dp', 'seq'), may hold values from -6 to 6
- segments: int32 [16, 256], P('dp', 'seq'), may hold values from 0 to 5, never falling along the last dimension, each value on 1 to 85 neighbouring positions
- cotangent: bfloat16 [16, 256, 1024], P('dp', 'seq'), may hold values from -6 to 6
- qkv_weight: bfloat16 [1024, 3, 1024], P('dp', None, 'seq')
- out_weight: bfloat16 [1024, 1024], P('seq', 'dp'), may hold values from -1.5 to 1.5
- in_weight: bfloat16 [1024, 2, 2624], P('dp', None, 'seq'), may hold values from -0.1875 to 0.1875
- down_weight: bfloat16 [2624, 1024], P('seq', 'dp'), may hold values from -0.125 to 0.125
- attn_gain: float32 [1024], P('dp'), may hold values from 0.25 to 1.75
- mlp_gain: float32 [1024], P('dp'), may hold values from 0.25 to 1.75
Outputs:
- layer_out: bfloat16 [16, 256, 1024], P('dp', 'seq')
- tokens_grad: bfloat16 [16, 256, 1024], P('dp', 'seq')
- qkv_grad: float32 [1024, 3, 1024], P('dp', None, 'seq')
- out_grad: float32 [1024, 1024], P('seq', 'dp')
- in_grad: float32 [1024, 2, 2624], P('dp', None, 'seq')
- down_grad: float32 [2624, 1024], P('seq', 'dp')
- attn_gain_grad: float32 [1024], P('dp')
- mlp_gain_grad: float32 [1024], P('dp')
The draws below stay inside these ranges and needn't reach their ends.
Inputs may be any that keep to these rules, and one draw needn't show every extreme that they name: `segments`: along each sequence the numbers never fall; each of the 6 documents has 1 to 85 tokens, and one has exactly 85.
All inputs are finite; a program needn't handle non-finite values.
Results may differ from the reference program's by a relative error of at most 0.034.
Values may be sent and summed in bfloat16 or wider, within the bound.
A program may use at most 128 MiB of HBM per device.

```python
import math
import jax
import jax.numpy as jnp
import numpy as np
from jax import lax

D = 1024
HEADS = 16
FF = 2624
DOCS = 6
HALO = 64
LEN = 256
SEQS = 16


def draw_qkv_weight(key, part):
    return (jax.random.normal(jax.random.fold_in(key, 13), (D, 3 * D), jnp.float32) * D ** (-0.5)).reshape(D, 3, D).astype(jnp.bfloat16)


def with_spikes(values, key, source, target, shards_of, factor):
    def block_of(position):
        return (jnp.arange(values.shape[position]) // (values.shape[position] // shards_of)).reshape((-1,) + (1,) * (values.ndim - 1 - position))

    first = jax.random.permutation(key, shards_of)[block_of(target)]
    far = (block_of(target) + shards_of // 2) % shards_of
    return jnp.where((block_of(source) == first) | (block_of(source) == far), factor * values, values)


def block_scale(rng, dims, split, least, top_value):
    factor_of = 1.0
    for dim, shards_of in split:
        heights = jax.random.uniform(jax.random.fold_in(jax.random.fold_in(rng, 6), dim), (shards_of,), jnp.float32, least / len(split), top_value / len(split))
        factor_of = factor_of * jnp.repeat(jnp.exp(heights), dims[dim] // shards_of).reshape((-1,) + (1,) * (len(dims) - 1 - dim))
    return factor_of


def split_up(amount, total, limit, slope):
    weights = [(1 << 20) // math.isqrt(standing ** slope) + 1 for standing in range(2, amount + 1)]
    rest, counts = total - limit - (amount - 1), [1] * (amount - 1)
    while rest > 0:
        movable = [i for i in range(amount - 1) if counts[i] < limit]
        mass, left = sum([weights[i] for i in movable]), rest
        for i in movable:
            addition = min(limit - counts[i], max(1, left * weights[i] // mass), rest)
            counts[i] = counts[i] + addition
            rest = rest - addition
    return np.array([limit] + counts)


def uneven(stream_key, number_of, total, most, skew):
    if number_of == 2:
        one = jax.random.randint(stream_key, (), max(1, total - most), min(most, total - 1) + 1)
        return jnp.stack([one, total - one])
    tallies = jnp.asarray(split_up(number_of, total, most, skew), jnp.int32)
    twos = (number_of - 1) // 2
    donor, taker = tallies[1:1 + 2 * twos:2], tallies[2:2 + 2 * twos:2]
    slack = jnp.minimum(donor - 1, most - taker)
    moved = jax.random.randint(jax.random.fold_in(stream_key, 1), (twos,), 0, 1 << 20) % (slack + 1)
    tallies = tallies.at[1:1 + 2 * twos:2].set(donor - moved).at[2:2 + 2 * twos:2].set(taker + moved)
    return tallies[jax.random.permutation(jax.random.fold_in(stream_key, 2), number_of)]


def centred(stream_key, shape, deviation, bound, cuts=(), held_as=jnp.bfloat16):
    entries = deviation * jax.random.normal(stream_key, shape, jnp.float32)
    if cuts:
        entries = entries * block_scale(stream_key, shape, cuts, -0.22, 0.18)
    return jnp.clip(entries, -bound, bound).astype(held_as)


def noise_with(key, extent, width, most, pieces, heavy, held_as=jnp.bfloat16):
    result = width * jax.random.normal(key, extent, jnp.float32)
    if pieces:
        result = result * block_scale(key, extent, pieces, -0.22, 0.18)
    return jnp.clip(with_spikes(result, jax.random.fold_in(key, 3), *heavy), -most, most).astype(held_as)


def setup_inputs(seed: int = 0) -> dict:
    key_list = jax.random.split(jax.random.key(seed), 10)
    tokens = noise_with(key_list[0], (SEQS, LEN, D), 1.0, 6.0, ((0, 16), (1, 2)), (1, 2, 2, 2.0))
    segments = jax.vmap(lambda own: jnp.searchsorted(jnp.cumsum(uneven(own, DOCS, LEN, LEN // 3, 1)), jnp.arange(LEN), side="right"))(jax.random.split(key_list[1], SEQS)).reshape((SEQS, LEN)).astype(jnp.int32)
    cotangent = noise_with(key_list[2], (SEQS, LEN, D), 1.0, 6.0, ((0, 16), (1, 2)), (1, 2, 2, 2.0))
    qkv_weight = draw_qkv_weight(jax.random.fold_in(key_list[9], 71), 0)
    out_weight = centred(key_list[4], (D, D), (D // 64) ** -0.5, 1.5, ((0, 2), (1, 16)))
    in_weight = centred(key_list[5], (D, 2, FF), D ** -0.5, 0.1875, ((0, 16), (2, 2)))
    down_weight = centred(key_list[6], (FF, D), FF ** -0.5, 0.125, ((0, 2), (1, 16)))
    attn_gain = jnp.clip(1.0 + 0.15 * jax.random.normal(key_list[7], (D,), jnp.float32), 0.25, 1.75)
    mlp_gain = jnp.clip(1.0 + 0.15 * jax.random.normal(key_list[8], (D,), jnp.float32), 0.25, 1.75)
    return {"tokens": tokens, "segments": segments, "cotangent": cotangent, "qkv_weight": qkv_weight, "out_weight": out_weight, "in_weight": in_weight, "down_weight": down_weight, "attn_gain": attn_gain, "mlp_gain": mlp_gain}


EPS = 1e-05
THETA = 10000.0
NEG_FILL = -1e+30

def norm_forward(values, gain):
    center = values - lax.optimization_barrier(jnp.mean(values, axis=-1, keepdims=True))
    inv_std = lax.rsqrt(lax.optimization_barrier(jnp.mean(center * center, axis=-1, keepdims=True)) + EPS)
    unit_rows = center * inv_std
    return (unit_rows * gain, unit_rows, inv_std)

def norm_backward(grad_rows, gain, unit_rows, inv_std):
    scaled = grad_rows * gain
    inner = scaled - lax.optimization_barrier(jnp.mean(scaled, axis=-1, keepdims=True)) - unit_rows * lax.optimization_barrier(jnp.mean(scaled * unit_rows, axis=-1, keepdims=True))
    return (inner * inv_std, lax.optimization_barrier(jnp.sum(grad_rows * unit_rows, axis=0)))

def gelu_value(inputs):
    return 0.5 * inputs * (1.0 + lax.erf(inputs * 0.7071067811865476))

def gelu_slope(inputs):
    return 0.5 * (1.0 + lax.erf(inputs * 0.7071067811865476)) + inputs * jnp.exp(-0.5 * inputs * inputs) * 0.3989422804014327

def rotary_tables(positions, head_size):
    half_size = head_size // 2
    freqs = jnp.power(THETA, -(2.0 / head_size) * jnp.arange(half_size, dtype=jnp.float32))
    angles = positions.astype(jnp.float32)[:, None] * freqs[None, :]
    return (jnp.cos(angles)[:, None, :], jnp.sin(angles)[:, None, :])

def rotate(values, cos_table, sin_table):
    half_size = values.shape[-1] // 2
    lower_half = values[..., :half_size]
    upper_half = values[..., half_size:]
    return jnp.concatenate([lower_half * cos_table - upper_half * sin_table, upper_half * cos_table + lower_half * sin_table], axis=-1)

def unrotate(grads, cos_table, sin_table):
    half_size = grads.shape[-1] // 2
    lower_half = grads[..., :half_size]
    upper_half = grads[..., half_size:]
    return jnp.concatenate([lower_half * cos_table + upper_half * sin_table, upper_half * cos_table - lower_half * sin_table], axis=-1)

def window_mask(query_pos, key_pos, query_seg, key_seg, halo_width, total_len):
    near = jnp.abs(query_pos[:, None] - key_pos[None, :]) <= halo_width
    inside = (key_pos >= 0) & (key_pos < total_len)
    return near & inside[None, :] & (query_seg[:, None] == key_seg[None, :])

def block_scores(queries, key_slab, allowed, scale):
    scores = jnp.einsum('qhd,khd->hqk', queries.astype(jnp.float32), key_slab.astype(jnp.float32)) * scale
    return jnp.where(allowed[None], scores, NEG_FILL)

def attend_block(queries, key_slab, value_slab, allowed, scale):
    scores = block_scores(queries, key_slab, allowed, scale)
    top_score = lax.optimization_barrier(jnp.max(scores, axis=-1, keepdims=True))
    total = lax.optimization_barrier(jnp.sum(jnp.exp(scores - top_score), axis=-1, keepdims=True))
    logsum = top_score + jnp.log(total)
    probs = jnp.exp(scores - logsum).astype(jnp.bfloat16)
    mixed = jnp.einsum('hqk,khd->qhd', probs.astype(jnp.float32), value_slab.astype(jnp.float32))
    return (mixed, logsum[..., 0])

def attend_back(queries, key_slab, value_slab, allowed, scale, logsum, mixed_b, dmixed_b):
    scores = block_scores(queries, key_slab, allowed, scale)
    probs = jnp.exp(scores - logsum[..., None])
    probs_b = probs.astype(jnp.bfloat16)
    dmixed32 = dmixed_b.astype(jnp.float32)
    dvalues = jnp.einsum('hqk,qhd->khd', probs_b.astype(jnp.float32), dmixed32)
    dprobs = jnp.einsum('qhd,khd->hqk', dmixed32, value_slab.astype(jnp.float32))
    delta = jnp.transpose(lax.optimization_barrier(jnp.sum(dmixed32 * mixed_b.astype(jnp.float32), axis=-1)))
    dscores = (probs * (dprobs - delta[..., None]) * scale).astype(jnp.bfloat16)
    dqueries = jnp.einsum('hqk,khd->qhd', dscores.astype(jnp.float32), key_slab.astype(jnp.float32))
    dkeys = jnp.einsum('hqk,qhd->khd', dscores.astype(jnp.float32), queries.astype(jnp.float32))
    return (dqueries, dkeys, dvalues)

def layer_sequence(seq_tokens, seq_segments, seq_cot, qkv_weight, out_weight, in_weight, down_weight, attn_gain, mlp_gain):
    seq_len = seq_tokens.shape[0]
    model_width = seq_tokens.shape[1]
    head_size = model_width // HEADS
    halo_width = HALO
    block_rows = min(seq_len, 512)
    scale = 1.0 / head_size ** 0.5
    hidden_units = down_weight.shape[0]
    inputs32 = seq_tokens.astype(jnp.float32)
    normed_one, unit_one, inv_one = norm_forward(inputs32, attn_gain)
    normed_one_b = normed_one.astype(jnp.bfloat16)
    projected = jnp.dot(normed_one_b, qkv_weight, preferred_element_type=jnp.float32)
    positions = jnp.arange(seq_len, dtype=jnp.int32)
    cos_table, sin_table = rotary_tables(positions, head_size)
    queries = rotate(projected[:, :model_width].reshape(seq_len, HEADS, head_size), cos_table, sin_table).astype(jnp.bfloat16)
    keys_rot = rotate(projected[:, model_width:2 * model_width].reshape(seq_len, HEADS, head_size), cos_table, sin_table).astype(jnp.bfloat16)
    values_b = projected[:, 2 * model_width:].reshape(seq_len, HEADS, head_size).astype(jnp.bfloat16)
    pad_spec = ((halo_width, halo_width), (0, 0), (0, 0))
    key_pad = jnp.pad(keys_rot, pad_spec)
    value_pad = jnp.pad(values_b, pad_spec)
    seg_pad = jnp.pad(seq_segments, (halo_width, halo_width), constant_values=-1)
    slab_rows = block_rows + 2 * halo_width
    mixed_parts = []
    logsum_parts = []
    masks = []
    for start in range(0, seq_len, block_rows):
        query_pos = start + jnp.arange(block_rows, dtype=jnp.int32)
        key_pos = start - halo_width + jnp.arange(slab_rows, dtype=jnp.int32)
        allowed = window_mask(query_pos, key_pos, seq_segments[start:start + block_rows], seg_pad[start:start + slab_rows], halo_width, seq_len)
        masks.append(allowed)
        mixed_part, logsum_part = attend_block(queries[start:start + block_rows], key_pad[start:start + slab_rows], value_pad[start:start + slab_rows], allowed, scale)
        mixed_parts.append(mixed_part)
        logsum_parts.append(logsum_part)
    mixed_b = jnp.concatenate(mixed_parts, axis=0).astype(jnp.bfloat16)
    mixed_flat = mixed_b.reshape(seq_len, model_width)
    residual = inputs32 + jnp.dot(mixed_flat, out_weight, preferred_element_type=jnp.float32)
    normed_two, unit_two, inv_two = norm_forward(residual, mlp_gain)
    normed_two_b = normed_two.astype(jnp.bfloat16)
    expanded = jnp.dot(normed_two_b, in_weight, preferred_element_type=jnp.float32)
    gate_in = expanded[:, :hidden_units]
    linear_in = expanded[:, hidden_units:]
    activated = gelu_value(gate_in)
    middle_b = (activated * linear_in).astype(jnp.bfloat16)
    layer_out = (residual + jnp.dot(middle_b, down_weight, preferred_element_type=jnp.float32)).astype(jnp.bfloat16)
    down_grad = jnp.dot(middle_b.T, seq_cot, preferred_element_type=jnp.float32)
    dmiddle = jnp.dot(seq_cot, down_weight.T, preferred_element_type=jnp.float32)
    dexpanded_b = jnp.concatenate([dmiddle * linear_in * gelu_slope(gate_in), dmiddle * activated], axis=1).astype(jnp.bfloat16)
    in_grad = jnp.dot(normed_two_b.T, dexpanded_b, preferred_element_type=jnp.float32)
    dnormed_two = jnp.dot(dexpanded_b, in_weight.T, preferred_element_type=jnp.float32)
    dres_norm, mlp_gain_grad = norm_backward(dnormed_two, mlp_gain, unit_two, inv_two)
    dresidual = seq_cot.astype(jnp.float32) + dres_norm
    dresidual_b = dresidual.astype(jnp.bfloat16)
    out_grad = jnp.dot(mixed_flat.T, dresidual_b, preferred_element_type=jnp.float32)
    dmixed_b = jnp.dot(dresidual_b, out_weight.T, preferred_element_type=jnp.float32).astype(jnp.bfloat16).reshape(seq_len, HEADS, head_size)
    dkey_pad = jnp.zeros((seq_len + 2 * halo_width, HEADS, head_size), jnp.float32)
    dvalue_pad = jnp.zeros((seq_len + 2 * halo_width, HEADS, head_size), jnp.float32)
    dquery_parts = []
    for index, start in enumerate(range(0, seq_len, block_rows)):
        dqueries, dkeys, dvalues = attend_back(queries[start:start + block_rows], key_pad[start:start + slab_rows], value_pad[start:start + slab_rows], masks[index], scale, logsum_parts[index], mixed_b[start:start + block_rows], dmixed_b[start:start + block_rows])
        dquery_parts.append(dqueries)
        dkey_pad = dkey_pad.at[start:start + slab_rows].add(dkeys)
        dvalue_pad = dvalue_pad.at[start:start + slab_rows].add(dvalues)
    dquery_all = unrotate(jnp.concatenate(dquery_parts, axis=0), cos_table, sin_table).reshape(seq_len, model_width)
    dkey_all = unrotate(dkey_pad[halo_width:halo_width + seq_len], cos_table, sin_table).reshape(seq_len, model_width)
    dvalue_all = dvalue_pad[halo_width:halo_width + seq_len].reshape(seq_len, model_width)
    dqkv_b = jnp.concatenate([dquery_all, dkey_all, dvalue_all], axis=1).astype(jnp.bfloat16)
    qkv_grad = jnp.dot(normed_one_b.T, dqkv_b, preferred_element_type=jnp.float32)
    dnormed_one = jnp.dot(dqkv_b, qkv_weight.T, preferred_element_type=jnp.float32)
    dinput_norm, attn_gain_grad = norm_backward(dnormed_one, attn_gain, unit_one, inv_one)
    tokens_grad = (dresidual + dinput_norm).astype(jnp.bfloat16)
    return (layer_out, tokens_grad, (qkv_grad, out_grad, in_grad, down_grad, attn_gain_grad, mlp_gain_grad))

def reference(tokens, segments, cotangent, qkv_weight, out_weight, in_weight, down_weight, attn_gain, mlp_gain):
    in_rows = qkv_weight.shape[0]
    qkv_flat = qkv_weight.reshape(in_rows, qkv_weight.shape[1] * qkv_weight.shape[2])
    in_flat = in_weight.reshape(in_rows, in_weight.shape[1] * in_weight.shape[2])
    initial = (jnp.zeros(qkv_flat.shape, jnp.float32), jnp.zeros(out_weight.shape, jnp.float32), jnp.zeros(in_flat.shape, jnp.float32), jnp.zeros(down_weight.shape, jnp.float32), jnp.zeros(attn_gain.shape, jnp.float32), jnp.zeros(mlp_gain.shape, jnp.float32))

    def one_sequence(carry, inputs):
        seq_tokens, seq_segments, seq_cot = inputs
        layer_out, tokens_grad, grads = layer_sequence(seq_tokens, seq_segments, seq_cot, qkv_flat, out_weight, in_flat, down_weight, attn_gain, mlp_gain)
        carry = tuple((total + piece for total, piece in zip(carry, grads)))
        return (carry, (layer_out, tokens_grad))
    totals, (layer_outs, tokens_grads) = lax.scan(one_sequence, initial, (tokens, segments, cotangent))
    return (layer_outs, tokens_grads, totals[0].reshape(qkv_weight.shape), totals[1], totals[2].reshape(in_weight.shape), totals[3], totals[4], totals[5])
```

```python
import functools
import math
import types

import jax
import jax.numpy as jnp
import numpy as np
from jax import lax
from jax.experimental import pallas as pl
from jax.experimental.pallas import tpu as pltpu
from jax.sharding import PartitionSpec as P

HEADS = 16
HALO = 64


EPS = 1e-05
THETA = 10000.0
NEG_FILL = -1e30


def norm_forward(values, gain):
    center = values - jnp.mean(values, axis=-1, keepdims=True)
    inv_std = lax.rsqrt(jnp.mean(center * center, axis=-1, keepdims=True) + EPS)
    unit_rows = center * inv_std
    return (unit_rows * gain, unit_rows, inv_std)


def norm_backward(grad_rows, gain, unit_rows, inv_std):
    scaled = grad_rows * gain
    inner = (
        scaled
        - jnp.mean(scaled, axis=-1, keepdims=True)
        - unit_rows * jnp.mean(scaled * unit_rows, axis=-1, keepdims=True)
    )
    return (inner * inv_std, jnp.sum(grad_rows * unit_rows, axis=0))


def gelu_value(inputs):
    return 0.5 * inputs * (1.0 + lax.erf(inputs * 0.7071067811865476))


def gelu_slope(inputs):
    return (
        0.5 * (1.0 + lax.erf(inputs * 0.7071067811865476))
        + inputs * jnp.exp(-0.5 * inputs * inputs) * 0.3989422804014327
    )


def rotary_tables(positions, head_size):
    half_size = head_size // 2
    freqs = jnp.power(THETA, -(2.0 / head_size) * jnp.arange(half_size, dtype=jnp.float32))
    angles = positions.astype(jnp.float32)[:, None] * freqs[None, :]
    return (jnp.cos(angles)[:, None, :], jnp.sin(angles)[:, None, :])


def rotate(values, cos_table, sin_table):
    half_size = values.shape[-1] // 2
    lower_half = values[..., :half_size]
    upper_half = values[..., half_size:]
    return jnp.concatenate(
        [
            lower_half * cos_table - upper_half * sin_table,
            upper_half * cos_table + lower_half * sin_table,
        ],
        axis=-1,
    )


def unrotate(grads, cos_table, sin_table):
    half_size = grads.shape[-1] // 2
    lower_half = grads[..., :half_size]
    upper_half = grads[..., half_size:]
    return jnp.concatenate(
        [
            lower_half * cos_table + upper_half * sin_table,
            upper_half * cos_table - lower_half * sin_table,
        ],
        axis=-1,
    )


def window_mask(query_pos, key_pos, query_seg, key_seg, halo_width, total_len):
    near = jnp.abs(query_pos[:, None] - key_pos[None, :]) <= halo_width
    inside = (key_pos >= 0) & (key_pos < total_len)
    return near & inside[None, :] & (query_seg[:, None] == key_seg[None, :])


def block_scores(queries, key_slab, allowed, scale):
    scores = (
        jnp.einsum("qhd,khd->hqk", queries, key_slab, preferred_element_type=jnp.float32) * scale
    )
    return jnp.where(allowed[None], scores, NEG_FILL)


def attend_block(queries, key_slab, value_slab, allowed, scale):
    scores = block_scores(queries, key_slab, allowed, scale)
    top_score = jnp.max(scores, axis=-1, keepdims=True)
    total = jnp.sum(jnp.exp(scores - top_score), axis=-1, keepdims=True)
    logsum = top_score + jnp.log(total)
    probs = jnp.exp(scores - logsum).astype(jnp.bfloat16)
    mixed = jnp.einsum("hqk,khd->qhd", probs, value_slab, preferred_element_type=jnp.float32)
    return (mixed, logsum[..., 0])


def attend_back(queries, key_slab, value_slab, allowed, scale, logsum, mixed_b, dmixed_b):
    scores = block_scores(queries, key_slab, allowed, scale)
    probs = jnp.exp(scores - logsum[..., None])
    probs_b = probs.astype(jnp.bfloat16)
    dvalues = jnp.einsum("hqk,qhd->khd", probs_b, dmixed_b, preferred_element_type=jnp.float32)
    dprobs = jnp.einsum("qhd,khd->hqk", dmixed_b, value_slab, preferred_element_type=jnp.float32)
    delta = jnp.transpose(
        jnp.sum(dmixed_b.astype(jnp.float32) * mixed_b.astype(jnp.float32), axis=-1)
    )
    dscores = (probs * (dprobs - delta[..., None]) * scale).astype(jnp.bfloat16)
    dqueries = jnp.einsum("hqk,khd->qhd", dscores, key_slab, preferred_element_type=jnp.float32)
    dkeys = jnp.einsum("hqk,qhd->khd", dscores, queries, preferred_element_type=jnp.float32)
    return (dqueries, dkeys, dvalues)


MESH = pl.DeviceIdType.MESH
VMEM_LIMIT = 60 * 1024 * 1024
LANES = 128


def ring_place(count):
    me = lax.axis_index("dp")
    core = me % 2
    chip = me // 2
    row, column = chip // 2, chip % 2
    place = (1 - column) * row + column * (count - 1 - row)
    return (core, place)


def chip_at(place, count):
    side = place // (count // 2)
    return (1 - side) * (2 * place) + side * (2 * (count - 1 - place) + 1)


def neighbours(core, place, count):
    right = chip_at((place + 1) % count, count) * 2 + core
    left = chip_at((place + count - 1) % count, count) * 2 + core
    return (right, left, lax.axis_index("dp") + 1 - 2 * core)


def greet(devices):
    barrier = pltpu.get_barrier_semaphore()
    for device in devices:
        pl.semaphore_signal(barrier, inc=1, device_id={"dp": device}, device_id_type=MESH)
    pl.semaphore_wait(barrier, len(devices))


def gather_kernel(count, streams, *refs):
    shards = refs[:streams]
    fulls = refs[streams : 2 * streams]
    own_sem, send_sem, recv_sem, pair_send, pair_recv = refs[2 * streams :]
    rows = shards[0].shape[0]
    half = rows // 2
    core, place = ring_place(count)
    right, left, partner = neighbours(core, place, count)
    targets = (right, left)
    lanes = [(way, stream) for stream in range(streams) for way in range(2)]

    def piece(way, step, stream):
        shift = count - step if way == 0 else step
        owner = chip_at((place + shift) % count, count) * 2 + core
        start = pl.multiple_of(owner * rows + way * half, half)
        return fulls[stream].at[pl.ds(start, half)]

    def hop(way, step, stream):
        ref = piece(way, step, stream)
        return pltpu.make_async_remote_copy(
            src_ref=ref,
            dst_ref=ref,
            send_sem=send_sem.at[stream, way, step],
            recv_sem=recv_sem.at[stream, way, step],
            device_id={"dp": targets[way]},
            device_id_type=MESH,
        )

    def share(way, step, stream):
        ref = piece(way, step, stream)
        return pltpu.make_async_remote_copy(
            src_ref=ref,
            dst_ref=ref,
            send_sem=pair_send.at[stream, way, step],
            recv_sem=pair_recv.at[stream, way, step],
            device_id={"dp": partner},
            device_id_type=MESH,
        )

    me = lax.axis_index("dp")
    owns = [
        pltpu.make_async_copy(
            shards[stream],
            fulls[stream].at[pl.ds(pl.multiple_of(me * rows, rows), rows)],
            own_sem.at[stream],
        )
        for stream in range(streams)
    ]
    for own in owns:
        own.start()
    greet((right, left, partner))
    for own in owns:
        own.wait()
    for way, stream in lanes:
        hop(way, 0, stream).start()
        share(way, 0, stream).start()

    def step_body(step, carry):
        for way, stream in lanes:
            hop(way, step - 1, stream).wait_recv()
            hop(way, step, stream).start()
            share(way, step, stream).start()
        return carry

    lax.fori_loop(1, count - 1, step_body, 0)
    for way, stream in lanes:
        hop(way, count - 2, stream).wait_recv()
        share(way, count - 1, stream).start()

    def drain_hops(step, carry):
        for way, stream in lanes:
            hop(way, step, stream).wait_send()
        return carry

    def drain_shares(step, carry):
        for way, stream in lanes:
            share(way, step, stream).wait_send()
            share(way, step, stream).wait_recv()
        return carry

    lax.fori_loop(0, count - 1, drain_hops, 0)
    lax.fori_loop(0, count, drain_shares, 0)


def ring_gather(shards, devices):
    count = devices // 2
    streams = len(shards)
    return pl.pallas_call(
        functools.partial(gather_kernel, count, streams),
        out_shape=[
            jax.ShapeDtypeStruct((devices * shard.shape[0], shard.shape[1]), shard.dtype)
            for shard in shards
        ],
        in_specs=[pl.BlockSpec(memory_space=pltpu.VMEM)] * streams,
        out_specs=[pl.BlockSpec(memory_space=pl.ANY)] * streams,
        scratch_shapes=[pltpu.SemaphoreType.DMA((streams,))]
        + [pltpu.SemaphoreType.DMA((streams, 2, count - 1))] * 2
        + [pltpu.SemaphoreType.DMA((streams, 2, count))] * 2,
        cost_estimate=pl.CostEstimate(
            flops=0, bytes_accessed=128 * 1024 * 1024, transcendentals=0
        ),
        compiler_params=pltpu.CompilerParams(
            collective_id=0, has_side_effects=True, vmem_limit_bytes=VMEM_LIMIT
        ),
        name="ring_gather",
    )(*shards)


def scatter_kernel(count, streams, *refs):
    grads = refs[:streams]
    outs = refs[streams : 2 * streams]
    pairs = refs[2 * streams : 3 * streams]
    sends = refs[3 * streams : 4 * streams]
    recvs = refs[4 * streams : 5 * streams]
    send_sem, recv_sem, pair_send, pair_recv = refs[5 * streams :]
    rows = outs[0].shape[0]
    half = rows // 2
    core, place = ring_place(count)
    right, left, partner = neighbours(core, place, count)
    targets = (right, left)

    def block(way, step, which):
        shift = 2 * count - 1 - step if way == 0 else 1 + step
        owner = chip_at((place + shift) % count, count) * 2 + which
        return pl.ds(pl.multiple_of(owner * rows + way * half, half), half)

    def share(way, step, stream):
        return pltpu.make_async_remote_copy(
            src_ref=grads[stream].at[block(way, step, 1 - core)],
            dst_ref=pairs[stream].at[way, step],
            send_sem=pair_send.at[stream, way, step],
            recv_sem=pair_recv.at[stream, way, step],
            device_id={"dp": partner},
            device_id_type=MESH,
        )

    def hop(way, step, stream):
        return pltpu.make_async_remote_copy(
            src_ref=sends[stream].at[way, step],
            dst_ref=recvs[stream].at[way, step],
            send_sem=send_sem.at[stream, way, step],
            recv_sem=recv_sem.at[stream, way, step],
            device_id={"dp": targets[way]},
            device_id_type=MESH,
        )

    def pair_sum(way, step, stream):
        share(way, step, stream).wait_recv()
        own = grads[stream][block(way, step, core), :].astype(jnp.float32)
        return own + pairs[stream][way, step].astype(jnp.float32)

    greet((right, left, partner))

    def start_shares(step, carry):
        for stream in range(streams):
            for way in range(2):
                share(way, step, stream).start()
        return carry

    lax.fori_loop(0, count, start_shares, 0)
    for stream in range(streams):
        for way in range(2):
            sends[stream][way, 0] = pair_sum(way, 0, stream).astype(jnp.bfloat16)
            hop(way, 0, stream).start()

    def step_body(step, carry):
        for stream in range(streams):
            for way in range(2):
                total = pair_sum(way, step, stream)
                hop(way, step - 1, stream).wait_recv()
                total = total + recvs[stream][way, step - 1].astype(jnp.float32)
                sends[stream][way, step] = total.astype(jnp.bfloat16)
                hop(way, step, stream).start()
        return carry

    lax.fori_loop(1, count - 1, step_body, 0)
    for stream in range(streams):
        for way in range(2):
            total = pair_sum(way, count - 1, stream)
            hop(way, count - 2, stream).wait_recv()
            total = total + recvs[stream][way, count - 2].astype(jnp.float32)
            outs[stream][way * half : (way + 1) * half, :] = total

    def drain_hops(step, carry):
        for stream in range(streams):
            for way in range(2):
                hop(way, step, stream).wait_send()
        return carry

    def drain_shares(step, carry):
        for stream in range(streams):
            for way in range(2):
                share(way, step, stream).wait_send()
        return carry

    lax.fori_loop(0, count - 1, drain_hops, 0)
    lax.fori_loop(0, count, drain_shares, 0)


def ring_scatter(grads, devices):
    count = devices // 2
    streams = len(grads)
    rows = grads[0].shape[0] // devices
    half = rows // 2
    widths = [grad.shape[1] for grad in grads]
    vmem = pl.BlockSpec(memory_space=pltpu.VMEM)
    return pl.pallas_call(
        functools.partial(scatter_kernel, count, streams),
        out_shape=[jax.ShapeDtypeStruct((rows, width), jnp.float32) for width in widths],
        in_specs=[vmem] * streams,
        out_specs=[vmem] * streams,
        scratch_shapes=[pltpu.VMEM((2, count, half, width), jnp.bfloat16) for width in widths]
        + [pltpu.VMEM((2, count - 1, half, width), jnp.bfloat16) for width in widths] * 2
        + [pltpu.SemaphoreType.DMA((streams, 2, count - 1))] * 2
        + [pltpu.SemaphoreType.DMA((streams, 2, count))] * 2,
        compiler_params=pltpu.CompilerParams(
            collective_id=1, has_side_effects=True, vmem_limit_bytes=40 * 1024 * 1024
        ),
        name="ring_scatter",
    )(*grads)


def turn(values, cos_table, sin_table, low_half):
    half = HEAD_HALF
    swapped = jnp.where(
        low_half, pltpu.roll(values, LANES - half, 1), pltpu.roll(values, half, 1)
    )
    return values * cos_table + swapped * sin_table


HEAD_HALF = 32


def lane_masks(rows):
    lane = lax.broadcasted_iota(jnp.int32, (rows, LANES), 1)
    return (lane % (2 * HEAD_HALF) < HEAD_HALF, lane < 2 * HEAD_HALF)


def allowed_pairs(pos_col, pos_row, seg_col, seg_row):
    near = jnp.abs(pos_col[...] - pos_row[...]) <= HALO
    return near & (seg_col[...] == seg_row[...])


def head_probs(queries, keys, allowed, scale):
    scores = (
        lax.dot_general(
            queries, keys, (((1,), (1,)), ((), ())), preferred_element_type=jnp.float32
        )
        * scale
    )
    scores = jnp.where(allowed, scores, NEG_FILL)
    top_score = jnp.max(scores, axis=-1, keepdims=True)
    total = jnp.sum(jnp.exp(scores - top_score), axis=-1, keepdims=True)
    return jnp.exp(scores - (top_score + jnp.log(total)))


def attend_kernel(
    scale, width, proj, cos_ref, sin_ref, pos_col, pos_row, seg_col, seg_row, qkv_out, mixed_out
):
    rows = proj.shape[0]
    low_half, first = lane_masks(rows)
    cos_table, sin_table = cos_ref[...], sin_ref[...]
    allowed = allowed_pairs(pos_col, pos_row, seg_col, seg_row)
    for start in range(0, width, LANES):
        queries = turn(proj[:, start : start + LANES], cos_table, sin_table, low_half)
        keys = turn(
            proj[:, width + start : width + start + LANES], cos_table, sin_table, low_half
        ).astype(jnp.bfloat16)
        values = proj[:, 2 * width + start : 2 * width + start + LANES]
        qkv_out[:, start : start + LANES] = queries.astype(jnp.bfloat16)
        qkv_out[:, width + start : width + start + LANES] = keys
        qkv_out[:, 2 * width + start : 2 * width + start + LANES] = values.astype(jnp.bfloat16)
        mixed = jnp.zeros((rows, LANES), jnp.float32)
        for head in range(2):
            mine = first if head == 0 else ~first
            probs = head_probs(
                jnp.where(mine, queries, 0.0).astype(jnp.bfloat16), keys, allowed, scale
            ).astype(jnp.bfloat16)
            mixed = mixed + jnp.dot(
                probs,
                jnp.where(mine, values, 0.0).astype(jnp.bfloat16),
                preferred_element_type=jnp.float32,
            )
        mixed_out[:, start : start + LANES] = mixed.astype(jnp.bfloat16)


def attend_back_kernel(
    scale,
    width,
    qkv,
    mixed_ref,
    dmixed_ref,
    cos_ref,
    sin_ref,
    pos_col,
    pos_row,
    seg_col,
    seg_row,
    dqkv_out,
):
    rows = qkv.shape[0]
    low_half, first = lane_masks(rows)
    cos_table, sin_table = cos_ref[...], -sin_ref[...]
    allowed = allowed_pairs(pos_col, pos_row, seg_col, seg_row)
    over_rows = (((0,), (0,)), ((), ()))
    over_lanes = (((1,), (1,)), ((), ()))
    for start in range(0, width, LANES):
        queries = qkv[:, start : start + LANES].astype(jnp.float32)
        keys = qkv[:, width + start : width + start + LANES]
        keys32 = keys.astype(jnp.float32)
        values = qkv[:, 2 * width + start : 2 * width + start + LANES]
        dmixed = dmixed_ref[:, start : start + LANES].astype(jnp.float32)
        products = dmixed * mixed_ref[:, start : start + LANES].astype(jnp.float32)
        dquery = jnp.zeros((rows, LANES), jnp.float32)
        dkey = jnp.zeros((rows, LANES), jnp.float32)
        dvalue = jnp.zeros((rows, LANES), jnp.float32)
        for head in range(2):
            mine = first if head == 0 else ~first
            head_queries = jnp.where(mine, queries, 0.0).astype(jnp.bfloat16)
            head_keys = jnp.where(mine, keys32, 0.0).astype(jnp.bfloat16)
            head_dmixed = jnp.where(mine, dmixed, 0.0).astype(jnp.bfloat16)
            delta = jnp.sum(jnp.where(mine, products, 0.0), axis=-1, keepdims=True)
            probs = head_probs(head_queries, keys, allowed, scale)
            dprobs = lax.dot_general(
                head_dmixed, values, over_lanes, preferred_element_type=jnp.float32
            )
            dscores = (probs * (dprobs - delta) * scale).astype(jnp.bfloat16)
            dvalue = dvalue + lax.dot_general(
                probs.astype(jnp.bfloat16),
                head_dmixed,
                over_rows,
                preferred_element_type=jnp.float32,
            )
            dkey = dkey + lax.dot_general(
                dscores, head_queries, over_rows, preferred_element_type=jnp.float32
            )
            dquery = dquery + jnp.dot(dscores, head_keys, preferred_element_type=jnp.float32)
        dquery = turn(dquery, cos_table, sin_table, low_half)
        dkey = turn(dkey, cos_table, sin_table, low_half)
        dqkv_out[:, start : start + LANES] = dquery.astype(jnp.bfloat16)
        dqkv_out[:, width + start : width + start + LANES] = dkey.astype(jnp.bfloat16)
        dqkv_out[:, 2 * width + start : 2 * width + start + LANES] = dvalue.astype(jnp.bfloat16)


def local_call(kernel, name, out_shape, operands, flops):
    vmem = pl.BlockSpec(memory_space=pltpu.VMEM)
    single = not isinstance(out_shape, list)
    return pl.pallas_call(
        kernel,
        out_shape=out_shape,
        in_specs=[vmem] * len(operands),
        out_specs=vmem if single else [vmem] * len(out_shape),
        cost_estimate=pl.CostEstimate(
            flops=flops, bytes_accessed=4 * 1024 * 1024, transcendentals=flops // 256
        ),
        compiler_params=pltpu.CompilerParams(vmem_limit_bytes=32 * 1024 * 1024),
        name=name,
    )(*operands)


class PairedAttention:
    def __init__(self, positions, segments, head_size, width):
        rows = positions.shape[0]
        cos_table, sin_table = rotary_tables(positions, head_size)
        cos_table, sin_table = cos_table[:, 0, :], sin_table[:, 0, :]
        self.width = width
        self.scale = 1.0 / math.sqrt(head_size)
        self.flops = 2 * rows * rows * LANES * (width // head_size)
        self.shared = (
            jnp.concatenate([cos_table] * 4, axis=1),
            jnp.concatenate([-sin_table, sin_table] * 2, axis=1),
            positions[:, None],
            positions[None, :],
            segments[:, None],
            segments[None, :],
        )

    def forward(self, projected):
        rows = projected.shape[0]
        self.qkv, self.mixed = local_call(
            functools.partial(attend_kernel, self.scale, self.width),
            "attend",
            [
                jax.ShapeDtypeStruct((rows, 3 * self.width), jnp.bfloat16),
                jax.ShapeDtypeStruct((rows, self.width), jnp.bfloat16),
            ],
            (projected,) + self.shared,
            2 * self.flops,
        )
        return self.mixed

    def backward(self, dmixed):
        rows = dmixed.shape[0]
        return local_call(
            functools.partial(attend_back_kernel, self.scale, self.width),
            "attend_back",
            jax.ShapeDtypeStruct((rows, 3 * self.width), jnp.bfloat16),
            (self.qkv, self.mixed, dmixed) + self.shared,
            5 * self.flops,
        )


class BlockAttention:
    def __init__(self, positions, segments, head_size, width):
        self.total_len = positions.shape[0]
        self.segments = segments
        self.head_size = head_size
        self.width = width
        self.scale = 1.0 / math.sqrt(head_size)
        self.cos_table, self.sin_table = rotary_tables(positions, head_size)

    def heads(self, values):
        return values.reshape(self.total_len, self.width // self.head_size, self.head_size)

    def forward(self, projected):
        width, total_len = self.width, self.total_len
        self.block_rows = min(total_len, 512)
        self.slab_rows = self.block_rows + 2 * HALO
        tables = (self.cos_table, self.sin_table)
        self.queries = rotate(self.heads(projected[:, :width]), *tables).astype(jnp.bfloat16)
        keys = rotate(self.heads(projected[:, width : 2 * width]), *tables).astype(jnp.bfloat16)
        values = self.heads(projected[:, 2 * width :]).astype(jnp.bfloat16)
        pad_spec = ((HALO, HALO), (0, 0), (0, 0))
        self.key_pad = jnp.pad(keys, pad_spec)
        self.value_pad = jnp.pad(values, pad_spec)
        seg_pad = jnp.pad(self.segments, (HALO, HALO), constant_values=-1)
        mixed_parts = []
        self.logsums = []
        self.masks = []
        for start in range(0, total_len, self.block_rows):
            own = slice(start, start + self.block_rows)
            slab = slice(start, start + self.slab_rows)
            allowed = window_mask(
                start + jnp.arange(self.block_rows, dtype=jnp.int32),
                start - HALO + jnp.arange(self.slab_rows, dtype=jnp.int32),
                self.segments[own],
                seg_pad[slab],
                HALO,
                total_len,
            )
            mixed, logsum = attend_block(
                self.queries[own], self.key_pad[slab], self.value_pad[slab], allowed, self.scale
            )
            self.masks.append(allowed)
            self.logsums.append(logsum)
            mixed_parts.append(mixed)
        self.mixed = jnp.concatenate(mixed_parts, axis=0).astype(jnp.bfloat16)
        return self.mixed.reshape(total_len, width)

    def backward(self, dmixed):
        total_len = self.total_len
        dmixed = self.heads(dmixed)
        padded = (total_len + 2 * HALO,) + dmixed.shape[1:]
        dkey_pad = jnp.zeros(padded, jnp.float32)
        dvalue_pad = jnp.zeros(padded, jnp.float32)
        dquery_parts = []
        for index, start in enumerate(range(0, total_len, self.block_rows)):
            own = slice(start, start + self.block_rows)
            slab = slice(start, start + self.slab_rows)
            dqueries, dkeys, dvalues = attend_back(
                self.queries[own],
                self.key_pad[slab],
                self.value_pad[slab],
                self.masks[index],
                self.scale,
                self.logsums[index],
                self.mixed[own],
                dmixed[own],
            )
            dquery_parts.append(dqueries)
            dkey_pad = dkey_pad.at[slab].add(dkeys)
            dvalue_pad = dvalue_pad.at[slab].add(dvalues)
        inner = slice(HALO, HALO + total_len)
        tables = (self.cos_table, self.sin_table)
        parts = [
            unrotate(jnp.concatenate(dquery_parts, axis=0), *tables),
            unrotate(dkey_pad[inner], *tables),
            dvalue_pad[inner],
        ]
        return jnp.concatenate(
            [part.reshape(total_len, self.width) for part in parts], axis=1
        ).astype(jnp.bfloat16)


def dot(left, right, left_dim, right_dim):
    return lax.dot_general(
        left,
        right,
        (((left_dim,), (right_dim,)), ((), ())),
        preferred_element_type=jnp.float32,
    )


def padded_to_lanes(values):
    return jnp.pad(values, ((0, 0), (0, -values.shape[1] % LANES)))


def high_and_low(gain):
    high = gain.astype(jnp.bfloat16)
    return [high[:, None], (gain - high.astype(jnp.float32)).astype(jnp.bfloat16)[:, None]]


def general_device(
    devices,
    seq_size,
    tokens,
    segments,
    cotangent,
    qkv_weight,
    out_weight,
    in_weight,
    down_weight,
    attn_gain,
    mlp_gain,
):
    layer_in = tokens[0]
    seg_local = segments[0]
    cot_local = cotangent[0]
    own_rows, model_width = layer_in.shape
    head_size = model_width // HEADS
    local_width = qkv_weight.shape[2]
    local_hidden = in_weight.shape[2]
    shard_rows = qkv_weight.shape[0]
    total_len = own_rows * seq_size
    paired = (
        seq_size == 2
        and total_len <= 512
        and local_width % LANES == 0
        and head_size == 2 * HEAD_HALF
    )
    swap = [(0, 1), (1, 0)]

    def rows_of_all(values):
        if paired:
            return jnp.concatenate([values, lax.ppermute(values, "seq", swap)], axis=0)
        return lax.all_gather(values, "seq", axis=0, tiled=True)

    def sum_to_owner(partial):
        if paired:
            other = lax.ppermute(partial[own_rows:].astype(jnp.bfloat16), "seq", swap)
            return partial[:own_rows] + other.astype(jnp.float32)
        return lax.psum_scatter(
            partial.astype(jnp.bfloat16), "seq", scatter_dimension=0, tiled=True
        ).astype(jnp.float32)

    def sum_over_seq(part):
        if paired:
            return part + lax.ppermute(part, "seq", swap)
        return lax.psum(part, "seq")

    first_pack = jnp.concatenate(
        [qkv_weight.reshape(shard_rows, 3 * local_width), out_weight.T], axis=1
    )
    wide = (local_hidden + 4 + LANES - 1) // LANES * LANES
    spare = jnp.zeros((shard_rows, wide - local_hidden), jnp.bfloat16)
    second_pack = jnp.concatenate(
        [in_weight[:, 0, :], spare, in_weight[:, 1, :], spare, down_weight.T]
        + high_and_low(attn_gain)
        + high_and_low(mlp_gain)
        + [spare[:, 4:]],
        axis=1,
    )
    first_full, second_full = ring_gather([first_pack, second_pack], devices)
    full_qkv = first_full[:, : 3 * local_width]
    full_out = first_full[:, 3 * local_width : 4 * local_width]
    gains_at = 2 * wide + local_hidden
    gains = second_full[:, gains_at : gains_at + 4].astype(jnp.float32)
    gain_attn = gains[:, 0] + gains[:, 1]
    gain_mlp = gains[:, 2] + gains[:, 3]
    full_in = second_full[:, : 2 * wide]
    full_down = second_full[:, 2 * wide :]

    inputs32 = layer_in.astype(jnp.float32)
    if paired:
        arrived = lax.ppermute(jnp.concatenate([layer_in, cot_local], axis=0), "seq", swap)
        all_inputs32 = jnp.concatenate([layer_in, arrived[:own_rows]], axis=0).astype(jnp.float32)
        cot_full = jnp.concatenate([cot_local, arrived[own_rows:]], axis=0)
    else:
        all_inputs32 = rows_of_all(layer_in).astype(jnp.float32)
        cot_full = rows_of_all(cot_local)
    normed_full = norm_forward(all_inputs32, gain_attn)[0].astype(jnp.bfloat16)
    unit_one, inv_one = norm_forward(inputs32, gain_attn)[1:]
    if paired:
        seg_full = rows_of_all(
            jnp.broadcast_to(seg_local.astype(jnp.float32)[:, None], (own_rows, LANES))
        )[:, 0].astype(jnp.int32)
        place = lax.axis_index("seq")
        arange = jnp.arange(own_rows, dtype=jnp.int32)
        positions = jnp.concatenate(
            [place * own_rows + arange, (1 - place) * own_rows + arange], axis=0
        )
        attention = PairedAttention(positions, seg_full, head_size, local_width)
    else:
        seg_full = rows_of_all(seg_local.astype(jnp.bfloat16)).astype(jnp.int32)
        positions = jnp.arange(total_len, dtype=jnp.int32)
        attention = BlockAttention(positions, seg_full, head_size, local_width)

    mixed = attention.forward(dot(normed_full, full_qkv, 1, 0))
    residual = inputs32 + sum_to_owner(dot(mixed, full_out, 1, 1))
    normed_two, unit_two, inv_two = norm_forward(residual, gain_mlp)
    normed_two_full = rows_of_all(normed_two.astype(jnp.bfloat16))
    expanded = dot(normed_two_full, full_in, 1, 0)
    gate_in = expanded[:, :wide]
    linear_in = expanded[:, wide:]
    activated = gelu_value(gate_in)
    middle_b = (activated * linear_in).astype(jnp.bfloat16)
    down_part = dot(middle_b, full_down, 1, 1)

    down_grad = dot(cot_full, middle_b, 0, 0).astype(jnp.bfloat16)
    dmiddle = dot(cot_full, full_down, 1, 0)
    dexpanded_b = jnp.concatenate(
        [dmiddle * linear_in * gelu_slope(gate_in), dmiddle * activated], axis=1
    ).astype(jnp.bfloat16)
    dnormed_two = sum_to_owner(dot(dexpanded_b, full_in, 1, 1))
    in_grad = dot(normed_two_full, dexpanded_b, 0, 0).astype(jnp.bfloat16)
    dres_norm, mlp_gain_part = norm_backward(dnormed_two, gain_mlp, unit_two, inv_two)
    dresidual = cot_local.astype(jnp.float32) + dres_norm
    dres_full = rows_of_all(dresidual.astype(jnp.bfloat16))
    down_part, dres_full = lax.optimization_barrier((down_part, dres_full))
    layer_out = (residual + sum_to_owner(down_part)).astype(jnp.bfloat16)
    dmixed = dot(dres_full, full_out, 1, 0).astype(jnp.bfloat16)
    out_grad = dot(dres_full, mixed, 0, 0).astype(jnp.bfloat16)
    dqkv_b = attention.backward(dmixed)
    layer_out, dqkv_b = lax.optimization_barrier((layer_out, dqkv_b))
    dnormed_one = sum_to_owner(dot(dqkv_b, full_qkv, 1, 1))
    qkv_grad = dot(normed_full, dqkv_b, 0, 0).astype(jnp.bfloat16)
    dinput_norm, attn_gain_part = norm_backward(dnormed_one, gain_attn, unit_one, inv_one)
    tokens_grad = (dresidual + dinput_norm).astype(jnp.bfloat16)
    gain_sums = sum_over_seq(jnp.stack([attn_gain_part, mlp_gain_part]))
    gain_grad = padded_to_lanes(gain_sums.T).astype(jnp.bfloat16)

    in_share, qkv_share, down_share, out_share, gain_share = ring_scatter(
        [in_grad, qkv_grad, down_grad, out_grad, gain_grad], devices
    )
    return (
        layer_out[None],
        tokens_grad[None],
        qkv_share.reshape(shard_rows, 3, local_width),
        out_share.T,
        jnp.stack([in_share[:, :local_hidden], in_share[:, wide : wide + local_hidden]], axis=1),
        down_share[:, :local_hidden].T,
        gain_share[:, 0],
        gain_share[:, 1],
    )


HIGH = (((1,), (1,)), ((), ()))
OVER_ROWS = (((0,), (0,)), ((), ()))


def fits_fused(devices, seq_size, own_rows, model_width, local_width, local_hidden):
    rest = local_hidden % LANES
    shard_rows = model_width // devices
    return (
        seq_size == 2
        and devices % 4 == 0
        and devices >= 8
        and own_rows == LANES
        and local_width % (2 * LANES) == 0
        and model_width % (2 * LANES) == 0
        and model_width // HEADS == 2 * HEAD_HALF
        and 3 * rest + 8 <= LANES
        and local_hidden // LANES >= 4
        and local_hidden // LANES % 2 == 0
        and shard_rows % 32 == 0
    )


def nt(left, right):
    return lax.dot_general(left, right, HIGH, preferred_element_type=jnp.float32)


def nn(left, right):
    return jnp.dot(left, right, preferred_element_type=jnp.float32)


def tiles(total, width, body):
    def step(index, carry):
        body(index, pl.ds(pl.multiple_of(index * width, width), width))
        return carry

    lax.fori_loop(0, total // width, step, 0)


def fused_kernel(sizes, layout, *refs):
    count, own_rows, width, hidden, rest, scale = sizes
    total_rows = 2 * own_rows
    r = types.SimpleNamespace(**dict(zip(layout, refs)))
    model = r.tokens.shape[1]
    streams = 5
    fulls = [getattr(r, "full%d" % i) for i in range(streams)]
    grads = [getattr(r, "grad%d" % i) for i in range(streams)]
    pairs = [getattr(r, "pair%d" % i) for i in range(streams)]
    ends = [getattr(r, "end%d" % i) for i in range(streams)]
    recvs = [getattr(r, "recv%d" % i) for i in range(streams)]
    rows = model // (2 * count)
    half = rows // 2
    turns = count // 2
    core, place = ring_place(count)
    right, left, partner = neighbours(core, place, count)
    targets = (right, left)
    me = lax.axis_index("dp")
    mine = lax.axis_index("seq")
    other = 1 - mine
    f32, bf16 = jnp.float32, jnp.bfloat16
    my_rows = pl.ds(pl.multiple_of(me * rows, rows), rows)

    def remote(src, dst, send, recv, device):
        return pltpu.make_async_remote_copy(
            src_ref=src,
            dst_ref=dst,
            send_sem=send,
            recv_sem=recv,
            device_id=device,
            device_id_type=MESH,
        )


    def piece(way, distance, stream, whole):
        shift = count - distance if way == 0 else distance
        owner = chip_at((place + shift) % count, count) * 2 + core
        if whole:
            where = pl.ds(pl.multiple_of(owner * rows, rows), rows)
        else:
            where = pl.ds(pl.multiple_of(owner * rows + way * half, half), half)
        return fulls[stream].at[where]

    def hop(way, step, stream):
        ref = piece(way, step, stream, step < turns - 1)
        sems = r.g_send.at[stream, way, step], r.g_recv.at[stream, way, step]
        return remote(ref, ref, *sems, {"dp": targets[way]})

    def share(way, step, stream):
        ref = piece(way, step, stream, step < turns)
        sems = r.gp_send.at[stream, way, step], r.gp_recv.at[stream, way, step]
        return remote(ref, ref, *sems, {"dp": partner})

    def gather_ops(stream):
        def start():
            for way in range(2):
                hop(way, 0, stream).start()
            share(0, 0, stream).start()

        def middle(step):
            for way in range(2):
                hop(way, step - 1, stream).wait_recv()
                hop(way, step, stream).start()
                share(way, step, stream).start()

        def last():
            for way in range(2):
                hop(way, turns - 1, stream).wait_recv()
                share(way, turns, stream).start()

        steps = [functools.partial(middle, step) for step in range(1, turns)]
        return [start] + steps + [last]

    def gather_shares(stream):
        return [share(0, 0, stream)] + [
            share(way, step, stream) for step in range(1, turns + 1) for way in range(2)
        ]

    def gather_arrived(stream):
        for part in gather_shares(stream):
            part.wait_recv()

    def gather_drain(stream):
        for step in range(turns):
            for way in range(2):
                hop(way, step, stream).wait_send()
        for part in gather_shares(stream):
            part.wait_send()


    def block(ahead, which):
        owner = chip_at((place + ahead) % count, count) * 2 + which
        return pl.ds(pl.multiple_of(owner * rows, rows), rows)

    def give(ahead, stream):
        return remote(
            grads[stream].at[block(ahead, 1 - core)],
            pairs[stream].at[ahead],
            r.sp_send.at[stream, ahead],
            r.sp_recv.at[stream, ahead],
            {"dp": partner},
        )

    def ahead_of(way, step):
        return turns - step if way == 0 else turns + step

    def push(way, step, stream):
        sems = r.s_send.at[stream, way, step], r.s_recv.at[stream, way, step]
        if step == 0:
            src = pairs[stream].at[turns, pl.ds(way * half, half)]
            return remote(src, ends[stream].at[way], *sems, {"dp": targets[way]})
        src = pairs[stream].at[ahead_of(way, step)]
        return remote(src, recvs[stream].at[way, step - 1], *sems, {"dp": targets[way]})

    def pair_sum(ahead, stream):
        give(ahead, stream).wait_recv()
        own = grads[stream][block(ahead, core), :].astype(f32)
        return own + pairs[stream][ahead].astype(f32)

    def scatter_ops(stream, finish):
        def start():
            order = [turns] + [turns + sign * d for d in range(1, turns) for sign in (-1, 1)] + [0]
            for ahead in order:
                give(ahead, stream).start()
            pairs[stream][turns] = pair_sum(turns, stream).astype(bf16)
            for way in range(2):
                push(way, 0, stream).start()

        def middle(step):
            for way in range(2):
                ahead = ahead_of(way, step)
                total = pair_sum(ahead, stream)
                push(way, step - 1, stream).wait_recv()
                if step == 1:
                    near = ends[stream][way].astype(f32)
                    parts = [total[:half], total[half:]]
                    parts[way] = parts[way] + near
                    total = jnp.concatenate(parts, axis=0)
                else:
                    total = total + recvs[stream][way, step - 2].astype(f32)
                pairs[stream][ahead] = total.astype(bf16)
                push(way, step, stream).start()

        def last():
            total = pair_sum(0, stream)
            for way in range(2):
                push(way, turns - 1, stream).wait_recv()
                total = total + recvs[stream][way, turns - 2].astype(f32)
            finish(total)

        steps = [functools.partial(middle, step) for step in range(1, turns)]
        return [start] + steps + [last]

    def scatter_drain(stream):
        for step in range(turns):
            for way in range(2):
                push(way, step, stream).wait_send()
        for ahead in range(count):
            give(ahead, stream).wait_send()


    def swap(index, src, dst):
        return pltpu.make_async_remote_copy(
            src_ref=src,
            dst_ref=dst,
            send_sem=r.y_send.at[index],
            recv_sem=r.y_recv.at[index],
            device_id={"seq": other},
            device_id_type=MESH,
        )

    own = pl.ds(0, own_rows)
    far = pl.ds(own_rows, own_rows)
    swaps = [
        swap(0, r.seg_own, r.seg_other),
        swap(1, r.tokens, r.tok_other),
        swap(2, r.cot, r.cot_all.at[far]),
        swap(3, r.out_send, r.out_recv),
        swap(4, r.n2.at[own], r.n2.at[far]),
        swap(5, r.down_send, r.down_recv),
        swap(6, r.dn2_send, r.dn2_recv),
        swap(7, r.dres.at[own], r.dres.at[far]),
        swap(8, r.dn1_send, r.dn1_recv),
        swap(9, r.gain_part, r.gain_recv),
    ]


    def normed(values):
        center = values - jnp.mean(values, axis=-1, keepdims=True)
        inv_std = lax.rsqrt(jnp.mean(center * center, axis=-1, keepdims=True) + EPS)
        return center * inv_std, inv_std

    def to_columns(src, dst):
        def body(index, lanes):
            dst[lanes, :] = src[:, lanes].astype(f32).T.astype(bf16)

        tiles(model, LANES, body)

    def partial_sums(terms, own_ref, send_ref):
        def body(index, lanes):
            total = sum(nt(left[...], right[lanes, :]) for left, right in terms)
            own_ref[:, lanes] = total[:own_rows]
            send_ref[:, lanes] = total[own_rows:].astype(bf16)

        tiles(model, 2 * LANES, body)

    def weight_grad(columns, right, out, at=0):
        size = right.shape[1]

        def body(index, lanes):
            value = nn(columns[...], right[:, lanes]).astype(bf16)
            out[:, pl.ds(pl.multiple_of(at + index * 2 * LANES, LANES), 2 * LANES)] = value

        tiles(size, 2 * LANES, body)

    blocks = width // LANES
    hidden_blocks = hidden // LANES
    lane = lax.broadcasted_iota(jnp.int32, (total_rows, LANES), 1)
    low_half = lane % (2 * HEAD_HALF) < HEAD_HALF
    first = lane < 2 * HEAD_HALF

    def setup():
        r.cos[own, :] = r.cos_table[pl.ds(pl.multiple_of(mine * own_rows, own_rows), own_rows), :]
        r.cos[far, :] = r.cos_table[pl.ds(pl.multiple_of(other * own_rows, own_rows), own_rows), :]
        r.sin[own, :] = r.sin_table[pl.ds(pl.multiple_of(mine * own_rows, own_rows), own_rows), :]
        r.sin[far, :] = r.sin_table[pl.ds(pl.multiple_of(other * own_rows, own_rows), own_rows), :]

    def position(dim):
        index = lax.broadcasted_iota(jnp.int32, (total_rows, total_rows), dim)
        return jnp.where(index < own_rows, index + mine * own_rows, index - mine * own_rows)

    def make_bias():
        seg_row = jnp.concatenate([r.seg_own[0:1, :], r.seg_other[0:1, :]], axis=1).astype(f32)
        across = jnp.broadcast_to(seg_row, (total_rows, total_rows))
        allowed = (jnp.abs(position(0) - position(1)) <= HALO) & (across == across.T)
        r.bias[...] = jnp.where(allowed, 0.0, NEG_FILL)

    def expand_special():
        spot = lax.broadcasted_iota(jnp.int32, (2 * LANES, LANES), 1)
        keep = spot < rest

        def body(index, here):
            part = fulls[1][here, 2 * width : 2 * width + LANES].astype(f32)
            r.gains[:, here] = part.T[3 * rest : 3 * rest + 8]
            r.sp_in[here, :LANES] = jnp.where(keep, part, 0.0).astype(bf16)
            r.sp_in[here, LANES:] = jnp.where(
                keep, pltpu.roll(part, LANES - rest, 1), 0.0
            ).astype(bf16)
            r.sp_down[here, :] = jnp.where(
                keep, pltpu.roll(part, LANES - 2 * rest, 1), 0.0
            ).astype(bf16)

        tiles(model, 2 * LANES, body)

    def attn_gain():
        return r.gains[0:1, :] + r.gains[1:2, :]

    def mlp_gain():
        return r.gains[2:3, :] + r.gains[3:4, :]

    def norm_one():
        for src, place_of in ((r.tokens, 0), (r.tok_other, own_rows)):
            def body(index, here):
                unit_rows, _ = normed(src[here, :].astype(f32))
                at = pl.ds(pl.multiple_of(index * 32 + place_of, 32), 32)
                r.n1[at, :] = (unit_rows * attn_gain()).astype(bf16)

            tiles(own_rows, 32, body)

    def values_of():
        def body(index, lanes):
            r.v[:, lanes] = nn(r.n1[...], fulls[1][:, lanes]).astype(bf16)

        tiles(width, 2 * LANES, body)

    def attend(index, wide, lanes):
        cos_table, sin_table = r.cos[...], r.sin[...]
        proj = nn(r.n1[...], fulls[0][:, wide])
        queries = turn(proj[:, :LANES], cos_table, sin_table, low_half)
        keys = turn(proj[:, LANES:], cos_table, sin_table, low_half).astype(bf16)
        r.qk[:, wide] = jnp.concatenate([queries.astype(bf16), keys], axis=1)
        values = r.v[:, lanes].astype(f32)
        mixed = jnp.zeros((total_rows, LANES), f32)
        for head in range(2):
            here = first if head == 0 else ~first
            scores = nt(jnp.where(here, queries, 0.0).astype(bf16), keys) * scale + r.bias[...]
            top_score = jnp.max(scores, axis=-1, keepdims=True)
            total = jnp.sum(jnp.exp(scores - top_score), axis=-1, keepdims=True)
            probs = jnp.exp(scores - (top_score + jnp.log(total)))
            r.probs[index * 2 + head] = probs
            mixed = mixed + nn(probs.astype(bf16), jnp.where(here, values, 0.0).astype(bf16))
        r.mixed[:, lanes] = mixed.astype(bf16)

    def attend_back(index, wide, lanes):
        cos_table, sin_table = r.cos[...], -r.sin[...]
        both = r.qk[:, wide]
        queries = both[:, :LANES].astype(f32)
        keys = both[:, LANES:].astype(f32)
        values = r.v[:, lanes]
        dmixed = r.dmixed[:, lanes].astype(f32)
        products = dmixed * r.mixed[:, lanes].astype(f32)
        dquery = jnp.zeros((total_rows, LANES), f32)
        dkey = jnp.zeros((total_rows, LANES), f32)
        dvalue = jnp.zeros((total_rows, LANES), f32)
        for head in range(2):
            here = first if head == 0 else ~first
            head_queries = jnp.where(here, queries, 0.0).astype(bf16)
            head_keys = jnp.where(here, keys, 0.0).astype(bf16)
            head_dmixed = jnp.where(here, dmixed, 0.0).astype(bf16)
            delta = jnp.sum(jnp.where(here, products, 0.0), axis=-1, keepdims=True)
            probs = r.probs[index * 2 + head]
            dprobs = nt(head_dmixed, values)
            dscores = (probs * (dprobs - delta) * scale).astype(bf16)
            dvalue = dvalue + lax.dot_general(
                probs.astype(bf16), head_dmixed, OVER_ROWS, preferred_element_type=f32
            )
            dkey = dkey + lax.dot_general(
                dscores, head_queries, OVER_ROWS, preferred_element_type=f32
            )
            dquery = dquery + nn(dscores, head_keys)
        dquery = turn(dquery, cos_table, sin_table, low_half)
        dkey = turn(dkey, cos_table, sin_table, low_half)
        r.dqk[:, wide] = jnp.concatenate([dquery, dkey], axis=1).astype(bf16)
        r.dv[:, lanes] = dvalue.astype(bf16)

    def over_heads(body, start, stop):
        def step(index, carry):
            body(
                index,
                pl.ds(pl.multiple_of(index * 2 * LANES, 2 * LANES), 2 * LANES),
                pl.ds(pl.multiple_of(index * LANES, LANES), LANES),
            )
            return carry

        lax.fori_loop(start, stop, step, 0)

    def norm_two():
        def body(index, here):
            residual = (
                r.tokens[here, :].astype(f32)
                + r.acc[here, :]
                + r.out_recv[here, :].astype(f32)
            )
            r.residual[here, :] = residual
            unit_rows, _ = normed(residual)
            r.n2[here, :] = (unit_rows * mlp_gain()).astype(bf16)

        tiles(own_rows, 32, body)

    def expand_tile(weight, at):
        both = nn(r.n2[...], weight)
        gate, linear = both[:, :LANES], both[:, LANES:]
        erf_part = 0.5 * (1.0 + lax.erf(gate * 0.7071067811865476))
        active = gate * erf_part
        slope = erf_part + gate * jnp.exp(-0.5 * gate * gate) * 0.3989422804014327
        r.mid[:, at] = (active * linear).astype(bf16)
        r.act[:, at] = active
        r.slope[:, at] = linear * slope

    def expand_stream(stream, offset):
        def body(index, lanes):
            at = pl.ds(pl.multiple_of((index + offset) * LANES, LANES), LANES)
            expand_tile(fulls[stream][:, lanes], at)

        tiles(fulls[stream].shape[1], 2 * LANES, body)

    spare = pl.ds(hidden, LANES)

    def dexpand(weight, at, to):
        dmiddle = nn(r.cot_all[...], weight)
        dgate = (dmiddle * r.slope[:, at]).astype(bf16)
        dlinear = (dmiddle * r.act[:, at]).astype(bf16)
        parts = []
        for start in range(0, dmiddle.shape[1], LANES):
            parts += [dgate[:, start : start + LANES], dlinear[:, start : start + LANES]]
        r.dexp[:, to] = jnp.concatenate(parts, axis=1)

    def dexpand_all():
        def body(index, lanes):
            to = pl.ds(pl.multiple_of(index * 4 * LANES, 4 * LANES), 4 * LANES)
            dexpand(fulls[4][:, lanes], lanes, to)

        tiles(hidden, 2 * LANES, body)
        dexpand(r.sp_down[...], spare, pl.ds(2 * hidden, 2 * LANES))

    split = fulls[2].shape[1]
    dexp_parts = [
        r.dexp.at[:, pl.ds(0, split)],
        r.dexp.at[:, pl.ds(split, 2 * hidden - split)],
        r.dexp.at[:, pl.ds(2 * hidden, 2 * LANES)],
    ]

    def special_grad():
        spot = lax.broadcasted_iota(jnp.int32, (2 * LANES, LANES), 1)

        def body(index, here):
            both = nn(r.n2_col[here, :], dexp_parts[2][...])
            down = nn(r.cot_col[here, :], r.mid[:, spare])
            value = jnp.where(
                spot < rest,
                both[:, :LANES],
                jnp.where(
                    spot < 2 * rest,
                    pltpu.roll(both[:, LANES:], rest, 1),
                    jnp.where(spot < 3 * rest, pltpu.roll(down, 2 * rest, 1), 0.0),
                ),
            )
            grads[1][here, 2 * width : 2 * width + LANES] = value.astype(bf16)

        tiles(model, 2 * LANES, body)

    def back_through_norm(grad_rows, gain, values):
        unit_rows, inv_std = normed(values)
        scaled = grad_rows * gain
        inner = (
            scaled
            - jnp.mean(scaled, axis=-1, keepdims=True)
            - unit_rows * jnp.mean(scaled * unit_rows, axis=-1, keepdims=True)
        )
        return inner * inv_std, jnp.sum(grad_rows * unit_rows, axis=0, keepdims=True)

    def norm_two_back():
        r.gain_part[...] = jnp.zeros_like(r.gain_part)

        def body(index, here):
            grad_rows = r.acc[here, :] + r.dn2_recv[here, :].astype(f32)
            part, gain_sum = back_through_norm(grad_rows, mlp_gain(), r.residual[here, :])
            dresidual = r.cot[here, :].astype(f32) + part
            r.dres_own[here, :] = dresidual
            r.dres[here, :] = dresidual.astype(bf16)
            r.gain_part[1:2, :] += gain_sum

        tiles(own_rows, 32, body)

    def norm_one_back():
        def body(index, here):
            grad_rows = r.acc[here, :] + r.dn1_recv[here, :].astype(f32)
            part, gain_sum = back_through_norm(
                grad_rows, attn_gain(), r.tokens[here, :].astype(f32)
            )
            r.tokens_grad[0, here, :] = (r.dres_own[here, :] + part).astype(bf16)
            r.gain_part[0:1, :] += gain_sum

        tiles(own_rows, 32, body)

    def layer_out():
        def body(index, here):
            r.layer_out[0, here, :] = (
                r.residual[here, :]
                + r.down_acc[here, :]
                + r.down_recv[here, :].astype(f32)
            ).astype(bf16)

        tiles(own_rows, 32, body)

    def gain_columns():
        spot = lax.broadcasted_iota(jnp.int32, (LANES, 2 * LANES), 0)

        def body(index, here):
            sums = r.gain_part[:, here] + r.gain_recv[:, here]
            value = jnp.where(
                spot == 3 * rest, sums[0:1], jnp.where(spot == 3 * rest + 1, sums[1:2], 0.0)
            ).T
            old = grads[1][here, 2 * width : 2 * width + LANES].astype(f32)
            grads[1][here, 2 * width : 2 * width + LANES] = (old + value).astype(bf16)

        tiles(model, 2 * LANES, body)

    def dmixed_of():
        def body(index, lanes):
            at = pl.ds(pl.multiple_of(width + index * 2 * LANES, 2 * LANES), 2 * LANES)
            r.dmixed[:, lanes] = nn(r.dres[...], fulls[1][:, at]).astype(bf16)

        tiles(width, 2 * LANES, body)


    def pack_first():
        for at in range(0, width, LANES):
            for which in range(2):
                to = 2 * at + which * LANES
                fulls[0][my_rows, to : to + LANES] = r.raw_qkv[:, which, at : at + LANES]
        fulls[1][my_rows, :width] = r.raw_qkv[:, 2, :]
        fulls[1][my_rows, width : 2 * width] = r.raw_out[...].astype(f32).T.astype(bf16)
        spot = lax.broadcasted_iota(jnp.int32, (LANES, rows), 0)
        gain_parts = []
        for gain in (r.attn_gain[...], r.mlp_gain[...]):
            spread = gain * 65537.0
            high = spread - (spread - gain)
            gain_parts += [high, gain - high]
        gains = jnp.zeros((LANES, rows), f32)
        for index, part in enumerate(gain_parts):
            gains = jnp.where(spot == 3 * rest + index, part, gains)
        if rest:
            parts = [
                r.raw_in[:, 0, hidden:].astype(f32),
                r.raw_in[:, 1, hidden:].astype(f32),
                r.raw_down[hidden:, :].astype(f32).T,
                jnp.zeros((rows, LANES - 3 * rest), f32),
            ]
            special = jnp.concatenate(parts, axis=1) + gains.T
        else:
            special = gains.T
        fulls[1][my_rows, 2 * width :] = special.astype(bf16)

    def pack_second():
        for at in range(0, hidden, LANES):
            stream, to = (2, 2 * at) if at < split // 2 else (3, 2 * at - split)
            for which in range(2):
                start = to + which * LANES
                fulls[stream][my_rows, start : start + LANES] = r.raw_in[:, which, at : at + LANES]
        fulls[4][my_rows, :] = r.raw_down[:hidden, :].astype(f32).T.astype(bf16)


    def finish_keys(total):
        for at in range(0, width, LANES):
            for which in range(2):
                to = 2 * at + which * LANES
                r.qkv_grad[:, which, at : at + LANES] = total[:, to : to + LANES]

    def finish_values(total):
        r.qkv_grad[:, 2, :] = total[:, :width]
        r.out_grad[...] = total[:, width : 2 * width].T
        special = total[:, 2 * width :]
        turned = special.T
        r.attn_gain_grad[...] = turned[3 * rest : 3 * rest + 1]
        r.mlp_gain_grad[...] = turned[3 * rest + 1 : 3 * rest + 2]
        if rest:
            r.in_grad[:, 0, hidden:] = special[:, :rest]
            r.in_grad[:, 1, hidden:] = special[:, rest : 2 * rest]
            r.down_grad[hidden:, :] = turned[2 * rest : 3 * rest]

    def finish_in(start):
        def finish(total):
            for at in range(0, total.shape[1], 2 * LANES):
                to = start + at // 2
                r.in_grad[:, 0, to : to + LANES] = total[:, at : at + LANES]
                r.in_grad[:, 1, to : to + LANES] = total[:, at + LANES : at + 2 * LANES]

        return finish

    def finish_down(total):
        r.down_grad[:hidden, :] = total.T

    gathers = [gather_ops(stream) for stream in range(streams)]
    finishes = [finish_keys, finish_values, finish_in(0), finish_in(split // 2), finish_down]
    scatters = [scatter_ops(stream, finishes[stream]) for stream in range(streams)]

    def go(ops, *chosen):
        for stream in chosen:
            if ops[stream]:
                ops[stream].pop(0)()

    def end(ops, *chosen):
        while any(ops[stream] for stream in chosen):
            go(ops, *chosen)


    loads = [
        pltpu.make_async_copy(src, dst, r.own_sem.at[index])
        for index, (src, dst) in enumerate(
            [
                (r.in_qkv, r.raw_qkv),
                (r.in_out, r.raw_out),
                (r.in_in, r.raw_in),
                (r.in_down, r.raw_down),
                (r.in_tokens.at[0], r.tokens),
                (r.in_cot.at[0], r.cot),
            ]
        )
    ]
    for load in loads:
        load.start()
    barrier = pltpu.get_barrier_semaphore()
    for device in (right, left, partner):
        pl.semaphore_signal(barrier, inc=1, device_id={"dp": device}, device_id_type=MESH)
    pl.semaphore_signal(barrier, inc=1, device_id={"seq": other}, device_id_type=MESH)
    r.seg_own[...] = jnp.broadcast_to(r.seg[...], r.seg_own.shape)
    for load in loads:
        load.wait()
    pack_first()
    pl.semaphore_wait(barrier, 4)
    go(gathers, 0, 1)
    for index in range(3):
        swaps[index].start()
    pack_second()
    r.cot_all[own, :] = r.cot[...]
    setup()
    go(gathers, 0, 1)
    for index in range(3):
        swaps[index].wait_recv()
    make_bias()
    go(gathers, 0, 1)
    to_columns(r.cot_all, r.cot_col)
    while len(gathers[0]) > 1:
        go(gathers, 0, 1)
    go(gathers, 2, 3)
    end(gathers, 0, 1)
    gather_arrived(0)
    gather_arrived(1)

    expand_special()
    norm_one()
    values_of()
    over_heads(attend, 0, blocks // 2)
    go(gathers, 2, 3)
    over_heads(attend, blocks // 2, blocks)
    partial_sums(
        [(r.mixed, fulls[1].at[:, pl.ds(width, width)])], r.acc, r.out_send
    )
    swaps[3].start()
    go(gathers, 2, 3, 4)
    to_columns(r.n1, r.n1_col)
    swaps[3].wait_recv()
    norm_two()
    swaps[4].start()
    while len(gathers[2]) > 1:
        go(gathers, 2, 3, 4)
    swaps[4].wait_recv()
    to_columns(r.n2, r.n2_col)
    end(gathers, 2, 3)
    go(gathers, 4)
    gather_arrived(2)
    expand_stream(2, 0)
    go(gathers, 4)
    gather_arrived(3)
    expand_stream(3, split // (2 * LANES))
    expand_tile(r.sp_in[...], spare)
    end(gathers, 4)
    weight_grad(r.cot_col, r.mid.at[:, pl.ds(0, hidden)], grads[4])
    go(scatters, 4)
    gather_arrived(4)

    dexpand_all()
    partial_sums(
        [
            (dexp_parts[0], fulls[2]),
            (dexp_parts[1], fulls[3]),
            (dexp_parts[2], r.sp_in),
        ],
        r.acc,
        r.dn2_send,
    )
    swaps[6].start()
    weight_grad(r.n2_col, dexp_parts[0], grads[2])
    go(scatters, 2)
    go(scatters, 4)
    weight_grad(r.n2_col, dexp_parts[1], grads[3])
    go(scatters, 3)
    special_grad()
    swaps[6].wait_recv()
    norm_two_back()
    swaps[7].start()
    go(scatters, 4, 2, 3)
    partial_sums(
        [
            (r.mid.at[:, pl.ds(0, hidden)], fulls[4]),
            (r.mid.at[:, spare], r.sp_down),
        ],
        r.down_acc,
        r.down_send,
    )
    swaps[5].start()
    go(scatters, 4)
    swaps[7].wait_recv()
    to_columns(r.dres, r.dres_col)
    dmixed_of()
    go(scatters, 2, 3)
    over_heads(attend_back, 0, blocks // 2)
    end(scatters, 4)
    over_heads(attend_back, blocks // 2, blocks)
    partial_sums(
        [(r.dqk, fulls[0]), (r.dv, fulls[1].at[:, pl.ds(0, width)])],
        r.acc,
        r.dn1_send,
    )
    swaps[8].start()
    go(scatters, 2, 3)
    weight_grad(r.n1_col, r.dqk, grads[0])
    go(scatters, 0)
    weight_grad(r.dres_col, r.mixed, grads[1], width)
    weight_grad(r.n1_col, r.dv, grads[1])
    end(scatters, 2, 3)
    swaps[8].wait_recv()
    norm_one_back()
    swaps[9].start()
    go(scatters, 0)
    swaps[5].wait_recv()
    layer_out()
    swaps[9].wait_recv()
    gain_columns()
    go(scatters, 1)
    end(scatters, 0, 1)

    for stream in range(streams):
        gather_drain(stream)
        scatter_drain(stream)
    for exchange in swaps:
        exchange.wait_send()


def fused_call(inputs, tables, devices, widths):
    names, arrays = zip(*inputs.items())
    whole = dict(inputs)
    count = devices // 2
    own_rows, model = whole["in_tokens"].shape[1:]
    total = 2 * own_rows
    rows, _, width = whole["in_qkv"].shape
    local_hidden = whole["in_in"].shape[2]
    rest = local_hidden % LANES
    hidden = local_hidden - rest
    half = rows // 2
    turns = count // 2
    f32, bf16 = jnp.float32, jnp.bfloat16
    streams = len(widths)
    heads = width // (2 * HEAD_HALF)
    outs = dict(
        layer_out=((1, own_rows, model), bf16),
        tokens_grad=((1, own_rows, model), bf16),
        qkv_grad=((rows, 3, width), f32),
        out_grad=((width, rows), f32),
        in_grad=((rows, 2, local_hidden), f32),
        down_grad=((local_hidden, rows), f32),
        attn_gain_grad=((1, rows), f32),
        mlp_gain_grad=((1, rows), f32),
    )
    shapes = dict(
        tokens=((own_rows, model), bf16),
        cot=((own_rows, model), bf16),
        seg_own=((8, own_rows), jnp.int32),
        seg_other=((8, own_rows), jnp.int32),
        raw_qkv=((rows, 3, width), bf16),
        raw_out=((width, rows), bf16),
        raw_in=((rows, 2, local_hidden), bf16),
        raw_down=((local_hidden, rows), bf16),
        tok_other=((own_rows, model), bf16),
        cot_all=((total, model), bf16),
        cot_col=((model, total), bf16),
        n1=((total, model), bf16),
        n1_col=((model, total), bf16),
        gains=((8, model), f32),
        cos=((total, LANES), f32),
        sin=((total, LANES), f32),
        bias=((total, total), f32),
        sp_in=((model, 2 * LANES), bf16),
        sp_down=((model, LANES), bf16),
        v=((total, width), bf16),
        qk=((total, 2 * width), bf16),
        probs=((heads, total, total), f32),
        mixed=((total, width), bf16),
        acc=((own_rows, model), f32),
        down_acc=((own_rows, model), f32),
        out_send=((own_rows, model), bf16),
        out_recv=((own_rows, model), bf16),
        down_send=((own_rows, model), bf16),
        down_recv=((own_rows, model), bf16),
        dn2_send=((own_rows, model), bf16),
        dn2_recv=((own_rows, model), bf16),
        dn1_send=((own_rows, model), bf16),
        dn1_recv=((own_rows, model), bf16),
        residual=((own_rows, model), f32),
        n2=((total, model), bf16),
        n2_col=((model, total), bf16),
        mid=((total, hidden + LANES), bf16),
        act=((total, hidden + LANES), f32),
        slope=((total, hidden + LANES), f32),
        dexp=((total, 2 * hidden + 2 * LANES), bf16),
        dres_own=((own_rows, model), f32),
        dres=((total, model), bf16),
        dres_col=((model, total), bf16),
        dmixed=((total, width), bf16),
        dqk=((total, 2 * width), bf16),
        dv=((total, width), bf16),
        gain_part=((8, model), f32),
        gain_recv=((8, model), f32),
    )
    for i, w in enumerate(widths):
        shapes["full%d" % i] = ((model, w), bf16)
        shapes["grad%d" % i] = ((model, w), bf16)
        shapes["pair%d" % i] = ((count, rows, w), bf16)
        shapes["end%d" % i] = ((2, half, w), bf16)
        shapes["recv%d" % i] = ((2, turns - 1, rows, w), bf16)
    scratch = {name: pltpu.VMEM(shape, dtype) for name, (shape, dtype) in shapes.items()}
    semaphores = dict(
        own_sem=(6,),
        g_send=(streams, 2, turns),
        g_recv=(streams, 2, turns),
        gp_send=(streams, 2, turns + 1),
        gp_recv=(streams, 2, turns + 1),
        s_send=(streams, 2, turns),
        s_recv=(streams, 2, turns),
        sp_send=(streams, count),
        sp_recv=(streams, count),
        y_send=(10,),
        y_recv=(10,),
    )
    for name, shape in semaphores.items():
        scratch[name] = pltpu.SemaphoreType.DMA(shape)
    vmem = pl.BlockSpec(memory_space=pltpu.VMEM)
    anywhere = pl.BlockSpec(memory_space=pl.ANY)
    sizes = (count, own_rows, width, hidden, rest, 1.0 / math.sqrt(2 * HEAD_HALF))
    layout = list(names) + ["cos_table", "sin_table"] + list(outs) + list(scratch)
    big = 6
    return pl.pallas_call(
        functools.partial(fused_kernel, sizes, layout),
        out_shape=[jax.ShapeDtypeStruct(shape, dtype) for shape, dtype in outs.values()],
        in_specs=[anywhere] * big + [vmem] * (len(layout) - big - len(outs) - len(scratch)),
        out_specs=[vmem] * len(outs),
        scratch_shapes=list(scratch.values()),
        compiler_params=pltpu.CompilerParams(
            collective_id=2, has_side_effects=True, vmem_limit_bytes=FUSED_LIMIT
        ),
        name="fused_layer",
    )(*arrays, *tables)


FUSED_LIMIT = 63 * 1024 * 1024


def position_tables(total, head_size):
    half_size = head_size // 2
    freqs = THETA ** (-(2.0 / head_size) * np.arange(half_size))
    angles = np.arange(total)[:, None] * freqs[None, :]
    cos_table = np.cos(angles).astype(np.float32)
    sin_table = np.sin(angles).astype(np.float32)
    return (
        jnp.asarray(np.concatenate([cos_table] * 4, axis=1)),
        jnp.asarray(np.concatenate([-sin_table, sin_table] * 2, axis=1)),
    )


def fused_device(
    devices,
    tokens,
    segments,
    cotangent,
    qkv_weight,
    out_weight,
    in_weight,
    down_weight,
    attn_gain,
    mlp_gain,
):
    own_rows = tokens.shape[1]
    width = qkv_weight.shape[2]
    blocks = in_weight.shape[2] // LANES
    first = blocks // 2 * 2 * LANES
    widths = [2 * width, 2 * width + LANES, first, 2 * blocks * LANES - first, blocks * LANES]
    inputs = dict(
        in_qkv=qkv_weight,
        in_out=out_weight,
        in_in=in_weight,
        in_down=down_weight,
        in_tokens=tokens,
        in_cot=cotangent,
        seg=segments,
        attn_gain=attn_gain[None],
        mlp_gain=mlp_gain[None],
    )
    tables = position_tables(2 * own_rows, 2 * HEAD_HALF)
    *results, attn_grad, mlp_grad = fused_call(inputs, tables, devices, widths)
    return (*results, attn_grad[0], mlp_grad[0])


def per_device(
    devices,
    seq_size,
    tokens,
    segments,
    cotangent,
    qkv_weight,
    out_weight,
    in_weight,
    down_weight,
    attn_gain,
    mlp_gain,
):
    args = (
        tokens,
        segments,
        cotangent,
        qkv_weight,
        out_weight,
        in_weight,
        down_weight,
        attn_gain,
        mlp_gain,
    )
    own_rows, model = tokens.shape[1:]
    sizes = (own_rows, model, qkv_weight.shape[2], in_weight.shape[2])
    if fits_fused(devices, seq_size, *sizes) and tokens.shape[0] == 1:
        return fused_device(devices, *args)
    return general_device(devices, seq_size, *args)


def solution(mesh):
    return jax.shard_map(
        functools.partial(per_device, mesh.shape["dp"], mesh.shape["seq"]),
        mesh=mesh,
        in_specs=(
            P("dp", "seq", None),
            P("dp", "seq"),
            P("dp", "seq", None),
            P("dp", None, "seq"),
            P("seq", "dp"),
            P("dp", None, "seq"),
            P("seq", "dp"),
            P("dp"),
            P("dp"),
        ),
        out_specs=(
            P("dp", "seq", None),
            P("dp", "seq", None),
            P("dp", None, "seq"),
            P("seq", "dp"),
            P("dp", None, "seq"),
            P("seq", "dp"),
            P("dp"),
            P("dp"),
        ),
        check_vma=False,
    )
```

```python
import functools
import math
import types

import jax
import jax.numpy as jnp
import numpy as np
from jax import lax
from jax.experimental import pallas as pl
from jax.experimental.pallas import tpu as pltpu
from jax.sharding import PartitionSpec as P

HEADS = 16
HALO = 64


EPS = 1e-05
THETA = 10000.0
NEG_FILL = -1e30


def norm_forward(values, gain):
    center = values - jnp.mean(values, axis=-1, keepdims=True)
    inv_std = lax.rsqrt(jnp.mean(center * center, axis=-1, keepdims=True) + EPS)
    unit_rows = center * inv_std
    return (unit_rows * gain, unit_rows, inv_std)


def norm_backward(grad_rows, gain, unit_rows, inv_std):
    scaled = grad_rows * gain
    inner = (
        scaled
        - jnp.mean(scaled, axis=-1, keepdims=True)
        - unit_rows * jnp.mean(scaled * unit_rows, axis=-1, keepdims=True)
    )
    return (inner * inv_std, jnp.sum(grad_rows * unit_rows, axis=0))


def gelu_value(inputs):
    return 0.5 * inputs * (1.0 + lax.erf(inputs * 0.7071067811865476))


def gelu_slope(inputs):
    return (
        0.5 * (1.0 + lax.erf(inputs * 0.7071067811865476))
        + inputs * jnp.exp(-0.5 * inputs * inputs) * 0.3989422804014327
    )


def rotary_tables(positions, head_size):
    half_size = head_size // 2
    freqs = jnp.power(THETA, -(2.0 / head_size) * jnp.arange(half_size, dtype=jnp.float32))
    angles = positions.astype(jnp.float32)[:, None] * freqs[None, :]
    return (jnp.cos(angles)[:, None, :], jnp.sin(angles)[:, None, :])


def rotate(values, cos_table, sin_table):
    half_size = values.shape[-1] // 2
    lower_half = values[..., :half_size]
    upper_half = values[..., half_size:]
    return jnp.concatenate(
        [
            lower_half * cos_table - upper_half * sin_table,
            upper_half * cos_table + lower_half * sin_table,
        ],
        axis=-1,
    )


def unrotate(grads, cos_table, sin_table):
    half_size = grads.shape[-1] // 2
    lower_half = grads[..., :half_size]
    upper_half = grads[..., half_size:]
    return jnp.concatenate(
        [
            lower_half * cos_table + upper_half * sin_table,
            upper_half * cos_table - lower_half * sin_table,
        ],
        axis=-1,
    )


def window_mask(query_pos, key_pos, query_seg, key_seg, halo_width, total_len):
    near = jnp.abs(query_pos[:, None] - key_pos[None, :]) <= halo_width
    inside = (key_pos >= 0) & (key_pos < total_len)
    return near & inside[None, :] & (query_seg[:, None] == key_seg[None, :])


def block_scores(queries, key_slab, allowed, scale):
    scores = (
        jnp.einsum("qhd,khd->hqk", queries, key_slab, preferred_element_type=jnp.float32) * scale
    )
    return jnp.where(allowed[None], scores, NEG_FILL)


def attend_block(queries, key_slab, value_slab, allowed, scale):
    scores = block_scores(queries, key_slab, allowed, scale)
    top_score = jnp.max(scores, axis=-1, keepdims=True)
    total = jnp.sum(jnp.exp(scores - top_score), axis=-1, keepdims=True)
    logsum = top_score + jnp.log(total)
    probs = jnp.exp(scores - logsum).astype(jnp.bfloat16)
    mixed = jnp.einsum("hqk,khd->qhd", probs, value_slab, preferred_element_type=jnp.float32)
    return (mixed, logsum[..., 0])


def attend_back(queries, key_slab, value_slab, allowed, scale, logsum, mixed_b, dmixed_b):
    scores = block_scores(queries, key_slab, allowed, scale)
    probs = jnp.exp(scores - logsum[..., None])
    probs_b = probs.astype(jnp.bfloat16)
    dvalues = jnp.einsum("hqk,qhd->khd", probs_b, dmixed_b, preferred_element_type=jnp.float32)
    dprobs = jnp.einsum("qhd,khd->hqk", dmixed_b, value_slab, preferred_element_type=jnp.float32)
    delta = jnp.transpose(
        jnp.sum(dmixed_b.astype(jnp.float32) * mixed_b.astype(jnp.float32), axis=-1)
    )
    dscores = (probs * (dprobs - delta[..., None]) * scale).astype(jnp.bfloat16)
    dqueries = jnp.einsum("hqk,khd->qhd", dscores, key_slab, preferred_element_type=jnp.float32)
    dkeys = jnp.einsum("hqk,qhd->khd", dscores, queries, preferred_element_type=jnp.float32)
    return (dqueries, dkeys, dvalues)


MESH = pl.DeviceIdType.MESH
VMEM_LIMIT = 60 * 1024 * 1024
LANES = 128


def ring_place(count):
    me = lax.axis_index("dp")
    core = me % 2
    chip = me // 2
    row, column = chip // 2, chip % 2
    place = (1 - column) * row + column * (count - 1 - row)
    return (core, place)


def chip_at(place, count):
    side = place // (count // 2)
    return (1 - side) * (2 * place) + side * (2 * (count - 1 - place) + 1)


def neighbours(core, place, count):
    right = chip_at((place + 1) % count, count) * 2 + core
    left = chip_at((place + count - 1) % count, count) * 2 + core
    return (right, left, lax.axis_index("dp") + 1 - 2 * core)


def greet(devices):
    barrier = pltpu.get_barrier_semaphore()
    for device in devices:
        pl.semaphore_signal(barrier, inc=1, device_id={"dp": device}, device_id_type=MESH)
    pl.semaphore_wait(barrier, len(devices))


def gather_kernel(count, streams, *refs):
    shards = refs[:streams]
    fulls = refs[streams : 2 * streams]
    own_sem, send_sem, recv_sem, pair_send, pair_recv = refs[2 * streams :]
    rows = shards[0].shape[0]
    half = rows // 2
    core, place = ring_place(count)
    right, left, partner = neighbours(core, place, count)
    targets = (right, left)
    lanes = [(way, stream) for stream in range(streams) for way in range(2)]

    def piece(way, step, stream):
        shift = count - step if way == 0 else step
        owner = chip_at((place + shift) % count, count) * 2 + core
        start = pl.multiple_of(owner * rows + way * half, half)
        return fulls[stream].at[pl.ds(start, half)]

    def hop(way, step, stream):
        ref = piece(way, step, stream)
        return pltpu.make_async_remote_copy(
            src_ref=ref,
            dst_ref=ref,
            send_sem=send_sem.at[stream, way, step],
            recv_sem=recv_sem.at[stream, way, step],
            device_id={"dp": targets[way]},
            device_id_type=MESH,
        )

    def share(way, step, stream):
        ref = piece(way, step, stream)
        return pltpu.make_async_remote_copy(
            src_ref=ref,
            dst_ref=ref,
            send_sem=pair_send.at[stream, way, step],
            recv_sem=pair_recv.at[stream, way, step],
            device_id={"dp": partner},
            device_id_type=MESH,
        )

    me = lax.axis_index("dp")
    owns = [
        pltpu.make_async_copy(
            shards[stream],
            fulls[stream].at[pl.ds(pl.multiple_of(me * rows, rows), rows)],
            own_sem.at[stream],
        )
        for stream in range(streams)
    ]
    for own in owns:
        own.start()
    greet((right, left, partner))
    for own in owns:
        own.wait()
    for way, stream in lanes:
        hop(way, 0, stream).start()
        share(way, 0, stream).start()

    def step_body(step, carry):
        for way, stream in lanes:
            hop(way, step - 1, stream).wait_recv()
            hop(way, step, stream).start()
            share(way, step, stream).start()
        return carry

    lax.fori_loop(1, count - 1, step_body, 0)
    for way, stream in lanes:
        hop(way, count - 2, stream).wait_recv()
        share(way, count - 1, stream).start()

    def drain_hops(step, carry):
        for way, stream in lanes:
            hop(way, step, stream).wait_send()
        return carry

    def drain_shares(step, carry):
        for way, stream in lanes:
            share(way, step, stream).wait_send()
            share(way, step, stream).wait_recv()
        return carry

    lax.fori_loop(0, count - 1, drain_hops, 0)
    lax.fori_loop(0, count, drain_shares, 0)


def ring_gather(shards, devices):
    count = devices // 2
    streams = len(shards)
    return pl.pallas_call(
        functools.partial(gather_kernel, count, streams),
        out_shape=[
            jax.ShapeDtypeStruct((devices * shard.shape[0], shard.shape[1]), shard.dtype)
            for shard in shards
        ],
        in_specs=[pl.BlockSpec(memory_space=pltpu.VMEM)] * streams,
        out_specs=[pl.BlockSpec(memory_space=pl.ANY)] * streams,
        scratch_shapes=[pltpu.SemaphoreType.DMA((streams,))]
        + [pltpu.SemaphoreType.DMA((streams, 2, count - 1))] * 2
        + [pltpu.SemaphoreType.DMA((streams, 2, count))] * 2,
        cost_estimate=pl.CostEstimate(
            flops=0, bytes_accessed=128 * 1024 * 1024, transcendentals=0
        ),
        compiler_params=pltpu.CompilerParams(
            collective_id=0, has_side_effects=True, vmem_limit_bytes=VMEM_LIMIT
        ),
        name="ring_gather",
    )(*shards)


def scatter_kernel(count, streams, *refs):
    grads = refs[:streams]
    outs = refs[streams : 2 * streams]
    pairs = refs[2 * streams : 3 * streams]
    sends = refs[3 * streams : 4 * streams]
    recvs = refs[4 * streams : 5 * streams]
    send_sem, recv_sem, pair_send, pair_recv = refs[5 * streams :]
    rows = outs[0].shape[0]
    half = rows // 2
    core, place = ring_place(count)
    right, left, partner = neighbours(core, place, count)
    targets = (right, left)

    def block(way, step, which):
        shift = 2 * count - 1 - step if way == 0 else 1 + step
        owner = chip_at((place + shift) % count, count) * 2 + which
        return pl.ds(pl.multiple_of(owner * rows + way * half, half), half)

    def share(way, step, stream):
        return pltpu.make_async_remote_copy(
            src_ref=grads[stream].at[block(way, step, 1 - core)],
            dst_ref=pairs[stream].at[way, step],
            send_sem=pair_send.at[stream, way, step],
            recv_sem=pair_recv.at[stream, way, step],
            device_id={"dp": partner},
            device_id_type=MESH,
        )

    def hop(way, step, stream):
        return pltpu.make_async_remote_copy(
            src_ref=sends[stream].at[way, step],
            dst_ref=recvs[stream].at[way, step],
            send_sem=send_sem.at[stream, way, step],
            recv_sem=recv_sem.at[stream, way, step],
            device_id={"dp": targets[way]},
            device_id_type=MESH,
        )

    def pair_sum(way, step, stream):
        share(way, step, stream).wait_recv()
        own = grads[stream][block(way, step, core), :].astype(jnp.float32)
        return own + pairs[stream][way, step].astype(jnp.float32)

    greet((right, left, partner))

    def start_shares(step, carry):
        for stream in range(streams):
            for way in range(2):
                share(way, step, stream).start()
        return carry

    lax.fori_loop(0, count, start_shares, 0)
    for stream in range(streams):
        for way in range(2):
            sends[stream][way, 0] = pair_sum(way, 0, stream).astype(jnp.bfloat16)
            hop(way, 0, stream).start()

    def step_body(step, carry):
        for stream in range(streams):
            for way in range(2):
                total = pair_sum(way, step, stream)
                hop(way, step - 1, stream).wait_recv()
                total = total + recvs[stream][way, step - 1].astype(jnp.float32)
                sends[stream][way, step] = total.astype(jnp.bfloat16)
                hop(way, step, stream).start()
        return carry

    lax.fori_loop(1, count - 1, step_body, 0)
    for stream in range(streams):
        for way in range(2):
            total = pair_sum(way, count - 1, stream)
            hop(way, count - 2, stream).wait_recv()
            total = total + recvs[stream][way, count - 2].astype(jnp.float32)
            outs[stream][way * half : (way + 1) * half, :] = total

    def drain_hops(step, carry):
        for stream in range(streams):
            for way in range(2):
                hop(way, step, stream).wait_send()
        return carry

    def drain_shares(step, carry):
        for stream in range(streams):
            for way in range(2):
                share(way, step, stream).wait_send()
        return carry

    lax.fori_loop(0, count - 1, drain_hops, 0)
    lax.fori_loop(0, count, drain_shares, 0)


def ring_scatter(grads, devices):
    count = devices // 2
    streams = len(grads)
    rows = grads[0].shape[0] // devices
    half = rows // 2
    widths = [grad.shape[1] for grad in grads]
    vmem = pl.BlockSpec(memory_space=pltpu.VMEM)
    return pl.pallas_call(
        functools.partial(scatter_kernel, count, streams),
        out_shape=[jax.ShapeDtypeStruct((rows, width), jnp.float32) for width in widths],
        in_specs=[vmem] * streams,
        out_specs=[vmem] * streams,
        scratch_shapes=[pltpu.VMEM((2, count, half, width), jnp.bfloat16) for width in widths]
        + [pltpu.VMEM((2, count - 1, half, width), jnp.bfloat16) for width in widths] * 2
        + [pltpu.SemaphoreType.DMA((streams, 2, count - 1))] * 2
        + [pltpu.SemaphoreType.DMA((streams, 2, count))] * 2,
        compiler_params=pltpu.CompilerParams(
            collective_id=1, has_side_effects=True, vmem_limit_bytes=40 * 1024 * 1024
        ),
        name="ring_scatter",
    )(*grads)


def turn(values, cos_table, sin_table, low_half):
    half = HEAD_HALF
    swapped = jnp.where(
        low_half, pltpu.roll(values, LANES - half, 1), pltpu.roll(values, half, 1)
    )
    return values * cos_table + swapped * sin_table


HEAD_HALF = 32


def lane_masks(rows):
    lane = lax.broadcasted_iota(jnp.int32, (rows, LANES), 1)
    return (lane % (2 * HEAD_HALF) < HEAD_HALF, lane < 2 * HEAD_HALF)


def allowed_pairs(pos_col, pos_row, seg_col, seg_row):
    near = jnp.abs(pos_col[...] - pos_row[...]) <= HALO
    return near & (seg_col[...] == seg_row[...])


def head_probs(queries, keys, allowed, scale):
    scores = (
        lax.dot_general(
            queries, keys, (((1,), (1,)), ((), ())), preferred_element_type=jnp.float32
        )
        * scale
    )
    scores = jnp.where(allowed, scores, NEG_FILL)
    top_score = jnp.max(scores, axis=-1, keepdims=True)
    total = jnp.sum(jnp.exp(scores - top_score), axis=-1, keepdims=True)
    return jnp.exp(scores - (top_score + jnp.log(total)))


def attend_kernel(
    scale, width, proj, cos_ref, sin_ref, pos_col, pos_row, seg_col, seg_row, qkv_out, mixed_out
):
    rows = proj.shape[0]
    low_half, first = lane_masks(rows)
    cos_table, sin_table = cos_ref[...], sin_ref[...]
    allowed = allowed_pairs(pos_col, pos_row, seg_col, seg_row)
    for start in range(0, width, LANES):
        queries = turn(proj[:, start : start + LANES], cos_table, sin_table, low_half)
        keys = turn(
            proj[:, width + start : width + start + LANES], cos_table, sin_table, low_half
        ).astype(jnp.bfloat16)
        values = proj[:, 2 * width + start : 2 * width + start + LANES]
        qkv_out[:, start : start + LANES] = queries.astype(jnp.bfloat16)
        qkv_out[:, width + start : width + start + LANES] = keys
        qkv_out[:, 2 * width + start : 2 * width + start + LANES] = values.astype(jnp.bfloat16)
        mixed = jnp.zeros((rows, LANES), jnp.float32)
        for head in range(2):
            mine = first if head == 0 else ~first
            probs = head_probs(
                jnp.where(mine, queries, 0.0).astype(jnp.bfloat16), keys, allowed, scale
            ).astype(jnp.bfloat16)
            mixed = mixed + jnp.dot(
                probs,
                jnp.where(mine, values, 0.0).astype(jnp.bfloat16),
                preferred_element_type=jnp.float32,
            )
        mixed_out[:, start : start + LANES] = mixed.astype(jnp.bfloat16)


def attend_back_kernel(
    scale,
    width,
    qkv,
    mixed_ref,
    dmixed_ref,
    cos_ref,
    sin_ref,
    pos_col,
    pos_row,
    seg_col,
    seg_row,
    dqkv_out,
):
    rows = qkv.shape[0]
    low_half, first = lane_masks(rows)
    cos_table, sin_table = cos_ref[...], -sin_ref[...]
    allowed = allowed_pairs(pos_col, pos_row, seg_col, seg_row)
    over_rows = (((0,), (0,)), ((), ()))
    over_lanes = (((1,), (1,)), ((), ()))
    for start in range(0, width, LANES):
        queries = qkv[:, start : start + LANES].astype(jnp.float32)
        keys = qkv[:, width + start : width + start + LANES]
        keys32 = keys.astype(jnp.float32)
        values = qkv[:, 2 * width + start : 2 * width + start + LANES]
        dmixed = dmixed_ref[:, start : start + LANES].astype(jnp.float32)
        products = dmixed * mixed_ref[:, start : start + LANES].astype(jnp.float32)
        dquery = jnp.zeros((rows, LANES), jnp.float32)
        dkey = jnp.zeros((rows, LANES), jnp.float32)
        dvalue = jnp.zeros((rows, LANES), jnp.float32)
        for head in range(2):
            mine = first if head == 0 else ~first
            head_queries = jnp.where(mine, queries, 0.0).astype(jnp.bfloat16)
            head_keys = jnp.where(mine, keys32, 0.0).astype(jnp.bfloat16)
            head_dmixed = jnp.where(mine, dmixed, 0.0).astype(jnp.bfloat16)
            delta = jnp.sum(jnp.where(mine, products, 0.0), axis=-1, keepdims=True)
            probs = head_probs(head_queries, keys, allowed, scale)
            dprobs = lax.dot_general(
                head_dmixed, values, over_lanes, preferred_element_type=jnp.float32
            )
            dscores = (probs * (dprobs - delta) * scale).astype(jnp.bfloat16)
            dvalue = dvalue + lax.dot_general(
                probs.astype(jnp.bfloat16),
                head_dmixed,
                over_rows,
                preferred_element_type=jnp.float32,
            )
            dkey = dkey + lax.dot_general(
                dscores, head_queries, over_rows, preferred_element_type=jnp.float32
            )
            dquery = dquery + jnp.dot(dscores, head_keys, preferred_element_type=jnp.float32)
        dquery = turn(dquery, cos_table, sin_table, low_half)
        dkey = turn(dkey, cos_table, sin_table, low_half)
        dqkv_out[:, start : start + LANES] = dquery.astype(jnp.bfloat16)
        dqkv_out[:, width + start : width + start + LANES] = dkey.astype(jnp.bfloat16)
        dqkv_out[:, 2 * width + start : 2 * width + start + LANES] = dvalue.astype(jnp.bfloat16)


def local_call(kernel, name, out_shape, operands, flops):
    vmem = pl.BlockSpec(memory_space=pltpu.VMEM)
    single = not isinstance(out_shape, list)
    return pl.pallas_call(
        kernel,
        out_shape=out_shape,
        in_specs=[vmem] * len(operands),
        out_specs=vmem if single else [vmem] * len(out_shape),
        cost_estimate=pl.CostEstimate(
            flops=flops, bytes_accessed=4 * 1024 * 1024, transcendentals=flops // 256
        ),
        compiler_params=pltpu.CompilerParams(vmem_limit_bytes=32 * 1024 * 1024),
        name=name,
    )(*operands)


class PairedAttention:
    def __init__(self, positions, segments, head_size, width):
        rows = positions.shape[0]
        cos_table, sin_table = rotary_tables(positions, head_size)
        cos_table, sin_table = cos_table[:, 0, :], sin_table[:, 0, :]
        self.width = width
        self.scale = 1.0 / math.sqrt(head_size)
        self.flops = 2 * rows * rows * LANES * (width // head_size)
        self.shared = (
            jnp.concatenate([cos_table] * 4, axis=1),
            jnp.concatenate([-sin_table, sin_table] * 2, axis=1),
            positions[:, None],
            positions[None, :],
            segments[:, None],
            segments[None, :],
        )

    def forward(self, projected):
        rows = projected.shape[0]
        self.qkv, self.mixed = local_call(
            functools.partial(attend_kernel, self.scale, self.width),
            "attend",
            [
                jax.ShapeDtypeStruct((rows, 3 * self.width), jnp.bfloat16),
                jax.ShapeDtypeStruct((rows, self.width), jnp.bfloat16),
            ],
            (projected,) + self.shared,
            2 * self.flops,
        )
        return self.mixed

    def backward(self, dmixed):
        rows = dmixed.shape[0]
        return local_call(
            functools.partial(attend_back_kernel, self.scale, self.width),
            "attend_back",
            jax.ShapeDtypeStruct((rows, 3 * self.width), jnp.bfloat16),
            (self.qkv, self.mixed, dmixed) + self.shared,
            5 * self.flops,
        )


class BlockAttention:
    def __init__(self, positions, segments, head_size, width):
        self.total_len = positions.shape[0]
        self.segments = segments
        self.head_size = head_size
        self.width = width
        self.scale = 1.0 / math.sqrt(head_size)
        self.cos_table, self.sin_table = rotary_tables(positions, head_size)

    def heads(self, values):
        return values.reshape(self.total_len, self.width // self.head_size, self.head_size)

    def forward(self, projected):
        width, total_len = self.width, self.total_len
        self.block_rows = min(total_len, 512)
        self.slab_rows = self.block_rows + 2 * HALO
        tables = (self.cos_table, self.sin_table)
        self.queries = rotate(self.heads(projected[:, :width]), *tables).astype(jnp.bfloat16)
        keys = rotate(self.heads(projected[:, width : 2 * width]), *tables).astype(jnp.bfloat16)
        values = self.heads(projected[:, 2 * width :]).astype(jnp.bfloat16)
        pad_spec = ((HALO, HALO), (0, 0), (0, 0))
        self.key_pad = jnp.pad(keys, pad_spec)
        self.value_pad = jnp.pad(values, pad_spec)
        seg_pad = jnp.pad(self.segments, (HALO, HALO), constant_values=-1)
        mixed_parts = []
        self.logsums = []
        self.masks = []
        for start in range(0, total_len, self.block_rows):
            own = slice(start, start + self.block_rows)
            slab = slice(start, start + self.slab_rows)
            allowed = window_mask(
                start + jnp.arange(self.block_rows, dtype=jnp.int32),
                start - HALO + jnp.arange(self.slab_rows, dtype=jnp.int32),
                self.segments[own],
                seg_pad[slab],
                HALO,
                total_len,
            )
            mixed, logsum = attend_block(
                self.queries[own], self.key_pad[slab], self.value_pad[slab], allowed, self.scale
            )
            self.masks.append(allowed)
            self.logsums.append(logsum)
            mixed_parts.append(mixed)
        self.mixed = jnp.concatenate(mixed_parts, axis=0).astype(jnp.bfloat16)
        return self.mixed.reshape(total_len, width)

    def backward(self, dmixed):
        total_len = self.total_len
        dmixed = self.heads(dmixed)
        padded = (total_len + 2 * HALO,) + dmixed.shape[1:]
        dkey_pad = jnp.zeros(padded, jnp.float32)
        dvalue_pad = jnp.zeros(padded, jnp.float32)
        dquery_parts = []
        for index, start in enumerate(range(0, total_len, self.block_rows)):
            own = slice(start, start + self.block_rows)
            slab = slice(start, start + self.slab_rows)
            dqueries, dkeys, dvalues = attend_back(
                self.queries[own],
                self.key_pad[slab],
                self.value_pad[slab],
                self.masks[index],
                self.scale,
                self.logsums[index],
                self.mixed[own],
                dmixed[own],
            )
            dquery_parts.append(dqueries)
            dkey_pad = dkey_pad.at[slab].add(dkeys)
            dvalue_pad = dvalue_pad.at[slab].add(dvalues)
        inner = slice(HALO, HALO + total_len)
        tables = (self.cos_table, self.sin_table)
        parts = [
            unrotate(jnp.concatenate(dquery_parts, axis=0), *tables),
            unrotate(dkey_pad[inner], *tables),
            dvalue_pad[inner],
        ]
        return jnp.concatenate(
            [part.reshape(total_len, self.width) for part in parts], axis=1
        ).astype(jnp.bfloat16)


def dot(left, right, left_dim, right_dim):
    return lax.dot_general(
        left,
        right,
        (((left_dim,), (right_dim,)), ((), ())),
        preferred_element_type=jnp.float32,
    )


def padded_to_lanes(values):
    return jnp.pad(values, ((0, 0), (0, -values.shape[1] % LANES)))


def high_and_low(gain):
    high = gain.astype(jnp.bfloat16)
    return [high[:, None], (gain - high.astype(jnp.float32)).astype(jnp.bfloat16)[:, None]]


def general_device(
    devices,
    seq_size,
    tokens,
    segments,
    cotangent,
    qkv_weight,
    out_weight,
    in_weight,
    down_weight,
    attn_gain,
    mlp_gain,
):
    layer_in = tokens[0]
    seg_local = segments[0]
    cot_local = cotangent[0]
    own_rows, model_width = layer_in.shape
    head_size = model_width // HEADS
    local_width = qkv_weight.shape[2]
    local_hidden = in_weight.shape[2]
    shard_rows = qkv_weight.shape[0]
    total_len = own_rows * seq_size
    paired = (
        seq_size == 2
        and total_len <= 512
        and local_width % LANES == 0
        and head_size == 2 * HEAD_HALF
    )
    swap = [(0, 1), (1, 0)]

    def rows_of_all(values):
        if paired:
            return jnp.concatenate([values, lax.ppermute(values, "seq", swap)], axis=0)
        return lax.all_gather(values, "seq", axis=0, tiled=True)

    def sum_to_owner(partial):
        if paired:
            other = lax.ppermute(partial[own_rows:].astype(jnp.bfloat16), "seq", swap)
            return partial[:own_rows] + other.astype(jnp.float32)
        return lax.psum_scatter(
            partial.astype(jnp.bfloat16), "seq", scatter_dimension=0, tiled=True
        ).astype(jnp.float32)

    def sum_over_seq(part):
        if paired:
            return part + lax.ppermute(part, "seq", swap)
        return lax.psum(part, "seq")

    first_pack = jnp.concatenate(
        [qkv_weight.reshape(shard_rows, 3 * local_width), out_weight.T], axis=1
    )
    wide = (local_hidden + 4 + LANES - 1) // LANES * LANES
    spare = jnp.zeros((shard_rows, wide - local_hidden), jnp.bfloat16)
    second_pack = jnp.concatenate(
        [in_weight[:, 0, :], spare, in_weight[:, 1, :], spare, down_weight.T]
        + high_and_low(attn_gain)
        + high_and_low(mlp_gain)
        + [spare[:, 4:]],
        axis=1,
    )
    first_full, second_full = ring_gather([first_pack, second_pack], devices)
    full_qkv = first_full[:, : 3 * local_width]
    full_out = first_full[:, 3 * local_width : 4 * local_width]
    gains_at = 2 * wide + local_hidden
    gains = second_full[:, gains_at : gains_at + 4].astype(jnp.float32)
    gain_attn = gains[:, 0] + gains[:, 1]
    gain_mlp = gains[:, 2] + gains[:, 3]
    full_in = second_full[:, : 2 * wide]
    full_down = second_full[:, 2 * wide :]

    inputs32 = layer_in.astype(jnp.float32)
    if paired:
        arrived = lax.ppermute(jnp.concatenate([layer_in, cot_local], axis=0), "seq", swap)
        all_inputs32 = jnp.concatenate([layer_in, arrived[:own_rows]], axis=0).astype(jnp.float32)
        cot_full = jnp.concatenate([cot_local, arrived[own_rows:]], axis=0)
    else:
        all_inputs32 = rows_of_all(layer_in).astype(jnp.float32)
        cot_full = rows_of_all(cot_local)
    normed_full = norm_forward(all_inputs32, gain_attn)[0].astype(jnp.bfloat16)
    unit_one, inv_one = norm_forward(inputs32, gain_attn)[1:]
    if paired:
        seg_full = rows_of_all(
            jnp.broadcast_to(seg_local.astype(jnp.float32)[:, None], (own_rows, LANES))
        )[:, 0].astype(jnp.int32)
        place = lax.axis_index("seq")
        arange = jnp.arange(own_rows, dtype=jnp.int32)
        positions = jnp.concatenate(
            [place * own_rows + arange, (1 - place) * own_rows + arange], axis=0
        )
        attention = PairedAttention(positions, seg_full, head_size, local_width)
    else:
        seg_full = rows_of_all(seg_local.astype(jnp.bfloat16)).astype(jnp.int32)
        positions = jnp.arange(total_len, dtype=jnp.int32)
        attention = BlockAttention(positions, seg_full, head_size, local_width)

    mixed = attention.forward(dot(normed_full, full_qkv, 1, 0))
    residual = inputs32 + sum_to_owner(dot(mixed, full_out, 1, 1))
    normed_two, unit_two, inv_two = norm_forward(residual, gain_mlp)
    normed_two_full = rows_of_all(normed_two.astype(jnp.bfloat16))
    expanded = dot(normed_two_full, full_in, 1, 0)
    gate_in = expanded[:, :wide]
    linear_in = expanded[:, wide:]
    activated = gelu_value(gate_in)
    middle_b = (activated * linear_in).astype(jnp.bfloat16)
    down_part = dot(middle_b, full_down, 1, 1)

    down_grad = dot(cot_full, middle_b, 0, 0).astype(jnp.bfloat16)
    dmiddle = dot(cot_full, full_down, 1, 0)
    dexpanded_b = jnp.concatenate(
        [dmiddle * linear_in * gelu_slope(gate_in), dmiddle * activated], axis=1
    ).astype(jnp.bfloat16)
    dnormed_two = sum_to_owner(dot(dexpanded_b, full_in, 1, 1))
    in_grad = dot(normed_two_full, dexpanded_b, 0, 0).astype(jnp.bfloat16)
    dres_norm, mlp_gain_part = norm_backward(dnormed_two, gain_mlp, unit_two, inv_two)
    dresidual = cot_local.astype(jnp.float32) + dres_norm
    dres_full = rows_of_all(dresidual.astype(jnp.bfloat16))
    down_part, dres_full = lax.optimization_barrier((down_part, dres_full))
    layer_out = (residual + sum_to_owner(down_part)).astype(jnp.bfloat16)
    dmixed = dot(dres_full, full_out, 1, 0).astype(jnp.bfloat16)
    out_grad = dot(dres_full, mixed, 0, 0).astype(jnp.bfloat16)
    dqkv_b = attention.backward(dmixed)
    layer_out, dqkv_b = lax.optimization_barrier((layer_out, dqkv_b))
    dnormed_one = sum_to_owner(dot(dqkv_b, full_qkv, 1, 1))
    qkv_grad = dot(normed_full, dqkv_b, 0, 0).astype(jnp.bfloat16)
    dinput_norm, attn_gain_part = norm_backward(dnormed_one, gain_attn, unit_one, inv_one)
    tokens_grad = (dresidual + dinput_norm).astype(jnp.bfloat16)
    gain_sums = sum_over_seq(jnp.stack([attn_gain_part, mlp_gain_part]))
    gain_grad = padded_to_lanes(gain_sums.T).astype(jnp.bfloat16)

    in_share, qkv_share, down_share, out_share, gain_share = ring_scatter(
        [in_grad, qkv_grad, down_grad, out_grad, gain_grad], devices
    )
    return (
        layer_out[None],
        tokens_grad[None],
        qkv_share.reshape(shard_rows, 3, local_width),
        out_share.T,
        jnp.stack([in_share[:, :local_hidden], in_share[:, wide : wide + local_hidden]], axis=1),
        down_share[:, :local_hidden].T,
        gain_share[:, 0],
        gain_share[:, 1],
    )


HIGH = (((1,), (1,)), ((), ()))
OVER_ROWS = (((0,), (0,)), ((), ()))


def fits_fused(devices, seq_size, own_rows, model_width, local_width, local_hidden):
    rest = local_hidden % LANES
    shard_rows = model_width // devices
    return (
        seq_size == 2
        and devices % 4 == 0
        and devices >= 8
        and own_rows == LANES
        and local_width % (2 * LANES) == 0
        and model_width % (2 * LANES) == 0
        and model_width // HEADS == 2 * HEAD_HALF
        and 3 * rest + 8 <= LANES
        and local_hidden // LANES >= 4
        and local_hidden // LANES % 2 == 0
        and shard_rows % 32 == 0
        and own_rows * 2 * LANES // model_width % 16 == 0
    )


def nt(left, right):
    return lax.dot_general(left, right, HIGH, preferred_element_type=jnp.float32)


def nn(left, right):
    return jnp.dot(left, right, preferred_element_type=jnp.float32)


def tiles(total, width, body):
    def step(index, carry):
        body(index, pl.ds(pl.multiple_of(index * width, width), width))
        return carry

    lax.fori_loop(0, total // width, step, 0)


def fused_kernel(sizes, layout, *refs):
    count, own_rows, width, hidden, rest, scale = sizes
    total_rows = 2 * own_rows
    r = types.SimpleNamespace(**dict(zip(layout, refs)))
    model = r.tokens.shape[1]
    streams = 7
    fulls = [getattr(r, "full%d" % i) for i in range(streams)]
    grads = [getattr(r, "grad%d" % i) for i in range(streams)]
    pairs = [getattr(r, "pair%d" % i) for i in range(streams)]
    ends = [getattr(r, "end%d" % i) for i in range(streams)]
    recvs = [getattr(r, "recv%d" % i) for i in range(streams)]
    rows = model // (2 * count)
    half = rows // 2
    turns = count // 2
    core, place = ring_place(count)
    right, left, partner = neighbours(core, place, count)
    targets = (right, left)
    me = lax.axis_index("dp")
    mine = lax.axis_index("seq")
    other = 1 - mine
    f32, bf16 = jnp.float32, jnp.bfloat16
    my_rows = pl.ds(pl.multiple_of(me * rows, rows), rows)

    def remote(src, dst, send, recv, device):
        return pltpu.make_async_remote_copy(
            src_ref=src,
            dst_ref=dst,
            send_sem=send,
            recv_sem=recv,
            device_id=device,
            device_id_type=MESH,
        )


    def piece(way, distance, stream, whole):
        shift = count - distance if way == 0 else distance
        owner = chip_at((place + shift) % count, count) * 2 + core
        if whole:
            where = pl.ds(pl.multiple_of(owner * rows, rows), rows)
        else:
            where = pl.ds(pl.multiple_of(owner * rows + way * half, half), half)
        return fulls[stream].at[where]

    def hop(way, step, stream):
        ref = piece(way, step, stream, step < turns - 1)
        sems = r.g_send.at[stream, way, step], r.g_recv.at[stream, way, step]
        return remote(ref, ref, *sems, {"dp": targets[way]})

    def share(way, step, stream):
        ref = piece(way, step, stream, step < turns)
        sems = r.gp_send.at[stream, way, step], r.gp_recv.at[stream, way, step]
        return remote(ref, ref, *sems, {"dp": partner})

    def gather_ops(stream):
        def start():
            for way in range(2):
                hop(way, 0, stream).start()
            share(0, 0, stream).start()

        def middle(step):
            for way in range(2):
                hop(way, step - 1, stream).wait_recv()
                hop(way, step, stream).start()
                share(way, step, stream).start()

        def last():
            for way in range(2):
                hop(way, turns - 1, stream).wait_recv()
                share(way, turns, stream).start()

        steps = [functools.partial(middle, step) for step in range(1, turns)]
        return [start] + steps + [last]

    def gather_shares(stream):
        return [share(0, 0, stream)] + [
            share(way, step, stream) for step in range(1, turns + 1) for way in range(2)
        ]

    def gather_arrived(stream):
        end(gathers, stream)
        for part in gather_shares(stream):
            part.wait_recv()

    def gather_drain(stream):
        for step in range(turns):
            for way in range(2):
                hop(way, step, stream).wait_send()
        for part in gather_shares(stream):
            part.wait_send()


    def block(ahead, which):
        owner = chip_at((place + ahead) % count, count) * 2 + which
        return pl.ds(pl.multiple_of(owner * rows, rows), rows)

    def give(ahead, stream):
        return remote(
            grads[stream].at[block(ahead, 1 - core)],
            pairs[stream].at[ahead],
            r.sp_send.at[stream, ahead],
            r.sp_recv.at[stream, ahead],
            {"dp": partner},
        )

    def ahead_of(way, step):
        return turns - step if way == 0 else turns + step

    def push(way, step, stream):
        sems = r.s_send.at[stream, way, step], r.s_recv.at[stream, way, step]
        if step == 0:
            src = pairs[stream].at[turns, pl.ds(way * half, half)]
            return remote(src, ends[stream].at[way], *sems, {"dp": targets[way]})
        src = pairs[stream].at[ahead_of(way, step)]
        return remote(src, recvs[stream].at[way, step - 1], *sems, {"dp": targets[way]})

    def pair_sum(ahead, stream):
        give(ahead, stream).wait_recv()
        own = grads[stream][block(ahead, core), :].astype(f32)
        return own + pairs[stream][ahead].astype(f32)

    def scatter_ops(stream, finish):
        def gives():
            order = [turns] + [turns + sign * d for d in range(1, turns) for sign in (-1, 1)] + [0]
            for ahead in order:
                give(ahead, stream).start()

        def start():
            pairs[stream][turns] = pair_sum(turns, stream).astype(bf16)
            for way in range(2):
                push(way, 0, stream).start()

        def middle(step):
            for way in range(2):
                ahead = ahead_of(way, step)
                total = pair_sum(ahead, stream)
                push(way, step - 1, stream).wait_recv()
                if step == 1:
                    near = ends[stream][way].astype(f32)
                    parts = [total[:half], total[half:]]
                    parts[way] = parts[way] + near
                    total = jnp.concatenate(parts, axis=0)
                else:
                    total = total + recvs[stream][way, step - 2].astype(f32)
                pairs[stream][ahead] = total.astype(bf16)
                push(way, step, stream).start()

        def last():
            total = pair_sum(0, stream)
            for way in range(2):
                push(way, turns - 1, stream).wait_recv()
                total = total + recvs[stream][way, turns - 2].astype(f32)
            finish(total)

        steps = [functools.partial(middle, step) for step in range(1, turns)]
        return [gives, start] + steps + [last]

    def scatter_drain(stream):
        for step in range(turns):
            for way in range(2):
                push(way, step, stream).wait_send()
        for ahead in range(count):
            give(ahead, stream).wait_send()


    own = pl.ds(0, own_rows)
    far = pl.ds(own_rows, own_rows)
    exchanged = [
        (r.seg_own, r.seg_other),
        (r.tokens, r.tok_other),
        (r.cot, r.cot_all.at[far]),
        (r.out_send, r.out_recv),
        (r.n2.at[own], r.n2.at[far]),
        (r.down_send, r.down_recv),
        (r.dn2_send, r.dn2_recv),
        (r.dres.at[own], r.dres.at[far]),
        (r.dn1_send, r.dn1_recv),
        (r.gain_part, r.gain_recv),
    ]
    by_lanes, by_rows = (3, 5, 6, 8), (4, 7)
    chunks = model // (2 * LANES)
    chunk_rows = own_rows // chunks

    def swap(index, part=0):
        src, dst = exchanged[index]
        if index in by_lanes:
            lanes = pl.ds(pl.multiple_of(part * 2 * LANES, 2 * LANES), 2 * LANES)
            src, dst = src.at[:, lanes], dst.at[:, lanes]
        elif index in by_rows:
            here = pl.ds(pl.multiple_of(part * chunk_rows, chunk_rows), chunk_rows)
            src, dst = src.at[here], dst.at[here]
        sems = r.y_send.at[index, part], r.y_recv.at[index, part]
        return remote(src, dst, *sems, {"seq": other})

    def parts_of(index):
        return chunks if index in by_lanes + by_rows else 1

    def arrived(index):
        def body(part, carry):
            swap(index, part).wait_recv()
            return carry

        lax.fori_loop(0, parts_of(index), body, 0)

    def swap_drain(index):
        def body(part, carry):
            swap(index, part).wait_send()
            return carry

        lax.fori_loop(0, parts_of(index), body, 0)


    def normed(values):
        center = values - jnp.mean(values, axis=-1, keepdims=True)
        inv_std = lax.rsqrt(jnp.mean(center * center, axis=-1, keepdims=True) + EPS)
        return center * inv_std, inv_std

    def to_columns(src, dst):
        def body(index, lanes):
            dst[lanes, :] = src[:, lanes].astype(f32).T.astype(bf16)

        tiles(model, LANES, body)

    def partial_sums(terms, own_ref, send_ref, exchange):
        def body(index, lanes):
            total = sum(nt(left[...], right[lanes, :]) for left, right in terms)
            own_ref[:, lanes] = total[:own_rows]
            send_ref[:, lanes] = total[own_rows:].astype(bf16)
            swap(exchange, index).start()

        tiles(model, 2 * LANES, body)

    def weight_grad(columns, right, out, at=0):
        size = right.shape[1]

        def body(index, lanes):
            value = nn(columns[...], right[:, lanes]).astype(bf16)
            out[:, pl.ds(pl.multiple_of(at + index * 2 * LANES, LANES), 2 * LANES)] = value

        tiles(size, 2 * LANES, body)

    blocks = width // LANES
    hidden_blocks = hidden // LANES
    lane = lax.broadcasted_iota(jnp.int32, (total_rows, LANES), 1)
    low_half = lane % (2 * HEAD_HALF) < HEAD_HALF
    first = lane < 2 * HEAD_HALF

    def setup():
        r.cos[own, :] = r.cos_table[pl.ds(pl.multiple_of(mine * own_rows, own_rows), own_rows), :]
        r.cos[far, :] = r.cos_table[pl.ds(pl.multiple_of(other * own_rows, own_rows), own_rows), :]
        r.sin[own, :] = r.sin_table[pl.ds(pl.multiple_of(mine * own_rows, own_rows), own_rows), :]
        r.sin[far, :] = r.sin_table[pl.ds(pl.multiple_of(other * own_rows, own_rows), own_rows), :]

    def position(dim):
        index = lax.broadcasted_iota(jnp.int32, (total_rows, total_rows), dim)
        return jnp.where(index < own_rows, index + mine * own_rows, index - mine * own_rows)

    def make_bias():
        seg_row = jnp.concatenate([r.seg_own[0:1, :], r.seg_other[0:1, :]], axis=1).astype(f32)
        across = jnp.broadcast_to(seg_row, (total_rows, total_rows))
        allowed = (jnp.abs(position(0) - position(1)) <= HALO) & (across == across.T)
        r.bias[...] = jnp.where(allowed, 0.0, NEG_FILL)

    def expand_special():
        spot = lax.broadcasted_iota(jnp.int32, (2 * LANES, LANES), 1)
        keep = spot < rest

        def body(index, here):
            part = fulls[6][here, :].astype(f32)
            r.gains[:, here] = part.T[3 * rest : 3 * rest + 8]
            r.sp_in[here, :LANES] = jnp.where(keep, part, 0.0).astype(bf16)
            r.sp_in[here, LANES:] = jnp.where(
                keep, pltpu.roll(part, LANES - rest, 1), 0.0
            ).astype(bf16)
            r.sp_down[here, :] = jnp.where(
                keep, pltpu.roll(part, LANES - 2 * rest, 1), 0.0
            ).astype(bf16)

        tiles(model, 2 * LANES, body)

    def attn_gain():
        return r.gains[0:1, :] + r.gains[1:2, :]

    def mlp_gain():
        return r.gains[2:3, :] + r.gains[3:4, :]

    def norm_one():
        for src, place_of in ((r.tokens, 0), (r.tok_other, own_rows)):
            def body(index, here):
                unit_rows, _ = normed(src[here, :].astype(f32))
                at = pl.ds(pl.multiple_of(index * 32 + place_of, 32), 32)
                r.n1[at, :] = (unit_rows * attn_gain()).astype(bf16)

            tiles(own_rows, 32, body)

    def values_of():
        def body(index, lanes):
            r.v[:, lanes] = nn(r.n1[...], fulls[1][:, lanes]).astype(bf16)

        tiles(width, 2 * LANES, body)

    def attend(index, wide, lanes):
        cos_table, sin_table = r.cos[...], r.sin[...]
        proj = nn(r.n1[...], fulls[0][:, wide])
        queries = turn(proj[:, :LANES], cos_table, sin_table, low_half)
        keys = turn(proj[:, LANES:], cos_table, sin_table, low_half).astype(bf16)
        r.qk[:, wide] = jnp.concatenate([queries.astype(bf16), keys], axis=1)
        values = r.v[:, lanes].astype(f32)
        mixed = jnp.zeros((total_rows, LANES), f32)
        for head in range(2):
            here = first if head == 0 else ~first
            scores = nt(jnp.where(here, queries, 0.0).astype(bf16), keys) * scale + r.bias[...]
            top_score = jnp.max(scores, axis=-1, keepdims=True)
            total = jnp.sum(jnp.exp(scores - top_score), axis=-1, keepdims=True)
            probs = jnp.exp(scores - (top_score + jnp.log(total)))
            r.probs[index * 2 + head] = probs
            mixed = mixed + nn(probs.astype(bf16), jnp.where(here, values, 0.0).astype(bf16))
        r.mixed[:, lanes] = mixed.astype(bf16)

    def attend_back(index, wide, lanes):
        cos_table, sin_table = r.cos[...], -r.sin[...]
        both = r.qk[:, wide]
        queries = both[:, :LANES].astype(f32)
        keys = both[:, LANES:].astype(f32)
        values = r.v[:, lanes]
        dmixed = r.dmixed[:, lanes].astype(f32)
        products = dmixed * r.mixed[:, lanes].astype(f32)
        dquery = jnp.zeros((total_rows, LANES), f32)
        dkey = jnp.zeros((total_rows, LANES), f32)
        dvalue = jnp.zeros((total_rows, LANES), f32)
        for head in range(2):
            here = first if head == 0 else ~first
            head_queries = jnp.where(here, queries, 0.0).astype(bf16)
            head_keys = jnp.where(here, keys, 0.0).astype(bf16)
            head_dmixed = jnp.where(here, dmixed, 0.0).astype(bf16)
            delta = jnp.sum(jnp.where(here, products, 0.0), axis=-1, keepdims=True)
            probs = r.probs[index * 2 + head]
            dprobs = nt(head_dmixed, values)
            dscores = (probs * (dprobs - delta) * scale).astype(bf16)
            dvalue = dvalue + lax.dot_general(
                probs.astype(bf16), head_dmixed, OVER_ROWS, preferred_element_type=f32
            )
            dkey = dkey + lax.dot_general(
                dscores, head_queries, OVER_ROWS, preferred_element_type=f32
            )
            dquery = dquery + nn(dscores, head_keys)
        dquery = turn(dquery, cos_table, sin_table, low_half)
        dkey = turn(dkey, cos_table, sin_table, low_half)
        r.dqk[:, wide] = jnp.concatenate([dquery, dkey], axis=1).astype(bf16)
        r.dv[:, lanes] = dvalue.astype(bf16)

    def over_heads(body, start, stop):
        def step(index, carry):
            body(
                index,
                pl.ds(pl.multiple_of(index * 2 * LANES, 2 * LANES), 2 * LANES),
                pl.ds(pl.multiple_of(index * LANES, LANES), LANES),
            )
            return carry

        lax.fori_loop(start, stop, step, 0)

    def norm_two():
        def body(index, here):
            residual = (
                r.tokens[here, :].astype(f32)
                + r.acc[here, :]
                + r.out_recv[here, :].astype(f32)
            )
            r.residual[here, :] = residual
            unit_rows, _ = normed(residual)
            r.n2[here, :] = (unit_rows * mlp_gain()).astype(bf16)
            swap(4, index).start()

        tiles(own_rows, chunk_rows, body)

    def expand_tile(weight, at):
        both = nn(r.n2[...], weight)
        gate, linear = both[:, :LANES], both[:, LANES:]
        erf_part = 0.5 * (1.0 + lax.erf(gate * 0.7071067811865476))
        active = gate * erf_part
        slope = erf_part + gate * jnp.exp(-0.5 * gate * gate) * 0.3989422804014327
        r.mid[:, at] = (active * linear).astype(bf16)
        r.act[:, at] = active
        r.slope[:, at] = linear * slope

    def expand_stream(stream, offset):
        def body(index, lanes):
            at = pl.ds(pl.multiple_of((index + offset) * LANES, LANES), LANES)
            expand_tile(fulls[stream][:, lanes], at)

        tiles(fulls[stream].shape[1], 2 * LANES, body)

    spare = pl.ds(hidden, LANES)

    def dexpand(weight, at, to):
        dmiddle = nn(r.cot_all[...], weight)
        dgate = (dmiddle * r.slope[:, at]).astype(bf16)
        dlinear = (dmiddle * r.act[:, at]).astype(bf16)
        parts = []
        for start in range(0, dmiddle.shape[1], LANES):
            parts += [dgate[:, start : start + LANES], dlinear[:, start : start + LANES]]
        r.dexp[:, to] = jnp.concatenate(parts, axis=1)

    def dexpand_all():
        def body(index, lanes):
            to = pl.ds(pl.multiple_of(index * 4 * LANES, 4 * LANES), 4 * LANES)
            dexpand(fulls[5][:, lanes], lanes, to)

        tiles(hidden, 2 * LANES, body)
        dexpand(r.sp_down[...], spare, pl.ds(2 * hidden, 2 * LANES))

    split = fulls[3].shape[1]
    dexp_parts = [
        r.dexp.at[:, pl.ds(0, split)],
        r.dexp.at[:, pl.ds(split, 2 * hidden - split)],
        r.dexp.at[:, pl.ds(2 * hidden, 2 * LANES)],
    ]

    def special_grad():
        spot = lax.broadcasted_iota(jnp.int32, (2 * LANES, LANES), 1)

        def body(index, here):
            both = nn(r.n2_col[here, :], dexp_parts[2][...])
            down = nn(r.cot_col[here, :], r.mid[:, spare])
            value = jnp.where(
                spot < rest,
                both[:, :LANES],
                jnp.where(
                    spot < 2 * rest,
                    pltpu.roll(both[:, LANES:], rest, 1),
                    jnp.where(spot < 3 * rest, pltpu.roll(down, 2 * rest, 1), 0.0),
                ),
            )
            grads[6][here, :] = value.astype(bf16)

        tiles(model, 2 * LANES, body)

    def back_through_norm(grad_rows, gain, values):
        unit_rows, inv_std = normed(values)
        scaled = grad_rows * gain
        inner = (
            scaled
            - jnp.mean(scaled, axis=-1, keepdims=True)
            - unit_rows * jnp.mean(scaled * unit_rows, axis=-1, keepdims=True)
        )
        return inner * inv_std, jnp.sum(grad_rows * unit_rows, axis=0, keepdims=True)

    def norm_two_back():
        r.gain_part[...] = jnp.zeros_like(r.gain_part)

        def body(index, here):
            grad_rows = r.acc[here, :] + r.dn2_recv[here, :].astype(f32)
            part, gain_sum = back_through_norm(grad_rows, mlp_gain(), r.residual[here, :])
            dresidual = r.cot[here, :].astype(f32) + part
            r.dres_own[here, :] = dresidual
            r.dres[here, :] = dresidual.astype(bf16)
            r.gain_part[1:2, :] += gain_sum
            swap(7, index).start()

        tiles(own_rows, chunk_rows, body)

    def norm_one_back():
        def body(index, here):
            grad_rows = r.acc[here, :] + r.dn1_recv[here, :].astype(f32)
            part, gain_sum = back_through_norm(
                grad_rows, attn_gain(), r.tokens[here, :].astype(f32)
            )
            r.tokens_grad[0, here, :] = (r.dres_own[here, :] + part).astype(bf16)
            r.gain_part[0:1, :] += gain_sum

        tiles(own_rows, 32, body)

    def layer_out():
        def body(index, here):
            r.layer_out[0, here, :] = (
                r.residual[here, :]
                + r.down_acc[here, :]
                + r.down_recv[here, :].astype(f32)
            ).astype(bf16)

        tiles(own_rows, 32, body)

    def gain_columns():
        spot = lax.broadcasted_iota(jnp.int32, (LANES, 2 * LANES), 0)

        def body(index, here):
            sums = r.gain_part[:, here] + r.gain_recv[:, here]
            value = jnp.where(
                spot == 3 * rest, sums[0:1], jnp.where(spot == 3 * rest + 1, sums[1:2], 0.0)
            ).T
            old = grads[6][here, :].astype(f32)
            grads[6][here, :] = (old + value).astype(bf16)

        tiles(model, 2 * LANES, body)

    def dmixed_of():
        def body(index, lanes):
            r.dmixed[:, lanes] = nn(r.dres[...], fulls[2][:, lanes]).astype(bf16)

        tiles(width, 2 * LANES, body)


    def pack_keys():
        for at in range(0, width, LANES):
            for which in range(2):
                to = 2 * at + which * LANES
                fulls[0][my_rows, to : to + LANES] = r.raw_qkv[which, :, at : at + LANES]
        fulls[1][my_rows, :] = r.raw_qkv[2]

    def pack_special():
        spot = lax.broadcasted_iota(jnp.int32, (LANES, rows), 0)
        gain_parts = []
        for gain in (r.attn_gain[...], r.mlp_gain[...]):
            spread = gain * 65537.0
            high = spread - (spread - gain)
            gain_parts += [high, gain - high]
        gains = jnp.zeros((LANES, rows), f32)
        for index, part in enumerate(gain_parts):
            gains = jnp.where(spot == 3 * rest + index, part, gains)
        special = gains.T
        if rest:
            parts = [
                r.raw_in[:, 0, hidden:].astype(f32),
                r.raw_in[:, 1, hidden:].astype(f32),
                r.raw_down[:, hidden:].astype(f32),
                jnp.zeros((rows, LANES - 3 * rest), f32),
            ]
            special = special + jnp.concatenate(parts, axis=1)
        fulls[6][my_rows, :] = special.astype(bf16)

    def pack_rest():
        fulls[2][my_rows, :] = r.raw_out[...]
        for at in range(0, hidden, LANES):
            stream, to = (3, 2 * at) if 2 * at < split else (4, 2 * at - split)
            for which in range(2):
                start = to + which * LANES
                fulls[stream][my_rows, start : start + LANES] = r.raw_in[:, which, at : at + LANES]
        fulls[5][my_rows, :] = r.raw_down[:, :hidden]


    def finish_keys(total):
        for at in range(0, width, LANES):
            for which in range(2):
                to = 2 * at + which * LANES
                r.qkv_grad[which, :, at : at + LANES] = total[:, to : to + LANES]

    def finish_values(total):
        r.qkv_grad[2] = total

    def finish_out(total):
        r.out_grad[...] = total

    def finish_special(total):
        turned = total.T
        r.attn_gain_grad[...] = turned[3 * rest : 3 * rest + 1]
        r.mlp_gain_grad[...] = turned[3 * rest + 1 : 3 * rest + 2]
        if rest:
            r.in_grad[:, 0, hidden:] = total[:, :rest]
            r.in_grad[:, 1, hidden:] = total[:, rest : 2 * rest]
            r.down_grad[:, hidden:] = total[:, 2 * rest : 3 * rest]

    def finish_in(start):
        def finish(total):
            for at in range(0, total.shape[1], 2 * LANES):
                to = start + at // 2
                r.in_grad[:, 0, to : to + LANES] = total[:, at : at + LANES]
                r.in_grad[:, 1, to : to + LANES] = total[:, at + LANES : at + 2 * LANES]

        return finish

    def finish_down(total):
        r.down_grad[:, :hidden] = total

    gathers = [gather_ops(stream) for stream in range(streams)]
    finishes = [finish_keys, finish_values, finish_out, finish_in(0), finish_in(split // 2)]
    finishes += [finish_down, finish_special]
    scatters = [scatter_ops(stream, finishes[stream]) for stream in range(streams)]

    def go(ops, *chosen):
        for stream in chosen:
            if ops[stream]:
                ops[stream].pop(0)()

    def end(ops, *chosen):
        while any(ops[stream] for stream in chosen):
            go(ops, *chosen)


    loads = [
        pltpu.make_async_copy(src, dst, r.own_sem.at[index])
        for index, (src, dst) in enumerate(
            [
                (r.in_qkv, r.raw_qkv),
                (r.in_in, r.raw_in),
                (r.in_down, r.raw_down),
                (r.in_tokens.at[0], r.tokens),
                (r.in_cot.at[0], r.cot),
                (r.in_out, r.raw_out),
            ]
        )
    ]
    for load in loads:
        load.start()
    barrier = pltpu.get_barrier_semaphore()
    for device in (right, left, partner):
        pl.semaphore_signal(barrier, inc=1, device_id={"dp": device}, device_id_type=MESH)
    pl.semaphore_signal(barrier, inc=1, device_id={"seq": other}, device_id_type=MESH)
    r.seg_own[...] = jnp.broadcast_to(r.seg[...], r.seg_own.shape)
    loads[0].wait()
    pack_keys()
    pl.semaphore_wait(barrier, 4)
    go(gathers, 0, 1)
    for load in loads[1:5]:
        load.wait()
    pack_special()
    go(gathers, 6)
    for index in range(3):
        swap(index).start()
    loads[5].wait()
    pack_rest()
    r.cot_all[own, :] = r.cot[...]
    setup()
    to_columns(r.cot_all.at[own], r.cot_col.at[:, own])
    arrived(0)
    make_bias()
    go(gathers, 0, 1, 6, 2)
    go(gathers, 0, 1, 6, 2, 3)
    go(gathers, 0, 1, 6, 2, 4, 3)
    go(gathers, 0, 1, 6)
    arrived(1)
    arrived(2)
    gather_arrived(6)
    expand_special()
    go(gathers, 2)
    norm_one()
    gather_arrived(1)
    values_of()
    gather_arrived(0)
    over_heads(attend, blocks * 0 // 4, blocks * 1 // 4)
    go(gathers, 4)
    over_heads(attend, blocks * 1 // 4, blocks * 2 // 4)
    over_heads(attend, blocks * 2 // 4, blocks * 3 // 4)
    over_heads(attend, blocks * 3 // 4, blocks * 4 // 4)
    go(gathers, 3, 2)
    gather_arrived(2)
    partial_sums([(r.mixed, fulls[2])], r.acc, r.out_send, 3)
    to_columns(r.n1, r.n1_col)
    to_columns(r.cot_all.at[far], r.cot_col.at[:, far])
    go(gathers, 4, 5, 3)
    arrived(3)
    norm_two()
    go(gathers, 4, 5, 3)
    go(gathers, 4)
    arrived(4)
    gather_arrived(3)
    expand_stream(3, 0)
    expand_tile(r.sp_in[...], spare)
    to_columns(r.n2, r.n2_col)
    gather_arrived(4)
    expand_stream(4, split // (2 * LANES))
    go(gathers, 5)
    weight_grad(r.cot_col, r.mid.at[:, pl.ds(0, hidden)], grads[5])
    go(scatters, 5)
    go(scatters, 5)
    go(gathers, 5)
    go(scatters, 5)
    go(gathers, 5)
    gather_arrived(5)
    dexpand_all()
    go(scatters, 5)
    partial_sums(
        [(dexp_parts[0], fulls[3]), (dexp_parts[1], fulls[4]), (dexp_parts[2], r.sp_in)],
        r.acc,
        r.dn2_send,
        6,
    )
    weight_grad(r.n2_col, dexp_parts[0], grads[3])
    go(scatters, 3)
    weight_grad(r.n2_col, dexp_parts[1], grads[4])
    go(scatters, 4, 3, 5)
    arrived(6)
    norm_two_back()
    go(scatters, 4, 3)
    special_grad()
    partial_sums(
        [(r.mid.at[:, pl.ds(0, hidden)], fulls[5]), (r.mid.at[:, spare], r.sp_down)],
        r.down_acc,
        r.down_send,
        5,
    )
    go(scatters, 5, 4)
    arrived(7)
    dmixed_of()
    over_heads(attend_back, blocks * 0 // 4, blocks * 1 // 4)
    over_heads(attend_back, blocks * 1 // 4, blocks * 2 // 4)
    go(scatters, 3)
    over_heads(attend_back, blocks * 2 // 4, blocks * 3 // 4)
    over_heads(attend_back, blocks * 3 // 4, blocks * 4 // 4)
    go(scatters, 4)
    partial_sums([(r.dqk, fulls[0]), (r.dv, fulls[1])], r.acc, r.dn1_send, 8)
    weight_grad(r.n1_col, r.dqk, grads[0])
    go(scatters, 0)
    weight_grad(r.n1_col, r.dv, grads[1])
    go(scatters, 3, 1, 0)
    to_columns(r.dres, r.dres_col)
    weight_grad(r.dres_col, r.mixed, grads[2])
    go(scatters, 2, 4, 1)
    go(scatters, 2)
    arrived(8)
    norm_one_back()
    swap(9).start()
    arrived(5)
    layer_out()
    go(scatters, 3, 0)
    arrived(9)
    gain_columns()
    go(scatters, 6)
    go(scatters, 6, 4, 1, 2, 0)
    go(scatters, 6, 1, 2, 0)
    go(scatters, 6, 1, 2, 0)
    go(scatters, 6, 1, 2)
    go(scatters, 6)
    end(scatters, *range(streams))

    for stream in range(streams):
        gather_drain(stream)
        scatter_drain(stream)
    for index in range(len(exchanged)):
        swap_drain(index)


def fused_call(inputs, tables, devices, widths):
    names, arrays = zip(*inputs.items())
    whole = dict(inputs)
    count = devices // 2
    own_rows, model = whole["in_tokens"].shape[1:]
    total = 2 * own_rows
    _, rows, width = whole["in_qkv"].shape
    local_hidden = whole["in_in"].shape[2]
    rest = local_hidden % LANES
    hidden = local_hidden - rest
    half = rows // 2
    turns = count // 2
    f32, bf16 = jnp.float32, jnp.bfloat16
    streams = len(widths)
    heads = width // (2 * HEAD_HALF)
    outs = dict(
        layer_out=((1, own_rows, model), bf16),
        tokens_grad=((1, own_rows, model), bf16),
        qkv_grad=((3, rows, width), f32),
        out_grad=((rows, width), f32),
        in_grad=((rows, 2, local_hidden), f32),
        down_grad=((rows, local_hidden), f32),
        attn_gain_grad=((1, rows), f32),
        mlp_gain_grad=((1, rows), f32),
    )
    shapes = dict(
        tokens=((own_rows, model), bf16),
        cot=((own_rows, model), bf16),
        seg_own=((8, own_rows), jnp.int32),
        seg_other=((8, own_rows), jnp.int32),
        raw_qkv=((3, rows, width), bf16),
        raw_out=((rows, width), bf16),
        raw_in=((rows, 2, local_hidden), bf16),
        raw_down=((rows, local_hidden), bf16),
        tok_other=((own_rows, model), bf16),
        cot_all=((total, model), bf16),
        cot_col=((model, total), bf16),
        n1=((total, model), bf16),
        n1_col=((model, total), bf16),
        gains=((8, model), f32),
        cos=((total, LANES), f32),
        sin=((total, LANES), f32),
        bias=((total, total), f32),
        sp_in=((model, 2 * LANES), bf16),
        sp_down=((model, LANES), bf16),
        v=((total, width), bf16),
        qk=((total, 2 * width), bf16),
        probs=((heads, total, total), f32),
        mixed=((total, width), bf16),
        acc=((own_rows, model), f32),
        down_acc=((own_rows, model), f32),
        out_send=((own_rows, model), bf16),
        out_recv=((own_rows, model), bf16),
        down_send=((own_rows, model), bf16),
        down_recv=((own_rows, model), bf16),
        dn2_send=((own_rows, model), bf16),
        dn2_recv=((own_rows, model), bf16),
        dn1_send=((own_rows, model), bf16),
        dn1_recv=((own_rows, model), bf16),
        residual=((own_rows, model), f32),
        n2=((total, model), bf16),
        n2_col=((model, total), bf16),
        mid=((total, hidden + LANES), bf16),
        act=((total, hidden + LANES), f32),
        slope=((total, hidden + LANES), f32),
        dexp=((total, 2 * hidden + 2 * LANES), bf16),
        dres_own=((own_rows, model), f32),
        dres=((total, model), bf16),
        dres_col=((model, total), bf16),
        dmixed=((total, width), bf16),
        dqk=((total, 2 * width), bf16),
        dv=((total, width), bf16),
        gain_part=((8, model), f32),
        gain_recv=((8, model), f32),
    )
    for i, w in enumerate(widths):
        shapes["full%d" % i] = ((model, w), bf16)
        shapes["grad%d" % i] = ((model, w), bf16)
        shapes["pair%d" % i] = ((count, rows, w), bf16)
        shapes["end%d" % i] = ((2, half, w), bf16)
        shapes["recv%d" % i] = ((2, turns - 1, rows, w), bf16)
    scratch = {name: pltpu.VMEM(shape, dtype) for name, (shape, dtype) in shapes.items()}
    semaphores = dict(
        own_sem=(6,),
        g_send=(streams, 2, turns),
        g_recv=(streams, 2, turns),
        gp_send=(streams, 2, turns + 1),
        gp_recv=(streams, 2, turns + 1),
        s_send=(streams, 2, turns),
        s_recv=(streams, 2, turns),
        sp_send=(streams, count),
        sp_recv=(streams, count),
        y_send=(10, model // (2 * LANES)),
        y_recv=(10, model // (2 * LANES)),
    )
    for name, shape in semaphores.items():
        scratch[name] = pltpu.SemaphoreType.DMA(shape)
    vmem = pl.BlockSpec(memory_space=pltpu.VMEM)
    anywhere = pl.BlockSpec(memory_space=pl.ANY)
    sizes = (count, own_rows, width, hidden, rest, 1.0 / math.sqrt(2 * HEAD_HALF))
    layout = list(names) + ["cos_table", "sin_table"] + list(outs) + list(scratch)
    big = 6
    return pl.pallas_call(
        functools.partial(fused_kernel, sizes, layout),
        out_shape=[jax.ShapeDtypeStruct(shape, dtype) for shape, dtype in outs.values()],
        in_specs=[anywhere] * big + [vmem] * (len(layout) - big - len(outs) - len(scratch)),
        out_specs=[vmem] * len(outs),
        scratch_shapes=list(scratch.values()),
        compiler_params=pltpu.CompilerParams(
            collective_id=2, has_side_effects=True, vmem_limit_bytes=FUSED_LIMIT
        ),
        name="fused_layer",
    )(*arrays, *tables)


def copy_kernel(count, *refs):
    sources, targets, buffers = refs[:count], refs[count : 2 * count], refs[2 * count : 3 * count]
    sems = refs[3 * count]
    ins = [
        pltpu.make_async_copy(sources[index], buffers[index], sems.at[0, index])
        for index in range(count)
    ]
    outs = [
        pltpu.make_async_copy(buffers[index], targets[index], sems.at[1, index])
        for index in range(count)
    ]
    for copy in ins:
        copy.start()
    for index in range(count):
        ins[index].wait()
        outs[index].start()
    for copy in outs:
        copy.wait()


def finish_call(arrays):
    anywhere = pl.BlockSpec(memory_space=pl.ANY)
    count = len(arrays)
    return pl.pallas_call(
        functools.partial(copy_kernel, count),
        out_shape=[jax.ShapeDtypeStruct(array.shape, array.dtype) for array in arrays],
        in_specs=[anywhere] * count,
        out_specs=[anywhere] * count,
        scratch_shapes=[pltpu.VMEM(array.shape, array.dtype) for array in arrays]
        + [pltpu.SemaphoreType.DMA((2, count))],
        name="finish",
    )(*arrays)


FUSED_LIMIT = 63 * 1024 * 1024


def position_tables(total, head_size):
    half_size = head_size // 2
    freqs = THETA ** (-(2.0 / head_size) * np.arange(half_size))
    angles = np.arange(total)[:, None] * freqs[None, :]
    cos_table = np.cos(angles).astype(np.float32)
    sin_table = np.sin(angles).astype(np.float32)
    return (
        jnp.asarray(np.concatenate([cos_table] * 4, axis=1)),
        jnp.asarray(np.concatenate([-sin_table, sin_table] * 2, axis=1)),
    )


def fused_device(
    devices,
    tokens,
    segments,
    cotangent,
    qkv_weight,
    out_weight,
    in_weight,
    down_weight,
    attn_gain,
    mlp_gain,
):
    own_rows = tokens.shape[1]
    width = qkv_weight.shape[2]
    blocks = in_weight.shape[2] // LANES
    first = blocks // 2 * 2 * LANES
    widths = [2 * width, width, width, first, 2 * blocks * LANES - first, blocks * LANES, LANES]
    inputs = dict(
        in_qkv=jnp.transpose(qkv_weight, (1, 0, 2)),
        in_out=out_weight.T,
        in_in=in_weight,
        in_down=down_weight.T,
        in_tokens=tokens,
        in_cot=cotangent,
        seg=segments,
        attn_gain=attn_gain[None],
        mlp_gain=mlp_gain[None],
    )
    tables = position_tables(2 * own_rows, 2 * HEAD_HALF)
    results = finish_call(fused_call(inputs, tables, devices, widths))
    layer_out, tokens_grad, qkv, out, in_grad, down, attn_grad, mlp_grad = results
    return (
        layer_out,
        tokens_grad,
        jnp.transpose(qkv, (1, 0, 2)),
        out.T,
        in_grad,
        down.T,
        attn_grad[0],
        mlp_grad[0],
    )


def per_device(
    devices,
    seq_size,
    tokens,
    segments,
    cotangent,
    qkv_weight,
    out_weight,
    in_weight,
    down_weight,
    attn_gain,
    mlp_gain,
):
    args = (
        tokens,
        segments,
        cotangent,
        qkv_weight,
        out_weight,
        in_weight,
        down_weight,
        attn_gain,
        mlp_gain,
    )
    own_rows, model = tokens.shape[1:]
    sizes = (own_rows, model, qkv_weight.shape[2], in_weight.shape[2])
    if fits_fused(devices, seq_size, *sizes) and tokens.shape[0] == 1:
        return fused_device(devices, *args)
    return general_device(devices, seq_size, *args)


def solution(mesh):
    return jax.shard_map(
        functools.partial(per_device, mesh.shape["dp"], mesh.shape["seq"]),
        mesh=mesh,
        in_specs=(
            P("dp", "seq", None),
            P("dp", "seq"),
            P("dp", "seq", None),
            P("dp", None, "seq"),
            P("seq", "dp"),
            P("dp", None, "seq"),
            P("seq", "dp"),
            P("dp"),
            P("dp"),
        ),
        out_specs=(
            P("dp", "seq", None),
            P("dp", "seq", None),
            P("dp", None, "seq"),
            P("seq", "dp"),
            P("dp", None, "seq"),
            P("seq", "dp"),
            P("dp"),
            P("dp"),
        ),
        check_vma=False,
    )
```

```python
import functools
import math
import types

import jax
import jax.numpy as jnp
import numpy as np
from jax import lax
from jax.experimental import pallas as pl
from jax.experimental.pallas import tpu as pltpu
from jax.sharding import PartitionSpec as P

HEADS = 16
HALO = 64


EPS = 1e-05
THETA = 10000.0
NEG_FILL = -1e30


def norm_forward(values, gain):
    center = values - jnp.mean(values, axis=-1, keepdims=True)
    inv_std = lax.rsqrt(jnp.mean(center * center, axis=-1, keepdims=True) + EPS)
    unit_rows = center * inv_std
    return (unit_rows * gain, unit_rows, inv_std)


def norm_backward(grad_rows, gain, unit_rows, inv_std):
    scaled = grad_rows * gain
    inner = (
        scaled
        - jnp.mean(scaled, axis=-1, keepdims=True)
        - unit_rows * jnp.mean(scaled * unit_rows, axis=-1, keepdims=True)
    )
    return (inner * inv_std, jnp.sum(grad_rows * unit_rows, axis=0))


def gelu_value(inputs):
    return 0.5 * inputs * (1.0 + lax.erf(inputs * 0.7071067811865476))


def gelu_slope(inputs):
    return (
        0.5 * (1.0 + lax.erf(inputs * 0.7071067811865476))
        + inputs * jnp.exp(-0.5 * inputs * inputs) * 0.3989422804014327
    )


def rotary_tables(positions, head_size):
    half_size = head_size // 2
    freqs = jnp.power(THETA, -(2.0 / head_size) * jnp.arange(half_size, dtype=jnp.float32))
    angles = positions.astype(jnp.float32)[:, None] * freqs[None, :]
    return (jnp.cos(angles)[:, None, :], jnp.sin(angles)[:, None, :])


def rotate(values, cos_table, sin_table):
    half_size = values.shape[-1] // 2
    lower_half = values[..., :half_size]
    upper_half = values[..., half_size:]
    return jnp.concatenate(
        [
            lower_half * cos_table - upper_half * sin_table,
            upper_half * cos_table + lower_half * sin_table,
        ],
        axis=-1,
    )


def unrotate(grads, cos_table, sin_table):
    half_size = grads.shape[-1] // 2
    lower_half = grads[..., :half_size]
    upper_half = grads[..., half_size:]
    return jnp.concatenate(
        [
            lower_half * cos_table + upper_half * sin_table,
            upper_half * cos_table - lower_half * sin_table,
        ],
        axis=-1,
    )


def window_mask(query_pos, key_pos, query_seg, key_seg, halo_width, total_len):
    near = jnp.abs(query_pos[:, None] - key_pos[None, :]) <= halo_width
    inside = (key_pos >= 0) & (key_pos < total_len)
    return near & inside[None, :] & (query_seg[:, None] == key_seg[None, :])


def block_scores(queries, key_slab, allowed, scale):
    scores = (
        jnp.einsum("qhd,khd->hqk", queries, key_slab, preferred_element_type=jnp.float32) * scale
    )
    return jnp.where(allowed[None], scores, NEG_FILL)


def attend_block(queries, key_slab, value_slab, allowed, scale):
    scores = block_scores(queries, key_slab, allowed, scale)
    top_score = jnp.max(scores, axis=-1, keepdims=True)
    total = jnp.sum(jnp.exp(scores - top_score), axis=-1, keepdims=True)
    logsum = top_score + jnp.log(total)
    probs = jnp.exp(scores - logsum).astype(jnp.bfloat16)
    mixed = jnp.einsum("hqk,khd->qhd", probs, value_slab, preferred_element_type=jnp.float32)
    return (mixed, logsum[..., 0])


def attend_back(queries, key_slab, value_slab, allowed, scale, logsum, mixed_b, dmixed_b):
    scores = block_scores(queries, key_slab, allowed, scale)
    probs = jnp.exp(scores - logsum[..., None])
    probs_b = probs.astype(jnp.bfloat16)
    dvalues = jnp.einsum("hqk,qhd->khd", probs_b, dmixed_b, preferred_element_type=jnp.float32)
    dprobs = jnp.einsum("qhd,khd->hqk", dmixed_b, value_slab, preferred_element_type=jnp.float32)
    delta = jnp.transpose(
        jnp.sum(dmixed_b.astype(jnp.float32) * mixed_b.astype(jnp.float32), axis=-1)
    )
    dscores = (probs * (dprobs - delta[..., None]) * scale).astype(jnp.bfloat16)
    dqueries = jnp.einsum("hqk,khd->qhd", dscores, key_slab, preferred_element_type=jnp.float32)
    dkeys = jnp.einsum("hqk,qhd->khd", dscores, queries, preferred_element_type=jnp.float32)
    return (dqueries, dkeys, dvalues)


MESH = pl.DeviceIdType.MESH
VMEM_LIMIT = 60 * 1024 * 1024
LANES = 128


def ring_place(count):
    me = lax.axis_index("dp")
    core = me % 2
    chip = me // 2
    row, column = chip // 2, chip % 2
    place = (1 - column) * row + column * (count - 1 - row)
    return (core, place)


def chip_at(place, count):
    side = place // (count // 2)
    return (1 - side) * (2 * place) + side * (2 * (count - 1 - place) + 1)


def neighbours(core, place, count):
    right = chip_at((place + 1) % count, count) * 2 + core
    left = chip_at((place + count - 1) % count, count) * 2 + core
    return (right, left, lax.axis_index("dp") + 1 - 2 * core)


def greet(devices):
    barrier = pltpu.get_barrier_semaphore()
    for device in devices:
        pl.semaphore_signal(barrier, inc=1, device_id={"dp": device}, device_id_type=MESH)
    pl.semaphore_wait(barrier, len(devices))


def gather_kernel(count, streams, *refs):
    shards = refs[:streams]
    fulls = refs[streams : 2 * streams]
    own_sem, send_sem, recv_sem, pair_send, pair_recv = refs[2 * streams :]
    rows = shards[0].shape[0]
    half = rows // 2
    core, place = ring_place(count)
    right, left, partner = neighbours(core, place, count)
    targets = (right, left)
    lanes = [(way, stream) for stream in range(streams) for way in range(2)]

    def piece(way, step, stream):
        shift = count - step if way == 0 else step
        owner = chip_at((place + shift) % count, count) * 2 + core
        start = pl.multiple_of(owner * rows + way * half, half)
        return fulls[stream].at[pl.ds(start, half)]

    def hop(way, step, stream):
        ref = piece(way, step, stream)
        return pltpu.make_async_remote_copy(
            src_ref=ref,
            dst_ref=ref,
            send_sem=send_sem.at[stream, way, step],
            recv_sem=recv_sem.at[stream, way, step],
            device_id={"dp": targets[way]},
            device_id_type=MESH,
        )

    def share(way, step, stream):
        ref = piece(way, step, stream)
        return pltpu.make_async_remote_copy(
            src_ref=ref,
            dst_ref=ref,
            send_sem=pair_send.at[stream, way, step],
            recv_sem=pair_recv.at[stream, way, step],
            device_id={"dp": partner},
            device_id_type=MESH,
        )

    me = lax.axis_index("dp")
    owns = [
        pltpu.make_async_copy(
            shards[stream],
            fulls[stream].at[pl.ds(pl.multiple_of(me * rows, rows), rows)],
            own_sem.at[stream],
        )
        for stream in range(streams)
    ]
    for own in owns:
        own.start()
    greet((right, left, partner))
    for own in owns:
        own.wait()
    for way, stream in lanes:
        hop(way, 0, stream).start()
        share(way, 0, stream).start()

    def step_body(step, carry):
        for way, stream in lanes:
            hop(way, step - 1, stream).wait_recv()
            hop(way, step, stream).start()
            share(way, step, stream).start()
        return carry

    lax.fori_loop(1, count - 1, step_body, 0)
    for way, stream in lanes:
        hop(way, count - 2, stream).wait_recv()
        share(way, count - 1, stream).start()

    def drain_hops(step, carry):
        for way, stream in lanes:
            hop(way, step, stream).wait_send()
        return carry

    def drain_shares(step, carry):
        for way, stream in lanes:
            share(way, step, stream).wait_send()
            share(way, step, stream).wait_recv()
        return carry

    lax.fori_loop(0, count - 1, drain_hops, 0)
    lax.fori_loop(0, count, drain_shares, 0)


def ring_gather(shards, devices):
    count = devices // 2
    streams = len(shards)
    return pl.pallas_call(
        functools.partial(gather_kernel, count, streams),
        out_shape=[
            jax.ShapeDtypeStruct((devices * shard.shape[0], shard.shape[1]), shard.dtype)
            for shard in shards
        ],
        in_specs=[pl.BlockSpec(memory_space=pltpu.VMEM)] * streams,
        out_specs=[pl.BlockSpec(memory_space=pl.ANY)] * streams,
        scratch_shapes=[pltpu.SemaphoreType.DMA((streams,))]
        + [pltpu.SemaphoreType.DMA((streams, 2, count - 1))] * 2
        + [pltpu.SemaphoreType.DMA((streams, 2, count))] * 2,
        cost_estimate=pl.CostEstimate(
            flops=0, bytes_accessed=128 * 1024 * 1024, transcendentals=0
        ),
        compiler_params=pltpu.CompilerParams(
            collective_id=0, has_side_effects=True, vmem_limit_bytes=VMEM_LIMIT
        ),
        name="ring_gather",
    )(*shards)


def scatter_kernel(count, streams, *refs):
    grads = refs[:streams]
    outs = refs[streams : 2 * streams]
    pairs = refs[2 * streams : 3 * streams]
    sends = refs[3 * streams : 4 * streams]
    recvs = refs[4 * streams : 5 * streams]
    send_sem, recv_sem, pair_send, pair_recv = refs[5 * streams :]
    rows = outs[0].shape[0]
    half = rows // 2
    core, place = ring_place(count)
    right, left, partner = neighbours(core, place, count)
    targets = (right, left)

    def block(way, step, which):
        shift = 2 * count - 1 - step if way == 0 else 1 + step
        owner = chip_at((place + shift) % count, count) * 2 + which
        return pl.ds(pl.multiple_of(owner * rows + way * half, half), half)

    def share(way, step, stream):
        return pltpu.make_async_remote_copy(
            src_ref=grads[stream].at[block(way, step, 1 - core)],
            dst_ref=pairs[stream].at[way, step],
            send_sem=pair_send.at[stream, way, step],
            recv_sem=pair_recv.at[stream, way, step],
            device_id={"dp": partner},
            device_id_type=MESH,
        )

    def hop(way, step, stream):
        return pltpu.make_async_remote_copy(
            src_ref=sends[stream].at[way, step],
            dst_ref=recvs[stream].at[way, step],
            send_sem=send_sem.at[stream, way, step],
            recv_sem=recv_sem.at[stream, way, step],
            device_id={"dp": targets[way]},
            device_id_type=MESH,
        )

    def pair_sum(way, step, stream):
        share(way, step, stream).wait_recv()
        own = grads[stream][block(way, step, core), :].astype(jnp.float32)
        return own + pairs[stream][way, step].astype(jnp.float32)

    greet((right, left, partner))

    def start_shares(step, carry):
        for stream in range(streams):
            for way in range(2):
                share(way, step, stream).start()
        return carry

    lax.fori_loop(0, count, start_shares, 0)
    for stream in range(streams):
        for way in range(2):
            sends[stream][way, 0] = pair_sum(way, 0, stream).astype(jnp.bfloat16)
            hop(way, 0, stream).start()

    def step_body(step, carry):
        for stream in range(streams):
            for way in range(2):
                total = pair_sum(way, step, stream)
                hop(way, step - 1, stream).wait_recv()
                total = total + recvs[stream][way, step - 1].astype(jnp.float32)
                sends[stream][way, step] = total.astype(jnp.bfloat16)
                hop(way, step, stream).start()
        return carry

    lax.fori_loop(1, count - 1, step_body, 0)
    for stream in range(streams):
        for way in range(2):
            total = pair_sum(way, count - 1, stream)
            hop(way, count - 2, stream).wait_recv()
            total = total + recvs[stream][way, count - 2].astype(jnp.float32)
            outs[stream][way * half : (way + 1) * half, :] = total

    def drain_hops(step, carry):
        for stream in range(streams):
            for way in range(2):
                hop(way, step, stream).wait_send()
        return carry

    def drain_shares(step, carry):
        for stream in range(streams):
            for way in range(2):
                share(way, step, stream).wait_send()
        return carry

    lax.fori_loop(0, count - 1, drain_hops, 0)
    lax.fori_loop(0, count, drain_shares, 0)


def ring_scatter(grads, devices):
    count = devices // 2
    streams = len(grads)
    rows = grads[0].shape[0] // devices
    half = rows // 2
    widths = [grad.shape[1] for grad in grads]
    vmem = pl.BlockSpec(memory_space=pltpu.VMEM)
    return pl.pallas_call(
        functools.partial(scatter_kernel, count, streams),
        out_shape=[jax.ShapeDtypeStruct((rows, width), jnp.float32) for width in widths],
        in_specs=[vmem] * streams,
        out_specs=[vmem] * streams,
        scratch_shapes=[pltpu.VMEM((2, count, half, width), jnp.bfloat16) for width in widths]
        + [pltpu.VMEM((2, count - 1, half, width), jnp.bfloat16) for width in widths] * 2
        + [pltpu.SemaphoreType.DMA((streams, 2, count - 1))] * 2
        + [pltpu.SemaphoreType.DMA((streams, 2, count))] * 2,
        compiler_params=pltpu.CompilerParams(
            collective_id=1, has_side_effects=True, vmem_limit_bytes=40 * 1024 * 1024
        ),
        name="ring_scatter",
    )(*grads)


def turn(values, cos_table, sin_table, low_half):
    half = HEAD_HALF
    swapped = jnp.where(
        low_half, pltpu.roll(values, LANES - half, 1), pltpu.roll(values, half, 1)
    )
    return values * cos_table + swapped * sin_table


HEAD_HALF = 32


def lane_masks(rows):
    lane = lax.broadcasted_iota(jnp.int32, (rows, LANES), 1)
    return (lane % (2 * HEAD_HALF) < HEAD_HALF, lane < 2 * HEAD_HALF)


def allowed_pairs(pos_col, pos_row, seg_col, seg_row):
    near = jnp.abs(pos_col[...] - pos_row[...]) <= HALO
    return near & (seg_col[...] == seg_row[...])


def head_probs(queries, keys, allowed, scale):
    scores = (
        lax.dot_general(
            queries, keys, (((1,), (1,)), ((), ())), preferred_element_type=jnp.float32
        )
        * scale
    )
    scores = jnp.where(allowed, scores, NEG_FILL)
    top_score = jnp.max(scores, axis=-1, keepdims=True)
    total = jnp.sum(jnp.exp(scores - top_score), axis=-1, keepdims=True)
    return jnp.exp(scores - (top_score + jnp.log(total)))


def attend_kernel(
    scale, width, proj, cos_ref, sin_ref, pos_col, pos_row, seg_col, seg_row, qkv_out, mixed_out
):
    rows = proj.shape[0]
    low_half, first = lane_masks(rows)
    cos_table, sin_table = cos_ref[...], sin_ref[...]
    allowed = allowed_pairs(pos_col, pos_row, seg_col, seg_row)
    for start in range(0, width, LANES):
        queries = turn(proj[:, start : start + LANES], cos_table, sin_table, low_half)
        keys = turn(
            proj[:, width + start : width + start + LANES], cos_table, sin_table, low_half
        ).astype(jnp.bfloat16)
        values = proj[:, 2 * width + start : 2 * width + start + LANES]
        qkv_out[:, start : start + LANES] = queries.astype(jnp.bfloat16)
        qkv_out[:, width + start : width + start + LANES] = keys
        qkv_out[:, 2 * width + start : 2 * width + start + LANES] = values.astype(jnp.bfloat16)
        mixed = jnp.zeros((rows, LANES), jnp.float32)
        for head in range(2):
            mine = first if head == 0 else ~first
            probs = head_probs(
                jnp.where(mine, queries, 0.0).astype(jnp.bfloat16), keys, allowed, scale
            ).astype(jnp.bfloat16)
            mixed = mixed + jnp.dot(
                probs,
                jnp.where(mine, values, 0.0).astype(jnp.bfloat16),
                preferred_element_type=jnp.float32,
            )
        mixed_out[:, start : start + LANES] = mixed.astype(jnp.bfloat16)


def attend_back_kernel(
    scale,
    width,
    qkv,
    mixed_ref,
    dmixed_ref,
    cos_ref,
    sin_ref,
    pos_col,
    pos_row,
    seg_col,
    seg_row,
    dqkv_out,
):
    rows = qkv.shape[0]
    low_half, first = lane_masks(rows)
    cos_table, sin_table = cos_ref[...], -sin_ref[...]
    allowed = allowed_pairs(pos_col, pos_row, seg_col, seg_row)
    over_rows = (((0,), (0,)), ((), ()))
    over_lanes = (((1,), (1,)), ((), ()))
    for start in range(0, width, LANES):
        queries = qkv[:, start : start + LANES].astype(jnp.float32)
        keys = qkv[:, width + start : width + start + LANES]
        keys32 = keys.astype(jnp.float32)
        values = qkv[:, 2 * width + start : 2 * width + start + LANES]
        dmixed = dmixed_ref[:, start : start + LANES].astype(jnp.float32)
        products = dmixed * mixed_ref[:, start : start + LANES].astype(jnp.float32)
        dquery = jnp.zeros((rows, LANES), jnp.float32)
        dkey = jnp.zeros((rows, LANES), jnp.float32)
        dvalue = jnp.zeros((rows, LANES), jnp.float32)
        for head in range(2):
            mine = first if head == 0 else ~first
            head_queries = jnp.where(mine, queries, 0.0).astype(jnp.bfloat16)
            head_keys = jnp.where(mine, keys32, 0.0).astype(jnp.bfloat16)
            head_dmixed = jnp.where(mine, dmixed, 0.0).astype(jnp.bfloat16)
            delta = jnp.sum(jnp.where(mine, products, 0.0), axis=-1, keepdims=True)
            probs = head_probs(head_queries, keys, allowed, scale)
            dprobs = lax.dot_general(
                head_dmixed, values, over_lanes, preferred_element_type=jnp.float32
            )
            dscores = (probs * (dprobs - delta) * scale).astype(jnp.bfloat16)
            dvalue = dvalue + lax.dot_general(
                probs.astype(jnp.bfloat16),
                head_dmixed,
                over_rows,
                preferred_element_type=jnp.float32,
            )
            dkey = dkey + lax.dot_general(
                dscores, head_queries, over_rows, preferred_element_type=jnp.float32
            )
            dquery = dquery + jnp.dot(dscores, head_keys, preferred_element_type=jnp.float32)
        dquery = turn(dquery, cos_table, sin_table, low_half)
        dkey = turn(dkey, cos_table, sin_table, low_half)
        dqkv_out[:, start : start + LANES] = dquery.astype(jnp.bfloat16)
        dqkv_out[:, width + start : width + start + LANES] = dkey.astype(jnp.bfloat16)
        dqkv_out[:, 2 * width + start : 2 * width + start + LANES] = dvalue.astype(jnp.bfloat16)


def local_call(kernel, name, out_shape, operands, flops):
    vmem = pl.BlockSpec(memory_space=pltpu.VMEM)
    single = not isinstance(out_shape, list)
    return pl.pallas_call(
        kernel,
        out_shape=out_shape,
        in_specs=[vmem] * len(operands),
        out_specs=vmem if single else [vmem] * len(out_shape),
        cost_estimate=pl.CostEstimate(
            flops=flops, bytes_accessed=4 * 1024 * 1024, transcendentals=flops // 256
        ),
        compiler_params=pltpu.CompilerParams(vmem_limit_bytes=32 * 1024 * 1024),
        name=name,
    )(*operands)


class PairedAttention:
    def __init__(self, positions, segments, head_size, width):
        rows = positions.shape[0]
        cos_table, sin_table = rotary_tables(positions, head_size)
        cos_table, sin_table = cos_table[:, 0, :], sin_table[:, 0, :]
        self.width = width
        self.scale = 1.0 / math.sqrt(head_size)
        self.flops = 2 * rows * rows * LANES * (width // head_size)
        self.shared = (
            jnp.concatenate([cos_table] * 4, axis=1),
            jnp.concatenate([-sin_table, sin_table] * 2, axis=1),
            positions[:, None],
            positions[None, :],
            segments[:, None],
            segments[None, :],
        )

    def forward(self, projected):
        rows = projected.shape[0]
        self.qkv, self.mixed = local_call(
            functools.partial(attend_kernel, self.scale, self.width),
            "attend",
            [
                jax.ShapeDtypeStruct((rows, 3 * self.width), jnp.bfloat16),
                jax.ShapeDtypeStruct((rows, self.width), jnp.bfloat16),
            ],
            (projected,) + self.shared,
            2 * self.flops,
        )
        return self.mixed

    def backward(self, dmixed):
        rows = dmixed.shape[0]
        return local_call(
            functools.partial(attend_back_kernel, self.scale, self.width),
            "attend_back",
            jax.ShapeDtypeStruct((rows, 3 * self.width), jnp.bfloat16),
            (self.qkv, self.mixed, dmixed) + self.shared,
            5 * self.flops,
        )


class BlockAttention:
    def __init__(self, positions, segments, head_size, width):
        self.total_len = positions.shape[0]
        self.segments = segments
        self.head_size = head_size
        self.width = width
        self.scale = 1.0 / math.sqrt(head_size)
        self.cos_table, self.sin_table = rotary_tables(positions, head_size)

    def heads(self, values):
        return values.reshape(self.total_len, self.width // self.head_size, self.head_size)

    def forward(self, projected):
        width, total_len = self.width, self.total_len
        self.block_rows = min(total_len, 512)
        self.slab_rows = self.block_rows + 2 * HALO
        tables = (self.cos_table, self.sin_table)
        self.queries = rotate(self.heads(projected[:, :width]), *tables).astype(jnp.bfloat16)
        keys = rotate(self.heads(projected[:, width : 2 * width]), *tables).astype(jnp.bfloat16)
        values = self.heads(projected[:, 2 * width :]).astype(jnp.bfloat16)
        pad_spec = ((HALO, HALO), (0, 0), (0, 0))
        self.key_pad = jnp.pad(keys, pad_spec)
        self.value_pad = jnp.pad(values, pad_spec)
        seg_pad = jnp.pad(self.segments, (HALO, HALO), constant_values=-1)
        mixed_parts = []
        self.logsums = []
        self.masks = []
        for start in range(0, total_len, self.block_rows):
            own = slice(start, start + self.block_rows)
            slab = slice(start, start + self.slab_rows)
            allowed = window_mask(
                start + jnp.arange(self.block_rows, dtype=jnp.int32),
                start - HALO + jnp.arange(self.slab_rows, dtype=jnp.int32),
                self.segments[own],
                seg_pad[slab],
                HALO,
                total_len,
            )
            mixed, logsum = attend_block(
                self.queries[own], self.key_pad[slab], self.value_pad[slab], allowed, self.scale
            )
            self.masks.append(allowed)
            self.logsums.append(logsum)
            mixed_parts.append(mixed)
        self.mixed = jnp.concatenate(mixed_parts, axis=0).astype(jnp.bfloat16)
        return self.mixed.reshape(total_len, width)

    def backward(self, dmixed):
        total_len = self.total_len
        dmixed = self.heads(dmixed)
        padded = (total_len + 2 * HALO,) + dmixed.shape[1:]
        dkey_pad = jnp.zeros(padded, jnp.float32)
        dvalue_pad = jnp.zeros(padded, jnp.float32)
        dquery_parts = []
        for index, start in enumerate(range(0, total_len, self.block_rows)):
            own = slice(start, start + self.block_rows)
            slab = slice(start, start + self.slab_rows)
            dqueries, dkeys, dvalues = attend_back(
                self.queries[own],
                self.key_pad[slab],
                self.value_pad[slab],
                self.masks[index],
                self.scale,
                self.logsums[index],
                self.mixed[own],
                dmixed[own],
            )
            dquery_parts.append(dqueries)
            dkey_pad = dkey_pad.at[slab].add(dkeys)
            dvalue_pad = dvalue_pad.at[slab].add(dvalues)
        inner = slice(HALO, HALO + total_len)
        tables = (self.cos_table, self.sin_table)
        parts = [
            unrotate(jnp.concatenate(dquery_parts, axis=0), *tables),
            unrotate(dkey_pad[inner], *tables),
            dvalue_pad[inner],
        ]
        return jnp.concatenate(
            [part.reshape(total_len, self.width) for part in parts], axis=1
        ).astype(jnp.bfloat16)


def dot(left, right, left_dim, right_dim):
    return lax.dot_general(
        left,
        right,
        (((left_dim,), (right_dim,)), ((), ())),
        preferred_element_type=jnp.float32,
    )


def padded_to_lanes(values):
    return jnp.pad(values, ((0, 0), (0, -values.shape[1] % LANES)))


def high_and_low(gain):
    high = gain.astype(jnp.bfloat16)
    return [high[:, None], (gain - high.astype(jnp.float32)).astype(jnp.bfloat16)[:, None]]


def general_device(
    devices,
    seq_size,
    tokens,
    segments,
    cotangent,
    qkv_weight,
    out_weight,
    in_weight,
    down_weight,
    attn_gain,
    mlp_gain,
):
    layer_in = tokens[0]
    seg_local = segments[0]
    cot_local = cotangent[0]
    own_rows, model_width = layer_in.shape
    head_size = model_width // HEADS
    local_width = qkv_weight.shape[2]
    local_hidden = in_weight.shape[2]
    shard_rows = qkv_weight.shape[0]
    total_len = own_rows * seq_size
    paired = (
        seq_size == 2
        and total_len <= 512
        and local_width % LANES == 0
        and head_size == 2 * HEAD_HALF
    )
    swap = [(0, 1), (1, 0)]

    def rows_of_all(values):
        if paired:
            return jnp.concatenate([values, lax.ppermute(values, "seq", swap)], axis=0)
        return lax.all_gather(values, "seq", axis=0, tiled=True)

    def sum_to_owner(partial):
        if paired:
            other = lax.ppermute(partial[own_rows:].astype(jnp.bfloat16), "seq", swap)
            return partial[:own_rows] + other.astype(jnp.float32)
        return lax.psum_scatter(
            partial.astype(jnp.bfloat16), "seq", scatter_dimension=0, tiled=True
        ).astype(jnp.float32)

    def sum_over_seq(part):
        if paired:
            return part + lax.ppermute(part, "seq", swap)
        return lax.psum(part, "seq")

    first_pack = jnp.concatenate(
        [qkv_weight.reshape(shard_rows, 3 * local_width), out_weight.T], axis=1
    )
    wide = (local_hidden + 4 + LANES - 1) // LANES * LANES
    spare = jnp.zeros((shard_rows, wide - local_hidden), jnp.bfloat16)
    second_pack = jnp.concatenate(
        [in_weight[:, 0, :], spare, in_weight[:, 1, :], spare, down_weight.T]
        + high_and_low(attn_gain)
        + high_and_low(mlp_gain)
        + [spare[:, 4:]],
        axis=1,
    )
    first_full, second_full = ring_gather([first_pack, second_pack], devices)
    full_qkv = first_full[:, : 3 * local_width]
    full_out = first_full[:, 3 * local_width : 4 * local_width]
    gains_at = 2 * wide + local_hidden
    gains = second_full[:, gains_at : gains_at + 4].astype(jnp.float32)
    gain_attn = gains[:, 0] + gains[:, 1]
    gain_mlp = gains[:, 2] + gains[:, 3]
    full_in = second_full[:, : 2 * wide]
    full_down = second_full[:, 2 * wide :]

    inputs32 = layer_in.astype(jnp.float32)
    if paired:
        arrived = lax.ppermute(jnp.concatenate([layer_in, cot_local], axis=0), "seq", swap)
        all_inputs32 = jnp.concatenate([layer_in, arrived[:own_rows]], axis=0).astype(jnp.float32)
        cot_full = jnp.concatenate([cot_local, arrived[own_rows:]], axis=0)
    else:
        all_inputs32 = rows_of_all(layer_in).astype(jnp.float32)
        cot_full = rows_of_all(cot_local)
    normed_full = norm_forward(all_inputs32, gain_attn)[0].astype(jnp.bfloat16)
    unit_one, inv_one = norm_forward(inputs32, gain_attn)[1:]
    if paired:
        seg_full = rows_of_all(
            jnp.broadcast_to(seg_local.astype(jnp.float32)[:, None], (own_rows, LANES))
        )[:, 0].astype(jnp.int32)
        place = lax.axis_index("seq")
        arange = jnp.arange(own_rows, dtype=jnp.int32)
        positions = jnp.concatenate(
            [place * own_rows + arange, (1 - place) * own_rows + arange], axis=0
        )
        attention = PairedAttention(positions, seg_full, head_size, local_width)
    else:
        seg_full = rows_of_all(seg_local.astype(jnp.bfloat16)).astype(jnp.int32)
        positions = jnp.arange(total_len, dtype=jnp.int32)
        attention = BlockAttention(positions, seg_full, head_size, local_width)

    mixed = attention.forward(dot(normed_full, full_qkv, 1, 0))
    residual = inputs32 + sum_to_owner(dot(mixed, full_out, 1, 1))
    normed_two, unit_two, inv_two = norm_forward(residual, gain_mlp)
    normed_two_full = rows_of_all(normed_two.astype(jnp.bfloat16))
    expanded = dot(normed_two_full, full_in, 1, 0)
    gate_in = expanded[:, :wide]
    linear_in = expanded[:, wide:]
    activated = gelu_value(gate_in)
    middle_b = (activated * linear_in).astype(jnp.bfloat16)
    down_part = dot(middle_b, full_down, 1, 1)

    down_grad = dot(cot_full, middle_b, 0, 0).astype(jnp.bfloat16)
    dmiddle = dot(cot_full, full_down, 1, 0)
    dexpanded_b = jnp.concatenate(
        [dmiddle * linear_in * gelu_slope(gate_in), dmiddle * activated], axis=1
    ).astype(jnp.bfloat16)
    dnormed_two = sum_to_owner(dot(dexpanded_b, full_in, 1, 1))
    in_grad = dot(normed_two_full, dexpanded_b, 0, 0).astype(jnp.bfloat16)
    dres_norm, mlp_gain_part = norm_backward(dnormed_two, gain_mlp, unit_two, inv_two)
    dresidual = cot_local.astype(jnp.float32) + dres_norm
    dres_full = rows_of_all(dresidual.astype(jnp.bfloat16))
    down_part, dres_full = lax.optimization_barrier((down_part, dres_full))
    layer_out = (residual + sum_to_owner(down_part)).astype(jnp.bfloat16)
    dmixed = dot(dres_full, full_out, 1, 0).astype(jnp.bfloat16)
    out_grad = dot(dres_full, mixed, 0, 0).astype(jnp.bfloat16)
    dqkv_b = attention.backward(dmixed)
    layer_out, dqkv_b = lax.optimization_barrier((layer_out, dqkv_b))
    dnormed_one = sum_to_owner(dot(dqkv_b, full_qkv, 1, 1))
    qkv_grad = dot(normed_full, dqkv_b, 0, 0).astype(jnp.bfloat16)
    dinput_norm, attn_gain_part = norm_backward(dnormed_one, gain_attn, unit_one, inv_one)
    tokens_grad = (dresidual + dinput_norm).astype(jnp.bfloat16)
    gain_sums = sum_over_seq(jnp.stack([attn_gain_part, mlp_gain_part]))
    gain_grad = padded_to_lanes(gain_sums.T).astype(jnp.bfloat16)

    in_share, qkv_share, down_share, out_share, gain_share = ring_scatter(
        [in_grad, qkv_grad, down_grad, out_grad, gain_grad], devices
    )
    return (
        layer_out[None],
        tokens_grad[None],
        qkv_share.reshape(shard_rows, 3, local_width),
        out_share.T,
        jnp.stack([in_share[:, :local_hidden], in_share[:, wide : wide + local_hidden]], axis=1),
        down_share[:, :local_hidden].T,
        gain_share[:, 0],
        gain_share[:, 1],
    )


HIGH = (((1,), (1,)), ((), ()))
OVER_ROWS = (((0,), (0,)), ((), ()))


def fits_fused(devices, seq_size, own_rows, model_width, local_width, local_hidden):
    rest = local_hidden % LANES
    shard_rows = model_width // devices
    return (
        seq_size == 2
        and devices % 4 == 0
        and devices >= 8
        and own_rows == LANES
        and local_width % (2 * LANES) == 0
        and model_width % (2 * LANES) == 0
        and model_width // HEADS == 2 * HEAD_HALF
        and 3 * rest + 8 <= LANES
        and local_hidden // LANES >= 4
        and local_hidden // LANES % 2 == 0
        and shard_rows % 32 == 0
        and own_rows * 2 * LANES // model_width % 16 == 0
    )


def nt(left, right):
    return lax.dot_general(left, right, HIGH, preferred_element_type=jnp.float32)


def nn(left, right):
    return jnp.dot(left, right, preferred_element_type=jnp.float32)


def tiles(total, width, body):
    def step(index, carry):
        body(index, pl.ds(pl.multiple_of(index * width, width), width))
        return carry

    lax.fori_loop(0, total // width, step, 0)


def fused_kernel(sizes, layout, *refs):
    count, own_rows, width, hidden, rest, scale = sizes
    total_rows = 2 * own_rows
    r = types.SimpleNamespace(**dict(zip(layout, refs)))
    model = r.tokens.shape[1]
    streams = 8
    fulls = [getattr(r, "full%d" % i) for i in range(streams)]
    grads = [getattr(r, "grad%d" % i) for i in range(streams)]
    pairs = [getattr(r, "pair%d" % i) for i in range(streams)]
    ends = [getattr(r, "end%d" % i) for i in range(streams)]
    recvs = [getattr(r, "recv%d" % i) for i in range(streams)]
    rows = model // (2 * count)
    half = rows // 2
    turns = count // 2
    core, place = ring_place(count)
    right, left, partner = neighbours(core, place, count)
    targets = (right, left)
    me = lax.axis_index("dp")
    mine = lax.axis_index("seq")
    other = 1 - mine
    f32, bf16 = jnp.float32, jnp.bfloat16
    my_rows = pl.ds(pl.multiple_of(me * rows, rows), rows)

    def remote(src, dst, send, recv, device):
        return pltpu.make_async_remote_copy(
            src_ref=src,
            dst_ref=dst,
            send_sem=send,
            recv_sem=recv,
            device_id=device,
            device_id_type=MESH,
        )


    def piece(way, distance, stream, whole):
        shift = count - distance if way == 0 else distance
        owner = chip_at((place + shift) % count, count) * 2 + core
        if whole:
            where = pl.ds(pl.multiple_of(owner * rows, rows), rows)
        else:
            where = pl.ds(pl.multiple_of(owner * rows + way * half, half), half)
        return fulls[stream].at[where]

    def hop(way, step, stream):
        ref = piece(way, step, stream, step < turns - 1)
        sems = r.g_send.at[stream, way, step], r.g_recv.at[stream, way, step]
        return remote(ref, ref, *sems, {"dp": targets[way]})

    def share(way, step, stream):
        ref = piece(way, step, stream, step < turns)
        sems = r.gp_send.at[stream, way, step], r.gp_recv.at[stream, way, step]
        return remote(ref, ref, *sems, {"dp": partner})

    def gather_ops(stream):
        def start():
            for way in range(2):
                hop(way, 0, stream).start()
            share(0, 0, stream).start()

        def middle(step):
            for way in range(2):
                hop(way, step - 1, stream).wait_recv()
                hop(way, step, stream).start()
                share(way, step, stream).start()

        def last():
            for way in range(2):
                hop(way, turns - 1, stream).wait_recv()
                share(way, turns, stream).start()

        steps = [functools.partial(middle, step) for step in range(1, turns)]
        return [start] + steps + [last]

    def gather_shares(stream):
        return [share(0, 0, stream)] + [
            share(way, step, stream) for step in range(1, turns + 1) for way in range(2)
        ]

    def gather_arrived(stream):
        end(gathers, stream)
        for part in gather_shares(stream):
            part.wait_recv()

    def gather_drain(stream):
        for step in range(turns):
            for way in range(2):
                hop(way, step, stream).wait_send()
        for part in gather_shares(stream):
            part.wait_send()


    def block(ahead, which):
        owner = chip_at((place + ahead) % count, count) * 2 + which
        return pl.ds(pl.multiple_of(owner * rows, rows), rows)

    def give(ahead, stream):
        return remote(
            grads[stream].at[block(ahead, 1 - core)],
            pairs[stream].at[ahead],
            r.sp_send.at[stream, ahead],
            r.sp_recv.at[stream, ahead],
            {"dp": partner},
        )

    def ahead_of(way, step):
        return turns - step if way == 0 else turns + step

    def push(way, step, stream):
        sems = r.s_send.at[stream, way, step], r.s_recv.at[stream, way, step]
        if step == 0:
            src = pairs[stream].at[turns, pl.ds(way * half, half)]
            return remote(src, ends[stream].at[way], *sems, {"dp": targets[way]})
        src = pairs[stream].at[ahead_of(way, step)]
        return remote(src, recvs[stream].at[way, step - 1], *sems, {"dp": targets[way]})

    def pair_sum(ahead, stream):
        give(ahead, stream).wait_recv()
        own = grads[stream][block(ahead, core), :].astype(f32)
        return own + pairs[stream][ahead].astype(f32)

    def scatter_ops(stream, finish):
        def gives():
            order = [turns] + [turns + sign * d for d in range(1, turns) for sign in (-1, 1)] + [0]
            for ahead in order:
                give(ahead, stream).start()

        def start():
            pairs[stream][turns] = pair_sum(turns, stream).astype(bf16)
            for way in range(2):
                push(way, 0, stream).start()

        def middle(step):
            for way in range(2):
                ahead = ahead_of(way, step)
                total = pair_sum(ahead, stream)
                push(way, step - 1, stream).wait_recv()
                if step == 1:
                    near = ends[stream][way].astype(f32)
                    parts = [total[:half], total[half:]]
                    parts[way] = parts[way] + near
                    total = jnp.concatenate(parts, axis=0)
                else:
                    total = total + recvs[stream][way, step - 2].astype(f32)
                pairs[stream][ahead] = total.astype(bf16)
                push(way, step, stream).start()

        def last():
            total = pair_sum(0, stream)
            for way in range(2):
                push(way, turns - 1, stream).wait_recv()
                total = total + recvs[stream][way, turns - 2].astype(f32)
            finish(total)

        steps = [functools.partial(middle, step) for step in range(1, turns)]
        return [gives, start] + steps + [last]

    def scatter_drain(stream):
        for step in range(turns):
            for way in range(2):
                push(way, step, stream).wait_send()
        for ahead in range(count):
            give(ahead, stream).wait_send()


    own = pl.ds(0, own_rows)
    far = pl.ds(own_rows, own_rows)
    exchanged = [
        (r.seg_own, r.seg_other),
        (r.tokens, r.tok_other),
        (r.cot, r.cot_all.at[far]),
        (r.out_send, r.out_recv),
        (r.n2.at[own], r.n2.at[far]),
        (r.down_send, r.down_recv),
        (r.dn2_send, r.dn2_recv),
        (r.dres.at[own], r.dres.at[far]),
        (r.dn1_send, r.dn1_recv),
        (r.gain_part, r.gain_recv),
    ]
    by_lanes, by_rows = (3, 5, 6, 8), (4, 7)
    chunks = model // (2 * LANES)
    chunk_rows = own_rows // chunks

    def swap(index, part=0):
        src, dst = exchanged[index]
        if index in by_lanes:
            lanes = pl.ds(pl.multiple_of(part * 2 * LANES, 2 * LANES), 2 * LANES)
            src, dst = src.at[:, lanes], dst.at[:, lanes]
        elif index in by_rows:
            here = pl.ds(pl.multiple_of(part * chunk_rows, chunk_rows), chunk_rows)
            src, dst = src.at[here], dst.at[here]
        sems = r.y_send.at[index, part], r.y_recv.at[index, part]
        return remote(src, dst, *sems, {"seq": other})

    def parts_of(index):
        return chunks if index in by_lanes + by_rows else 1

    def arrived(index):
        def body(part, carry):
            swap(index, part).wait_recv()
            return carry

        lax.fori_loop(0, parts_of(index), body, 0)

    def swap_drain(index):
        def body(part, carry):
            swap(index, part).wait_send()
            return carry

        lax.fori_loop(0, parts_of(index), body, 0)


    def normed(values):
        center = values - jnp.mean(values, axis=-1, keepdims=True)
        inv_std = lax.rsqrt(jnp.mean(center * center, axis=-1, keepdims=True) + EPS)
        return center * inv_std, inv_std

    def to_columns(src, dst):
        def body(index, lanes):
            dst[lanes, :] = src[:, lanes].astype(f32).T.astype(bf16)

        tiles(model, LANES, body)

    def partial_sums(terms, own_ref, send_ref, exchange):
        def body(index, lanes):
            total = sum(nt(left[...], right[lanes, :]) for left, right in terms)
            own_ref[:, lanes] = total[:own_rows]
            send_ref[:, lanes] = total[own_rows:].astype(bf16)
            swap(exchange, index).start()

        tiles(model, 2 * LANES, body)

    def weight_grad(columns, right, out):
        size = right.shape[1]

        def body(index, lanes):
            out[:, lanes] = nn(columns[...], right[:, lanes]).astype(bf16)

        whole = size // (2 * LANES) * 2 * LANES
        tiles(whole, 2 * LANES, body)
        if whole < size:
            body(0, pl.ds(whole, size - whole))

    blocks = width // LANES
    hidden_blocks = hidden // LANES
    lane = lax.broadcasted_iota(jnp.int32, (total_rows, LANES), 1)
    low_half = lane % (2 * HEAD_HALF) < HEAD_HALF
    first = lane < 2 * HEAD_HALF

    def setup():
        r.cos[own, :] = r.cos_table[pl.ds(pl.multiple_of(mine * own_rows, own_rows), own_rows), :]
        r.cos[far, :] = r.cos_table[pl.ds(pl.multiple_of(other * own_rows, own_rows), own_rows), :]
        r.sin[own, :] = r.sin_table[pl.ds(pl.multiple_of(mine * own_rows, own_rows), own_rows), :]
        r.sin[far, :] = r.sin_table[pl.ds(pl.multiple_of(other * own_rows, own_rows), own_rows), :]

    def position(dim):
        index = lax.broadcasted_iota(jnp.int32, (total_rows, total_rows), dim)
        return jnp.where(index < own_rows, index + mine * own_rows, index - mine * own_rows)

    def make_bias():
        seg_row = jnp.concatenate([r.seg_own[0:1, :], r.seg_other[0:1, :]], axis=1).astype(f32)
        across = jnp.broadcast_to(seg_row, (total_rows, total_rows))
        allowed = (jnp.abs(position(0) - position(1)) <= HALO) & (across == across.T)
        r.bias[...] = jnp.where(allowed, 0.0, NEG_FILL)

    def expand_special():
        spot = lax.broadcasted_iota(jnp.int32, (2 * LANES, LANES), 1)
        keep = spot < rest

        def body(index, here):
            part = fulls[6][here, :].astype(f32)
            r.gains[:, here] = part.T[3 * rest : 3 * rest + 8]
            r.sp_in[here, :LANES] = jnp.where(keep, part, 0.0).astype(bf16)
            r.sp_in[here, LANES:] = jnp.where(
                keep, pltpu.roll(part, LANES - rest, 1), 0.0
            ).astype(bf16)
            r.sp_down[here, :] = jnp.where(
                keep, pltpu.roll(part, LANES - 2 * rest, 1), 0.0
            ).astype(bf16)

        tiles(model, 2 * LANES, body)

    def attn_gain():
        return r.gains[0:1, :] + r.gains[1:2, :]

    def mlp_gain():
        return r.gains[2:3, :] + r.gains[3:4, :]

    def norm_one():
        for src, place_of in ((r.tokens, 0), (r.tok_other, own_rows)):
            def body(index, here):
                unit_rows, _ = normed(src[here, :].astype(f32))
                at = pl.ds(pl.multiple_of(index * 32 + place_of, 32), 32)
                r.n1[at, :] = (unit_rows * attn_gain()).astype(bf16)

            tiles(own_rows, 32, body)

    def values_of():
        def body(index, lanes):
            r.v[:, lanes] = nn(r.n1[...], fulls[1][:, lanes]).astype(bf16)

        tiles(width, 2 * LANES, body)

    def attend(index, wide, lanes):
        cos_table, sin_table = r.cos[...], r.sin[...]
        proj = nn(r.n1[...], fulls[0][:, wide])
        queries = turn(proj[:, :LANES], cos_table, sin_table, low_half)
        keys = turn(proj[:, LANES:], cos_table, sin_table, low_half).astype(bf16)
        r.qk[:, wide] = jnp.concatenate([queries.astype(bf16), keys], axis=1)
        values = r.v[:, lanes].astype(f32)
        mixed = jnp.zeros((total_rows, LANES), f32)
        for head in range(2):
            here = first if head == 0 else ~first
            scores = nt(jnp.where(here, queries, 0.0).astype(bf16), keys) * scale + r.bias[...]
            top_score = jnp.max(scores, axis=-1, keepdims=True)
            total = jnp.sum(jnp.exp(scores - top_score), axis=-1, keepdims=True)
            probs = jnp.exp(scores - (top_score + jnp.log(total)))
            r.probs[index * 2 + head] = probs
            mixed = mixed + nn(probs.astype(bf16), jnp.where(here, values, 0.0).astype(bf16))
        r.mixed[:, lanes] = mixed.astype(bf16)

    def attend_back(index, wide, lanes):
        cos_table, sin_table = r.cos[...], -r.sin[...]
        both = r.qk[:, wide]
        queries = both[:, :LANES].astype(f32)
        keys = both[:, LANES:].astype(f32)
        values = r.v[:, lanes]
        dmixed = r.dmixed[:, lanes].astype(f32)
        products = dmixed * r.mixed[:, lanes].astype(f32)
        dquery = jnp.zeros((total_rows, LANES), f32)
        dkey = jnp.zeros((total_rows, LANES), f32)
        dvalue = jnp.zeros((total_rows, LANES), f32)
        for head in range(2):
            here = first if head == 0 else ~first
            head_queries = jnp.where(here, queries, 0.0).astype(bf16)
            head_keys = jnp.where(here, keys, 0.0).astype(bf16)
            head_dmixed = jnp.where(here, dmixed, 0.0).astype(bf16)
            delta = jnp.sum(jnp.where(here, products, 0.0), axis=-1, keepdims=True)
            probs = r.probs[index * 2 + head]
            dprobs = nt(head_dmixed, values)
            dscores = (probs * (dprobs - delta) * scale).astype(bf16)
            dvalue = dvalue + lax.dot_general(
                probs.astype(bf16), head_dmixed, OVER_ROWS, preferred_element_type=f32
            )
            dkey = dkey + lax.dot_general(
                dscores, head_queries, OVER_ROWS, preferred_element_type=f32
            )
            dquery = dquery + nn(dscores, head_keys)
        dquery = turn(dquery, cos_table, sin_table, low_half)
        dkey = turn(dkey, cos_table, sin_table, low_half)
        r.dqk[:, wide] = jnp.concatenate([dquery, dkey], axis=1).astype(bf16)
        r.dv[:, lanes] = dvalue.astype(bf16)

    def over_heads(body, start, stop):
        def step(index, carry):
            body(
                index,
                pl.ds(pl.multiple_of(index * 2 * LANES, 2 * LANES), 2 * LANES),
                pl.ds(pl.multiple_of(index * LANES, LANES), LANES),
            )
            return carry

        lax.fori_loop(start, stop, step, 0)

    def norm_two():
        def body(index, here):
            residual = (
                r.tokens[here, :].astype(f32)
                + r.acc[here, :]
                + r.out_recv[here, :].astype(f32)
            )
            r.residual[here, :] = residual
            unit_rows, _ = normed(residual)
            r.n2[here, :] = (unit_rows * mlp_gain()).astype(bf16)
            swap(4, index).start()

        tiles(own_rows, chunk_rows, body)

    def expand_tile(weight, at):
        both = nn(r.n2[...], weight)
        gate, linear = both[:, :LANES], both[:, LANES:]
        erf_part = 0.5 * (1.0 + lax.erf(gate * 0.7071067811865476))
        active = gate * erf_part
        slope = erf_part + gate * jnp.exp(-0.5 * gate * gate) * 0.3989422804014327
        r.mid[:, at] = (active * linear).astype(bf16)
        r.act[:, at] = active
        r.slope[:, at] = linear * slope

    def expand_stream(stream, offset):
        def body(index, lanes):
            at = pl.ds(pl.multiple_of((index + offset) * LANES, LANES), LANES)
            expand_tile(fulls[stream][:, lanes], at)

        tiles(fulls[stream].shape[1], 2 * LANES, body)

    spare = pl.ds(hidden, LANES)

    def dexpand(weight, at, to):
        dmiddle = nn(r.cot_all[...], weight)
        dgate = (dmiddle * r.slope[:, at]).astype(bf16)
        dlinear = (dmiddle * r.act[:, at]).astype(bf16)
        parts = []
        for start in range(0, dmiddle.shape[1], LANES):
            parts += [dgate[:, start : start + LANES], dlinear[:, start : start + LANES]]
        r.dexp[:, to] = jnp.concatenate(parts, axis=1)

    def dexpand_stream(stream, offset):
        def body(index, lanes):
            at = pl.ds(pl.multiple_of(offset * LANES + index * LANES, LANES), LANES)
            to = pl.ds(
                pl.multiple_of(offset * 2 * LANES + index * 2 * LANES, 2 * LANES), 2 * LANES
            )
            dexpand(fulls[stream][:, lanes], at, to)

        tiles(fulls[stream].shape[1], LANES, body)

    split = fulls[3].shape[1]
    mid_parts = [
        r.mid.at[:, pl.ds(0, split // 2)],
        r.mid.at[:, pl.ds(split // 2, hidden - split // 2)],
    ]
    dexp_parts = [
        r.dexp.at[:, pl.ds(0, split)],
        r.dexp.at[:, pl.ds(split, 2 * hidden - split)],
        r.dexp.at[:, pl.ds(2 * hidden, 2 * LANES)],
    ]

    def special_grad():
        spot = lax.broadcasted_iota(jnp.int32, (2 * LANES, LANES), 1)

        def body(index, here):
            both = nn(r.n2_col[here, :], dexp_parts[2][...])
            down = nn(r.cot_col[here, :], r.mid[:, spare])
            value = jnp.where(
                spot < rest,
                both[:, :LANES],
                jnp.where(
                    spot < 2 * rest,
                    pltpu.roll(both[:, LANES:], rest, 1),
                    jnp.where(spot < 3 * rest, pltpu.roll(down, 2 * rest, 1), 0.0),
                ),
            )
            grads[6][here, :] = value.astype(bf16)

        tiles(model, 2 * LANES, body)

    def back_through_norm(grad_rows, gain, values):
        unit_rows, inv_std = normed(values)
        scaled = grad_rows * gain
        inner = (
            scaled
            - jnp.mean(scaled, axis=-1, keepdims=True)
            - unit_rows * jnp.mean(scaled * unit_rows, axis=-1, keepdims=True)
        )
        return inner * inv_std, jnp.sum(grad_rows * unit_rows, axis=0, keepdims=True)

    def norm_two_back():
        r.gain_part[...] = jnp.zeros_like(r.gain_part)

        def body(index, here):
            grad_rows = r.acc[here, :] + r.dn2_recv[here, :].astype(f32)
            part, gain_sum = back_through_norm(grad_rows, mlp_gain(), r.residual[here, :])
            dresidual = r.cot[here, :].astype(f32) + part
            r.dres_own[here, :] = dresidual
            r.dres[here, :] = dresidual.astype(bf16)
            r.gain_part[1:2, :] += gain_sum
            swap(7, index).start()

        tiles(own_rows, chunk_rows, body)

    def norm_one_back():
        def body(index, here):
            grad_rows = r.acc[here, :] + r.dn1_recv[here, :].astype(f32)
            part, gain_sum = back_through_norm(
                grad_rows, attn_gain(), r.tokens[here, :].astype(f32)
            )
            r.tokens_grad[0, here, :] = (r.dres_own[here, :] + part).astype(bf16)
            r.gain_part[0:1, :] += gain_sum

        tiles(own_rows, 32, body)

    def layer_out():
        def body(index, here):
            r.layer_out[0, here, :] = (
                r.residual[here, :]
                + r.down_acc[here, :]
                + r.down_recv[here, :].astype(f32)
            ).astype(bf16)

        tiles(own_rows, 32, body)

    def gain_columns():
        spot = lax.broadcasted_iota(jnp.int32, (LANES, 2 * LANES), 0)

        def body(index, here):
            sums = r.gain_part[:, here] + r.gain_recv[:, here]
            value = jnp.where(
                spot == 3 * rest, sums[0:1], jnp.where(spot == 3 * rest + 1, sums[1:2], 0.0)
            ).T
            old = grads[6][here, :].astype(f32)
            grads[6][here, :] = (old + value).astype(bf16)

        tiles(model, 2 * LANES, body)

    def dmixed_of():
        def body(index, lanes):
            r.dmixed[:, lanes] = nn(r.dres[...], fulls[2][:, lanes]).astype(bf16)

        tiles(width, 2 * LANES, body)


    def pack_keys():
        for at in range(0, width, LANES):
            for which in range(2):
                to = 2 * at + which * LANES
                fulls[0][my_rows, to : to + LANES] = r.raw_qkv[which, :, at : at + LANES]
        fulls[1][my_rows, :] = r.raw_qkv[2]

    def pack_special():
        spot = lax.broadcasted_iota(jnp.int32, (LANES, rows), 0)
        gain_parts = []
        for gain in (r.attn_gain[...], r.mlp_gain[...]):
            spread = gain * 65537.0
            high = spread - (spread - gain)
            gain_parts += [high, gain - high]
        gains = jnp.zeros((LANES, rows), f32)
        for index, part in enumerate(gain_parts):
            gains = jnp.where(spot == 3 * rest + index, part, gains)
        special = gains.T
        if rest:
            parts = [
                r.raw_in[:, 0, hidden:].astype(f32),
                r.raw_in[:, 1, hidden:].astype(f32),
                r.raw_down[:, hidden:].astype(f32),
                jnp.zeros((rows, LANES - 3 * rest), f32),
            ]
            special = special + jnp.concatenate(parts, axis=1)
        fulls[6][my_rows, :] = special.astype(bf16)

    def pack_rest():
        fulls[2][my_rows, :] = r.raw_out[...]
        for at in range(0, hidden, LANES):
            stream, to = (3, 2 * at) if 2 * at < split else (4, 2 * at - split)
            for which in range(2):
                start = to + which * LANES
                fulls[stream][my_rows, start : start + LANES] = r.raw_in[:, which, at : at + LANES]
        fulls[5][my_rows, :] = r.raw_down[:, : split // 2]
        fulls[7][my_rows, :] = r.raw_down[:, split // 2 : hidden]


    def finish_keys(total):
        for at in range(0, width, LANES):
            for which in range(2):
                to = 2 * at + which * LANES
                r.qkv_grad[which, :, at : at + LANES] = total[:, to : to + LANES]

    def finish_values(total):
        r.qkv_grad[2] = total

    def finish_out(total):
        r.out_grad[...] = total

    def finish_special(total):
        turned = total.T
        r.attn_gain_grad[...] = turned[3 * rest : 3 * rest + 1]
        r.mlp_gain_grad[...] = turned[3 * rest + 1 : 3 * rest + 2]
        if rest:
            r.in_grad[:, 0, hidden:] = total[:, :rest]
            r.in_grad[:, 1, hidden:] = total[:, rest : 2 * rest]
            r.down_grad[:, hidden:] = total[:, 2 * rest : 3 * rest]

    def finish_in(start):
        def finish(total):
            for at in range(0, total.shape[1], 2 * LANES):
                to = start + at // 2
                r.in_grad[:, 0, to : to + LANES] = total[:, at : at + LANES]
                r.in_grad[:, 1, to : to + LANES] = total[:, at + LANES : at + 2 * LANES]

        return finish

    def finish_down(start):
        def finish(total):
            r.down_grad[:, start : start + total.shape[1]] = total

        return finish

    gathers = [gather_ops(stream) for stream in range(streams)]
    finishes = [finish_keys, finish_values, finish_out, finish_in(0), finish_in(split // 2)]
    finishes += [finish_down(0), finish_special, finish_down(split // 2)]
    scatters = [scatter_ops(stream, finishes[stream]) for stream in range(streams)]

    def go(ops, *chosen):
        for stream in chosen:
            if ops[stream]:
                ops[stream].pop(0)()

    def end(ops, *chosen):
        while any(ops[stream] for stream in chosen):
            go(ops, *chosen)


    barrier = pltpu.get_barrier_semaphore()
    for device in (right, left, partner):
        pl.semaphore_signal(barrier, inc=1, device_id={"dp": device}, device_id_type=MESH)
    pl.semaphore_signal(barrier, inc=1, device_id={"seq": other}, device_id_type=MESH)
    loads = [
        pltpu.make_async_copy(src, dst, r.own_sem.at[index])
        for index, (src, dst) in enumerate(
            [
                (r.in_qkv, r.raw_qkv),
                (r.in_in, r.raw_in),
                (r.in_down, r.raw_down),
                (r.in_attn_gain, r.attn_gain),
                (r.in_mlp_gain, r.mlp_gain),
                (r.in_seg, r.seg),
                (r.in_tokens.at[0], r.tokens),
                (r.in_cot.at[0], r.cot),
                (r.in_out, r.raw_out),
                (r.in_cos, r.cos_table),
                (r.in_sin, r.sin_table),
            ]
        )
    ]
    for load in loads:
        load.start()
    loads[0].wait()
    pack_keys()
    pl.semaphore_wait(barrier, 4)
    go(gathers, 0, 1)
    for load in loads[1:8]:
        load.wait()
    pack_special()
    go(gathers, 6)
    r.seg_own[...] = jnp.broadcast_to(r.seg[...], r.seg_own.shape)
    for index in range(3):
        swap(index).start()
    loads[8].wait()
    pack_rest()
    r.cot_all[own, :] = r.cot[...]
    for load in loads[9:]:
        load.wait()
    setup()
    to_columns(r.cot_all.at[own], r.cot_col.at[:, own])
    arrived(0)
    make_bias()
    go(gathers, 0, 1, 6, 2)
    go(gathers, 0, 1, 6, 2, 3)
    go(gathers, 0, 1, 6, 2, 3, 5)
    go(gathers, 0, 1, 6)
    arrived(1)
    arrived(2)
    gather_arrived(6)
    expand_special()
    go(gathers, 2)
    norm_one()
    gather_arrived(1)
    values_of()
    gather_arrived(0)
    over_heads(attend, blocks * 0 // 4, blocks * 1 // 4)
    go(gathers, 3)
    over_heads(attend, blocks * 1 // 4, blocks * 2 // 4)
    over_heads(attend, blocks * 2 // 4, blocks * 3 // 4)
    go(gathers, 5)
    over_heads(attend, blocks * 3 // 4, blocks * 4 // 4)
    go(gathers, 2, 4, 7)
    gather_arrived(2)
    partial_sums([(r.mixed, fulls[2])], r.acc, r.out_send, 3)
    to_columns(r.n1, r.n1_col)
    to_columns(r.cot_all.at[far], r.cot_col.at[:, far])
    go(gathers, 3, 5, 4)
    arrived(3)
    norm_two()
    go(gathers, 7, 3, 5, 4)
    arrived(4)
    gather_arrived(3)
    expand_stream(3, 0)
    go(gathers, 7)
    weight_grad(r.cot_col, mid_parts[0], grads[5])
    go(gathers, 5)
    go(scatters, 5)
    to_columns(r.n2, r.n2_col)
    expand_tile(r.sp_in[...], spare)
    gather_arrived(5)
    dexpand_stream(5, 0)
    go(scatters, 5)
    dexpand(r.sp_down[...], spare, pl.ds(2 * hidden, 2 * LANES))
    weight_grad(r.n2_col, dexp_parts[0], grads[3])
    go(gathers, 4)
    go(scatters, 3)
    go(gathers, 7)
    go(scatters, 5, 3)
    go(gathers, 4, 7)
    gather_arrived(4)
    expand_stream(4, split // (2 * LANES))
    go(scatters, 5)
    weight_grad(r.cot_col, mid_parts[1], grads[7])
    go(scatters, 3, 7)
    gather_arrived(7)
    dexpand_stream(7, split // (2 * LANES))
    partial_sums(
        [(dexp_parts[0], fulls[3]), (dexp_parts[1], fulls[4]), (dexp_parts[2], r.sp_in)],
        r.acc,
        r.dn2_send,
        6,
    )
    go(scatters, 5, 7)
    weight_grad(r.n2_col, dexp_parts[1], grads[4])
    go(scatters, 4)
    go(scatters, 4, 3, 5, 7)
    arrived(6)
    norm_two_back()
    go(scatters, 4)
    special_grad()
    partial_sums(
        [(mid_parts[0], fulls[5]), (mid_parts[1], fulls[7]), (r.mid.at[:, spare], r.sp_down)],
        r.down_acc,
        r.down_send,
        5,
    )
    go(scatters, 3, 7)
    arrived(7)
    dmixed_of()
    over_heads(attend_back, blocks * 0 // 4, blocks * 1 // 4)
    over_heads(attend_back, blocks * 1 // 4, blocks * 2 // 4)
    go(scatters, 4)
    over_heads(attend_back, blocks * 2 // 4, blocks * 3 // 4)
    over_heads(attend_back, blocks * 3 // 4, blocks * 4 // 4)
    partial_sums([(r.dqk, fulls[0]), (r.dv, fulls[1])], r.acc, r.dn1_send, 8)
    go(scatters, 3)
    weight_grad(r.n1_col, r.dqk, grads[0])
    go(scatters, 7, 0)
    weight_grad(r.n1_col, r.dv, grads[1])
    go(scatters, 1)
    to_columns(r.dres, r.dres_col)
    go(scatters, 0)
    weight_grad(r.dres_col, r.mixed, grads[2])
    go(scatters, 4, 2, 1, 7)
    arrived(8)
    norm_one_back()
    swap(9).start()
    go(scatters, 2, 0)
    arrived(5)
    layer_out()
    arrived(9)
    gain_columns()
    go(scatters, 6, 4, 1)
    go(scatters, 6, 2, 0)
    go(scatters, 6, 1, 2, 0)
    go(scatters, 6, 1, 2, 0)
    go(scatters, 6, 1, 2)
    go(scatters, 6)
    end(scatters, *range(streams))

    for stream in range(streams):
        gather_drain(stream)
        scatter_drain(stream)
    for index in range(len(exchanged)):
        swap_drain(index)


def fused_call(inputs, devices, widths):
    names, arrays = zip(*inputs.items())
    whole = dict(inputs)
    count = devices // 2
    own_rows, model = whole["in_tokens"].shape[1:]
    total = 2 * own_rows
    _, rows, width = whole["in_qkv"].shape
    local_hidden = whole["in_in"].shape[2]
    rest = local_hidden % LANES
    hidden = local_hidden - rest
    half = rows // 2
    turns = count // 2
    f32, bf16 = jnp.float32, jnp.bfloat16
    streams = len(widths)
    heads = width // (2 * HEAD_HALF)
    outs = dict(
        layer_out=((1, own_rows, model), bf16),
        tokens_grad=((1, own_rows, model), bf16),
        qkv_grad=((3, rows, width), f32),
        out_grad=((rows, width), f32),
        in_grad=((rows, 2, local_hidden), f32),
        down_grad=((rows, local_hidden), f32),
        attn_gain_grad=((1, rows), f32),
        mlp_gain_grad=((1, rows), f32),
    )
    shapes = dict(
        tokens=((own_rows, model), bf16),
        cot=((own_rows, model), bf16),
        seg=((1, own_rows), jnp.int32),
        attn_gain=((1, rows), f32),
        mlp_gain=((1, rows), f32),
        cos_table=((total, LANES), f32),
        sin_table=((total, LANES), f32),
        seg_own=((8, own_rows), jnp.int32),
        seg_other=((8, own_rows), jnp.int32),
        raw_qkv=((3, rows, width), bf16),
        raw_out=((rows, width), bf16),
        raw_in=((rows, 2, local_hidden), bf16),
        raw_down=((rows, local_hidden), bf16),
        tok_other=((own_rows, model), bf16),
        cot_all=((total, model), bf16),
        cot_col=((model, total), bf16),
        n1=((total, model), bf16),
        n1_col=((model, total), bf16),
        gains=((8, model), f32),
        cos=((total, LANES), f32),
        sin=((total, LANES), f32),
        bias=((total, total), f32),
        sp_in=((model, 2 * LANES), bf16),
        sp_down=((model, LANES), bf16),
        v=((total, width), bf16),
        qk=((total, 2 * width), bf16),
        probs=((heads, total, total), f32),
        mixed=((total, width), bf16),
        acc=((own_rows, model), f32),
        down_acc=((own_rows, model), f32),
        out_send=((own_rows, model), bf16),
        out_recv=((own_rows, model), bf16),
        down_send=((own_rows, model), bf16),
        down_recv=((own_rows, model), bf16),
        dn2_send=((own_rows, model), bf16),
        dn2_recv=((own_rows, model), bf16),
        dn1_send=((own_rows, model), bf16),
        dn1_recv=((own_rows, model), bf16),
        residual=((own_rows, model), f32),
        n2=((total, model), bf16),
        n2_col=((model, total), bf16),
        mid=((total, hidden + LANES), bf16),
        act=((total, hidden + LANES), f32),
        slope=((total, hidden + LANES), f32),
        dexp=((total, 2 * hidden + 2 * LANES), bf16),
        dres_own=((own_rows, model), f32),
        dres=((total, model), bf16),
        dres_col=((model, total), bf16),
        dmixed=((total, width), bf16),
        dqk=((total, 2 * width), bf16),
        dv=((total, width), bf16),
        gain_part=((8, model), f32),
        gain_recv=((8, model), f32),
    )
    for i, w in enumerate(widths):
        shapes["full%d" % i] = ((model, w), bf16)
        shapes["grad%d" % i] = ((model, w), bf16)
        shapes["pair%d" % i] = ((count, rows, w), bf16)
        shapes["end%d" % i] = ((2, half, w), bf16)
        shapes["recv%d" % i] = ((2, turns - 1, rows, w), bf16)
    scratch = {name: pltpu.VMEM(shape, dtype) for name, (shape, dtype) in shapes.items()}
    semaphores = dict(
        own_sem=(11,),
        g_send=(streams, 2, turns),
        g_recv=(streams, 2, turns),
        gp_send=(streams, 2, turns + 1),
        gp_recv=(streams, 2, turns + 1),
        s_send=(streams, 2, turns),
        s_recv=(streams, 2, turns),
        sp_send=(streams, count),
        sp_recv=(streams, count),
        y_send=(10, model // (2 * LANES)),
        y_recv=(10, model // (2 * LANES)),
    )
    for name, shape in semaphores.items():
        scratch[name] = pltpu.SemaphoreType.DMA(shape)
    vmem = pl.BlockSpec(memory_space=pltpu.VMEM)
    anywhere = pl.BlockSpec(memory_space=pl.ANY)
    sizes = (count, own_rows, width, hidden, rest, 1.0 / math.sqrt(2 * HEAD_HALF))
    layout = list(names) + list(outs) + list(scratch)
    return pl.pallas_call(
        functools.partial(fused_kernel, sizes, layout),
        out_shape=[jax.ShapeDtypeStruct(shape, dtype) for shape, dtype in outs.values()],
        in_specs=[anywhere] * len(names),
        out_specs=[vmem] * len(outs),
        scratch_shapes=list(scratch.values()),
        compiler_params=pltpu.CompilerParams(
            collective_id=2, has_side_effects=True, vmem_limit_bytes=FUSED_LIMIT
        ),
        name="fused_layer",
    )(*arrays)


def copy_kernel(count, *refs):
    sources, targets, buffers = refs[:count], refs[count : 2 * count], refs[2 * count : 3 * count]
    sems = refs[3 * count]
    ins = [
        pltpu.make_async_copy(sources[index], buffers[index], sems.at[0, index])
        for index in range(count)
    ]
    outs = [
        pltpu.make_async_copy(buffers[index], targets[index], sems.at[1, index])
        for index in range(count)
    ]
    for copy in ins:
        copy.start()
    for index in range(count):
        ins[index].wait()
        outs[index].start()
    for copy in outs:
        copy.wait()


def finish_call(arrays):
    anywhere = pl.BlockSpec(memory_space=pl.ANY)
    count = len(arrays)
    return pl.pallas_call(
        functools.partial(copy_kernel, count),
        out_shape=[jax.ShapeDtypeStruct(array.shape, array.dtype) for array in arrays],
        in_specs=[anywhere] * count,
        out_specs=[anywhere] * count,
        scratch_shapes=[pltpu.VMEM(array.shape, array.dtype) for array in arrays]
        + [pltpu.SemaphoreType.DMA((2, count))],
        name="finish",
    )(*arrays)


FUSED_LIMIT = 63 * 1024 * 1024


def position_tables(total, head_size):
    half_size = head_size // 2
    freqs = THETA ** (-(2.0 / head_size) * np.arange(half_size))
    angles = np.arange(total)[:, None] * freqs[None, :]
    cos_table = np.cos(angles).astype(np.float32)
    sin_table = np.sin(angles).astype(np.float32)
    return (
        jnp.asarray(np.concatenate([cos_table] * 4, axis=1)),
        jnp.asarray(np.concatenate([-sin_table, sin_table] * 2, axis=1)),
    )


def fused_device(
    devices,
    tokens,
    segments,
    cotangent,
    qkv_weight,
    out_weight,
    in_weight,
    down_weight,
    attn_gain,
    mlp_gain,
):
    own_rows = tokens.shape[1]
    width = qkv_weight.shape[2]
    blocks = in_weight.shape[2] // LANES
    first = blocks // 2 * 2 * LANES
    second = 2 * blocks * LANES - first
    widths = [2 * width, width, width, first, second, first // 2, LANES, second // 2]
    cos_table, sin_table = position_tables(2 * own_rows, 2 * HEAD_HALF)
    inputs = dict(
        in_qkv=jnp.transpose(qkv_weight, (1, 0, 2)),
        in_out=out_weight.T,
        in_in=in_weight,
        in_down=down_weight.T,
        in_tokens=tokens,
        in_cot=cotangent,
        in_seg=segments,
        in_attn_gain=attn_gain[None],
        in_mlp_gain=mlp_gain[None],
        in_cos=cos_table,
        in_sin=sin_table,
    )
    results = finish_call(fused_call(inputs, devices, widths))
    layer_out, tokens_grad, qkv, out, in_grad, down, attn_grad, mlp_grad = results
    return (
        layer_out,
        tokens_grad,
        jnp.transpose(qkv, (1, 0, 2)),
        out.T,
        in_grad,
        down.T,
        attn_grad[0],
        mlp_grad[0],
    )


def per_device(
    devices,
    seq_size,
    tokens,
    segments,
    cotangent,
    qkv_weight,
    out_weight,
    in_weight,
    down_weight,
    attn_gain,
    mlp_gain,
):
    args = (
        tokens,
        segments,
        cotangent,
        qkv_weight,
        out_weight,
        in_weight,
        down_weight,
        attn_gain,
        mlp_gain,
    )
    own_rows, model = tokens.shape[1:]
    sizes = (own_rows, model, qkv_weight.shape[2], in_weight.shape[2])
    if fits_fused(devices, seq_size, *sizes) and tokens.shape[0] == 1:
        return fused_device(devices, *args)
    return general_device(devices, seq_size, *args)


def solution(mesh):
    return jax.shard_map(
        functools.partial(per_device, mesh.shape["dp"], mesh.shape["seq"]),
        mesh=mesh,
        in_specs=(
            P("dp", "seq", None),
            P("dp", "seq"),
            P("dp", "seq", None),
            P("dp", None, "seq"),
            P("seq", "dp"),
            P("dp", None, "seq"),
            P("seq", "dp"),
            P("dp"),
            P("dp"),
        ),
        out_specs=(
            P("dp", "seq", None),
            P("dp", "seq", None),
            P("dp", None, "seq"),
            P("seq", "dp"),
            P("dp", None, "seq"),
            P("seq", "dp"),
            P("dp"),
            P("dp"),
        ),
        check_vma=False,
    )
```

```python
import functools
import math
import types

import jax
import jax.numpy as jnp
import numpy as np
from jax import lax
from jax.experimental import pallas as pl
from jax.experimental.pallas import tpu as pltpu
from jax.sharding import PartitionSpec as P

HEADS = 16
HALO = 64


EPS = 1e-05
THETA = 10000.0
NEG_FILL = -1e30


def norm_forward(values, gain):
    center = values - jnp.mean(values, axis=-1, keepdims=True)
    inv_std = lax.rsqrt(jnp.mean(center * center, axis=-1, keepdims=True) + EPS)
    unit_rows = center * inv_std
    return (unit_rows * gain, unit_rows, inv_std)


def norm_backward(grad_rows, gain, unit_rows, inv_std):
    scaled = grad_rows * gain
    inner = (
        scaled
        - jnp.mean(scaled, axis=-1, keepdims=True)
        - unit_rows * jnp.mean(scaled * unit_rows, axis=-1, keepdims=True)
    )
    return (inner * inv_std, jnp.sum(grad_rows * unit_rows, axis=0))


def gelu_value(inputs):
    return 0.5 * inputs * (1.0 + lax.erf(inputs * 0.7071067811865476))


def gelu_slope(inputs):
    return (
        0.5 * (1.0 + lax.erf(inputs * 0.7071067811865476))
        + inputs * jnp.exp(-0.5 * inputs * inputs) * 0.3989422804014327
    )


def rotary_tables(positions, head_size):
    half_size = head_size // 2
    freqs = jnp.power(THETA, -(2.0 / head_size) * jnp.arange(half_size, dtype=jnp.float32))
    angles = positions.astype(jnp.float32)[:, None] * freqs[None, :]
    return (jnp.cos(angles)[:, None, :], jnp.sin(angles)[:, None, :])


def rotate(values, cos_table, sin_table):
    half_size = values.shape[-1] // 2
    lower_half = values[..., :half_size]
    upper_half = values[..., half_size:]
    return jnp.concatenate(
        [
            lower_half * cos_table - upper_half * sin_table,
            upper_half * cos_table + lower_half * sin_table,
        ],
        axis=-1,
    )


def unrotate(grads, cos_table, sin_table):
    half_size = grads.shape[-1] // 2
    lower_half = grads[..., :half_size]
    upper_half = grads[..., half_size:]
    return jnp.concatenate(
        [
            lower_half * cos_table + upper_half * sin_table,
            upper_half * cos_table - lower_half * sin_table,
        ],
        axis=-1,
    )


def window_mask(query_pos, key_pos, query_seg, key_seg, halo_width, total_len):
    near = jnp.abs(query_pos[:, None] - key_pos[None, :]) <= halo_width
    inside = (key_pos >= 0) & (key_pos < total_len)
    return near & inside[None, :] & (query_seg[:, None] == key_seg[None, :])


def block_scores(queries, key_slab, allowed, scale):
    scores = (
        jnp.einsum("qhd,khd->hqk", queries, key_slab, preferred_element_type=jnp.float32) * scale
    )
    return jnp.where(allowed[None], scores, NEG_FILL)


def attend_block(queries, key_slab, value_slab, allowed, scale):
    scores = block_scores(queries, key_slab, allowed, scale)
    top_score = jnp.max(scores, axis=-1, keepdims=True)
    total = jnp.sum(jnp.exp(scores - top_score), axis=-1, keepdims=True)
    logsum = top_score + jnp.log(total)
    probs = jnp.exp(scores - logsum).astype(jnp.bfloat16)
    mixed = jnp.einsum("hqk,khd->qhd", probs, value_slab, preferred_element_type=jnp.float32)
    return (mixed, logsum[..., 0])


def attend_back(queries, key_slab, value_slab, allowed, scale, logsum, mixed_b, dmixed_b):
    scores = block_scores(queries, key_slab, allowed, scale)
    probs = jnp.exp(scores - logsum[..., None])
    probs_b = probs.astype(jnp.bfloat16)
    dvalues = jnp.einsum("hqk,qhd->khd", probs_b, dmixed_b, preferred_element_type=jnp.float32)
    dprobs = jnp.einsum("qhd,khd->hqk", dmixed_b, value_slab, preferred_element_type=jnp.float32)
    delta = jnp.transpose(
        jnp.sum(dmixed_b.astype(jnp.float32) * mixed_b.astype(jnp.float32), axis=-1)
    )
    dscores = (probs * (dprobs - delta[..., None]) * scale).astype(jnp.bfloat16)
    dqueries = jnp.einsum("hqk,khd->qhd", dscores, key_slab, preferred_element_type=jnp.float32)
    dkeys = jnp.einsum("hqk,qhd->khd", dscores, queries, preferred_element_type=jnp.float32)
    return (dqueries, dkeys, dvalues)


MESH = pl.DeviceIdType.MESH
VMEM_LIMIT = 60 * 1024 * 1024
LANES = 128


def ring_place(count):
    me = lax.axis_index("dp")
    core = me % 2
    chip = me // 2
    row, column = chip // 2, chip % 2
    place = (1 - column) * row + column * (count - 1 - row)
    return (core, place)


def chip_at(place, count):
    side = place // (count // 2)
    return (1 - side) * (2 * place) + side * (2 * (count - 1 - place) + 1)


def neighbours(core, place, count):
    right = chip_at((place + 1) % count, count) * 2 + core
    left = chip_at((place + count - 1) % count, count) * 2 + core
    return (right, left, lax.axis_index("dp") + 1 - 2 * core)


def greet(devices):
    barrier = pltpu.get_barrier_semaphore()
    for device in devices:
        pl.semaphore_signal(barrier, inc=1, device_id={"dp": device}, device_id_type=MESH)
    pl.semaphore_wait(barrier, len(devices))


def gather_kernel(count, streams, *refs):
    shards = refs[:streams]
    fulls = refs[streams : 2 * streams]
    own_sem, send_sem, recv_sem, pair_send, pair_recv = refs[2 * streams :]
    rows = shards[0].shape[0]
    half = rows // 2
    core, place = ring_place(count)
    right, left, partner = neighbours(core, place, count)
    targets = (right, left)
    lanes = [(way, stream) for stream in range(streams) for way in range(2)]

    def piece(way, step, stream):
        shift = count - step if way == 0 else step
        owner = chip_at((place + shift) % count, count) * 2 + core
        start = pl.multiple_of(owner * rows + way * half, half)
        return fulls[stream].at[pl.ds(start, half)]

    def hop(way, step, stream):
        ref = piece(way, step, stream)
        return pltpu.make_async_remote_copy(
            src_ref=ref,
            dst_ref=ref,
            send_sem=send_sem.at[stream, way, step],
            recv_sem=recv_sem.at[stream, way, step],
            device_id={"dp": targets[way]},
            device_id_type=MESH,
        )

    def share(way, step, stream):
        ref = piece(way, step, stream)
        return pltpu.make_async_remote_copy(
            src_ref=ref,
            dst_ref=ref,
            send_sem=pair_send.at[stream, way, step],
            recv_sem=pair_recv.at[stream, way, step],
            device_id={"dp": partner},
            device_id_type=MESH,
        )

    me = lax.axis_index("dp")
    owns = [
        pltpu.make_async_copy(
            shards[stream],
            fulls[stream].at[pl.ds(pl.multiple_of(me * rows, rows), rows)],
            own_sem.at[stream],
        )
        for stream in range(streams)
    ]
    for own in owns:
        own.start()
    greet((right, left, partner))
    for own in owns:
        own.wait()
    for way, stream in lanes:
        hop(way, 0, stream).start()
        share(way, 0, stream).start()

    def step_body(step, carry):
        for way, stream in lanes:
            hop(way, step - 1, stream).wait_recv()
            hop(way, step, stream).start()
            share(way, step, stream).start()
        return carry

    lax.fori_loop(1, count - 1, step_body, 0)
    for way, stream in lanes:
        hop(way, count - 2, stream).wait_recv()
        share(way, count - 1, stream).start()

    def drain_hops(step, carry):
        for way, stream in lanes:
            hop(way, step, stream).wait_send()
        return carry

    def drain_shares(step, carry):
        for way, stream in lanes:
            share(way, step, stream).wait_send()
            share(way, step, stream).wait_recv()
        return carry

    lax.fori_loop(0, count - 1, drain_hops, 0)
    lax.fori_loop(0, count, drain_shares, 0)


def ring_gather(shards, devices):
    count = devices // 2
    streams = len(shards)
    return pl.pallas_call(
        functools.partial(gather_kernel, count, streams),
        out_shape=[
            jax.ShapeDtypeStruct((devices * shard.shape[0], shard.shape[1]), shard.dtype)
            for shard in shards
        ],
        in_specs=[pl.BlockSpec(memory_space=pltpu.VMEM)] * streams,
        out_specs=[pl.BlockSpec(memory_space=pl.ANY)] * streams,
        scratch_shapes=[pltpu.SemaphoreType.DMA((streams,))]
        + [pltpu.SemaphoreType.DMA((streams, 2, count - 1))] * 2
        + [pltpu.SemaphoreType.DMA((streams, 2, count))] * 2,
        cost_estimate=pl.CostEstimate(
            flops=0, bytes_accessed=128 * 1024 * 1024, transcendentals=0
        ),
        compiler_params=pltpu.CompilerParams(
            collective_id=0, has_side_effects=True, vmem_limit_bytes=VMEM_LIMIT
        ),
        name="ring_gather",
    )(*shards)


def scatter_kernel(count, streams, *refs):
    grads = refs[:streams]
    outs = refs[streams : 2 * streams]
    pairs = refs[2 * streams : 3 * streams]
    sends = refs[3 * streams : 4 * streams]
    recvs = refs[4 * streams : 5 * streams]
    send_sem, recv_sem, pair_send, pair_recv = refs[5 * streams :]
    rows = outs[0].shape[0]
    half = rows // 2
    core, place = ring_place(count)
    right, left, partner = neighbours(core, place, count)
    targets = (right, left)

    def block(way, step, which):
        shift = 2 * count - 1 - step if way == 0 else 1 + step
        owner = chip_at((place + shift) % count, count) * 2 + which
        return pl.ds(pl.multiple_of(owner * rows + way * half, half), half)

    def share(way, step, stream):
        return pltpu.make_async_remote_copy(
            src_ref=grads[stream].at[block(way, step, 1 - core)],
            dst_ref=pairs[stream].at[way, step],
            send_sem=pair_send.at[stream, way, step],
            recv_sem=pair_recv.at[stream, way, step],
            device_id={"dp": partner},
            device_id_type=MESH,
        )

    def hop(way, step, stream):
        return pltpu.make_async_remote_copy(
            src_ref=sends[stream].at[way, step],
            dst_ref=recvs[stream].at[way, step],
            send_sem=send_sem.at[stream, way, step],
            recv_sem=recv_sem.at[stream, way, step],
            device_id={"dp": targets[way]},
            device_id_type=MESH,
        )

    def pair_sum(way, step, stream):
        share(way, step, stream).wait_recv()
        own = grads[stream][block(way, step, core), :].astype(jnp.float32)
        return own + pairs[stream][way, step].astype(jnp.float32)

    greet((right, left, partner))

    def start_shares(step, carry):
        for stream in range(streams):
            for way in range(2):
                share(way, step, stream).start()
        return carry

    lax.fori_loop(0, count, start_shares, 0)
    for stream in range(streams):
        for way in range(2):
            sends[stream][way, 0] = pair_sum(way, 0, stream).astype(jnp.bfloat16)
            hop(way, 0, stream).start()

    def step_body(step, carry):
        for stream in range(streams):
            for way in range(2):
                total = pair_sum(way, step, stream)
                hop(way, step - 1, stream).wait_recv()
                total = total + recvs[stream][way, step - 1].astype(jnp.float32)
                sends[stream][way, step] = total.astype(jnp.bfloat16)
                hop(way, step, stream).start()
        return carry

    lax.fori_loop(1, count - 1, step_body, 0)
    for stream in range(streams):
        for way in range(2):
            total = pair_sum(way, count - 1, stream)
            hop(way, count - 2, stream).wait_recv()
            total = total + recvs[stream][way, count - 2].astype(jnp.float32)
            outs[stream][way * half : (way + 1) * half, :] = total

    def drain_hops(step, carry):
        for stream in range(streams):
            for way in range(2):
                hop(way, step, stream).wait_send()
        return carry

    def drain_shares(step, carry):
        for stream in range(streams):
            for way in range(2):
                share(way, step, stream).wait_send()
        return carry

    lax.fori_loop(0, count - 1, drain_hops, 0)
    lax.fori_loop(0, count, drain_shares, 0)


def ring_scatter(grads, devices):
    count = devices // 2
    streams = len(grads)
    rows = grads[0].shape[0] // devices
    half = rows // 2
    widths = [grad.shape[1] for grad in grads]
    vmem = pl.BlockSpec(memory_space=pltpu.VMEM)
    return pl.pallas_call(
        functools.partial(scatter_kernel, count, streams),
        out_shape=[jax.ShapeDtypeStruct((rows, width), jnp.float32) for width in widths],
        in_specs=[vmem] * streams,
        out_specs=[vmem] * streams,
        scratch_shapes=[pltpu.VMEM((2, count, half, width), jnp.bfloat16) for width in widths]
        + [pltpu.VMEM((2, count - 1, half, width), jnp.bfloat16) for width in widths] * 2
        + [pltpu.SemaphoreType.DMA((streams, 2, count - 1))] * 2
        + [pltpu.SemaphoreType.DMA((streams, 2, count))] * 2,
        compiler_params=pltpu.CompilerParams(
            collective_id=1, has_side_effects=True, vmem_limit_bytes=40 * 1024 * 1024
        ),
        name="ring_scatter",
    )(*grads)


def turn(values, cos_table, sin_table, low_half):
    half = HEAD_HALF
    swapped = jnp.where(
        low_half, pltpu.roll(values, LANES - half, 1), pltpu.roll(values, half, 1)
    )
    return values * cos_table + swapped * sin_table


HEAD_HALF = 32


def lane_masks(rows):
    lane = lax.broadcasted_iota(jnp.int32, (rows, LANES), 1)
    return (lane % (2 * HEAD_HALF) < HEAD_HALF, lane < 2 * HEAD_HALF)


def allowed_pairs(pos_col, pos_row, seg_col, seg_row):
    near = jnp.abs(pos_col[...] - pos_row[...]) <= HALO
    return near & (seg_col[...] == seg_row[...])


def head_probs(queries, keys, allowed, scale):
    scores = (
        lax.dot_general(
            queries, keys, (((1,), (1,)), ((), ())), preferred_element_type=jnp.float32
        )
        * scale
    )
    scores = jnp.where(allowed, scores, NEG_FILL)
    top_score = jnp.max(scores, axis=-1, keepdims=True)
    total = jnp.sum(jnp.exp(scores - top_score), axis=-1, keepdims=True)
    return jnp.exp(scores - (top_score + jnp.log(total)))


def attend_kernel(
    scale, width, proj, cos_ref, sin_ref, pos_col, pos_row, seg_col, seg_row, qkv_out, mixed_out
):
    rows = proj.shape[0]
    low_half, first = lane_masks(rows)
    cos_table, sin_table = cos_ref[...], sin_ref[...]
    allowed = allowed_pairs(pos_col, pos_row, seg_col, seg_row)
    for start in range(0, width, LANES):
        queries = turn(proj[:, start : start + LANES], cos_table, sin_table, low_half)
        keys = turn(
            proj[:, width + start : width + start + LANES], cos_table, sin_table, low_half
        ).astype(jnp.bfloat16)
        values = proj[:, 2 * width + start : 2 * width + start + LANES]
        qkv_out[:, start : start + LANES] = queries.astype(jnp.bfloat16)
        qkv_out[:, width + start : width + start + LANES] = keys
        qkv_out[:, 2 * width + start : 2 * width + start + LANES] = values.astype(jnp.bfloat16)
        mixed = jnp.zeros((rows, LANES), jnp.float32)
        for head in range(2):
            mine = first if head == 0 else ~first
            probs = head_probs(
                jnp.where(mine, queries, 0.0).astype(jnp.bfloat16), keys, allowed, scale
            ).astype(jnp.bfloat16)
            mixed = mixed + jnp.dot(
                probs,
                jnp.where(mine, values, 0.0).astype(jnp.bfloat16),
                preferred_element_type=jnp.float32,
            )
        mixed_out[:, start : start + LANES] = mixed.astype(jnp.bfloat16)


def attend_back_kernel(
    scale,
    width,
    qkv,
    mixed_ref,
    dmixed_ref,
    cos_ref,
    sin_ref,
    pos_col,
    pos_row,
    seg_col,
    seg_row,
    dqkv_out,
):
    rows = qkv.shape[0]
    low_half, first = lane_masks(rows)
    cos_table, sin_table = cos_ref[...], -sin_ref[...]
    allowed = allowed_pairs(pos_col, pos_row, seg_col, seg_row)
    over_rows = (((0,), (0,)), ((), ()))
    over_lanes = (((1,), (1,)), ((), ()))
    for start in range(0, width, LANES):
        queries = qkv[:, start : start + LANES].astype(jnp.float32)
        keys = qkv[:, width + start : width + start + LANES]
        keys32 = keys.astype(jnp.float32)
        values = qkv[:, 2 * width + start : 2 * width + start + LANES]
        dmixed = dmixed_ref[:, start : start + LANES].astype(jnp.float32)
        products = dmixed * mixed_ref[:, start : start + LANES].astype(jnp.float32)
        dquery = jnp.zeros((rows, LANES), jnp.float32)
        dkey = jnp.zeros((rows, LANES), jnp.float32)
        dvalue = jnp.zeros((rows, LANES), jnp.float32)
        for head in range(2):
            mine = first if head == 0 else ~first
            head_queries = jnp.where(mine, queries, 0.0).astype(jnp.bfloat16)
            head_keys = jnp.where(mine, keys32, 0.0).astype(jnp.bfloat16)
            head_dmixed = jnp.where(mine, dmixed, 0.0).astype(jnp.bfloat16)
            delta = jnp.sum(jnp.where(mine, products, 0.0), axis=-1, keepdims=True)
            probs = head_probs(head_queries, keys, allowed, scale)
            dprobs = lax.dot_general(
                head_dmixed, values, over_lanes, preferred_element_type=jnp.float32
            )
            dscores = (probs * (dprobs - delta) * scale).astype(jnp.bfloat16)
            dvalue = dvalue + lax.dot_general(
                probs.astype(jnp.bfloat16),
                head_dmixed,
                over_rows,
                preferred_element_type=jnp.float32,
            )
            dkey = dkey + lax.dot_general(
                dscores, head_queries, over_rows, preferred_element_type=jnp.float32
            )
            dquery = dquery + jnp.dot(dscores, head_keys, preferred_element_type=jnp.float32)
        dquery = turn(dquery, cos_table, sin_table, low_half)
        dkey = turn(dkey, cos_table, sin_table, low_half)
        dqkv_out[:, start : start + LANES] = dquery.astype(jnp.bfloat16)
        dqkv_out[:, width + start : width + start + LANES] = dkey.astype(jnp.bfloat16)
        dqkv_out[:, 2 * width + start : 2 * width + start + LANES] = dvalue.astype(jnp.bfloat16)


def local_call(kernel, name, out_shape, operands, flops):
    vmem = pl.BlockSpec(memory_space=pltpu.VMEM)
    single = not isinstance(out_shape, list)
    return pl.pallas_call(
        kernel,
        out_shape=out_shape,
        in_specs=[vmem] * len(operands),
        out_specs=vmem if single else [vmem] * len(out_shape),
        cost_estimate=pl.CostEstimate(
            flops=flops, bytes_accessed=4 * 1024 * 1024, transcendentals=flops // 256
        ),
        compiler_params=pltpu.CompilerParams(vmem_limit_bytes=32 * 1024 * 1024),
        name=name,
    )(*operands)


class PairedAttention:
    def __init__(self, positions, segments, head_size, width):
        rows = positions.shape[0]
        cos_table, sin_table = rotary_tables(positions, head_size)
        cos_table, sin_table = cos_table[:, 0, :], sin_table[:, 0, :]
        self.width = width
        self.scale = 1.0 / math.sqrt(head_size)
        self.flops = 2 * rows * rows * LANES * (width // head_size)
        self.shared = (
            jnp.concatenate([cos_table] * 4, axis=1),
            jnp.concatenate([-sin_table, sin_table] * 2, axis=1),
            positions[:, None],
            positions[None, :],
            segments[:, None],
            segments[None, :],
        )

    def forward(self, projected):
        rows = projected.shape[0]
        self.qkv, self.mixed = local_call(
            functools.partial(attend_kernel, self.scale, self.width),
            "attend",
            [
                jax.ShapeDtypeStruct((rows, 3 * self.width), jnp.bfloat16),
                jax.ShapeDtypeStruct((rows, self.width), jnp.bfloat16),
            ],
            (projected,) + self.shared,
            2 * self.flops,
        )
        return self.mixed

    def backward(self, dmixed):
        rows = dmixed.shape[0]
        return local_call(
            functools.partial(attend_back_kernel, self.scale, self.width),
            "attend_back",
            jax.ShapeDtypeStruct((rows, 3 * self.width), jnp.bfloat16),
            (self.qkv, self.mixed, dmixed) + self.shared,
            5 * self.flops,
        )


class BlockAttention:
    def __init__(self, positions, segments, head_size, width):
        self.total_len = positions.shape[0]
        self.segments = segments
        self.head_size = head_size
        self.width = width
        self.scale = 1.0 / math.sqrt(head_size)
        self.cos_table, self.sin_table = rotary_tables(positions, head_size)

    def heads(self, values):
        return values.reshape(self.total_len, self.width // self.head_size, self.head_size)

    def forward(self, projected):
        width, total_len = self.width, self.total_len
        self.block_rows = min(total_len, 512)
        self.slab_rows = self.block_rows + 2 * HALO
        tables = (self.cos_table, self.sin_table)
        self.queries = rotate(self.heads(projected[:, :width]), *tables).astype(jnp.bfloat16)
        keys = rotate(self.heads(projected[:, width : 2 * width]), *tables).astype(jnp.bfloat16)
        values = self.heads(projected[:, 2 * width :]).astype(jnp.bfloat16)
        pad_spec = ((HALO, HALO), (0, 0), (0, 0))
        self.key_pad = jnp.pad(keys, pad_spec)
        self.value_pad = jnp.pad(values, pad_spec)
        seg_pad = jnp.pad(self.segments, (HALO, HALO), constant_values=-1)
        mixed_parts = []
        self.logsums = []
        self.masks = []
        for start in range(0, total_len, self.block_rows):
            own = slice(start, start + self.block_rows)
            slab = slice(start, start + self.slab_rows)
            allowed = window_mask(
                start + jnp.arange(self.block_rows, dtype=jnp.int32),
                start - HALO + jnp.arange(self.slab_rows, dtype=jnp.int32),
                self.segments[own],
                seg_pad[slab],
                HALO,
                total_len,
            )
            mixed, logsum = attend_block(
                self.queries[own], self.key_pad[slab], self.value_pad[slab], allowed, self.scale
            )
            self.masks.append(allowed)
            self.logsums.append(logsum)
            mixed_parts.append(mixed)
        self.mixed = jnp.concatenate(mixed_parts, axis=0).astype(jnp.bfloat16)
        return self.mixed.reshape(total_len, width)

    def backward(self, dmixed):
        total_len = self.total_len
        dmixed = self.heads(dmixed)
        padded = (total_len + 2 * HALO,) + dmixed.shape[1:]
        dkey_pad = jnp.zeros(padded, jnp.float32)
        dvalue_pad = jnp.zeros(padded, jnp.float32)
        dquery_parts = []
        for index, start in enumerate(range(0, total_len, self.block_rows)):
            own = slice(start, start + self.block_rows)
            slab = slice(start, start + self.slab_rows)
            dqueries, dkeys, dvalues = attend_back(
                self.queries[own],
                self.key_pad[slab],
                self.value_pad[slab],
                self.masks[index],
                self.scale,
                self.logsums[index],
                self.mixed[own],
                dmixed[own],
            )
            dquery_parts.append(dqueries)
            dkey_pad = dkey_pad.at[slab].add(dkeys)
            dvalue_pad = dvalue_pad.at[slab].add(dvalues)
        inner = slice(HALO, HALO + total_len)
        tables = (self.cos_table, self.sin_table)
        parts = [
            unrotate(jnp.concatenate(dquery_parts, axis=0), *tables),
            unrotate(dkey_pad[inner], *tables),
            dvalue_pad[inner],
        ]
        return jnp.concatenate(
            [part.reshape(total_len, self.width) for part in parts], axis=1
        ).astype(jnp.bfloat16)


def dot(left, right, left_dim, right_dim):
    return lax.dot_general(
        left,
        right,
        (((left_dim,), (right_dim,)), ((), ())),
        preferred_element_type=jnp.float32,
    )


def padded_to_lanes(values):
    return jnp.pad(values, ((0, 0), (0, -values.shape[1] % LANES)))


def high_and_low(gain):
    high = gain.astype(jnp.bfloat16)
    return [high[:, None], (gain - high.astype(jnp.float32)).astype(jnp.bfloat16)[:, None]]


def general_device(
    devices,
    seq_size,
    tokens,
    segments,
    cotangent,
    qkv_weight,
    out_weight,
    in_weight,
    down_weight,
    attn_gain,
    mlp_gain,
):
    layer_in = tokens[0]
    seg_local = segments[0]
    cot_local = cotangent[0]
    own_rows, model_width = layer_in.shape
    head_size = model_width // HEADS
    local_width = qkv_weight.shape[2]
    local_hidden = in_weight.shape[2]
    shard_rows = qkv_weight.shape[0]
    total_len = own_rows * seq_size
    paired = (
        seq_size == 2
        and total_len <= 512
        and local_width % LANES == 0
        and head_size == 2 * HEAD_HALF
    )
    swap = [(0, 1), (1, 0)]

    def rows_of_all(values):
        if paired:
            return jnp.concatenate([values, lax.ppermute(values, "seq", swap)], axis=0)
        return lax.all_gather(values, "seq", axis=0, tiled=True)

    def sum_to_owner(partial):
        if paired:
            other = lax.ppermute(partial[own_rows:].astype(jnp.bfloat16), "seq", swap)
            return partial[:own_rows] + other.astype(jnp.float32)
        return lax.psum_scatter(
            partial.astype(jnp.bfloat16), "seq", scatter_dimension=0, tiled=True
        ).astype(jnp.float32)

    def sum_over_seq(part):
        if paired:
            return part + lax.ppermute(part, "seq", swap)
        return lax.psum(part, "seq")

    first_pack = jnp.concatenate(
        [qkv_weight.reshape(shard_rows, 3 * local_width), out_weight.T], axis=1
    )
    wide = (local_hidden + 4 + LANES - 1) // LANES * LANES
    spare = jnp.zeros((shard_rows, wide - local_hidden), jnp.bfloat16)
    second_pack = jnp.concatenate(
        [in_weight[:, 0, :], spare, in_weight[:, 1, :], spare, down_weight.T]
        + high_and_low(attn_gain)
        + high_and_low(mlp_gain)
        + [spare[:, 4:]],
        axis=1,
    )
    first_full, second_full = ring_gather([first_pack, second_pack], devices)
    full_qkv = first_full[:, : 3 * local_width]
    full_out = first_full[:, 3 * local_width : 4 * local_width]
    gains_at = 2 * wide + local_hidden
    gains = second_full[:, gains_at : gains_at + 4].astype(jnp.float32)
    gain_attn = gains[:, 0] + gains[:, 1]
    gain_mlp = gains[:, 2] + gains[:, 3]
    full_in = second_full[:, : 2 * wide]
    full_down = second_full[:, 2 * wide :]

    inputs32 = layer_in.astype(jnp.float32)
    if paired:
        arrived = lax.ppermute(jnp.concatenate([layer_in, cot_local], axis=0), "seq", swap)
        all_inputs32 = jnp.concatenate([layer_in, arrived[:own_rows]], axis=0).astype(jnp.float32)
        cot_full = jnp.concatenate([cot_local, arrived[own_rows:]], axis=0)
    else:
        all_inputs32 = rows_of_all(layer_in).astype(jnp.float32)
        cot_full = rows_of_all(cot_local)
    normed_full = norm_forward(all_inputs32, gain_attn)[0].astype(jnp.bfloat16)
    unit_one, inv_one = norm_forward(inputs32, gain_attn)[1:]
    if paired:
        seg_full = rows_of_all(
            jnp.broadcast_to(seg_local.astype(jnp.float32)[:, None], (own_rows, LANES))
        )[:, 0].astype(jnp.int32)
        place = lax.axis_index("seq")
        arange = jnp.arange(own_rows, dtype=jnp.int32)
        positions = jnp.concatenate(
            [place * own_rows + arange, (1 - place) * own_rows + arange], axis=0
        )
        attention = PairedAttention(positions, seg_full, head_size, local_width)
    else:
        seg_full = rows_of_all(seg_local.astype(jnp.bfloat16)).astype(jnp.int32)
        positions = jnp.arange(total_len, dtype=jnp.int32)
        attention = BlockAttention(positions, seg_full, head_size, local_width)

    mixed = attention.forward(dot(normed_full, full_qkv, 1, 0))
    residual = inputs32 + sum_to_owner(dot(mixed, full_out, 1, 1))
    normed_two, unit_two, inv_two = norm_forward(residual, gain_mlp)
    normed_two_full = rows_of_all(normed_two.astype(jnp.bfloat16))
    expanded = dot(normed_two_full, full_in, 1, 0)
    gate_in = expanded[:, :wide]
    linear_in = expanded[:, wide:]
    activated = gelu_value(gate_in)
    middle_b = (activated * linear_in).astype(jnp.bfloat16)
    down_part = dot(middle_b, full_down, 1, 1)

    down_grad = dot(cot_full, middle_b, 0, 0).astype(jnp.bfloat16)
    dmiddle = dot(cot_full, full_down, 1, 0)
    dexpanded_b = jnp.concatenate(
        [dmiddle * linear_in * gelu_slope(gate_in), dmiddle * activated], axis=1
    ).astype(jnp.bfloat16)
    dnormed_two = sum_to_owner(dot(dexpanded_b, full_in, 1, 1))
    in_grad = dot(normed_two_full, dexpanded_b, 0, 0).astype(jnp.bfloat16)
    dres_norm, mlp_gain_part = norm_backward(dnormed_two, gain_mlp, unit_two, inv_two)
    dresidual = cot_local.astype(jnp.float32) + dres_norm
    dres_full = rows_of_all(dresidual.astype(jnp.bfloat16))
    down_part, dres_full = lax.optimization_barrier((down_part, dres_full))
    layer_out = (residual + sum_to_owner(down_part)).astype(jnp.bfloat16)
    dmixed = dot(dres_full, full_out, 1, 0).astype(jnp.bfloat16)
    out_grad = dot(dres_full, mixed, 0, 0).astype(jnp.bfloat16)
    dqkv_b = attention.backward(dmixed)
    layer_out, dqkv_b = lax.optimization_barrier((layer_out, dqkv_b))
    dnormed_one = sum_to_owner(dot(dqkv_b, full_qkv, 1, 1))
    qkv_grad = dot(normed_full, dqkv_b, 0, 0).astype(jnp.bfloat16)
    dinput_norm, attn_gain_part = norm_backward(dnormed_one, gain_attn, unit_one, inv_one)
    tokens_grad = (dresidual + dinput_norm).astype(jnp.bfloat16)
    gain_sums = sum_over_seq(jnp.stack([attn_gain_part, mlp_gain_part]))
    gain_grad = padded_to_lanes(gain_sums.T).astype(jnp.bfloat16)

    in_share, qkv_share, down_share, out_share, gain_share = ring_scatter(
        [in_grad, qkv_grad, down_grad, out_grad, gain_grad], devices
    )
    return (
        layer_out[None],
        tokens_grad[None],
        qkv_share.reshape(shard_rows, 3, local_width),
        out_share.T,
        jnp.stack([in_share[:, :local_hidden], in_share[:, wide : wide + local_hidden]], axis=1),
        down_share[:, :local_hidden].T,
        gain_share[:, 0],
        gain_share[:, 1],
    )


HIGH = (((1,), (1,)), ((), ()))
OVER_ROWS = (((0,), (0,)), ((), ()))


def fits_fused(devices, seq_size, own_rows, model_width, local_width, local_hidden):
    rest = local_hidden % LANES
    shard_rows = model_width // devices
    return (
        seq_size == 2
        and devices % 4 == 0
        and devices >= 8
        and own_rows == LANES
        and local_width % (2 * LANES) == 0
        and model_width % (2 * LANES) == 0
        and model_width // HEADS == 2 * HEAD_HALF
        and 3 * rest + 8 <= LANES
        and local_hidden // LANES >= 4
        and local_hidden // LANES % 2 == 0
        and shard_rows % 32 == 0
        and own_rows * 2 * LANES // model_width % 16 == 0
    )


def nt(left, right):
    return lax.dot_general(left, right, HIGH, preferred_element_type=jnp.float32)


def nn(left, right):
    return jnp.dot(left, right, preferred_element_type=jnp.float32)


def tiles(total, width, body):
    def step(index, carry):
        body(index, pl.ds(pl.multiple_of(index * width, width), width))
        return carry

    lax.fori_loop(0, total // width, step, 0)


def fused_kernel(sizes, layout, *refs):
    count, own_rows, width, hidden, rest, scale = sizes
    total_rows = 2 * own_rows
    r = types.SimpleNamespace(**dict(zip(layout, refs)))
    model = r.tokens.shape[1]
    streams = 8
    fulls = [getattr(r, "full%d" % i) for i in range(streams)]
    grads = [getattr(r, "grad%d" % i) for i in range(streams)]
    pairs = [getattr(r, "pair%d" % i) for i in range(streams)]
    ends = [getattr(r, "end%d" % i) for i in range(streams)]
    recvs = [getattr(r, "recv%d" % i) for i in range(streams)]
    rows = model // (2 * count)
    half = rows // 2
    turns = count // 2
    core, place = ring_place(count)
    right, left, partner = neighbours(core, place, count)
    targets = (right, left)
    me = lax.axis_index("dp")
    mine = lax.axis_index("seq")
    other = 1 - mine
    f32, bf16 = jnp.float32, jnp.bfloat16
    my_rows = pl.ds(pl.multiple_of(me * rows, rows), rows)

    def remote(src, dst, send, recv, device):
        return pltpu.make_async_remote_copy(
            src_ref=src,
            dst_ref=dst,
            send_sem=send,
            recv_sem=recv,
            device_id=device,
            device_id_type=MESH,
        )


    def piece(way, distance, stream, whole):
        shift = count - distance if way == 0 else distance
        owner = chip_at((place + shift) % count, count) * 2 + core
        if whole:
            where = pl.ds(pl.multiple_of(owner * rows, rows), rows)
        else:
            where = pl.ds(pl.multiple_of(owner * rows + way * half, half), half)
        return fulls[stream].at[where]

    def hop(way, step, stream):
        ref = piece(way, step, stream, step < turns - 1)
        sems = r.g_send.at[stream], r.g_recv.at[stream, step]
        return remote(ref, ref, *sems, {"dp": targets[way]})

    def both_hops(step, stream):
        ref = fulls[stream].at[pl.ds(0, 2 * rows if step < turns - 1 else 2 * half)]
        return remote(ref, ref, r.g_send.at[stream], r.g_recv.at[stream, step], {"dp": right})

    def share(way, step, stream):
        ref = piece(way, step, stream, step < turns)
        return remote(ref, ref, r.gp_send.at[stream], r.gp_recv.at[stream], {"dp": partner})

    def all_shares(stream):
        ref = fulls[stream].at[pl.ds(0, count * rows)]
        return remote(ref, ref, r.gp_send.at[stream], r.gp_recv.at[stream], {"dp": partner})

    def gather_ops(stream):
        def start():
            for way in range(2):
                hop(way, 0, stream).start()
            share(0, 0, stream).start()

        def middle(step):
            both_hops(step - 1, stream).wait_recv()
            for way in range(2):
                hop(way, step, stream).start()
                share(way, step, stream).start()

        def last():
            both_hops(turns - 1, stream).wait_recv()
            for way in range(2):
                share(way, turns, stream).start()

        steps = [functools.partial(middle, step) for step in range(1, turns)]
        return [start] + steps + [last]

    def gather_arrived(stream):
        end(gathers, stream)
        all_shares(stream).wait_recv()

    def sent_rows(stream):
        return pl.ds(0, 2 * (turns - 1) * rows + 2 * half)

    def gather_drain(stream):
        ref = fulls[stream].at[sent_rows(stream)]
        sems = r.g_send.at[stream], r.g_recv.at[stream, 0]
        remote(ref, ref, *sems, {"dp": right}).wait_send()
        all_shares(stream).wait_send()


    def block(ahead, which):
        owner = chip_at((place + ahead) % count, count) * 2 + which
        return pl.ds(pl.multiple_of(owner * rows, rows), rows)

    def give(ahead, stream):
        return remote(
            grads[stream].at[block(ahead, 1 - core)],
            pairs[stream].at[ahead],
            r.sp_send.at[stream],
            r.sp_recv.at[stream, abs(ahead - turns)],
            {"dp": partner},
        )

    def given(step, stream):
        blocks_of = 1 if step in (0, turns) else 2
        ref = pairs[stream].at[pl.ds(0, blocks_of)]
        sems = r.sp_send.at[stream], r.sp_recv.at[stream, step]
        return remote(ref, ref, *sems, {"dp": partner})

    def ahead_of(way, step):
        return turns - step if way == 0 else turns + step

    def push(way, step, stream):
        sems = r.s_send.at[stream], r.s_recv.at[stream, step]
        if step == 0:
            src = pairs[stream].at[turns, pl.ds(way * half, half)]
            return remote(src, ends[stream].at[way], *sems, {"dp": targets[way]})
        src = pairs[stream].at[ahead_of(way, step)]
        return remote(src, recvs[stream].at[way, step - 1], *sems, {"dp": targets[way]})

    def both_pushes(step, stream):
        ref = ends[stream] if step == 0 else recvs[stream].at[:, step - 1]
        return remote(ref, ref, r.s_send.at[stream], r.s_recv.at[stream, step], {"dp": right})

    def pair_sum(ahead, stream):
        own = grads[stream][block(ahead, core), :].astype(f32)
        return own + pairs[stream][ahead].astype(f32)

    def scatter_ops(stream, finish):
        def gives():
            order = [turns] + [turns + sign * d for d in range(1, turns) for sign in (-1, 1)] + [0]
            for ahead in order:
                give(ahead, stream).start()

        def start():
            given(0, stream).wait_recv()
            pairs[stream][turns] = pair_sum(turns, stream).astype(bf16)
            for way in range(2):
                push(way, 0, stream).start()

        def middle(step):
            given(step, stream).wait_recv()
            both_pushes(step - 1, stream).wait_recv()
            for way in range(2):
                ahead = ahead_of(way, step)
                total = pair_sum(ahead, stream)
                if step == 1:
                    near = ends[stream][way].astype(f32)
                    parts = [total[:half], total[half:]]
                    parts[way] = parts[way] + near
                    total = jnp.concatenate(parts, axis=0)
                else:
                    total = total + recvs[stream][way, step - 2].astype(f32)
                pairs[stream][ahead] = total.astype(bf16)
                push(way, step, stream).start()

        def last():
            given(turns, stream).wait_recv()
            both_pushes(turns - 1, stream).wait_recv()
            total = pair_sum(0, stream)
            for way in range(2):
                total = total + recvs[stream][way, turns - 2].astype(f32)
            finish(total)

        steps = [functools.partial(middle, step) for step in range(1, turns)]
        return [gives, start] + steps + [last]

    def scatter_drain(stream):
        ref = fulls[stream].at[sent_rows(stream)]
        sems = r.s_send.at[stream], r.s_recv.at[stream, 0]
        remote(ref, ref, *sems, {"dp": right}).wait_send()
        ref = fulls[stream].at[pl.ds(0, count * rows)]
        sems = r.sp_send.at[stream], r.sp_recv.at[stream, 0]
        remote(ref, ref, *sems, {"dp": partner}).wait_send()


    own = pl.ds(0, own_rows)
    far = pl.ds(own_rows, own_rows)
    exchanged = [
        (r.seg_own, r.seg_other),
        (r.tokens, r.tok_other),
        (r.cot, r.cot_all.at[far]),
        (r.out_send, r.out_recv),
        (r.n2.at[own], r.n2.at[far]),
        (r.down_send, r.down_recv),
        (r.dn2_send, r.dn2_recv),
        (r.dres.at[own], r.dres.at[far]),
        (r.dn1_send, r.dn1_recv),
        (r.gain_part, r.gain_recv),
    ]
    by_lanes, by_rows = (3, 5, 6, 8), (4, 7)
    chunks = model // (2 * LANES)
    chunk_rows = own_rows // chunks

    def swap(index, part=0):
        src, dst = exchanged[index]
        if index in by_lanes:
            lanes = pl.ds(pl.multiple_of(part * 2 * LANES, 2 * LANES), 2 * LANES)
            src, dst = src.at[:, lanes], dst.at[:, lanes]
        elif index in by_rows:
            here = pl.ds(pl.multiple_of(part * chunk_rows, chunk_rows), chunk_rows)
            src, dst = src.at[here], dst.at[here]
        return remote(src, dst, r.y_send.at[index], r.y_recv.at[index], {"seq": other})

    def whole_swap(index):
        src, dst = exchanged[index]
        return remote(src, dst, r.y_send.at[index], r.y_recv.at[index], {"seq": other})

    def arrived(index):
        whole_swap(index).wait_recv()

    def swap_drain(index):
        whole_swap(index).wait_send()


    def normed(values):
        center = values - jnp.mean(values, axis=-1, keepdims=True)
        inv_std = lax.rsqrt(jnp.mean(center * center, axis=-1, keepdims=True) + EPS)
        return center * inv_std, inv_std

    def to_columns(src, dst):
        def body(index, lanes):
            dst[lanes, :] = src[:, lanes].astype(f32).T.astype(bf16)

        tiles(model, LANES, body)

    def partial_sums(terms, own_ref, send_ref, exchange):
        def body(index, lanes):
            total = sum(nt(left[...], right[lanes, :]) for left, right in terms)
            own_ref[:, lanes] = total[:own_rows]
            send_ref[:, lanes] = total[own_rows:].astype(bf16)
            swap(exchange, index).start()

        tiles(model, 2 * LANES, body)

    def weight_grad(columns, right, out):
        size = right.shape[1]

        def body(index, lanes):
            out[:, lanes] = nn(columns[...], right[:, lanes]).astype(bf16)

        whole = size // (2 * LANES) * 2 * LANES
        tiles(whole, 2 * LANES, body)
        if whole < size:
            body(0, pl.ds(whole, size - whole))

    blocks = width // LANES
    hidden_blocks = hidden // LANES
    lane = lax.broadcasted_iota(jnp.int32, (total_rows, LANES), 1)
    low_half = lane % (2 * HEAD_HALF) < HEAD_HALF
    first = lane < 2 * HEAD_HALF

    def setup():
        r.cos[own, :] = r.cos_table[pl.ds(pl.multiple_of(mine * own_rows, own_rows), own_rows), :]
        r.cos[far, :] = r.cos_table[pl.ds(pl.multiple_of(other * own_rows, own_rows), own_rows), :]
        r.sin[own, :] = r.sin_table[pl.ds(pl.multiple_of(mine * own_rows, own_rows), own_rows), :]
        r.sin[far, :] = r.sin_table[pl.ds(pl.multiple_of(other * own_rows, own_rows), own_rows), :]

    def position(dim):
        index = lax.broadcasted_iota(jnp.int32, (total_rows, total_rows), dim)
        return jnp.where(index < own_rows, index + mine * own_rows, index - mine * own_rows)

    def make_bias():
        seg_row = jnp.concatenate([r.seg_own[0:1, :], r.seg_other[0:1, :]], axis=1).astype(f32)
        across = jnp.broadcast_to(seg_row, (total_rows, total_rows))
        allowed = (jnp.abs(position(0) - position(1)) <= HALO) & (across == across.T)
        r.bias[...] = jnp.where(allowed, 0.0, NEG_FILL)

    def expand_special():
        spot = lax.broadcasted_iota(jnp.int32, (2 * LANES, LANES), 1)
        keep = spot < rest

        def body(index, here):
            part = fulls[6][here, :].astype(f32)
            r.gains[:, here] = part.T[3 * rest : 3 * rest + 8]
            r.sp_in[here, :LANES] = jnp.where(keep, part, 0.0).astype(bf16)
            r.sp_in[here, LANES:] = jnp.where(
                keep, pltpu.roll(part, LANES - rest, 1), 0.0
            ).astype(bf16)
            r.sp_down[here, :] = jnp.where(
                keep, pltpu.roll(part, LANES - 2 * rest, 1), 0.0
            ).astype(bf16)

        tiles(model, 2 * LANES, body)

    def attn_gain():
        return r.gains[0:1, :] + r.gains[1:2, :]

    def mlp_gain():
        return r.gains[2:3, :] + r.gains[3:4, :]

    def norm_one():
        for src, place_of in ((r.tokens, 0), (r.tok_other, own_rows)):
            def body(index, here):
                unit_rows, _ = normed(src[here, :].astype(f32))
                at = pl.ds(pl.multiple_of(index * 32 + place_of, 32), 32)
                r.n1[at, :] = (unit_rows * attn_gain()).astype(bf16)

            tiles(own_rows, 32, body)

    def values_of():
        def body(index, lanes):
            r.v[:, lanes] = nn(r.n1[...], fulls[1][:, lanes]).astype(bf16)

        tiles(width, 2 * LANES, body)

    def attend(index, wide, lanes):
        cos_table, sin_table = r.cos[...], r.sin[...]
        proj = nn(r.n1[...], fulls[0][:, wide])
        queries = turn(proj[:, :LANES], cos_table, sin_table, low_half)
        keys = turn(proj[:, LANES:], cos_table, sin_table, low_half).astype(bf16)
        r.qk[:, wide] = jnp.concatenate([queries.astype(bf16), keys], axis=1)
        values = r.v[:, lanes].astype(f32)
        mixed = jnp.zeros((total_rows, LANES), f32)
        for head in range(2):
            here = first if head == 0 else ~first
            scores = nt(jnp.where(here, queries, 0.0).astype(bf16), keys) * scale + r.bias[...]
            top_score = jnp.max(scores, axis=-1, keepdims=True)
            total = jnp.sum(jnp.exp(scores - top_score), axis=-1, keepdims=True)
            probs = jnp.exp(scores - (top_score + jnp.log(total)))
            r.probs[index * 2 + head] = probs
            mixed = mixed + nn(probs.astype(bf16), jnp.where(here, values, 0.0).astype(bf16))
        r.mixed[:, lanes] = mixed.astype(bf16)

    def attend_back(index, wide, lanes):
        cos_table, sin_table = r.cos[...], -r.sin[...]
        both = r.qk[:, wide]
        queries = both[:, :LANES].astype(f32)
        keys = both[:, LANES:].astype(f32)
        values = r.v[:, lanes]
        dmixed = r.dmixed[:, lanes].astype(f32)
        products = dmixed * r.mixed[:, lanes].astype(f32)
        dquery = jnp.zeros((total_rows, LANES), f32)
        dkey = jnp.zeros((total_rows, LANES), f32)
        dvalue = jnp.zeros((total_rows, LANES), f32)
        for head in range(2):
            here = first if head == 0 else ~first
            head_queries = jnp.where(here, queries, 0.0).astype(bf16)
            head_keys = jnp.where(here, keys, 0.0).astype(bf16)
            head_dmixed = jnp.where(here, dmixed, 0.0).astype(bf16)
            delta = jnp.sum(jnp.where(here, products, 0.0), axis=-1, keepdims=True)
            probs = r.probs[index * 2 + head]
            dprobs = nt(head_dmixed, values)
            dscores = (probs * (dprobs - delta) * scale).astype(bf16)
            dvalue = dvalue + lax.dot_general(
                probs.astype(bf16), head_dmixed, OVER_ROWS, preferred_element_type=f32
            )
            dkey = dkey + lax.dot_general(
                dscores, head_queries, OVER_ROWS, preferred_element_type=f32
            )
            dquery = dquery + nn(dscores, head_keys)
        dquery = turn(dquery, cos_table, sin_table, low_half)
        dkey = turn(dkey, cos_table, sin_table, low_half)
        r.dqk[:, wide] = jnp.concatenate([dquery, dkey], axis=1).astype(bf16)
        r.dv[:, lanes] = dvalue.astype(bf16)

    def over_heads(body, start, stop):
        def step(index, carry):
            body(
                index,
                pl.ds(pl.multiple_of(index * 2 * LANES, 2 * LANES), 2 * LANES),
                pl.ds(pl.multiple_of(index * LANES, LANES), LANES),
            )
            return carry

        lax.fori_loop(start, stop, step, 0)

    def norm_two():
        def body(index, here):
            residual = (
                r.tokens[here, :].astype(f32)
                + r.acc[here, :]
                + r.out_recv[here, :].astype(f32)
            )
            r.residual[here, :] = residual
            unit_rows, _ = normed(residual)
            r.n2[here, :] = (unit_rows * mlp_gain()).astype(bf16)
            swap(4, index).start()

        tiles(own_rows, chunk_rows, body)

    def expand_tile(weight, at):
        both = nn(r.n2[...], weight)
        gate, linear = both[:, :LANES], both[:, LANES:]
        erf_part = 0.5 * (1.0 + lax.erf(gate * 0.7071067811865476))
        active = gate * erf_part
        slope = erf_part + gate * jnp.exp(-0.5 * gate * gate) * 0.3989422804014327
        r.mid[:, at] = (active * linear).astype(bf16)
        r.act[:, at] = active
        r.slope[:, at] = linear * slope

    def expand_stream(stream, offset):
        def body(index, lanes):
            at = pl.ds(pl.multiple_of((index + offset) * LANES, LANES), LANES)
            expand_tile(fulls[stream][:, lanes], at)

        tiles(fulls[stream].shape[1], 2 * LANES, body)

    spare = pl.ds(hidden, LANES)

    def dexpand(weight, at, to):
        dmiddle = nn(r.cot_all[...], weight)
        dgate = (dmiddle * r.slope[:, at]).astype(bf16)
        dlinear = (dmiddle * r.act[:, at]).astype(bf16)
        parts = []
        for start in range(0, dmiddle.shape[1], LANES):
            parts += [dgate[:, start : start + LANES], dlinear[:, start : start + LANES]]
        r.dexp[:, to] = jnp.concatenate(parts, axis=1)

    def dexpand_stream(stream, offset):
        def body(index, lanes):
            at = pl.ds(pl.multiple_of(offset * LANES + index * LANES, LANES), LANES)
            to = pl.ds(
                pl.multiple_of(offset * 2 * LANES + index * 2 * LANES, 2 * LANES), 2 * LANES
            )
            dexpand(fulls[stream][:, lanes], at, to)

        tiles(fulls[stream].shape[1], LANES, body)

    split = fulls[3].shape[1]
    mid_parts = [
        r.mid.at[:, pl.ds(0, split // 2)],
        r.mid.at[:, pl.ds(split // 2, hidden - split // 2)],
    ]
    dexp_parts = [
        r.dexp.at[:, pl.ds(0, split)],
        r.dexp.at[:, pl.ds(split, 2 * hidden - split)],
        r.dexp.at[:, pl.ds(2 * hidden, 2 * LANES)],
    ]

    def special_grad():
        spot = lax.broadcasted_iota(jnp.int32, (2 * LANES, LANES), 1)

        def body(index, here):
            both = nn(r.n2_col[here, :], dexp_parts[2][...])
            down = nn(r.cot_col[here, :], r.mid[:, spare])
            value = jnp.where(
                spot < rest,
                both[:, :LANES],
                jnp.where(
                    spot < 2 * rest,
                    pltpu.roll(both[:, LANES:], rest, 1),
                    jnp.where(spot < 3 * rest, pltpu.roll(down, 2 * rest, 1), 0.0),
                ),
            )
            grads[6][here, :] = value.astype(bf16)

        tiles(model, 2 * LANES, body)

    def back_through_norm(grad_rows, gain, values):
        unit_rows, inv_std = normed(values)
        scaled = grad_rows * gain
        inner = (
            scaled
            - jnp.mean(scaled, axis=-1, keepdims=True)
            - unit_rows * jnp.mean(scaled * unit_rows, axis=-1, keepdims=True)
        )
        return inner * inv_std, jnp.sum(grad_rows * unit_rows, axis=0, keepdims=True)

    def norm_two_back():
        r.gain_part[...] = jnp.zeros_like(r.gain_part)

        def body(index, here):
            grad_rows = r.acc[here, :] + r.dn2_recv[here, :].astype(f32)
            part, gain_sum = back_through_norm(grad_rows, mlp_gain(), r.residual[here, :])
            dresidual = r.cot[here, :].astype(f32) + part
            r.dres_own[here, :] = dresidual
            r.dres[here, :] = dresidual.astype(bf16)
            r.gain_part[1:2, :] += gain_sum
            swap(7, index).start()

        tiles(own_rows, chunk_rows, body)

    def norm_one_back():
        def body(index, here):
            grad_rows = r.acc[here, :] + r.dn1_recv[here, :].astype(f32)
            part, gain_sum = back_through_norm(
                grad_rows, attn_gain(), r.tokens[here, :].astype(f32)
            )
            r.tokens_grad[0, here, :] = (r.dres_own[here, :] + part).astype(bf16)
            r.gain_part[0:1, :] += gain_sum

        tiles(own_rows, 32, body)

    def layer_out():
        def body(index, here):
            r.layer_out[0, here, :] = (
                r.residual[here, :]
                + r.down_acc[here, :]
                + r.down_recv[here, :].astype(f32)
            ).astype(bf16)

        tiles(own_rows, 32, body)

    def gain_columns():
        spot = lax.broadcasted_iota(jnp.int32, (LANES, 2 * LANES), 0)

        def body(index, here):
            sums = r.gain_part[:, here] + r.gain_recv[:, here]
            value = jnp.where(
                spot == 3 * rest, sums[0:1], jnp.where(spot == 3 * rest + 1, sums[1:2], 0.0)
            ).T
            old = grads[6][here, :].astype(f32)
            grads[6][here, :] = (old + value).astype(bf16)

        tiles(model, 2 * LANES, body)

    def dmixed_of():
        def body(index, lanes):
            r.dmixed[:, lanes] = nn(r.dres[...], fulls[2][:, lanes]).astype(bf16)

        tiles(width, 2 * LANES, body)


    def pack_keys():
        for at in range(0, width, LANES):
            for which in range(2):
                to = 2 * at + which * LANES
                fulls[0][my_rows, to : to + LANES] = r.raw_qkv[which, :, at : at + LANES]
        fulls[1][my_rows, :] = r.raw_qkv[2]

    def pack_special():
        spot = lax.broadcasted_iota(jnp.int32, (LANES, rows), 0)
        gain_parts = []
        for gain in (r.attn_gain[...], r.mlp_gain[...]):
            spread = gain * 65537.0
            high = spread - (spread - gain)
            gain_parts += [high, gain - high]
        gains = jnp.zeros((LANES, rows), f32)
        for index, part in enumerate(gain_parts):
            gains = jnp.where(spot == 3 * rest + index, part, gains)
        special = gains.T
        if rest:
            parts = [
                r.raw_in[:, 0, hidden:].astype(f32),
                r.raw_in[:, 1, hidden:].astype(f32),
                r.raw_down[:, hidden:].astype(f32),
                jnp.zeros((rows, LANES - 3 * rest), f32),
            ]
            special = special + jnp.concatenate(parts, axis=1)
        fulls[6][my_rows, :] = special.astype(bf16)

    def pack_rest():
        fulls[2][my_rows, :] = r.raw_out[...]
        for at in range(0, hidden, LANES):
            stream, to = (3, 2 * at) if 2 * at < split else (4, 2 * at - split)
            for which in range(2):
                start = to + which * LANES
                fulls[stream][my_rows, start : start + LANES] = r.raw_in[:, which, at : at + LANES]
        fulls[5][my_rows, :] = r.raw_down[:, : split // 2]
        fulls[7][my_rows, :] = r.raw_down[:, split // 2 : hidden]


    def finish_keys(total):
        for at in range(0, width, LANES):
            for which in range(2):
                to = 2 * at + which * LANES
                r.qkv_grad[which, :, at : at + LANES] = total[:, to : to + LANES]

    def finish_values(total):
        r.qkv_grad[2] = total

    def finish_out(total):
        r.out_grad[...] = total

    def finish_special(total):
        turned = total.T
        r.attn_gain_grad[...] = turned[3 * rest : 3 * rest + 1]
        r.mlp_gain_grad[...] = turned[3 * rest + 1 : 3 * rest + 2]
        if rest:
            r.in_grad[:, 0, hidden:] = total[:, :rest]
            r.in_grad[:, 1, hidden:] = total[:, rest : 2 * rest]
            r.down_grad[:, hidden:] = total[:, 2 * rest : 3 * rest]

    def finish_in(start):
        def finish(total):
            for at in range(0, total.shape[1], 2 * LANES):
                to = start + at // 2
                r.in_grad[:, 0, to : to + LANES] = total[:, at : at + LANES]
                r.in_grad[:, 1, to : to + LANES] = total[:, at + LANES : at + 2 * LANES]

        return finish

    def finish_down(start):
        def finish(total):
            r.down_grad[:, start : start + total.shape[1]] = total

        return finish

    gathers = [gather_ops(stream) for stream in range(streams)]
    finishes = [finish_keys, finish_values, finish_out, finish_in(0), finish_in(split // 2)]
    finishes += [finish_down(0), finish_special, finish_down(split // 2)]
    scatters = [scatter_ops(stream, finishes[stream]) for stream in range(streams)]

    def go(ops, *chosen):
        for stream in chosen:
            if ops[stream]:
                ops[stream].pop(0)()

    def end(ops, *chosen):
        while any(ops[stream] for stream in chosen):
            go(ops, *chosen)


    barrier = pltpu.get_barrier_semaphore()
    for device in (right, left, partner):
        pl.semaphore_signal(barrier, inc=1, device_id={"dp": device}, device_id_type=MESH)
    pl.semaphore_signal(barrier, inc=1, device_id={"seq": other}, device_id_type=MESH)
    loads = [
        pltpu.make_async_copy(src, dst, r.own_sem.at[index])
        for index, (src, dst) in enumerate(
            [
                (r.in_qkv, r.raw_qkv),
                (r.in_in, r.raw_in),
                (r.in_down, r.raw_down),
                (r.in_attn_gain, r.attn_gain),
                (r.in_mlp_gain, r.mlp_gain),
                (r.in_seg, r.seg),
                (r.in_tokens.at[0], r.tokens),
                (r.in_cot.at[0], r.cot),
                (r.in_out, r.raw_out),
                (r.in_cos, r.cos_table),
                (r.in_sin, r.sin_table),
            ]
        )
    ]
    for load in loads:
        load.start()
    loads[0].wait()
    pack_keys()
    pl.semaphore_wait(barrier, 4)
    go(gathers, 0, 1)
    for load in loads[1:8]:
        load.wait()
    pack_special()
    go(gathers, 6)
    r.seg_own[...] = jnp.broadcast_to(r.seg[...], r.seg_own.shape)
    for index in range(3):
        swap(index).start()
    loads[8].wait()
    pack_rest()
    r.cot_all[own, :] = r.cot[...]
    for load in loads[9:]:
        load.wait()
    setup()
    to_columns(r.cot_all.at[own], r.cot_col.at[:, own])
    arrived(0)
    make_bias()
    go(gathers, 0, 1, 6, 2)
    go(gathers, 0, 1, 6, 2, 3)
    go(gathers, 0, 1, 6, 2, 3, 5)
    go(gathers, 0, 1, 6)
    arrived(1)
    arrived(2)
    gather_arrived(6)
    expand_special()
    go(gathers, 2)
    norm_one()
    gather_arrived(1)
    values_of()
    gather_arrived(0)
    over_heads(attend, blocks * 0 // 4, blocks * 1 // 4)
    go(gathers, 3)
    over_heads(attend, blocks * 1 // 4, blocks * 2 // 4)
    over_heads(attend, blocks * 2 // 4, blocks * 3 // 4)
    go(gathers, 5)
    over_heads(attend, blocks * 3 // 4, blocks * 4 // 4)
    go(gathers, 2, 4, 7)
    gather_arrived(2)
    partial_sums([(r.mixed, fulls[2])], r.acc, r.out_send, 3)
    to_columns(r.n1, r.n1_col)
    to_columns(r.cot_all.at[far], r.cot_col.at[:, far])
    go(gathers, 3, 5, 4)
    arrived(3)
    norm_two()
    go(gathers, 7, 3, 5, 4)
    arrived(4)
    gather_arrived(3)
    expand_stream(3, 0)
    go(gathers, 7)
    weight_grad(r.cot_col, mid_parts[0], grads[5])
    go(gathers, 5)
    go(scatters, 5)
    to_columns(r.n2, r.n2_col)
    expand_tile(r.sp_in[...], spare)
    gather_arrived(5)
    dexpand_stream(5, 0)
    go(scatters, 5)
    dexpand(r.sp_down[...], spare, pl.ds(2 * hidden, 2 * LANES))
    weight_grad(r.n2_col, dexp_parts[0], grads[3])
    go(gathers, 4)
    go(scatters, 3)
    go(gathers, 7)
    go(scatters, 5, 3)
    go(gathers, 4, 7)
    gather_arrived(4)
    expand_stream(4, split // (2 * LANES))
    go(scatters, 5)
    weight_grad(r.cot_col, mid_parts[1], grads[7])
    go(scatters, 3, 7)
    gather_arrived(7)
    dexpand_stream(7, split // (2 * LANES))
    partial_sums(
        [(dexp_parts[0], fulls[3]), (dexp_parts[1], fulls[4]), (dexp_parts[2], r.sp_in)],
        r.acc,
        r.dn2_send,
        6,
    )
    go(scatters, 5, 7)
    weight_grad(r.n2_col, dexp_parts[1], grads[4])
    go(scatters, 4)
    go(scatters, 4, 3, 5, 7)
    arrived(6)
    norm_two_back()
    go(scatters, 4)
    special_grad()
    partial_sums(
        [(mid_parts[0], fulls[5]), (mid_parts[1], fulls[7]), (r.mid.at[:, spare], r.sp_down)],
        r.down_acc,
        r.down_send,
        5,
    )
    go(scatters, 3, 7)
    arrived(7)
    dmixed_of()
    over_heads(attend_back, blocks * 0 // 4, blocks * 1 // 4)
    over_heads(attend_back, blocks * 1 // 4, blocks * 2 // 4)
    go(scatters, 4)
    over_heads(attend_back, blocks * 2 // 4, blocks * 3 // 4)
    over_heads(attend_back, blocks * 3 // 4, blocks * 4 // 4)
    partial_sums([(r.dqk, fulls[0]), (r.dv, fulls[1])], r.acc, r.dn1_send, 8)
    go(scatters, 3)
    weight_grad(r.n1_col, r.dqk, grads[0])
    go(scatters, 7, 0)
    weight_grad(r.n1_col, r.dv, grads[1])
    go(scatters, 1)
    to_columns(r.dres, r.dres_col)
    go(scatters, 0)
    weight_grad(r.dres_col, r.mixed, grads[2])
    go(scatters, 4, 2, 1, 7)
    arrived(8)
    norm_one_back()
    swap(9).start()
    go(scatters, 2, 0)
    arrived(5)
    layer_out()
    arrived(9)
    gain_columns()
    go(scatters, 6, 4, 1)
    go(scatters, 6, 2, 0)
    go(scatters, 6, 1, 2, 0)
    go(scatters, 6, 1, 2, 0)
    go(scatters, 6, 1, 2)
    go(scatters, 6)
    end(scatters, *range(streams))

    for stream in range(streams):
        gather_drain(stream)
        scatter_drain(stream)
    for index in range(len(exchanged)):
        swap_drain(index)


def fused_call(inputs, devices, widths):
    names, arrays = zip(*inputs.items())
    whole = dict(inputs)
    count = devices // 2
    own_rows, model = whole["in_tokens"].shape[1:]
    total = 2 * own_rows
    _, rows, width = whole["in_qkv"].shape
    local_hidden = whole["in_in"].shape[2]
    rest = local_hidden % LANES
    hidden = local_hidden - rest
    half = rows // 2
    turns = count // 2
    f32, bf16 = jnp.float32, jnp.bfloat16
    streams = len(widths)
    heads = width // (2 * HEAD_HALF)
    outs = dict(
        layer_out=((1, own_rows, model), bf16),
        tokens_grad=((1, own_rows, model), bf16),
        qkv_grad=((3, rows, width), f32),
        out_grad=((rows, width), f32),
        in_grad=((rows, 2, local_hidden), f32),
        down_grad=((rows, local_hidden), f32),
        attn_gain_grad=((1, rows), f32),
        mlp_gain_grad=((1, rows), f32),
    )
    shapes = dict(
        tokens=((own_rows, model), bf16),
        cot=((own_rows, model), bf16),
        seg=((1, own_rows), jnp.int32),
        attn_gain=((1, rows), f32),
        mlp_gain=((1, rows), f32),
        cos_table=((total, LANES), f32),
        sin_table=((total, LANES), f32),
        seg_own=((8, own_rows), jnp.int32),
        seg_other=((8, own_rows), jnp.int32),
        raw_qkv=((3, rows, width), bf16),
        raw_out=((rows, width), bf16),
        raw_in=((rows, 2, local_hidden), bf16),
        raw_down=((rows, local_hidden), bf16),
        tok_other=((own_rows, model), bf16),
        cot_all=((total, model), bf16),
        cot_col=((model, total), bf16),
        n1=((total, model), bf16),
        n1_col=((model, total), bf16),
        gains=((8, model), f32),
        cos=((total, LANES), f32),
        sin=((total, LANES), f32),
        bias=((total, total), f32),
        sp_in=((model, 2 * LANES), bf16),
        sp_down=((model, LANES), bf16),
        v=((total, width), bf16),
        qk=((total, 2 * width), bf16),
        probs=((heads, total, total), f32),
        mixed=((total, width), bf16),
        acc=((own_rows, model), f32),
        down_acc=((own_rows, model), f32),
        out_send=((own_rows, model), bf16),
        out_recv=((own_rows, model), bf16),
        down_send=((own_rows, model), bf16),
        down_recv=((own_rows, model), bf16),
        dn2_send=((own_rows, model), bf16),
        dn2_recv=((own_rows, model), bf16),
        dn1_send=((own_rows, model), bf16),
        dn1_recv=((own_rows, model), bf16),
        residual=((own_rows, model), f32),
        n2=((total, model), bf16),
        n2_col=((model, total), bf16),
        mid=((total, hidden + LANES), bf16),
        act=((total, hidden + LANES), f32),
        slope=((total, hidden + LANES), f32),
        dexp=((total, 2 * hidden + 2 * LANES), bf16),
        dres_own=((own_rows, model), f32),
        dres=((total, model), bf16),
        dres_col=((model, total), bf16),
        dmixed=((total, width), bf16),
        dqk=((total, 2 * width), bf16),
        dv=((total, width), bf16),
        gain_part=((8, model), f32),
        gain_recv=((8, model), f32),
    )
    for i, w in enumerate(widths):
        shapes["full%d" % i] = ((model, w), bf16)
        shapes["grad%d" % i] = ((model, w), bf16)
        shapes["pair%d" % i] = ((count, rows, w), bf16)
        shapes["end%d" % i] = ((2, half, w), bf16)
        shapes["recv%d" % i] = ((2, turns - 1, rows, w), bf16)
    scratch = {name: pltpu.VMEM(shape, dtype) for name, (shape, dtype) in shapes.items()}
    semaphores = dict(
        own_sem=(11,),
        g_send=(streams,),
        g_recv=(streams, turns),
        gp_send=(streams,),
        gp_recv=(streams,),
        s_send=(streams,),
        s_recv=(streams, turns),
        sp_send=(streams,),
        sp_recv=(streams, turns + 1),
        y_send=(10,),
        y_recv=(10,),
    )
    for name, shape in semaphores.items():
        scratch[name] = pltpu.SemaphoreType.DMA(shape)
    vmem = pl.BlockSpec(memory_space=pltpu.VMEM)
    anywhere = pl.BlockSpec(memory_space=pl.ANY)
    sizes = (count, own_rows, width, hidden, rest, 1.0 / math.sqrt(2 * HEAD_HALF))
    layout = list(names) + list(outs) + list(scratch)
    return pl.pallas_call(
        functools.partial(fused_kernel, sizes, layout),
        out_shape=[jax.ShapeDtypeStruct(shape, dtype) for shape, dtype in outs.values()],
        in_specs=[anywhere] * len(names),
        out_specs=[vmem] * len(outs),
        scratch_shapes=list(scratch.values()),
        compiler_params=pltpu.CompilerParams(
            collective_id=2, has_side_effects=True, vmem_limit_bytes=FUSED_LIMIT
        ),
        name="fused_layer",
    )(*arrays)


def copy_kernel(count, *refs):
    sources, targets, buffers = refs[:count], refs[count : 2 * count], refs[2 * count : 3 * count]
    sems = refs[3 * count]
    ins = [
        pltpu.make_async_copy(sources[index], buffers[index], sems.at[0, index])
        for index in range(count)
    ]
    outs = [
        pltpu.make_async_copy(buffers[index], targets[index], sems.at[1, index])
        for index in range(count)
    ]
    for copy in ins:
        copy.start()
    for index in range(count):
        ins[index].wait()
        outs[index].start()
    for copy in outs:
        copy.wait()


def finish_call(arrays):
    anywhere = pl.BlockSpec(memory_space=pl.ANY)
    count = len(arrays)
    return pl.pallas_call(
        functools.partial(copy_kernel, count),
        out_shape=[jax.ShapeDtypeStruct(array.shape, array.dtype) for array in arrays],
        in_specs=[anywhere] * count,
        out_specs=[anywhere] * count,
        scratch_shapes=[pltpu.VMEM(array.shape, array.dtype) for array in arrays]
        + [pltpu.SemaphoreType.DMA((2, count))],
        name="finish",
    )(*arrays)


FUSED_LIMIT = 63 * 1024 * 1024


def position_tables(total, head_size):
    half_size = head_size // 2
    freqs = THETA ** (-(2.0 / head_size) * np.arange(half_size))
    angles = np.arange(total)[:, None] * freqs[None, :]
    cos_table = np.cos(angles).astype(np.float32)
    sin_table = np.sin(angles).astype(np.float32)
    return (
        jnp.asarray(np.concatenate([cos_table] * 4, axis=1)),
        jnp.asarray(np.concatenate([-sin_table, sin_table] * 2, axis=1)),
    )


def fused_device(
    devices,
    tokens,
    segments,
    cotangent,
    qkv_weight,
    out_weight,
    in_weight,
    down_weight,
    attn_gain,
    mlp_gain,
):
    own_rows = tokens.shape[1]
    width = qkv_weight.shape[2]
    blocks = in_weight.shape[2] // LANES
    first = blocks // 2 * 2 * LANES
    second = 2 * blocks * LANES - first
    widths = [2 * width, width, width, first, second, first // 2, LANES, second // 2]
    cos_table, sin_table = position_tables(2 * own_rows, 2 * HEAD_HALF)
    inputs = dict(
        in_qkv=jnp.transpose(qkv_weight, (1, 0, 2)),
        in_out=out_weight.T,
        in_in=in_weight,
        in_down=down_weight.T,
        in_tokens=tokens,
        in_cot=cotangent,
        in_seg=segments,
        in_attn_gain=attn_gain[None],
        in_mlp_gain=mlp_gain[None],
        in_cos=cos_table,
        in_sin=sin_table,
    )
    results = finish_call(fused_call(inputs, devices, widths))
    layer_out, tokens_grad, qkv, out, in_grad, down, attn_grad, mlp_grad = results
    return (
        layer_out,
        tokens_grad,
        jnp.transpose(qkv, (1, 0, 2)),
        out.T,
        in_grad,
        down.T,
        attn_grad[0],
        mlp_grad[0],
    )


def per_device(
    devices,
    seq_size,
    tokens,
    segments,
    cotangent,
    qkv_weight,
    out_weight,
    in_weight,
    down_weight,
    attn_gain,
    mlp_gain,
):
    args = (
        tokens,
        segments,
        cotangent,
        qkv_weight,
        out_weight,
        in_weight,
        down_weight,
        attn_gain,
        mlp_gain,
    )
    own_rows, model = tokens.shape[1:]
    sizes = (own_rows, model, qkv_weight.shape[2], in_weight.shape[2])
    if fits_fused(devices, seq_size, *sizes) and tokens.shape[0] == 1:
        return fused_device(devices, *args)
    return general_device(devices, seq_size, *args)


def solution(mesh):
    return jax.shard_map(
        functools.partial(per_device, mesh.shape["dp"], mesh.shape["seq"]),
        mesh=mesh,
        in_specs=(
            P("dp", "seq", None),
            P("dp", "seq"),
            P("dp", "seq", None),
            P("dp", None, "seq"),
            P("seq", "dp"),
            P("dp", None, "seq"),
            P("seq", "dp"),
            P("dp"),
            P("dp"),
        ),
        out_specs=(
            P("dp", "seq", None),
            P("dp", "seq", None),
            P("dp", None, "seq"),
            P("seq", "dp"),
            P("dp", None, "seq"),
            P("seq", "dp"),
            P("dp"),
            P("dp"),
        ),
        check_vma=False,
    )
```

```python
import functools
import math
import types

import jax
import jax.numpy as jnp
import numpy as np
from jax import lax
from jax.experimental import pallas as pl
from jax.experimental.pallas import tpu as pltpu
from jax.sharding import PartitionSpec as P

HEADS = 16
HALO = 64


EPS = 1e-05
THETA = 10000.0
NEG_FILL = -1e30


def norm_forward(values, gain):
    center = values - jnp.mean(values, axis=-1, keepdims=True)
    inv_std = lax.rsqrt(jnp.mean(center * center, axis=-1, keepdims=True) + EPS)
    unit_rows = center * inv_std
    return (unit_rows * gain, unit_rows, inv_std)


def norm_backward(grad_rows, gain, unit_rows, inv_std):
    scaled = grad_rows * gain
    inner = (
        scaled
        - jnp.mean(scaled, axis=-1, keepdims=True)
        - unit_rows * jnp.mean(scaled * unit_rows, axis=-1, keepdims=True)
    )
    return (inner * inv_std, jnp.sum(grad_rows * unit_rows, axis=0))


def gelu_value(inputs):
    return 0.5 * inputs * (1.0 + lax.erf(inputs * 0.7071067811865476))


def gelu_slope(inputs):
    return (
        0.5 * (1.0 + lax.erf(inputs * 0.7071067811865476))
        + inputs * jnp.exp(-0.5 * inputs * inputs) * 0.3989422804014327
    )


def rotary_tables(positions, head_size):
    half_size = head_size // 2
    freqs = jnp.power(THETA, -(2.0 / head_size) * jnp.arange(half_size, dtype=jnp.float32))
    angles = positions.astype(jnp.float32)[:, None] * freqs[None, :]
    return (jnp.cos(angles)[:, None, :], jnp.sin(angles)[:, None, :])


def rotate(values, cos_table, sin_table):
    half_size = values.shape[-1] // 2
    lower_half = values[..., :half_size]
    upper_half = values[..., half_size:]
    return jnp.concatenate(
        [
            lower_half * cos_table - upper_half * sin_table,
            upper_half * cos_table + lower_half * sin_table,
        ],
        axis=-1,
    )


def unrotate(grads, cos_table, sin_table):
    half_size = grads.shape[-1] // 2
    lower_half = grads[..., :half_size]
    upper_half = grads[..., half_size:]
    return jnp.concatenate(
        [
            lower_half * cos_table + upper_half * sin_table,
            upper_half * cos_table - lower_half * sin_table,
        ],
        axis=-1,
    )


def window_mask(query_pos, key_pos, query_seg, key_seg, halo_width, total_len):
    near = jnp.abs(query_pos[:, None] - key_pos[None, :]) <= halo_width
    inside = (key_pos >= 0) & (key_pos < total_len)
    return near & inside[None, :] & (query_seg[:, None] == key_seg[None, :])


def block_scores(queries, key_slab, allowed, scale):
    scores = (
        jnp.einsum("qhd,khd->hqk", queries, key_slab, preferred_element_type=jnp.float32) * scale
    )
    return jnp.where(allowed[None], scores, NEG_FILL)


def attend_block(queries, key_slab, value_slab, allowed, scale):
    scores = block_scores(queries, key_slab, allowed, scale)
    top_score = jnp.max(scores, axis=-1, keepdims=True)
    total = jnp.sum(jnp.exp(scores - top_score), axis=-1, keepdims=True)
    logsum = top_score + jnp.log(total)
    probs = jnp.exp(scores - logsum).astype(jnp.bfloat16)
    mixed = jnp.einsum("hqk,khd->qhd", probs, value_slab, preferred_element_type=jnp.float32)
    return (mixed, logsum[..., 0])


def attend_back(queries, key_slab, value_slab, allowed, scale, logsum, mixed_b, dmixed_b):
    scores = block_scores(queries, key_slab, allowed, scale)
    probs = jnp.exp(scores - logsum[..., None])
    probs_b = probs.astype(jnp.bfloat16)
    dvalues = jnp.einsum("hqk,qhd->khd", probs_b, dmixed_b, preferred_element_type=jnp.float32)
    dprobs = jnp.einsum("qhd,khd->hqk", dmixed_b, value_slab, preferred_element_type=jnp.float32)
    delta = jnp.transpose(
        jnp.sum(dmixed_b.astype(jnp.float32) * mixed_b.astype(jnp.float32), axis=-1)
    )
    dscores = (probs * (dprobs - delta[..., None]) * scale).astype(jnp.bfloat16)
    dqueries = jnp.einsum("hqk,khd->qhd", dscores, key_slab, preferred_element_type=jnp.float32)
    dkeys = jnp.einsum("hqk,qhd->khd", dscores, queries, preferred_element_type=jnp.float32)
    return (dqueries, dkeys, dvalues)


MESH = pl.DeviceIdType.MESH
VMEM_LIMIT = 60 * 1024 * 1024
LANES = 128


def ring_place(count):
    me = lax.axis_index("dp")
    core = me % 2
    chip = me // 2
    row, column = chip // 2, chip % 2
    place = (1 - column) * row + column * (count - 1 - row)
    return (core, place)


def chip_at(place, count):
    side = place // (count // 2)
    return (1 - side) * (2 * place) + side * (2 * (count - 1 - place) + 1)


def neighbours(core, place, count):
    right = chip_at((place + 1) % count, count) * 2 + core
    left = chip_at((place + count - 1) % count, count) * 2 + core
    return (right, left, lax.axis_index("dp") + 1 - 2 * core)


def greet(devices):
    barrier = pltpu.get_barrier_semaphore()
    for device in devices:
        pl.semaphore_signal(barrier, inc=1, device_id={"dp": device}, device_id_type=MESH)
    pl.semaphore_wait(barrier, len(devices))


def gather_kernel(count, streams, *refs):
    shards = refs[:streams]
    fulls = refs[streams : 2 * streams]
    own_sem, send_sem, recv_sem, pair_send, pair_recv = refs[2 * streams :]
    rows = shards[0].shape[0]
    half = rows // 2
    core, place = ring_place(count)
    right, left, partner = neighbours(core, place, count)
    targets = (right, left)
    lanes = [(way, stream) for stream in range(streams) for way in range(2)]

    def piece(way, step, stream):
        shift = count - step if way == 0 else step
        owner = chip_at((place + shift) % count, count) * 2 + core
        start = pl.multiple_of(owner * rows + way * half, half)
        return fulls[stream].at[pl.ds(start, half)]

    def hop(way, step, stream):
        ref = piece(way, step, stream)
        return pltpu.make_async_remote_copy(
            src_ref=ref,
            dst_ref=ref,
            send_sem=send_sem.at[stream, way, step],
            recv_sem=recv_sem.at[stream, way, step],
            device_id={"dp": targets[way]},
            device_id_type=MESH,
        )

    def share(way, step, stream):
        ref = piece(way, step, stream)
        return pltpu.make_async_remote_copy(
            src_ref=ref,
            dst_ref=ref,
            send_sem=pair_send.at[stream, way, step],
            recv_sem=pair_recv.at[stream, way, step],
            device_id={"dp": partner},
            device_id_type=MESH,
        )

    me = lax.axis_index("dp")
    owns = [
        pltpu.make_async_copy(
            shards[stream],
            fulls[stream].at[pl.ds(pl.multiple_of(me * rows, rows), rows)],
            own_sem.at[stream],
        )
        for stream in range(streams)
    ]
    for own in owns:
        own.start()
    greet((right, left, partner))
    for own in owns:
        own.wait()
    for way, stream in lanes:
        hop(way, 0, stream).start()
        share(way, 0, stream).start()

    def step_body(step, carry):
        for way, stream in lanes:
            hop(way, step - 1, stream).wait_recv()
            hop(way, step, stream).start()
            share(way, step, stream).start()
        return carry

    lax.fori_loop(1, count - 1, step_body, 0)
    for way, stream in lanes:
        hop(way, count - 2, stream).wait_recv()
        share(way, count - 1, stream).start()

    def drain_hops(step, carry):
        for way, stream in lanes:
            hop(way, step, stream).wait_send()
        return carry

    def drain_shares(step, carry):
        for way, stream in lanes:
            share(way, step, stream).wait_send()
            share(way, step, stream).wait_recv()
        return carry

    lax.fori_loop(0, count - 1, drain_hops, 0)
    lax.fori_loop(0, count, drain_shares, 0)


def ring_gather(shards, devices):
    count = devices // 2
    streams = len(shards)
    return pl.pallas_call(
        functools.partial(gather_kernel, count, streams),
        out_shape=[
            jax.ShapeDtypeStruct((devices * shard.shape[0], shard.shape[1]), shard.dtype)
            for shard in shards
        ],
        in_specs=[pl.BlockSpec(memory_space=pltpu.VMEM)] * streams,
        out_specs=[pl.BlockSpec(memory_space=pl.ANY)] * streams,
        scratch_shapes=[pltpu.SemaphoreType.DMA((streams,))]
        + [pltpu.SemaphoreType.DMA((streams, 2, count - 1))] * 2
        + [pltpu.SemaphoreType.DMA((streams, 2, count))] * 2,
        cost_estimate=pl.CostEstimate(
            flops=0, bytes_accessed=128 * 1024 * 1024, transcendentals=0
        ),
        compiler_params=pltpu.CompilerParams(
            collective_id=0, has_side_effects=True, vmem_limit_bytes=VMEM_LIMIT
        ),
        name="ring_gather",
    )(*shards)


def scatter_kernel(count, streams, *refs):
    grads = refs[:streams]
    outs = refs[streams : 2 * streams]
    pairs = refs[2 * streams : 3 * streams]
    sends = refs[3 * streams : 4 * streams]
    recvs = refs[4 * streams : 5 * streams]
    send_sem, recv_sem, pair_send, pair_recv = refs[5 * streams :]
    rows = outs[0].shape[0]
    half = rows // 2
    core, place = ring_place(count)
    right, left, partner = neighbours(core, place, count)
    targets = (right, left)

    def block(way, step, which):
        shift = 2 * count - 1 - step if way == 0 else 1 + step
        owner = chip_at((place + shift) % count, count) * 2 + which
        return pl.ds(pl.multiple_of(owner * rows + way * half, half), half)

    def share(way, step, stream):
        return pltpu.make_async_remote_copy(
            src_ref=grads[stream].at[block(way, step, 1 - core)],
            dst_ref=pairs[stream].at[way, step],
            send_sem=pair_send.at[stream, way, step],
            recv_sem=pair_recv.at[stream, way, step],
            device_id={"dp": partner},
            device_id_type=MESH,
        )

    def hop(way, step, stream):
        return pltpu.make_async_remote_copy(
            src_ref=sends[stream].at[way, step],
            dst_ref=recvs[stream].at[way, step],
            send_sem=send_sem.at[stream, way, step],
            recv_sem=recv_sem.at[stream, way, step],
            device_id={"dp": targets[way]},
            device_id_type=MESH,
        )

    def pair_sum(way, step, stream):
        share(way, step, stream).wait_recv()
        own = grads[stream][block(way, step, core), :].astype(jnp.float32)
        return own + pairs[stream][way, step].astype(jnp.float32)

    greet((right, left, partner))

    def start_shares(step, carry):
        for stream in range(streams):
            for way in range(2):
                share(way, step, stream).start()
        return carry

    lax.fori_loop(0, count, start_shares, 0)
    for stream in range(streams):
        for way in range(2):
            sends[stream][way, 0] = pair_sum(way, 0, stream).astype(jnp.bfloat16)
            hop(way, 0, stream).start()

    def step_body(step, carry):
        for stream in range(streams):
            for way in range(2):
                total = pair_sum(way, step, stream)
                hop(way, step - 1, stream).wait_recv()
                total = total + recvs[stream][way, step - 1].astype(jnp.float32)
                sends[stream][way, step] = total.astype(jnp.bfloat16)
                hop(way, step, stream).start()
        return carry

    lax.fori_loop(1, count - 1, step_body, 0)
    for stream in range(streams):
        for way in range(2):
            total = pair_sum(way, count - 1, stream)
            hop(way, count - 2, stream).wait_recv()
            total = total + recvs[stream][way, count - 2].astype(jnp.float32)
            outs[stream][way * half : (way + 1) * half, :] = total

    def drain_hops(step, carry):
        for stream in range(streams):
            for way in range(2):
                hop(way, step, stream).wait_send()
        return carry

    def drain_shares(step, carry):
        for stream in range(streams):
            for way in range(2):
                share(way, step, stream).wait_send()
        return carry

    lax.fori_loop(0, count - 1, drain_hops, 0)
    lax.fori_loop(0, count, drain_shares, 0)


def ring_scatter(grads, devices):
    count = devices // 2
    streams = len(grads)
    rows = grads[0].shape[0] // devices
    half = rows // 2
    widths = [grad.shape[1] for grad in grads]
    vmem = pl.BlockSpec(memory_space=pltpu.VMEM)
    return pl.pallas_call(
        functools.partial(scatter_kernel, count, streams),
        out_shape=[jax.ShapeDtypeStruct((rows, width), jnp.float32) for width in widths],
        in_specs=[vmem] * streams,
        out_specs=[vmem] * streams,
        scratch_shapes=[pltpu.VMEM((2, count, half, width), jnp.bfloat16) for width in widths]
        + [pltpu.VMEM((2, count - 1, half, width), jnp.bfloat16) for width in widths] * 2
        + [pltpu.SemaphoreType.DMA((streams, 2, count - 1))] * 2
        + [pltpu.SemaphoreType.DMA((streams, 2, count))] * 2,
        compiler_params=pltpu.CompilerParams(
            collective_id=1, has_side_effects=True, vmem_limit_bytes=40 * 1024 * 1024
        ),
        name="ring_scatter",
    )(*grads)


def turn(values, cos_table, sin_table, low_half):
    half = HEAD_HALF
    swapped = jnp.where(
        low_half, pltpu.roll(values, LANES - half, 1), pltpu.roll(values, half, 1)
    )
    return values * cos_table + swapped * sin_table


HEAD_HALF = 32


def lane_masks(rows):
    lane = lax.broadcasted_iota(jnp.int32, (rows, LANES), 1)
    return (lane % (2 * HEAD_HALF) < HEAD_HALF, lane < 2 * HEAD_HALF)


def allowed_pairs(pos_col, pos_row, seg_col, seg_row):
    near = jnp.abs(pos_col[...] - pos_row[...]) <= HALO
    return near & (seg_col[...] == seg_row[...])


def head_probs(queries, keys, allowed, scale):
    scores = (
        lax.dot_general(
            queries, keys, (((1,), (1,)), ((), ())), preferred_element_type=jnp.float32
        )
        * scale
    )
    scores = jnp.where(allowed, scores, NEG_FILL)
    top_score = jnp.max(scores, axis=-1, keepdims=True)
    total = jnp.sum(jnp.exp(scores - top_score), axis=-1, keepdims=True)
    return jnp.exp(scores - (top_score + jnp.log(total)))


def attend_kernel(
    scale, width, proj, cos_ref, sin_ref, pos_col, pos_row, seg_col, seg_row, qkv_out, mixed_out
):
    rows = proj.shape[0]
    low_half, first = lane_masks(rows)
    cos_table, sin_table = cos_ref[...], sin_ref[...]
    allowed = allowed_pairs(pos_col, pos_row, seg_col, seg_row)
    for start in range(0, width, LANES):
        queries = turn(proj[:, start : start + LANES], cos_table, sin_table, low_half)
        keys = turn(
            proj[:, width + start : width + start + LANES], cos_table, sin_table, low_half
        ).astype(jnp.bfloat16)
        values = proj[:, 2 * width + start : 2 * width + start + LANES]
        qkv_out[:, start : start + LANES] = queries.astype(jnp.bfloat16)
        qkv_out[:, width + start : width + start + LANES] = keys
        qkv_out[:, 2 * width + start : 2 * width + start + LANES] = values.astype(jnp.bfloat16)
        mixed = jnp.zeros((rows, LANES), jnp.float32)
        for head in range(2):
            mine = first if head == 0 else ~first
            probs = head_probs(
                jnp.where(mine, queries, 0.0).astype(jnp.bfloat16), keys, allowed, scale
            ).astype(jnp.bfloat16)
            mixed = mixed + jnp.dot(
                probs,
                jnp.where(mine, values, 0.0).astype(jnp.bfloat16),
                preferred_element_type=jnp.float32,
            )
        mixed_out[:, start : start + LANES] = mixed.astype(jnp.bfloat16)


def attend_back_kernel(
    scale,
    width,
    qkv,
    mixed_ref,
    dmixed_ref,
    cos_ref,
    sin_ref,
    pos_col,
    pos_row,
    seg_col,
    seg_row,
    dqkv_out,
):
    rows = qkv.shape[0]
    low_half, first = lane_masks(rows)
    cos_table, sin_table = cos_ref[...], -sin_ref[...]
    allowed = allowed_pairs(pos_col, pos_row, seg_col, seg_row)
    over_rows = (((0,), (0,)), ((), ()))
    over_lanes = (((1,), (1,)), ((), ()))
    for start in range(0, width, LANES):
        queries = qkv[:, start : start + LANES].astype(jnp.float32)
        keys = qkv[:, width + start : width + start + LANES]
        keys32 = keys.astype(jnp.float32)
        values = qkv[:, 2 * width + start : 2 * width + start + LANES]
        dmixed = dmixed_ref[:, start : start + LANES].astype(jnp.float32)
        products = dmixed * mixed_ref[:, start : start + LANES].astype(jnp.float32)
        dquery = jnp.zeros((rows, LANES), jnp.float32)
        dkey = jnp.zeros((rows, LANES), jnp.float32)
        dvalue = jnp.zeros((rows, LANES), jnp.float32)
        for head in range(2):
            mine = first if head == 0 else ~first
            head_queries = jnp.where(mine, queries, 0.0).astype(jnp.bfloat16)
            head_keys = jnp.where(mine, keys32, 0.0).astype(jnp.bfloat16)
            head_dmixed = jnp.where(mine, dmixed, 0.0).astype(jnp.bfloat16)
            delta = jnp.sum(jnp.where(mine, products, 0.0), axis=-1, keepdims=True)
            probs = head_probs(head_queries, keys, allowed, scale)
            dprobs = lax.dot_general(
                head_dmixed, values, over_lanes, preferred_element_type=jnp.float32
            )
            dscores = (probs * (dprobs - delta) * scale).astype(jnp.bfloat16)
            dvalue = dvalue + lax.dot_general(
                probs.astype(jnp.bfloat16),
                head_dmixed,
                over_rows,
                preferred_element_type=jnp.float32,
            )
            dkey = dkey + lax.dot_general(
                dscores, head_queries, over_rows, preferred_element_type=jnp.float32
            )
            dquery = dquery + jnp.dot(dscores, head_keys, preferred_element_type=jnp.float32)
        dquery = turn(dquery, cos_table, sin_table, low_half)
        dkey = turn(dkey, cos_table, sin_table, low_half)
        dqkv_out[:, start : start + LANES] = dquery.astype(jnp.bfloat16)
        dqkv_out[:, width + start : width + start + LANES] = dkey.astype(jnp.bfloat16)
        dqkv_out[:, 2 * width + start : 2 * width + start + LANES] = dvalue.astype(jnp.bfloat16)


def local_call(kernel, name, out_shape, operands, flops):
    vmem = pl.BlockSpec(memory_space=pltpu.VMEM)
    single = not isinstance(out_shape, list)
    return pl.pallas_call(
        kernel,
        out_shape=out_shape,
        in_specs=[vmem] * len(operands),
        out_specs=vmem if single else [vmem] * len(out_shape),
        cost_estimate=pl.CostEstimate(
            flops=flops, bytes_accessed=4 * 1024 * 1024, transcendentals=flops // 256
        ),
        compiler_params=pltpu.CompilerParams(vmem_limit_bytes=32 * 1024 * 1024),
        name=name,
    )(*operands)


class PairedAttention:
    def __init__(self, positions, segments, head_size, width):
        rows = positions.shape[0]
        cos_table, sin_table = rotary_tables(positions, head_size)
        cos_table, sin_table = cos_table[:, 0, :], sin_table[:, 0, :]
        self.width = width
        self.scale = 1.0 / math.sqrt(head_size)
        self.flops = 2 * rows * rows * LANES * (width // head_size)
        self.shared = (
            jnp.concatenate([cos_table] * 4, axis=1),
            jnp.concatenate([-sin_table, sin_table] * 2, axis=1),
            positions[:, None],
            positions[None, :],
            segments[:, None],
            segments[None, :],
        )

    def forward(self, projected):
        rows = projected.shape[0]
        self.qkv, self.mixed = local_call(
            functools.partial(attend_kernel, self.scale, self.width),
            "attend",
            [
                jax.ShapeDtypeStruct((rows, 3 * self.width), jnp.bfloat16),
                jax.ShapeDtypeStruct((rows, self.width), jnp.bfloat16),
            ],
            (projected,) + self.shared,
            2 * self.flops,
        )
        return self.mixed

    def backward(self, dmixed):
        rows = dmixed.shape[0]
        return local_call(
            functools.partial(attend_back_kernel, self.scale, self.width),
            "attend_back",
            jax.ShapeDtypeStruct((rows, 3 * self.width), jnp.bfloat16),
            (self.qkv, self.mixed, dmixed) + self.shared,
            5 * self.flops,
        )


class BlockAttention:
    def __init__(self, positions, segments, head_size, width):
        self.total_len = positions.shape[0]
        self.segments = segments
        self.head_size = head_size
        self.width = width
        self.scale = 1.0 / math.sqrt(head_size)
        self.cos_table, self.sin_table = rotary_tables(positions, head_size)

    def heads(self, values):
        return values.reshape(self.total_len, self.width // self.head_size, self.head_size)

    def forward(self, projected):
        width, total_len = self.width, self.total_len
        self.block_rows = min(total_len, 512)
        self.slab_rows = self.block_rows + 2 * HALO
        tables = (self.cos_table, self.sin_table)
        self.queries = rotate(self.heads(projected[:, :width]), *tables).astype(jnp.bfloat16)
        keys = rotate(self.heads(projected[:, width : 2 * width]), *tables).astype(jnp.bfloat16)
        values = self.heads(projected[:, 2 * width :]).astype(jnp.bfloat16)
        pad_spec = ((HALO, HALO), (0, 0), (0, 0))
        self.key_pad = jnp.pad(keys, pad_spec)
        self.value_pad = jnp.pad(values, pad_spec)
        seg_pad = jnp.pad(self.segments, (HALO, HALO), constant_values=-1)
        mixed_parts = []
        self.logsums = []
        self.masks = []
        for start in range(0, total_len, self.block_rows):
            own = slice(start, start + self.block_rows)
            slab = slice(start, start + self.slab_rows)
            allowed = window_mask(
                start + jnp.arange(self.block_rows, dtype=jnp.int32),
                start - HALO + jnp.arange(self.slab_rows, dtype=jnp.int32),
                self.segments[own],
                seg_pad[slab],
                HALO,
                total_len,
            )
            mixed, logsum = attend_block(
                self.queries[own], self.key_pad[slab], self.value_pad[slab], allowed, self.scale
            )
            self.masks.append(allowed)
            self.logsums.append(logsum)
            mixed_parts.append(mixed)
        self.mixed = jnp.concatenate(mixed_parts, axis=0).astype(jnp.bfloat16)
        return self.mixed.reshape(total_len, width)

    def backward(self, dmixed):
        total_len = self.total_len
        dmixed = self.heads(dmixed)
        padded = (total_len + 2 * HALO,) + dmixed.shape[1:]
        dkey_pad = jnp.zeros(padded, jnp.float32)
        dvalue_pad = jnp.zeros(padded, jnp.float32)
        dquery_parts = []
        for index, start in enumerate(range(0, total_len, self.block_rows)):
            own = slice(start, start + self.block_rows)
            slab = slice(start, start + self.slab_rows)
            dqueries, dkeys, dvalues = attend_back(
                self.queries[own],
                self.key_pad[slab],
                self.value_pad[slab],
                self.masks[index],
                self.scale,
                self.logsums[index],
                self.mixed[own],
                dmixed[own],
            )
            dquery_parts.append(dqueries)
            dkey_pad = dkey_pad.at[slab].add(dkeys)
            dvalue_pad = dvalue_pad.at[slab].add(dvalues)
        inner = slice(HALO, HALO + total_len)
        tables = (self.cos_table, self.sin_table)
        parts = [
            unrotate(jnp.concatenate(dquery_parts, axis=0), *tables),
            unrotate(dkey_pad[inner], *tables),
            dvalue_pad[inner],
        ]
        return jnp.concatenate(
            [part.reshape(total_len, self.width) for part in parts], axis=1
        ).astype(jnp.bfloat16)


def dot(left, right, left_dim, right_dim):
    return lax.dot_general(
        left,
        right,
        (((left_dim,), (right_dim,)), ((), ())),
        preferred_element_type=jnp.float32,
    )


def padded_to_lanes(values):
    return jnp.pad(values, ((0, 0), (0, -values.shape[1] % LANES)))


def high_and_low(gain):
    high = gain.astype(jnp.bfloat16)
    return [high[:, None], (gain - high.astype(jnp.float32)).astype(jnp.bfloat16)[:, None]]


def general_device(
    devices,
    seq_size,
    tokens,
    segments,
    cotangent,
    qkv_weight,
    out_weight,
    in_weight,
    down_weight,
    attn_gain,
    mlp_gain,
):
    layer_in = tokens[0]
    seg_local = segments[0]
    cot_local = cotangent[0]
    own_rows, model_width = layer_in.shape
    head_size = model_width // HEADS
    local_width = qkv_weight.shape[2]
    local_hidden = in_weight.shape[2]
    shard_rows = qkv_weight.shape[0]
    total_len = own_rows * seq_size
    paired = (
        seq_size == 2
        and total_len <= 512
        and local_width % LANES == 0
        and head_size == 2 * HEAD_HALF
    )
    swap = [(0, 1), (1, 0)]

    def rows_of_all(values):
        if paired:
            return jnp.concatenate([values, lax.ppermute(values, "seq", swap)], axis=0)
        return lax.all_gather(values, "seq", axis=0, tiled=True)

    def sum_to_owner(partial):
        if paired:
            other = lax.ppermute(partial[own_rows:].astype(jnp.bfloat16), "seq", swap)
            return partial[:own_rows] + other.astype(jnp.float32)
        return lax.psum_scatter(
            partial.astype(jnp.bfloat16), "seq", scatter_dimension=0, tiled=True
        ).astype(jnp.float32)

    def sum_over_seq(part):
        if paired:
            return part + lax.ppermute(part, "seq", swap)
        return lax.psum(part, "seq")

    first_pack = jnp.concatenate(
        [qkv_weight.reshape(shard_rows, 3 * local_width), out_weight.T], axis=1
    )
    wide = (local_hidden + 4 + LANES - 1) // LANES * LANES
    spare = jnp.zeros((shard_rows, wide - local_hidden), jnp.bfloat16)
    second_pack = jnp.concatenate(
        [in_weight[:, 0, :], spare, in_weight[:, 1, :], spare, down_weight.T]
        + high_and_low(attn_gain)
        + high_and_low(mlp_gain)
        + [spare[:, 4:]],
        axis=1,
    )
    first_full, second_full = ring_gather([first_pack, second_pack], devices)
    full_qkv = first_full[:, : 3 * local_width]
    full_out = first_full[:, 3 * local_width : 4 * local_width]
    gains_at = 2 * wide + local_hidden
    gains = second_full[:, gains_at : gains_at + 4].astype(jnp.float32)
    gain_attn = gains[:, 0] + gains[:, 1]
    gain_mlp = gains[:, 2] + gains[:, 3]
    full_in = second_full[:, : 2 * wide]
    full_down = second_full[:, 2 * wide :]

    inputs32 = layer_in.astype(jnp.float32)
    if paired:
        arrived = lax.ppermute(jnp.concatenate([layer_in, cot_local], axis=0), "seq", swap)
        all_inputs32 = jnp.concatenate([layer_in, arrived[:own_rows]], axis=0).astype(jnp.float32)
        cot_full = jnp.concatenate([cot_local, arrived[own_rows:]], axis=0)
    else:
        all_inputs32 = rows_of_all(layer_in).astype(jnp.float32)
        cot_full = rows_of_all(cot_local)
    normed_full = norm_forward(all_inputs32, gain_attn)[0].astype(jnp.bfloat16)
    unit_one, inv_one = norm_forward(inputs32, gain_attn)[1:]
    if paired:
        seg_full = rows_of_all(
            jnp.broadcast_to(seg_local.astype(jnp.float32)[:, None], (own_rows, LANES))
        )[:, 0].astype(jnp.int32)
        place = lax.axis_index("seq")
        arange = jnp.arange(own_rows, dtype=jnp.int32)
        positions = jnp.concatenate(
            [place * own_rows + arange, (1 - place) * own_rows + arange], axis=0
        )
        attention = PairedAttention(positions, seg_full, head_size, local_width)
    else:
        seg_full = rows_of_all(seg_local.astype(jnp.bfloat16)).astype(jnp.int32)
        positions = jnp.arange(total_len, dtype=jnp.int32)
        attention = BlockAttention(positions, seg_full, head_size, local_width)

    mixed = attention.forward(dot(normed_full, full_qkv, 1, 0))
    residual = inputs32 + sum_to_owner(dot(mixed, full_out, 1, 1))
    normed_two, unit_two, inv_two = norm_forward(residual, gain_mlp)
    normed_two_full = rows_of_all(normed_two.astype(jnp.bfloat16))
    expanded = dot(normed_two_full, full_in, 1, 0)
    gate_in = expanded[:, :wide]
    linear_in = expanded[:, wide:]
    activated = gelu_value(gate_in)
    middle_b = (activated * linear_in).astype(jnp.bfloat16)
    down_part = dot(middle_b, full_down, 1, 1)

    down_grad = dot(cot_full, middle_b, 0, 0).astype(jnp.bfloat16)
    dmiddle = dot(cot_full, full_down, 1, 0)
    dexpanded_b = jnp.concatenate(
        [dmiddle * linear_in * gelu_slope(gate_in), dmiddle * activated], axis=1
    ).astype(jnp.bfloat16)
    dnormed_two = sum_to_owner(dot(dexpanded_b, full_in, 1, 1))
    in_grad = dot(normed_two_full, dexpanded_b, 0, 0).astype(jnp.bfloat16)
    dres_norm, mlp_gain_part = norm_backward(dnormed_two, gain_mlp, unit_two, inv_two)
    dresidual = cot_local.astype(jnp.float32) + dres_norm
    dres_full = rows_of_all(dresidual.astype(jnp.bfloat16))
    down_part, dres_full = lax.optimization_barrier((down_part, dres_full))
    layer_out = (residual + sum_to_owner(down_part)).astype(jnp.bfloat16)
    dmixed = dot(dres_full, full_out, 1, 0).astype(jnp.bfloat16)
    out_grad = dot(dres_full, mixed, 0, 0).astype(jnp.bfloat16)
    dqkv_b = attention.backward(dmixed)
    layer_out, dqkv_b = lax.optimization_barrier((layer_out, dqkv_b))
    dnormed_one = sum_to_owner(dot(dqkv_b, full_qkv, 1, 1))
    qkv_grad = dot(normed_full, dqkv_b, 0, 0).astype(jnp.bfloat16)
    dinput_norm, attn_gain_part = norm_backward(dnormed_one, gain_attn, unit_one, inv_one)
    tokens_grad = (dresidual + dinput_norm).astype(jnp.bfloat16)
    gain_sums = sum_over_seq(jnp.stack([attn_gain_part, mlp_gain_part]))
    gain_grad = padded_to_lanes(gain_sums.T).astype(jnp.bfloat16)

    in_share, qkv_share, down_share, out_share, gain_share = ring_scatter(
        [in_grad, qkv_grad, down_grad, out_grad, gain_grad], devices
    )
    return (
        layer_out[None],
        tokens_grad[None],
        qkv_share.reshape(shard_rows, 3, local_width),
        out_share.T,
        jnp.stack([in_share[:, :local_hidden], in_share[:, wide : wide + local_hidden]], axis=1),
        down_share[:, :local_hidden].T,
        gain_share[:, 0],
        gain_share[:, 1],
    )


HIGH = (((1,), (1,)), ((), ()))
OVER_ROWS = (((0,), (0,)), ((), ()))


def fits_fused(devices, seq_size, own_rows, model_width, local_width, local_hidden):
    rest = local_hidden % LANES
    shard_rows = model_width // devices
    return (
        seq_size == 2
        and devices % 4 == 0
        and devices >= 8
        and own_rows == LANES
        and local_width % (2 * LANES) == 0
        and model_width % (2 * LANES) == 0
        and model_width // HEADS == 2 * HEAD_HALF
        and 3 * rest + 8 <= LANES
        and local_hidden // LANES >= 4
        and local_hidden // LANES % 2 == 0
        and shard_rows % 32 == 0
        and own_rows * 2 * LANES // model_width % 16 == 0
    )


def nt(left, right):
    return lax.dot_general(left, right, HIGH, preferred_element_type=jnp.float32)


def nn(left, right):
    return jnp.dot(left, right, preferred_element_type=jnp.float32)


def tiles(total, width, body):
    def step(index, carry):
        body(index, pl.ds(pl.multiple_of(index * width, width), width))
        return carry

    lax.fori_loop(0, total // width, step, 0)


def fused_kernel(sizes, layout, *refs):
    count, own_rows, width, hidden, rest, scale = sizes
    total_rows = 2 * own_rows
    r = types.SimpleNamespace(**dict(zip(layout, refs)))
    model = r.tokens.shape[1]
    streams = 8
    fulls = [getattr(r, "full%d" % i) for i in range(streams)]
    grads = [getattr(r, "grad%d" % i) for i in range(streams)]
    pairs = [getattr(r, "pair%d" % i) for i in range(streams)]
    ends = [getattr(r, "end%d" % i) for i in range(streams)]
    recvs = [getattr(r, "recv%d" % i) for i in range(streams)]
    rows = model // (2 * count)
    half = rows // 2
    turns = count // 2
    core, place = ring_place(count)
    right, left, partner = neighbours(core, place, count)
    targets = (right, left)
    me = lax.axis_index("dp")
    mine = lax.axis_index("seq")
    other = 1 - mine
    f32, bf16 = jnp.float32, jnp.bfloat16
    my_rows = pl.ds(pl.multiple_of(me * rows, rows), rows)

    def remote(src, dst, send, recv, device):
        return pltpu.make_async_remote_copy(
            src_ref=src,
            dst_ref=dst,
            send_sem=send,
            recv_sem=recv,
            device_id=device,
            device_id_type=MESH,
        )


    def piece(way, distance, stream, whole):
        shift = count - distance if way == 0 else distance
        owner = chip_at((place + shift) % count, count) * 2 + core
        if whole:
            where = pl.ds(pl.multiple_of(owner * rows, rows), rows)
        else:
            where = pl.ds(pl.multiple_of(owner * rows + way * half, half), half)
        return fulls[stream].at[where]

    def hop(way, step, stream):
        ref = piece(way, step, stream, step < turns - 1)
        sems = r.g_send.at[stream], r.g_recv.at[stream, step]
        return remote(ref, ref, *sems, {"dp": targets[way]})

    def both_hops(step, stream):
        ref = fulls[stream].at[pl.ds(0, 2 * rows if step < turns - 1 else 2 * half)]
        return remote(ref, ref, r.g_send.at[stream], r.g_recv.at[stream, step], {"dp": right})

    def share(way, step, stream):
        ref = piece(way, step, stream, step < turns)
        return remote(ref, ref, r.gp_send.at[stream], r.gp_recv.at[stream], {"dp": partner})

    def all_shares(stream):
        ref = fulls[stream].at[pl.ds(0, count * rows)]
        return remote(ref, ref, r.gp_send.at[stream], r.gp_recv.at[stream], {"dp": partner})

    def gather_ops(stream):
        def start():
            for way in range(2):
                hop(way, 0, stream).start()
            share(0, 0, stream).start()

        def middle(step):
            both_hops(step - 1, stream).wait_recv()
            for way in range(2):
                hop(way, step, stream).start()
                share(way, step, stream).start()

        def last():
            both_hops(turns - 1, stream).wait_recv()
            for way in range(2):
                share(way, turns, stream).start()

        steps = [functools.partial(middle, step) for step in range(1, turns)]
        return [start] + steps + [last]

    def gather_arrived(stream):
        end(gathers, stream)
        all_shares(stream).wait_recv()

    def sent_rows(stream):
        return pl.ds(0, 2 * (turns - 1) * rows + 2 * half)

    def gather_drain(stream):
        ref = fulls[stream].at[sent_rows(stream)]
        sems = r.g_send.at[stream], r.g_recv.at[stream, 0]
        remote(ref, ref, *sems, {"dp": right}).wait_send()
        all_shares(stream).wait_send()


    def block(ahead, which):
        owner = chip_at((place + ahead) % count, count) * 2 + which
        return pl.ds(pl.multiple_of(owner * rows, rows), rows)

    def give(ahead, stream):
        return remote(
            grads[stream].at[block(ahead, 1 - core)],
            pairs[stream].at[ahead],
            r.sp_send.at[stream],
            r.sp_recv.at[stream, 0 if ahead == turns else 1],
            {"dp": partner},
        )

    def given(step, stream):
        ref = pairs[stream].at[pl.ds(0, 1 if step == 0 else count - 1)]
        sems = r.sp_send.at[stream], r.sp_recv.at[stream, step]
        return remote(ref, ref, *sems, {"dp": partner})

    def ahead_of(way, step):
        return turns - step if way == 0 else turns + step

    def push(way, step, stream):
        sems = r.s_send.at[stream], r.s_recv.at[stream, step]
        if step == 0:
            src = pairs[stream].at[turns, pl.ds(way * half, half)]
            return remote(src, ends[stream].at[way], *sems, {"dp": targets[way]})
        src = pairs[stream].at[ahead_of(way, step)]
        return remote(src, recvs[stream].at[way, step - 1], *sems, {"dp": targets[way]})

    def both_pushes(step, stream):
        ref = ends[stream] if step == 0 else recvs[stream].at[:, step - 1]
        return remote(ref, ref, r.s_send.at[stream], r.s_recv.at[stream, step], {"dp": right})

    def pair_sum(ahead, stream):
        own = grads[stream][block(ahead, core), :].astype(f32)
        return own + pairs[stream][ahead].astype(f32)

    def scatter_ops(stream, finish):
        def gives():
            order = [turns] + [turns + sign * d for d in range(1, turns) for sign in (-1, 1)] + [0]
            for ahead in order:
                give(ahead, stream).start()

        def start():
            given(0, stream).wait_recv()
            pairs[stream][turns] = pair_sum(turns, stream).astype(bf16)
            for way in range(2):
                push(way, 0, stream).start()

        def middle(step):
            if step == 1:
                given(1, stream).wait_recv()
            both_pushes(step - 1, stream).wait_recv()
            for way in range(2):
                ahead = ahead_of(way, step)
                total = pair_sum(ahead, stream)
                if step == 1:
                    near = ends[stream][way].astype(f32)
                    parts = [total[:half], total[half:]]
                    parts[way] = parts[way] + near
                    total = jnp.concatenate(parts, axis=0)
                else:
                    total = total + recvs[stream][way, step - 2].astype(f32)
                pairs[stream][ahead] = total.astype(bf16)
                push(way, step, stream).start()

        def last():
            both_pushes(turns - 1, stream).wait_recv()
            total = pair_sum(0, stream)
            for way in range(2):
                total = total + recvs[stream][way, turns - 2].astype(f32)
            finish(total)

        steps = [functools.partial(middle, step) for step in range(1, turns)]
        return [gives, start] + steps + [last]

    def scatter_drain(stream):
        ref = fulls[stream].at[sent_rows(stream)]
        sems = r.s_send.at[stream], r.s_recv.at[stream, 0]
        remote(ref, ref, *sems, {"dp": right}).wait_send()
        ref = fulls[stream].at[pl.ds(0, count * rows)]
        sems = r.sp_send.at[stream], r.sp_recv.at[stream, 0]
        remote(ref, ref, *sems, {"dp": partner}).wait_send()


    own = pl.ds(0, own_rows)
    far = pl.ds(own_rows, own_rows)
    exchanged = [
        (r.seg_own, r.seg_other),
        (r.tokens, r.tok_other),
        (r.cot, r.cot_all.at[far]),
        (r.out_send, r.out_recv),
        (r.n2.at[own], r.n2.at[far]),
        (r.down_send, r.down_recv),
        (r.dn2_send, r.dn2_recv),
        (r.dres.at[own], r.dres.at[far]),
        (r.dn1_send, r.dn1_recv),
        (r.gain_part, r.gain_recv),
    ]
    by_lanes, by_rows = (3, 5, 6, 8), (4, 7)
    chunks = model // (2 * LANES)
    chunk_rows = own_rows // chunks

    def swap(index, part=0):
        src, dst = exchanged[index]
        if index in by_lanes:
            lanes = pl.ds(pl.multiple_of(part * 2 * LANES, 2 * LANES), 2 * LANES)
            src, dst = src.at[:, lanes], dst.at[:, lanes]
        elif index in by_rows:
            here = pl.ds(pl.multiple_of(part * chunk_rows, chunk_rows), chunk_rows)
            src, dst = src.at[here], dst.at[here]
        return remote(src, dst, r.y_send.at[index], r.y_recv.at[index], {"seq": other})

    def whole_swap(index):
        src, dst = exchanged[index]
        return remote(src, dst, r.y_send.at[index], r.y_recv.at[index], {"seq": other})

    def arrived(index):
        whole_swap(index).wait_recv()

    def swap_drain(index):
        whole_swap(index).wait_send()


    def normed(values):
        center = values - jnp.mean(values, axis=-1, keepdims=True)
        inv_std = lax.rsqrt(jnp.mean(center * center, axis=-1, keepdims=True) + EPS)
        return center * inv_std, inv_std

    def to_columns(src, dst):
        def body(index, lanes):
            dst[lanes, :] = src[:, lanes].astype(f32).T.astype(bf16)

        tiles(model, LANES, body)

    def partial_sums(terms, own_ref, send_ref, exchange):
        def body(index, lanes):
            total = sum(nt(left[...], right[lanes, :]) for left, right in terms)
            own_ref[:, lanes] = total[:own_rows]
            send_ref[:, lanes] = total[own_rows:].astype(bf16)
            swap(exchange, index).start()

        tiles(model, 2 * LANES, body)

    def weight_grad(columns, right, out):
        size = right.shape[1]

        def body(index, lanes):
            out[:, lanes] = nn(columns[...], right[:, lanes]).astype(bf16)

        whole = size // (2 * LANES) * 2 * LANES
        tiles(whole, 2 * LANES, body)
        if whole < size:
            body(0, pl.ds(whole, size - whole))

    blocks = width // LANES
    hidden_blocks = hidden // LANES
    lane = lax.broadcasted_iota(jnp.int32, (total_rows, LANES), 1)
    low_half = lane % (2 * HEAD_HALF) < HEAD_HALF
    first = lane < 2 * HEAD_HALF

    def setup():
        r.cos[own, :] = r.cos_table[pl.ds(pl.multiple_of(mine * own_rows, own_rows), own_rows), :]
        r.cos[far, :] = r.cos_table[pl.ds(pl.multiple_of(other * own_rows, own_rows), own_rows), :]
        r.sin[own, :] = r.sin_table[pl.ds(pl.multiple_of(mine * own_rows, own_rows), own_rows), :]
        r.sin[far, :] = r.sin_table[pl.ds(pl.multiple_of(other * own_rows, own_rows), own_rows), :]

    def position(dim):
        index = lax.broadcasted_iota(jnp.int32, (total_rows, total_rows), dim)
        return jnp.where(index < own_rows, index + mine * own_rows, index - mine * own_rows)

    def make_bias():
        seg_row = jnp.concatenate([r.seg_own[0:1, :], r.seg_other[0:1, :]], axis=1).astype(f32)
        across = jnp.broadcast_to(seg_row, (total_rows, total_rows))
        allowed = (jnp.abs(position(0) - position(1)) <= HALO) & (across == across.T)
        r.bias[...] = jnp.where(allowed, 0.0, NEG_FILL)

    def expand_special():
        spot = lax.broadcasted_iota(jnp.int32, (2 * LANES, LANES), 1)
        keep = spot < rest

        def body(index, here):
            part = fulls[6][here, :].astype(f32)
            r.gains[:, here] = part.T[3 * rest : 3 * rest + 8]
            r.sp_in[here, :LANES] = jnp.where(keep, part, 0.0).astype(bf16)
            r.sp_in[here, LANES:] = jnp.where(
                keep, pltpu.roll(part, LANES - rest, 1), 0.0
            ).astype(bf16)
            r.sp_down[here, :] = jnp.where(
                keep, pltpu.roll(part, LANES - 2 * rest, 1), 0.0
            ).astype(bf16)

        tiles(model, 2 * LANES, body)

    def attn_gain():
        return r.gains[0:1, :] + r.gains[1:2, :]

    def mlp_gain():
        return r.gains[2:3, :] + r.gains[3:4, :]

    def norm_one():
        for src, place_of in ((r.tokens, 0), (r.tok_other, own_rows)):
            def body(index, here):
                unit_rows, _ = normed(src[here, :].astype(f32))
                at = pl.ds(pl.multiple_of(index * 32 + place_of, 32), 32)
                r.n1[at, :] = (unit_rows * attn_gain()).astype(bf16)

            tiles(own_rows, 32, body)

    def values_of():
        def body(index, lanes):
            r.v[:, lanes] = nn(r.n1[...], fulls[1][:, lanes]).astype(bf16)

        tiles(width, 2 * LANES, body)

    def attend(index, wide, lanes):
        cos_table, sin_table = r.cos[...], r.sin[...]
        proj = nn(r.n1[...], fulls[0][:, wide])
        queries = turn(proj[:, :LANES], cos_table, sin_table, low_half)
        keys = turn(proj[:, LANES:], cos_table, sin_table, low_half).astype(bf16)
        r.qk[:, wide] = jnp.concatenate([queries.astype(bf16), keys], axis=1)
        values = r.v[:, lanes].astype(f32)
        mixed = jnp.zeros((total_rows, LANES), f32)
        for head in range(2):
            here = first if head == 0 else ~first
            scores = nt(jnp.where(here, queries, 0.0).astype(bf16), keys) * scale + r.bias[...]
            top_score = jnp.max(scores, axis=-1, keepdims=True)
            total = jnp.sum(jnp.exp(scores - top_score), axis=-1, keepdims=True)
            probs = jnp.exp(scores - (top_score + jnp.log(total)))
            r.probs[index * 2 + head] = probs
            mixed = mixed + nn(probs.astype(bf16), jnp.where(here, values, 0.0).astype(bf16))
        r.mixed[:, lanes] = mixed.astype(bf16)

    def attend_back(index, wide, lanes):
        cos_table, sin_table = r.cos[...], -r.sin[...]
        both = r.qk[:, wide]
        queries = both[:, :LANES].astype(f32)
        keys = both[:, LANES:].astype(f32)
        values = r.v[:, lanes]
        dmixed = r.dmixed[:, lanes].astype(f32)
        products = dmixed * r.mixed[:, lanes].astype(f32)
        dquery = jnp.zeros((total_rows, LANES), f32)
        dkey = jnp.zeros((total_rows, LANES), f32)
        dvalue = jnp.zeros((total_rows, LANES), f32)
        for head in range(2):
            here = first if head == 0 else ~first
            head_queries = jnp.where(here, queries, 0.0).astype(bf16)
            head_keys = jnp.where(here, keys, 0.0).astype(bf16)
            head_dmixed = jnp.where(here, dmixed, 0.0).astype(bf16)
            delta = jnp.sum(jnp.where(here, products, 0.0), axis=-1, keepdims=True)
            probs = r.probs[index * 2 + head]
            dprobs = nt(head_dmixed, values)
            dscores = (probs * (dprobs - delta) * scale).astype(bf16)
            dvalue = dvalue + lax.dot_general(
                probs.astype(bf16), head_dmixed, OVER_ROWS, preferred_element_type=f32
            )
            dkey = dkey + lax.dot_general(
                dscores, head_queries, OVER_ROWS, preferred_element_type=f32
            )
            dquery = dquery + nn(dscores, head_keys)
        dquery = turn(dquery, cos_table, sin_table, low_half)
        dkey = turn(dkey, cos_table, sin_table, low_half)
        r.dqk[:, wide] = jnp.concatenate([dquery, dkey], axis=1).astype(bf16)
        r.dv[:, lanes] = dvalue.astype(bf16)

    def over_heads(body, start, stop):
        def step(index, carry):
            body(
                index,
                pl.ds(pl.multiple_of(index * 2 * LANES, 2 * LANES), 2 * LANES),
                pl.ds(pl.multiple_of(index * LANES, LANES), LANES),
            )
            return carry

        lax.fori_loop(start, stop, step, 0)

    def norm_two():
        def body(index, here):
            residual = (
                r.tokens[here, :].astype(f32)
                + r.acc[here, :]
                + r.out_recv[here, :].astype(f32)
            )
            r.residual[here, :] = residual
            unit_rows, _ = normed(residual)
            r.n2[here, :] = (unit_rows * mlp_gain()).astype(bf16)
            swap(4, index).start()

        tiles(own_rows, chunk_rows, body)

    def expand_tile(weight, at):
        both = nn(r.n2[...], weight)
        gate, linear = both[:, :LANES], both[:, LANES:]
        erf_part = 0.5 * (1.0 + lax.erf(gate * 0.7071067811865476))
        active = gate * erf_part
        slope = erf_part + gate * jnp.exp(-0.5 * gate * gate) * 0.3989422804014327
        r.mid[:, at] = (active * linear).astype(bf16)
        r.act[:, at] = active
        r.slope[:, at] = linear * slope

    def expand_stream(stream, offset):
        def body(index, lanes):
            at = pl.ds(pl.multiple_of((index + offset) * LANES, LANES), LANES)
            expand_tile(fulls[stream][:, lanes], at)

        tiles(fulls[stream].shape[1], 2 * LANES, body)

    spare = pl.ds(hidden, LANES)

    def dexpand(weight, at, to):
        dmiddle = nn(r.cot_all[...], weight)
        dgate = (dmiddle * r.slope[:, at]).astype(bf16)
        dlinear = (dmiddle * r.act[:, at]).astype(bf16)
        parts = []
        for start in range(0, dmiddle.shape[1], LANES):
            parts += [dgate[:, start : start + LANES], dlinear[:, start : start + LANES]]
        r.dexp[:, to] = jnp.concatenate(parts, axis=1)

    def dexpand_stream(stream, offset):
        def body(index, lanes):
            at = pl.ds(pl.multiple_of(offset * LANES + index * LANES, LANES), LANES)
            to = pl.ds(
                pl.multiple_of(offset * 2 * LANES + index * 2 * LANES, 2 * LANES), 2 * LANES
            )
            dexpand(fulls[stream][:, lanes], at, to)

        tiles(fulls[stream].shape[1], LANES, body)

    split = fulls[3].shape[1]
    mid_parts = [
        r.mid.at[:, pl.ds(0, split // 2)],
        r.mid.at[:, pl.ds(split // 2, hidden - split // 2)],
    ]
    dexp_parts = [
        r.dexp.at[:, pl.ds(0, split)],
        r.dexp.at[:, pl.ds(split, 2 * hidden - split)],
        r.dexp.at[:, pl.ds(2 * hidden, 2 * LANES)],
    ]

    def special_grad():
        spot = lax.broadcasted_iota(jnp.int32, (2 * LANES, LANES), 1)

        def body(index, here):
            both = nn(r.n2_col[here, :], dexp_parts[2][...])
            down = nn(r.cot_col[here, :], r.mid[:, spare])
            value = jnp.where(
                spot < rest,
                both[:, :LANES],
                jnp.where(
                    spot < 2 * rest,
                    pltpu.roll(both[:, LANES:], rest, 1),
                    jnp.where(spot < 3 * rest, pltpu.roll(down, 2 * rest, 1), 0.0),
                ),
            )
            grads[6][here, :] = value.astype(bf16)

        tiles(model, 2 * LANES, body)

    def back_through_norm(grad_rows, gain, values):
        unit_rows, inv_std = normed(values)
        scaled = grad_rows * gain
        inner = (
            scaled
            - jnp.mean(scaled, axis=-1, keepdims=True)
            - unit_rows * jnp.mean(scaled * unit_rows, axis=-1, keepdims=True)
        )
        return inner * inv_std, jnp.sum(grad_rows * unit_rows, axis=0, keepdims=True)

    def norm_two_back():
        r.gain_part[...] = jnp.zeros_like(r.gain_part)

        def body(index, here):
            grad_rows = r.acc[here, :] + r.dn2_recv[here, :].astype(f32)
            part, gain_sum = back_through_norm(grad_rows, mlp_gain(), r.residual[here, :])
            dresidual = r.cot[here, :].astype(f32) + part
            r.dres_own[here, :] = dresidual
            r.dres[here, :] = dresidual.astype(bf16)
            r.gain_part[1:2, :] += gain_sum
            swap(7, index).start()

        tiles(own_rows, chunk_rows, body)

    def norm_one_back():
        def body(index, here):
            grad_rows = r.acc[here, :] + r.dn1_recv[here, :].astype(f32)
            part, gain_sum = back_through_norm(
                grad_rows, attn_gain(), r.tokens[here, :].astype(f32)
            )
            r.tokens_grad[0, here, :] = (r.dres_own[here, :] + part).astype(bf16)
            r.gain_part[0:1, :] += gain_sum

        tiles(own_rows, 32, body)

    def layer_out():
        def body(index, here):
            r.layer_out[0, here, :] = (
                r.residual[here, :]
                + r.down_acc[here, :]
                + r.down_recv[here, :].astype(f32)
            ).astype(bf16)

        tiles(own_rows, 32, body)

    def gain_columns():
        spot = lax.broadcasted_iota(jnp.int32, (LANES, 2 * LANES), 0)

        def body(index, here):
            sums = r.gain_part[:, here] + r.gain_recv[:, here]
            value = jnp.where(
                spot == 3 * rest, sums[0:1], jnp.where(spot == 3 * rest + 1, sums[1:2], 0.0)
            ).T
            old = grads[6][here, :].astype(f32)
            grads[6][here, :] = (old + value).astype(bf16)

        tiles(model, 2 * LANES, body)

    def dmixed_of():
        def body(index, lanes):
            r.dmixed[:, lanes] = nn(r.dres[...], fulls[2][:, lanes]).astype(bf16)

        tiles(width, 2 * LANES, body)


    def pack_keys():
        for at in range(0, width, LANES):
            for which in range(2):
                to = 2 * at + which * LANES
                fulls[0][my_rows, to : to + LANES] = r.raw_qkv[which, :, at : at + LANES]
        fulls[1][my_rows, :] = r.raw_qkv[2]

    def pack_special():
        spot = lax.broadcasted_iota(jnp.int32, (LANES, rows), 0)
        gain_parts = []
        for gain in (r.attn_gain[...], r.mlp_gain[...]):
            spread = gain * 65537.0
            high = spread - (spread - gain)
            gain_parts += [high, gain - high]
        gains = jnp.zeros((LANES, rows), f32)
        for index, part in enumerate(gain_parts):
            gains = jnp.where(spot == 3 * rest + index, part, gains)
        special = gains.T
        if rest:
            parts = [
                r.raw_in[:, 0, hidden:].astype(f32),
                r.raw_in[:, 1, hidden:].astype(f32),
                r.raw_down[:, hidden:].astype(f32),
                jnp.zeros((rows, LANES - 3 * rest), f32),
            ]
            special = special + jnp.concatenate(parts, axis=1)
        fulls[6][my_rows, :] = special.astype(bf16)

    def pack_rest():
        fulls[2][my_rows, :] = r.raw_out[...]
        for at in range(0, hidden, LANES):
            stream, to = (3, 2 * at) if 2 * at < split else (4, 2 * at - split)
            for which in range(2):
                start = to + which * LANES
                fulls[stream][my_rows, start : start + LANES] = r.raw_in[:, which, at : at + LANES]
        fulls[5][my_rows, :] = r.raw_down[:, : split // 2]
        fulls[7][my_rows, :] = r.raw_down[:, split // 2 : hidden]


    def finish_keys(total):
        for at in range(0, width, LANES):
            for which in range(2):
                to = 2 * at + which * LANES
                r.qkv_grad[which, :, at : at + LANES] = total[:, to : to + LANES]

    def finish_values(total):
        r.qkv_grad[2] = total

    def finish_out(total):
        r.out_grad[...] = total

    def finish_special(total):
        turned = total.T
        r.attn_gain_grad[...] = turned[3 * rest : 3 * rest + 1]
        r.mlp_gain_grad[...] = turned[3 * rest + 1 : 3 * rest + 2]
        if rest:
            r.in_grad[:, 0, hidden:] = total[:, :rest]
            r.in_grad[:, 1, hidden:] = total[:, rest : 2 * rest]
            r.down_grad[:, hidden:] = total[:, 2 * rest : 3 * rest]

    def finish_in(start):
        def finish(total):
            for at in range(0, total.shape[1], 2 * LANES):
                to = start + at // 2
                r.in_grad[:, 0, to : to + LANES] = total[:, at : at + LANES]
                r.in_grad[:, 1, to : to + LANES] = total[:, at + LANES : at + 2 * LANES]

        return finish

    def finish_down(start):
        def finish(total):
            r.down_grad[:, start : start + total.shape[1]] = total

        return finish

    gathers = [gather_ops(stream) for stream in range(streams)]
    finishes = [finish_keys, finish_values, finish_out, finish_in(0), finish_in(split // 2)]
    finishes += [finish_down(0), finish_special, finish_down(split // 2)]
    scatters = [scatter_ops(stream, finishes[stream]) for stream in range(streams)]

    def go(ops, *chosen):
        for stream in chosen:
            if ops[stream]:
                ops[stream].pop(0)()

    def end(ops, *chosen):
        while any(ops[stream] for stream in chosen):
            go(ops, *chosen)

    stores = [
        pltpu.make_async_copy(r.layer_out, r.to_layer_out, r.own_sem.at[11]),
        pltpu.make_async_copy(r.tokens_grad, r.to_tokens_grad, r.own_sem.at[12]),
    ]


    barrier = pltpu.get_barrier_semaphore()
    for device in (right, left, partner):
        pl.semaphore_signal(barrier, inc=1, device_id={"dp": device}, device_id_type=MESH)
    pl.semaphore_signal(barrier, inc=1, device_id={"seq": other}, device_id_type=MESH)
    loads = [
        pltpu.make_async_copy(src, dst, r.own_sem.at[index])
        for index, (src, dst) in enumerate(
            [
                (r.in_qkv, r.raw_qkv),
                (r.in_in, r.raw_in),
                (r.in_down, r.raw_down),
                (r.in_attn_gain, r.attn_gain),
                (r.in_mlp_gain, r.mlp_gain),
                (r.in_seg, r.seg),
                (r.in_tokens.at[0], r.tokens),
                (r.in_cot.at[0], r.cot),
                (r.in_out, r.raw_out),
                (r.in_cos, r.cos_table),
                (r.in_sin, r.sin_table),
            ]
        )
    ]
    for load in loads:
        load.start()
    loads[0].wait()
    pack_keys()
    pl.semaphore_wait(barrier, 4)
    go(gathers, 0)
    for load in loads[1:8]:
        load.wait()
    pack_special()
    r.seg_own[...] = jnp.broadcast_to(r.seg[...], r.seg_own.shape)
    for index in range(3):
        swap(index).start()
    loads[8].wait()
    pack_rest()
    r.cot_all[own, :] = r.cot[...]
    go(gathers, 1)
    for load in loads[9:]:
        load.wait()
    setup()
    to_columns(r.cot_all.at[own], r.cot_col.at[:, own])
    go(gathers, 6)
    arrived(0)
    make_bias()
    go(gathers, 2, 0, 1, 6)
    go(gathers, 2, 0, 1, 6)
    go(gathers, 2, 3, 0, 1, 6)
    go(gathers, 2, 5, 3, 0, 1, 6)
    go(gathers, 2)
    arrived(1)
    arrived(2)
    gather_arrived(6)
    expand_special()
    norm_one()
    go(gathers, 5)
    gather_arrived(1)
    values_of()
    go(gathers, 4)
    gather_arrived(0)
    over_heads(attend, blocks * 0 // 4, blocks * 1 // 4)
    over_heads(attend, blocks * 1 // 4, blocks * 2 // 4)
    go(gathers, 3)
    over_heads(attend, blocks * 2 // 4, blocks * 3 // 4)
    over_heads(attend, blocks * 3 // 4, blocks * 4 // 4)
    go(gathers, 5)
    gather_arrived(2)
    partial_sums([(r.mixed, fulls[2])], r.acc, r.out_send, 3)
    to_columns(r.n1, r.n1_col)
    to_columns(r.cot_all.at[far], r.cot_col.at[:, far])
    go(gathers, 4, 3)
    arrived(3)
    norm_two()
    go(gathers, 5, 7, 4, 3)
    go(gathers, 5)
    arrived(4)
    gather_arrived(3)
    expand_stream(3, 0)
    go(gathers, 7)
    weight_grad(r.cot_col, mid_parts[0], grads[5])
    go(scatters, 5)
    to_columns(r.n2, r.n2_col)
    go(scatters, 5)
    go(gathers, 4)
    expand_tile(r.sp_in[...], spare)
    gather_arrived(5)
    dexpand_stream(5, 0)
    go(gathers, 7)
    dexpand(r.sp_down[...], spare, pl.ds(2 * hidden, 2 * LANES))
    go(scatters, 5)
    weight_grad(r.n2_col, dexp_parts[0], grads[3])
    go(gathers, 4)
    go(scatters, 3)
    go(gathers, 7)
    go(scatters, 3)
    gather_arrived(4)
    expand_stream(4, split // (2 * LANES))
    go(gathers, 7)
    go(scatters, 5)
    weight_grad(r.cot_col, mid_parts[1], grads[7])
    go(scatters, 7)
    gather_arrived(7)
    dexpand_stream(7, split // (2 * LANES))
    go(scatters, 7, 3)
    partial_sums(
        [(dexp_parts[0], fulls[3]), (dexp_parts[1], fulls[4]), (dexp_parts[2], r.sp_in)],
        r.acc,
        r.dn2_send,
        6,
    )
    go(scatters, 7, 5)
    weight_grad(r.n2_col, dexp_parts[1], grads[4])
    go(scatters, 4)
    go(scatters, 4, 3, 7)
    arrived(6)
    norm_two_back()
    go(scatters, 5)
    special_grad()
    partial_sums(
        [(mid_parts[0], fulls[5]), (mid_parts[1], fulls[7]), (r.mid.at[:, spare], r.sp_down)],
        r.down_acc,
        r.down_send,
        5,
    )
    go(scatters, 4, 3)
    arrived(7)
    dmixed_of()
    go(scatters, 7)
    over_heads(attend_back, blocks * 0 // 4, blocks * 1 // 4)
    over_heads(attend_back, blocks * 1 // 4, blocks * 2 // 4)
    over_heads(attend_back, blocks * 2 // 4, blocks * 3 // 4)
    go(scatters, 4)
    over_heads(attend_back, blocks * 3 // 4, blocks * 4 // 4)
    partial_sums([(r.dqk, fulls[0]), (r.dv, fulls[1])], r.acc, r.dn1_send, 8)
    go(scatters, 3)
    weight_grad(r.n1_col, r.dv, grads[1])
    go(scatters, 1)
    weight_grad(r.n1_col, r.dqk, grads[0])
    go(scatters, 7, 1, 0)
    to_columns(r.dres, r.dres_col)
    go(scatters, 0)
    weight_grad(r.dres_col, r.mixed, grads[2])
    go(scatters, 2, 4, 1)
    go(scatters, 2)
    arrived(8)
    norm_one_back()
    swap(9).start()
    stores[1].start()
    go(scatters, 0)
    arrived(5)
    layer_out()
    stores[0].start()
    arrived(9)
    gain_columns()
    go(scatters, 6, 4)
    go(scatters, 6, 1, 2)
    go(scatters, 6, 0, 1, 2)
    go(scatters, 6, 0, 1, 2)
    go(scatters, 6, 0, 2)
    go(scatters, 6)
    end(scatters, *range(streams))

    for stream in range(streams):
        gather_drain(stream)
        scatter_drain(stream)
    for index in range(len(exchanged)):
        swap_drain(index)
    for store in stores:
        store.wait()


def fused_call(inputs, devices, widths):
    names, arrays = zip(*inputs.items())
    whole = dict(inputs)
    count = devices // 2
    own_rows, model = whole["in_tokens"].shape[1:]
    total = 2 * own_rows
    _, rows, width = whole["in_qkv"].shape
    local_hidden = whole["in_in"].shape[2]
    rest = local_hidden % LANES
    hidden = local_hidden - rest
    half = rows // 2
    turns = count // 2
    f32, bf16 = jnp.float32, jnp.bfloat16
    streams = len(widths)
    heads = width // (2 * HEAD_HALF)
    outs = dict(
        to_layer_out=((1, own_rows, model), bf16),
        to_tokens_grad=((1, own_rows, model), bf16),
        qkv_grad=((3, rows, width), f32),
        out_grad=((rows, width), f32),
        in_grad=((rows, 2, local_hidden), f32),
        down_grad=((rows, local_hidden), f32),
        attn_gain_grad=((1, rows), f32),
        mlp_gain_grad=((1, rows), f32),
    )
    shapes = dict(
        tokens=((own_rows, model), bf16),
        cot=((own_rows, model), bf16),
        seg=((1, own_rows), jnp.int32),
        attn_gain=((1, rows), f32),
        mlp_gain=((1, rows), f32),
        cos_table=((total, LANES), f32),
        sin_table=((total, LANES), f32),
        seg_own=((8, own_rows), jnp.int32),
        seg_other=((8, own_rows), jnp.int32),
        layer_out=((1, own_rows, model), bf16),
        tokens_grad=((1, own_rows, model), bf16),
        raw_qkv=((3, rows, width), bf16),
        raw_out=((rows, width), bf16),
        raw_in=((rows, 2, local_hidden), bf16),
        raw_down=((rows, local_hidden), bf16),
        tok_other=((own_rows, model), bf16),
        cot_all=((total, model), bf16),
        cot_col=((model, total), bf16),
        n1=((total, model), bf16),
        n1_col=((model, total), bf16),
        gains=((8, model), f32),
        cos=((total, LANES), f32),
        sin=((total, LANES), f32),
        bias=((total, total), f32),
        sp_in=((model, 2 * LANES), bf16),
        sp_down=((model, LANES), bf16),
        v=((total, width), bf16),
        qk=((total, 2 * width), bf16),
        probs=((heads, total, total), f32),
        mixed=((total, width), bf16),
        acc=((own_rows, model), f32),
        down_acc=((own_rows, model), f32),
        out_send=((own_rows, model), bf16),
        out_recv=((own_rows, model), bf16),
        down_send=((own_rows, model), bf16),
        down_recv=((own_rows, model), bf16),
        dn2_send=((own_rows, model), bf16),
        dn2_recv=((own_rows, model), bf16),
        dn1_send=((own_rows, model), bf16),
        dn1_recv=((own_rows, model), bf16),
        residual=((own_rows, model), f32),
        n2=((total, model), bf16),
        n2_col=((model, total), bf16),
        mid=((total, hidden + LANES), bf16),
        act=((total, hidden + LANES), f32),
        slope=((total, hidden + LANES), f32),
        dexp=((total, 2 * hidden + 2 * LANES), bf16),
        dres_own=((own_rows, model), f32),
        dres=((total, model), bf16),
        dres_col=((model, total), bf16),
        dmixed=((total, width), bf16),
        dqk=((total, 2 * width), bf16),
        dv=((total, width), bf16),
        gain_part=((8, model), f32),
        gain_recv=((8, model), f32),
    )
    for i, w in enumerate(widths):
        shapes["full%d" % i] = ((model, w), bf16)
        shapes["grad%d" % i] = ((model, w), bf16)
        shapes["pair%d" % i] = ((count, rows, w), bf16)
        shapes["end%d" % i] = ((2, half, w), bf16)
        shapes["recv%d" % i] = ((2, turns - 1, rows, w), bf16)
    scratch = {name: pltpu.VMEM(shape, dtype) for name, (shape, dtype) in shapes.items()}
    semaphores = dict(
        own_sem=(13,),
        g_send=(streams,),
        g_recv=(streams, turns),
        gp_send=(streams,),
        gp_recv=(streams,),
        s_send=(streams,),
        s_recv=(streams, turns),
        sp_send=(streams,),
        sp_recv=(streams, 2),
        y_send=(10,),
        y_recv=(10,),
    )
    for name, shape in semaphores.items():
        scratch[name] = pltpu.SemaphoreType.DMA(shape)
    vmem = pl.BlockSpec(memory_space=pltpu.VMEM)
    anywhere = pl.BlockSpec(memory_space=pl.ANY)
    sizes = (count, own_rows, width, hidden, rest, 1.0 / math.sqrt(2 * HEAD_HALF))
    layout = list(names) + list(outs) + list(scratch)
    return pl.pallas_call(
        functools.partial(fused_kernel, sizes, layout),
        out_shape=[jax.ShapeDtypeStruct(shape, dtype) for shape, dtype in outs.values()],
        in_specs=[anywhere] * len(names),
        out_specs=[anywhere] * 2 + [vmem] * (len(outs) - 2),
        scratch_shapes=list(scratch.values()),
        compiler_params=pltpu.CompilerParams(
            collective_id=2, has_side_effects=True, vmem_limit_bytes=FUSED_LIMIT
        ),
        name="fused_layer",
    )(*arrays)


def copy_kernel(count, *refs):
    sources, targets, buffers = refs[:count], refs[count : 2 * count], refs[2 * count : 3 * count]
    sems = refs[3 * count]
    ins = [
        pltpu.make_async_copy(sources[index], buffers[index], sems.at[0, index])
        for index in range(count)
    ]
    outs = [
        pltpu.make_async_copy(buffers[index], targets[index], sems.at[1, index])
        for index in range(count)
    ]
    for copy in ins:
        copy.start()
    for index in range(count):
        ins[index].wait()
        outs[index].start()
    for copy in outs:
        copy.wait()


def finish_call(arrays):
    anywhere = pl.BlockSpec(memory_space=pl.ANY)
    count = len(arrays)
    return pl.pallas_call(
        functools.partial(copy_kernel, count),
        out_shape=[jax.ShapeDtypeStruct(array.shape, array.dtype) for array in arrays],
        in_specs=[anywhere] * count,
        out_specs=[anywhere] * count,
        scratch_shapes=[pltpu.VMEM(array.shape, array.dtype) for array in arrays]
        + [pltpu.SemaphoreType.DMA((2, count))],
        name="finish",
    )(*arrays)


FUSED_LIMIT = 63 * 1024 * 1024


def position_tables(total, head_size):
    half_size = head_size // 2
    freqs = THETA ** (-(2.0 / head_size) * np.arange(half_size))
    angles = np.arange(total)[:, None] * freqs[None, :]
    cos_table = np.cos(angles).astype(np.float32)
    sin_table = np.sin(angles).astype(np.float32)
    return (
        jnp.asarray(np.concatenate([cos_table] * 4, axis=1)),
        jnp.asarray(np.concatenate([-sin_table, sin_table] * 2, axis=1)),
    )


def fused_device(
    devices,
    tokens,
    segments,
    cotangent,
    qkv_weight,
    out_weight,
    in_weight,
    down_weight,
    attn_gain,
    mlp_gain,
):
    own_rows = tokens.shape[1]
    width = qkv_weight.shape[2]
    blocks = in_weight.shape[2] // LANES
    first = blocks // 2 * 2 * LANES
    second = 2 * blocks * LANES - first
    widths = [2 * width, width, width, first, second, first // 2, LANES, second // 2]
    cos_table, sin_table = position_tables(2 * own_rows, 2 * HEAD_HALF)
    inputs = dict(
        in_qkv=jnp.transpose(qkv_weight, (1, 0, 2)),
        in_out=out_weight.T,
        in_in=in_weight,
        in_down=down_weight.T,
        in_tokens=tokens,
        in_cot=cotangent,
        in_seg=segments,
        in_attn_gain=attn_gain[None],
        in_mlp_gain=mlp_gain[None],
        in_cos=cos_table,
        in_sin=sin_table,
    )
    results = finish_call(fused_call(inputs, devices, widths))
    layer_out, tokens_grad, qkv, out, in_grad, down, attn_grad, mlp_grad = results
    return (
        layer_out,
        tokens_grad,
        jnp.transpose(qkv, (1, 0, 2)),
        out.T,
        in_grad,
        down.T,
        attn_grad[0],
        mlp_grad[0],
    )


def per_device(
    devices,
    seq_size,
    tokens,
    segments,
    cotangent,
    qkv_weight,
    out_weight,
    in_weight,
    down_weight,
    attn_gain,
    mlp_gain,
):
    args = (
        tokens,
        segments,
        cotangent,
        qkv_weight,
        out_weight,
        in_weight,
        down_weight,
        attn_gain,
        mlp_gain,
    )
    own_rows, model = tokens.shape[1:]
    sizes = (own_rows, model, qkv_weight.shape[2], in_weight.shape[2])
    if fits_fused(devices, seq_size, *sizes) and tokens.shape[0] == 1:
        return fused_device(devices, *args)
    return general_device(devices, seq_size, *args)


def solution(mesh):
    return jax.shard_map(
        functools.partial(per_device, mesh.shape["dp"], mesh.shape["seq"]),
        mesh=mesh,
        in_specs=(
            P("dp", "seq", None),
            P("dp", "seq"),
            P("dp", "seq", None),
            P("dp", None, "seq"),
            P("seq", "dp"),
            P("dp", None, "seq"),
            P("seq", "dp"),
            P("dp"),
            P("dp"),
        ),
        out_specs=(
            P("dp", "seq", None),
            P("dp", "seq", None),
            P("dp", None, "seq"),
            P("seq", "dp"),
            P("dp", None, "seq"),
            P("seq", "dp"),
            P("dp"),
            P("dp"),
        ),
        check_vma=False,
    )
```

```python
import functools
import math
import types

import jax
import jax.numpy as jnp
import numpy as np
from jax import lax
from jax.experimental import pallas as pl
from jax.experimental.pallas import tpu as pltpu
from jax.sharding import PartitionSpec as P

HEADS = 16
HALO = 64


EPS = 1e-05
THETA = 10000.0
NEG_FILL = -1e30


def norm_forward(values, gain):
    center = values - jnp.mean(values, axis=-1, keepdims=True)
    inv_std = lax.rsqrt(jnp.mean(center * center, axis=-1, keepdims=True) + EPS)
    unit_rows = center * inv_std
    return (unit_rows * gain, unit_rows, inv_std)


def norm_backward(grad_rows, gain, unit_rows, inv_std):
    scaled = grad_rows * gain
    inner = (
        scaled
        - jnp.mean(scaled, axis=-1, keepdims=True)
        - unit_rows * jnp.mean(scaled * unit_rows, axis=-1, keepdims=True)
    )
    return (inner * inv_std, jnp.sum(grad_rows * unit_rows, axis=0))


def gelu_value(inputs):
    return 0.5 * inputs * (1.0 + lax.erf(inputs * 0.7071067811865476))


def gelu_slope(inputs):
    return (
        0.5 * (1.0 + lax.erf(inputs * 0.7071067811865476))
        + inputs * jnp.exp(-0.5 * inputs * inputs) * 0.3989422804014327
    )


def rotary_tables(positions, head_size):
    half_size = head_size // 2
    freqs = jnp.power(THETA, -(2.0 / head_size) * jnp.arange(half_size, dtype=jnp.float32))
    angles = positions.astype(jnp.float32)[:, None] * freqs[None, :]
    return (jnp.cos(angles)[:, None, :], jnp.sin(angles)[:, None, :])


def rotate(values, cos_table, sin_table):
    half_size = values.shape[-1] // 2
    lower_half = values[..., :half_size]
    upper_half = values[..., half_size:]
    return jnp.concatenate(
        [
            lower_half * cos_table - upper_half * sin_table,
            upper_half * cos_table + lower_half * sin_table,
        ],
        axis=-1,
    )


def unrotate(grads, cos_table, sin_table):
    half_size = grads.shape[-1] // 2
    lower_half = grads[..., :half_size]
    upper_half = grads[..., half_size:]
    return jnp.concatenate(
        [
            lower_half * cos_table + upper_half * sin_table,
            upper_half * cos_table - lower_half * sin_table,
        ],
        axis=-1,
    )


def window_mask(query_pos, key_pos, query_seg, key_seg, halo_width, total_len):
    near = jnp.abs(query_pos[:, None] - key_pos[None, :]) <= halo_width
    inside = (key_pos >= 0) & (key_pos < total_len)
    return near & inside[None, :] & (query_seg[:, None] == key_seg[None, :])


def block_scores(queries, key_slab, allowed, scale):
    scores = (
        jnp.einsum("qhd,khd->hqk", queries, key_slab, preferred_element_type=jnp.float32) * scale
    )
    return jnp.where(allowed[None], scores, NEG_FILL)


def attend_block(queries, key_slab, value_slab, allowed, scale):
    scores = block_scores(queries, key_slab, allowed, scale)
    top_score = jnp.max(scores, axis=-1, keepdims=True)
    total = jnp.sum(jnp.exp(scores - top_score), axis=-1, keepdims=True)
    logsum = top_score + jnp.log(total)
    probs = jnp.exp(scores - logsum).astype(jnp.bfloat16)
    mixed = jnp.einsum("hqk,khd->qhd", probs, value_slab, preferred_element_type=jnp.float32)
    return (mixed, logsum[..., 0])


def attend_back(queries, key_slab, value_slab, allowed, scale, logsum, mixed_b, dmixed_b):
    scores = block_scores(queries, key_slab, allowed, scale)
    probs = jnp.exp(scores - logsum[..., None])
    probs_b = probs.astype(jnp.bfloat16)
    dvalues = jnp.einsum("hqk,qhd->khd", probs_b, dmixed_b, preferred_element_type=jnp.float32)
    dprobs = jnp.einsum("qhd,khd->hqk", dmixed_b, value_slab, preferred_element_type=jnp.float32)
    delta = jnp.transpose(
        jnp.sum(dmixed_b.astype(jnp.float32) * mixed_b.astype(jnp.float32), axis=-1)
    )
    dscores = (probs * (dprobs - delta[..., None]) * scale).astype(jnp.bfloat16)
    dqueries = jnp.einsum("hqk,khd->qhd", dscores, key_slab, preferred_element_type=jnp.float32)
    dkeys = jnp.einsum("hqk,qhd->khd", dscores, queries, preferred_element_type=jnp.float32)
    return (dqueries, dkeys, dvalues)


MESH = pl.DeviceIdType.MESH
VMEM_LIMIT = 60 * 1024 * 1024
LANES = 128


def ring_place(count):
    me = lax.axis_index("dp")
    core = me % 2
    chip = me // 2
    row, column = chip // 2, chip % 2
    place = (1 - column) * row + column * (count - 1 - row)
    return (core, place)


def chip_at(place, count):
    side = place // (count // 2)
    return (1 - side) * (2 * place) + side * (2 * (count - 1 - place) + 1)


def neighbours(core, place, count):
    right = chip_at((place + 1) % count, count) * 2 + core
    left = chip_at((place + count - 1) % count, count) * 2 + core
    return (right, left, lax.axis_index("dp") + 1 - 2 * core)


def greet(devices):
    barrier = pltpu.get_barrier_semaphore()
    for device in devices:
        pl.semaphore_signal(barrier, inc=1, device_id={"dp": device}, device_id_type=MESH)
    pl.semaphore_wait(barrier, len(devices))


def gather_kernel(count, streams, *refs):
    shards = refs[:streams]
    fulls = refs[streams : 2 * streams]
    own_sem, send_sem, recv_sem, pair_send, pair_recv = refs[2 * streams :]
    rows = shards[0].shape[0]
    half = rows // 2
    core, place = ring_place(count)
    right, left, partner = neighbours(core, place, count)
    targets = (right, left)
    lanes = [(way, stream) for stream in range(streams) for way in range(2)]

    def piece(way, step, stream):
        shift = count - step if way == 0 else step
        owner = chip_at((place + shift) % count, count) * 2 + core
        start = pl.multiple_of(owner * rows + way * half, half)
        return fulls[stream].at[pl.ds(start, half)]

    def hop(way, step, stream):
        ref = piece(way, step, stream)
        return pltpu.make_async_remote_copy(
            src_ref=ref,
            dst_ref=ref,
            send_sem=send_sem.at[stream, way, step],
            recv_sem=recv_sem.at[stream, way, step],
            device_id={"dp": targets[way]},
            device_id_type=MESH,
        )

    def share(way, step, stream):
        ref = piece(way, step, stream)
        return pltpu.make_async_remote_copy(
            src_ref=ref,
            dst_ref=ref,
            send_sem=pair_send.at[stream, way, step],
            recv_sem=pair_recv.at[stream, way, step],
            device_id={"dp": partner},
            device_id_type=MESH,
        )

    me = lax.axis_index("dp")
    owns = [
        pltpu.make_async_copy(
            shards[stream],
            fulls[stream].at[pl.ds(pl.multiple_of(me * rows, rows), rows)],
            own_sem.at[stream],
        )
        for stream in range(streams)
    ]
    for own in owns:
        own.start()
    greet((right, left, partner))
    for own in owns:
        own.wait()
    for way, stream in lanes:
        hop(way, 0, stream).start()
        share(way, 0, stream).start()

    def step_body(step, carry):
        for way, stream in lanes:
            hop(way, step - 1, stream).wait_recv()
            hop(way, step, stream).start()
            share(way, step, stream).start()
        return carry

    lax.fori_loop(1, count - 1, step_body, 0)
    for way, stream in lanes:
        hop(way, count - 2, stream).wait_recv()
        share(way, count - 1, stream).start()

    def drain_hops(step, carry):
        for way, stream in lanes:
            hop(way, step, stream).wait_send()
        return carry

    def drain_shares(step, carry):
        for way, stream in lanes:
            share(way, step, stream).wait_send()
            share(way, step, stream).wait_recv()
        return carry

    lax.fori_loop(0, count - 1, drain_hops, 0)
    lax.fori_loop(0, count, drain_shares, 0)


def ring_gather(shards, devices):
    count = devices // 2
    streams = len(shards)
    return pl.pallas_call(
        functools.partial(gather_kernel, count, streams),
        out_shape=[
            jax.ShapeDtypeStruct((devices * shard.shape[0], shard.shape[1]), shard.dtype)
            for shard in shards
        ],
        in_specs=[pl.BlockSpec(memory_space=pltpu.VMEM)] * streams,
        out_specs=[pl.BlockSpec(memory_space=pl.ANY)] * streams,
        scratch_shapes=[pltpu.SemaphoreType.DMA((streams,))]
        + [pltpu.SemaphoreType.DMA((streams, 2, count - 1))] * 2
        + [pltpu.SemaphoreType.DMA((streams, 2, count))] * 2,
        cost_estimate=pl.CostEstimate(
            flops=0, bytes_accessed=128 * 1024 * 1024, transcendentals=0
        ),
        compiler_params=pltpu.CompilerParams(
            collective_id=0, has_side_effects=True, vmem_limit_bytes=VMEM_LIMIT
        ),
        name="ring_gather",
    )(*shards)


def scatter_kernel(count, streams, *refs):
    grads = refs[:streams]
    outs = refs[streams : 2 * streams]
    pairs = refs[2 * streams : 3 * streams]
    sends = refs[3 * streams : 4 * streams]
    recvs = refs[4 * streams : 5 * streams]
    send_sem, recv_sem, pair_send, pair_recv = refs[5 * streams :]
    rows = outs[0].shape[0]
    half = rows // 2
    core, place = ring_place(count)
    right, left, partner = neighbours(core, place, count)
    targets = (right, left)

    def block(way, step, which):
        shift = 2 * count - 1 - step if way == 0 else 1 + step
        owner = chip_at((place + shift) % count, count) * 2 + which
        return pl.ds(pl.multiple_of(owner * rows + way * half, half), half)

    def share(way, step, stream):
        return pltpu.make_async_remote_copy(
            src_ref=grads[stream].at[block(way, step, 1 - core)],
            dst_ref=pairs[stream].at[way, step],
            send_sem=pair_send.at[stream, way, step],
            recv_sem=pair_recv.at[stream, way, step],
            device_id={"dp": partner},
            device_id_type=MESH,
        )

    def hop(way, step, stream):
        return pltpu.make_async_remote_copy(
            src_ref=sends[stream].at[way, step],
            dst_ref=recvs[stream].at[way, step],
            send_sem=send_sem.at[stream, way, step],
            recv_sem=recv_sem.at[stream, way, step],
            device_id={"dp": targets[way]},
            device_id_type=MESH,
        )

    def pair_sum(way, step, stream):
        share(way, step, stream).wait_recv()
        own = grads[stream][block(way, step, core), :].astype(jnp.float32)
        return own + pairs[stream][way, step].astype(jnp.float32)

    greet((right, left, partner))

    def start_shares(step, carry):
        for stream in range(streams):
            for way in range(2):
                share(way, step, stream).start()
        return carry

    lax.fori_loop(0, count, start_shares, 0)
    for stream in range(streams):
        for way in range(2):
            sends[stream][way, 0] = pair_sum(way, 0, stream).astype(jnp.bfloat16)
            hop(way, 0, stream).start()

    def step_body(step, carry):
        for stream in range(streams):
            for way in range(2):
                total = pair_sum(way, step, stream)
                hop(way, step - 1, stream).wait_recv()
                total = total + recvs[stream][way, step - 1].astype(jnp.float32)
                sends[stream][way, step] = total.astype(jnp.bfloat16)
                hop(way, step, stream).start()
        return carry

    lax.fori_loop(1, count - 1, step_body, 0)
    for stream in range(streams):
        for way in range(2):
            total = pair_sum(way, count - 1, stream)
            hop(way, count - 2, stream).wait_recv()
            total = total + recvs[stream][way, count - 2].astype(jnp.float32)
            outs[stream][way * half : (way + 1) * half, :] = total

    def drain_hops(step, carry):
        for stream in range(streams):
            for way in range(2):
                hop(way, step, stream).wait_send()
        return carry

    def drain_shares(step, carry):
        for stream in range(streams):
            for way in range(2):
                share(way, step, stream).wait_send()
        return carry

    lax.fori_loop(0, count - 1, drain_hops, 0)
    lax.fori_loop(0, count, drain_shares, 0)


def ring_scatter(grads, devices):
    count = devices // 2
    streams = len(grads)
    rows = grads[0].shape[0] // devices
    half = rows // 2
    widths = [grad.shape[1] for grad in grads]
    vmem = pl.BlockSpec(memory_space=pltpu.VMEM)
    return pl.pallas_call(
        functools.partial(scatter_kernel, count, streams),
        out_shape=[jax.ShapeDtypeStruct((rows, width), jnp.float32) for width in widths],
        in_specs=[vmem] * streams,
        out_specs=[vmem] * streams,
        scratch_shapes=[pltpu.VMEM((2, count, half, width), jnp.bfloat16) for width in widths]
        + [pltpu.VMEM((2, count - 1, half, width), jnp.bfloat16) for width in widths] * 2
        + [pltpu.SemaphoreType.DMA((streams, 2, count - 1))] * 2
        + [pltpu.SemaphoreType.DMA((streams, 2, count))] * 2,
        compiler_params=pltpu.CompilerParams(
            collective_id=1, has_side_effects=True, vmem_limit_bytes=40 * 1024 * 1024
        ),
        name="ring_scatter",
    )(*grads)


def turn(values, cos_table, sin_table, low_half):
    half = HEAD_HALF
    swapped = jnp.where(
        low_half, pltpu.roll(values, LANES - half, 1), pltpu.roll(values, half, 1)
    )
    return values * cos_table + swapped * sin_table


HEAD_HALF = 32


def lane_masks(rows):
    lane = lax.broadcasted_iota(jnp.int32, (rows, LANES), 1)
    return (lane % (2 * HEAD_HALF) < HEAD_HALF, lane < 2 * HEAD_HALF)


def allowed_pairs(pos_col, pos_row, seg_col, seg_row):
    near = jnp.abs(pos_col[...] - pos_row[...]) <= HALO
    return near & (seg_col[...] == seg_row[...])


def head_probs(queries, keys, allowed, scale):
    scores = (
        lax.dot_general(
            queries, keys, (((1,), (1,)), ((), ())), preferred_element_type=jnp.float32
        )
        * scale
    )
    scores = jnp.where(allowed, scores, NEG_FILL)
    top_score = jnp.max(scores, axis=-1, keepdims=True)
    total = jnp.sum(jnp.exp(scores - top_score), axis=-1, keepdims=True)
    return jnp.exp(scores - (top_score + jnp.log(total)))


def attend_kernel(
    scale, width, proj, cos_ref, sin_ref, pos_col, pos_row, seg_col, seg_row, qkv_out, mixed_out
):
    rows = proj.shape[0]
    low_half, first = lane_masks(rows)
    cos_table, sin_table = cos_ref[...], sin_ref[...]
    allowed = allowed_pairs(pos_col, pos_row, seg_col, seg_row)
    for start in range(0, width, LANES):
        queries = turn(proj[:, start : start + LANES], cos_table, sin_table, low_half)
        keys = turn(
            proj[:, width + start : width + start + LANES], cos_table, sin_table, low_half
        ).astype(jnp.bfloat16)
        values = proj[:, 2 * width + start : 2 * width + start + LANES]
        qkv_out[:, start : start + LANES] = queries.astype(jnp.bfloat16)
        qkv_out[:, width + start : width + start + LANES] = keys
        qkv_out[:, 2 * width + start : 2 * width + start + LANES] = values.astype(jnp.bfloat16)
        mixed = jnp.zeros((rows, LANES), jnp.float32)
        for head in range(2):
            mine = first if head == 0 else ~first
            probs = head_probs(
                jnp.where(mine, queries, 0.0).astype(jnp.bfloat16), keys, allowed, scale
            ).astype(jnp.bfloat16)
            mixed = mixed + jnp.dot(
                probs,
                jnp.where(mine, values, 0.0).astype(jnp.bfloat16),
                preferred_element_type=jnp.float32,
            )
        mixed_out[:, start : start + LANES] = mixed.astype(jnp.bfloat16)


def attend_back_kernel(
    scale,
    width,
    qkv,
    mixed_ref,
    dmixed_ref,
    cos_ref,
    sin_ref,
    pos_col,
    pos_row,
    seg_col,
    seg_row,
    dqkv_out,
):
    rows = qkv.shape[0]
    low_half, first = lane_masks(rows)
    cos_table, sin_table = cos_ref[...], -sin_ref[...]
    allowed = allowed_pairs(pos_col, pos_row, seg_col, seg_row)
    over_rows = (((0,), (0,)), ((), ()))
    over_lanes = (((1,), (1,)), ((), ()))
    for start in range(0, width, LANES):
        queries = qkv[:, start : start + LANES].astype(jnp.float32)
        keys = qkv[:, width + start : width + start + LANES]
        keys32 = keys.astype(jnp.float32)
        values = qkv[:, 2 * width + start : 2 * width + start + LANES]
        dmixed = dmixed_ref[:, start : start + LANES].astype(jnp.float32)
        products = dmixed * mixed_ref[:, start : start + LANES].astype(jnp.float32)
        dquery = jnp.zeros((rows, LANES), jnp.float32)
        dkey = jnp.zeros((rows, LANES), jnp.float32)
        dvalue = jnp.zeros((rows, LANES), jnp.float32)
        for head in range(2):
            mine = first if head == 0 else ~first
            head_queries = jnp.where(mine, queries, 0.0).astype(jnp.bfloat16)
            head_keys = jnp.where(mine, keys32, 0.0).astype(jnp.bfloat16)
            head_dmixed = jnp.where(mine, dmixed, 0.0).astype(jnp.bfloat16)
            delta = jnp.sum(jnp.where(mine, products, 0.0), axis=-1, keepdims=True)
            probs = head_probs(head_queries, keys, allowed, scale)
            dprobs = lax.dot_general(
                head_dmixed, values, over_lanes, preferred_element_type=jnp.float32
            )
            dscores = (probs * (dprobs - delta) * scale).astype(jnp.bfloat16)
            dvalue = dvalue + lax.dot_general(
                probs.astype(jnp.bfloat16),
                head_dmixed,
                over_rows,
                preferred_element_type=jnp.float32,
            )
            dkey = dkey + lax.dot_general(
                dscores, head_queries, over_rows, preferred_element_type=jnp.float32
            )
            dquery = dquery + jnp.dot(dscores, head_keys, preferred_element_type=jnp.float32)
        dquery = turn(dquery, cos_table, sin_table, low_half)
        dkey = turn(dkey, cos_table, sin_table, low_half)
        dqkv_out[:, start : start + LANES] = dquery.astype(jnp.bfloat16)
        dqkv_out[:, width + start : width + start + LANES] = dkey.astype(jnp.bfloat16)
        dqkv_out[:, 2 * width + start : 2 * width + start + LANES] = dvalue.astype(jnp.bfloat16)


def local_call(kernel, name, out_shape, operands, flops):
    vmem = pl.BlockSpec(memory_space=pltpu.VMEM)
    single = not isinstance(out_shape, list)
    return pl.pallas_call(
        kernel,
        out_shape=out_shape,
        in_specs=[vmem] * len(operands),
        out_specs=vmem if single else [vmem] * len(out_shape),
        cost_estimate=pl.CostEstimate(
            flops=flops, bytes_accessed=4 * 1024 * 1024, transcendentals=flops // 256
        ),
        compiler_params=pltpu.CompilerParams(vmem_limit_bytes=32 * 1024 * 1024),
        name=name,
    )(*operands)


class PairedAttention:
    def __init__(self, positions, segments, head_size, width):
        rows = positions.shape[0]
        cos_table, sin_table = rotary_tables(positions, head_size)
        cos_table, sin_table = cos_table[:, 0, :], sin_table[:, 0, :]
        self.width = width
        self.scale = 1.0 / math.sqrt(head_size)
        self.flops = 2 * rows * rows * LANES * (width // head_size)
        self.shared = (
            jnp.concatenate([cos_table] * 4, axis=1),
            jnp.concatenate([-sin_table, sin_table] * 2, axis=1),
            positions[:, None],
            positions[None, :],
            segments[:, None],
            segments[None, :],
        )

    def forward(self, projected):
        rows = projected.shape[0]
        self.qkv, self.mixed = local_call(
            functools.partial(attend_kernel, self.scale, self.width),
            "attend",
            [
                jax.ShapeDtypeStruct((rows, 3 * self.width), jnp.bfloat16),
                jax.ShapeDtypeStruct((rows, self.width), jnp.bfloat16),
            ],
            (projected,) + self.shared,
            2 * self.flops,
        )
        return self.mixed

    def backward(self, dmixed):
        rows = dmixed.shape[0]
        return local_call(
            functools.partial(attend_back_kernel, self.scale, self.width),
            "attend_back",
            jax.ShapeDtypeStruct((rows, 3 * self.width), jnp.bfloat16),
            (self.qkv, self.mixed, dmixed) + self.shared,
            5 * self.flops,
        )


class BlockAttention:
    def __init__(self, positions, segments, head_size, width):
        self.total_len = positions.shape[0]
        self.segments = segments
        self.head_size = head_size
        self.width = width
        self.scale = 1.0 / math.sqrt(head_size)
        self.cos_table, self.sin_table = rotary_tables(positions, head_size)

    def heads(self, values):
        return values.reshape(self.total_len, self.width // self.head_size, self.head_size)

    def forward(self, projected):
        width, total_len = self.width, self.total_len
        self.block_rows = min(total_len, 512)
        self.slab_rows = self.block_rows + 2 * HALO
        tables = (self.cos_table, self.sin_table)
        self.queries = rotate(self.heads(projected[:, :width]), *tables).astype(jnp.bfloat16)
        keys = rotate(self.heads(projected[:, width : 2 * width]), *tables).astype(jnp.bfloat16)
        values = self.heads(projected[:, 2 * width :]).astype(jnp.bfloat16)
        pad_spec = ((HALO, HALO), (0, 0), (0, 0))
        self.key_pad = jnp.pad(keys, pad_spec)
        self.value_pad = jnp.pad(values, pad_spec)
        seg_pad = jnp.pad(self.segments, (HALO, HALO), constant_values=-1)
        mixed_parts = []
        self.logsums = []
        self.masks = []
        for start in range(0, total_len, self.block_rows):
            own = slice(start, start + self.block_rows)
            slab = slice(start, start + self.slab_rows)
            allowed = window_mask(
                start + jnp.arange(self.block_rows, dtype=jnp.int32),
                start - HALO + jnp.arange(self.slab_rows, dtype=jnp.int32),
                self.segments[own],
                seg_pad[slab],
                HALO,
                total_len,
            )
            mixed, logsum = attend_block(
                self.queries[own], self.key_pad[slab], self.value_pad[slab], allowed, self.scale
            )
            self.masks.append(allowed)
            self.logsums.append(logsum)
            mixed_parts.append(mixed)
        self.mixed = jnp.concatenate(mixed_parts, axis=0).astype(jnp.bfloat16)
        return self.mixed.reshape(total_len, width)

    def backward(self, dmixed):
        total_len = self.total_len
        dmixed = self.heads(dmixed)
        padded = (total_len + 2 * HALO,) + dmixed.shape[1:]
        dkey_pad = jnp.zeros(padded, jnp.float32)
        dvalue_pad = jnp.zeros(padded, jnp.float32)
        dquery_parts = []
        for index, start in enumerate(range(0, total_len, self.block_rows)):
            own = slice(start, start + self.block_rows)
            slab = slice(start, start + self.slab_rows)
            dqueries, dkeys, dvalues = attend_back(
                self.queries[own],
                self.key_pad[slab],
                self.value_pad[slab],
                self.masks[index],
                self.scale,
                self.logsums[index],
                self.mixed[own],
                dmixed[own],
            )
            dquery_parts.append(dqueries)
            dkey_pad = dkey_pad.at[slab].add(dkeys)
            dvalue_pad = dvalue_pad.at[slab].add(dvalues)
        inner = slice(HALO, HALO + total_len)
        tables = (self.cos_table, self.sin_table)
        parts = [
            unrotate(jnp.concatenate(dquery_parts, axis=0), *tables),
            unrotate(dkey_pad[inner], *tables),
            dvalue_pad[inner],
        ]
        return jnp.concatenate(
            [part.reshape(total_len, self.width) for part in parts], axis=1
        ).astype(jnp.bfloat16)


def dot(left, right, left_dim, right_dim):
    return lax.dot_general(
        left,
        right,
        (((left_dim,), (right_dim,)), ((), ())),
        preferred_element_type=jnp.float32,
    )


def padded_to_lanes(values):
    return jnp.pad(values, ((0, 0), (0, -values.shape[1] % LANES)))


def high_and_low(gain):
    high = gain.astype(jnp.bfloat16)
    return [high[:, None], (gain - high.astype(jnp.float32)).astype(jnp.bfloat16)[:, None]]


def general_device(
    devices,
    seq_size,
    tokens,
    segments,
    cotangent,
    qkv_weight,
    out_weight,
    in_weight,
    down_weight,
    attn_gain,
    mlp_gain,
):
    layer_in = tokens[0]
    seg_local = segments[0]
    cot_local = cotangent[0]
    own_rows, model_width = layer_in.shape
    head_size = model_width // HEADS
    local_width = qkv_weight.shape[2]
    local_hidden = in_weight.shape[2]
    shard_rows = qkv_weight.shape[0]
    total_len = own_rows * seq_size
    paired = (
        seq_size == 2
        and total_len <= 512
        and local_width % LANES == 0
        and head_size == 2 * HEAD_HALF
    )
    swap = [(0, 1), (1, 0)]

    def rows_of_all(values):
        if paired:
            return jnp.concatenate([values, lax.ppermute(values, "seq", swap)], axis=0)
        return lax.all_gather(values, "seq", axis=0, tiled=True)

    def sum_to_owner(partial):
        if paired:
            other = lax.ppermute(partial[own_rows:].astype(jnp.bfloat16), "seq", swap)
            return partial[:own_rows] + other.astype(jnp.float32)
        return lax.psum_scatter(
            partial.astype(jnp.bfloat16), "seq", scatter_dimension=0, tiled=True
        ).astype(jnp.float32)

    def sum_over_seq(part):
        if paired:
            return part + lax.ppermute(part, "seq", swap)
        return lax.psum(part, "seq")

    first_pack = jnp.concatenate(
        [qkv_weight.reshape(shard_rows, 3 * local_width), out_weight.T], axis=1
    )
    wide = (local_hidden + 4 + LANES - 1) // LANES * LANES
    spare = jnp.zeros((shard_rows, wide - local_hidden), jnp.bfloat16)
    second_pack = jnp.concatenate(
        [in_weight[:, 0, :], spare, in_weight[:, 1, :], spare, down_weight.T]
        + high_and_low(attn_gain)
        + high_and_low(mlp_gain)
        + [spare[:, 4:]],
        axis=1,
    )
    first_full, second_full = ring_gather([first_pack, second_pack], devices)
    full_qkv = first_full[:, : 3 * local_width]
    full_out = first_full[:, 3 * local_width : 4 * local_width]
    gains_at = 2 * wide + local_hidden
    gains = second_full[:, gains_at : gains_at + 4].astype(jnp.float32)
    gain_attn = gains[:, 0] + gains[:, 1]
    gain_mlp = gains[:, 2] + gains[:, 3]
    full_in = second_full[:, : 2 * wide]
    full_down = second_full[:, 2 * wide :]

    inputs32 = layer_in.astype(jnp.float32)
    if paired:
        arrived = lax.ppermute(jnp.concatenate([layer_in, cot_local], axis=0), "seq", swap)
        all_inputs32 = jnp.concatenate([layer_in, arrived[:own_rows]], axis=0).astype(jnp.float32)
        cot_full = jnp.concatenate([cot_local, arrived[own_rows:]], axis=0)
    else:
        all_inputs32 = rows_of_all(layer_in).astype(jnp.float32)
        cot_full = rows_of_all(cot_local)
    normed_full = norm_forward(all_inputs32, gain_attn)[0].astype(jnp.bfloat16)
    unit_one, inv_one = norm_forward(inputs32, gain_attn)[1:]
    if paired:
        seg_full = rows_of_all(
            jnp.broadcast_to(seg_local.astype(jnp.float32)[:, None], (own_rows, LANES))
        )[:, 0].astype(jnp.int32)
        place = lax.axis_index("seq")
        arange = jnp.arange(own_rows, dtype=jnp.int32)
        positions = jnp.concatenate(
            [place * own_rows + arange, (1 - place) * own_rows + arange], axis=0
        )
        attention = PairedAttention(positions, seg_full, head_size, local_width)
    else:
        seg_full = rows_of_all(seg_local.astype(jnp.bfloat16)).astype(jnp.int32)
        positions = jnp.arange(total_len, dtype=jnp.int32)
        attention = BlockAttention(positions, seg_full, head_size, local_width)

    mixed = attention.forward(dot(normed_full, full_qkv, 1, 0))
    residual = inputs32 + sum_to_owner(dot(mixed, full_out, 1, 1))
    normed_two, unit_two, inv_two = norm_forward(residual, gain_mlp)
    normed_two_full = rows_of_all(normed_two.astype(jnp.bfloat16))
    expanded = dot(normed_two_full, full_in, 1, 0)
    gate_in = expanded[:, :wide]
    linear_in = expanded[:, wide:]
    activated = gelu_value(gate_in)
    middle_b = (activated * linear_in).astype(jnp.bfloat16)
    down_part = dot(middle_b, full_down, 1, 1)

    down_grad = dot(cot_full, middle_b, 0, 0).astype(jnp.bfloat16)
    dmiddle = dot(cot_full, full_down, 1, 0)
    dexpanded_b = jnp.concatenate(
        [dmiddle * linear_in * gelu_slope(gate_in), dmiddle * activated], axis=1
    ).astype(jnp.bfloat16)
    dnormed_two = sum_to_owner(dot(dexpanded_b, full_in, 1, 1))
    in_grad = dot(normed_two_full, dexpanded_b, 0, 0).astype(jnp.bfloat16)
    dres_norm, mlp_gain_part = norm_backward(dnormed_two, gain_mlp, unit_two, inv_two)
    dresidual = cot_local.astype(jnp.float32) + dres_norm
    dres_full = rows_of_all(dresidual.astype(jnp.bfloat16))
    down_part, dres_full = lax.optimization_barrier((down_part, dres_full))
    layer_out = (residual + sum_to_owner(down_part)).astype(jnp.bfloat16)
    dmixed = dot(dres_full, full_out, 1, 0).astype(jnp.bfloat16)
    out_grad = dot(dres_full, mixed, 0, 0).astype(jnp.bfloat16)
    dqkv_b = attention.backward(dmixed)
    layer_out, dqkv_b = lax.optimization_barrier((layer_out, dqkv_b))
    dnormed_one = sum_to_owner(dot(dqkv_b, full_qkv, 1, 1))
    qkv_grad = dot(normed_full, dqkv_b, 0, 0).astype(jnp.bfloat16)
    dinput_norm, attn_gain_part = norm_backward(dnormed_one, gain_attn, unit_one, inv_one)
    tokens_grad = (dresidual + dinput_norm).astype(jnp.bfloat16)
    gain_sums = sum_over_seq(jnp.stack([attn_gain_part, mlp_gain_part]))
    gain_grad = padded_to_lanes(gain_sums.T).astype(jnp.bfloat16)

    in_share, qkv_share, down_share, out_share, gain_share = ring_scatter(
        [in_grad, qkv_grad, down_grad, out_grad, gain_grad], devices
    )
    return (
        layer_out[None],
        tokens_grad[None],
        qkv_share.reshape(shard_rows, 3, local_width),
        out_share.T,
        jnp.stack([in_share[:, :local_hidden], in_share[:, wide : wide + local_hidden]], axis=1),
        down_share[:, :local_hidden].T,
        gain_share[:, 0],
        gain_share[:, 1],
    )


HIGH = (((1,), (1,)), ((), ()))
OVER_ROWS = (((0,), (0,)), ((), ()))


def fits_fused(devices, seq_size, own_rows, model_width, local_width, local_hidden):
    rest = local_hidden % LANES
    shard_rows = model_width // devices
    return (
        seq_size == 2
        and devices % 4 == 0
        and devices >= 8
        and own_rows == LANES
        and local_width % (2 * LANES) == 0
        and model_width % (2 * LANES) == 0
        and model_width // HEADS == 2 * HEAD_HALF
        and 3 * rest + 8 <= LANES
        and local_hidden // LANES >= 4
        and local_hidden // LANES % 2 == 0
        and shard_rows % 32 == 0
        and own_rows * 2 * LANES // model_width % 16 == 0
    )


def nt(left, right):
    return lax.dot_general(left, right, HIGH, preferred_element_type=jnp.float32)


def nn(left, right):
    return jnp.dot(left, right, preferred_element_type=jnp.float32)


def tiles(total, width, body):
    def step(index, carry):
        body(index, pl.ds(pl.multiple_of(index * width, width), width))
        return carry

    lax.fori_loop(0, total // width, step, 0)


def fused_kernel(sizes, layout, *refs):
    count, own_rows, width, hidden, rest, scale = sizes
    total_rows = 2 * own_rows
    r = types.SimpleNamespace(**dict(zip(layout, refs)))
    model = r.tokens.shape[1]
    streams = 8
    fulls = [getattr(r, "full%d" % i) for i in range(streams)]
    grads = [getattr(r, "grad%d" % i) for i in range(streams)]
    pairs = [getattr(r, "pair%d" % i) for i in range(streams)]
    ends = [getattr(r, "end%d" % i) for i in range(streams)]
    recvs = [getattr(r, "recv%d" % i) for i in range(streams)]
    rows = model // (2 * count)
    half = rows // 2
    turns = count // 2
    core, place = ring_place(count)
    right, left, partner = neighbours(core, place, count)
    targets = (right, left)
    me = lax.axis_index("dp")
    mine = lax.axis_index("seq")
    other = 1 - mine
    f32, bf16 = jnp.float32, jnp.bfloat16
    my_rows = pl.ds(pl.multiple_of(me * rows, rows), rows)

    def remote(src, dst, send, recv, device):
        return pltpu.make_async_remote_copy(
            src_ref=src,
            dst_ref=dst,
            send_sem=send,
            recv_sem=recv,
            device_id=device,
            device_id_type=MESH,
        )


    def piece(way, distance, stream, whole):
        shift = count - distance if way == 0 else distance
        owner = chip_at((place + shift) % count, count) * 2 + core
        if whole:
            where = pl.ds(pl.multiple_of(owner * rows, rows), rows)
        else:
            where = pl.ds(pl.multiple_of(owner * rows + way * half, half), half)
        return fulls[stream].at[where]

    def hop(way, step, stream):
        ref = piece(way, step, stream, step < turns - 1)
        sems = r.g_send.at[stream], r.g_recv.at[stream, step]
        return remote(ref, ref, *sems, {"dp": targets[way]})

    def both_hops(step, stream):
        ref = fulls[stream].at[pl.ds(0, 2 * rows if step < turns - 1 else 2 * half)]
        return remote(ref, ref, r.g_send.at[stream], r.g_recv.at[stream, step], {"dp": right})

    def share(way, step, stream):
        ref = piece(way, step, stream, step < turns)
        return remote(ref, ref, r.gp_send.at[stream], r.gp_recv.at[stream], {"dp": partner})

    def all_shares(stream):
        ref = fulls[stream].at[pl.ds(0, count * rows)]
        return remote(ref, ref, r.gp_send.at[stream], r.gp_recv.at[stream], {"dp": partner})

    def gather_ops(stream):
        def start():
            for way in range(2):
                hop(way, 0, stream).start()
            share(0, 0, stream).start()

        def middle(step):
            both_hops(step - 1, stream).wait_recv()
            for way in range(2):
                hop(way, step, stream).start()
                share(way, step, stream).start()

        def last():
            both_hops(turns - 1, stream).wait_recv()
            for way in range(2):
                share(way, turns, stream).start()

        steps = [functools.partial(middle, step) for step in range(1, turns)]
        return [start] + steps + [last]

    def gather_arrived(stream):
        end(gathers, stream)
        all_shares(stream).wait_recv()

    def sent_rows(stream):
        return pl.ds(0, 2 * (turns - 1) * rows + 2 * half)

    def gather_drain(stream):
        ref = fulls[stream].at[sent_rows(stream)]
        sems = r.g_send.at[stream], r.g_recv.at[stream, 0]
        remote(ref, ref, *sems, {"dp": right}).wait_send()
        all_shares(stream).wait_send()


    def block(ahead, which):
        owner = chip_at((place + ahead) % count, count) * 2 + which
        return pl.ds(pl.multiple_of(owner * rows, rows), rows)

    def give(ahead, stream):
        return remote(
            grads[stream].at[block(ahead, 1 - core)],
            pairs[stream].at[ahead],
            r.sp_send.at[stream],
            r.sp_recv.at[stream, 0 if ahead == turns else 1],
            {"dp": partner},
        )

    def given(step, stream):
        ref = pairs[stream].at[pl.ds(0, 1 if step == 0 else count - 1)]
        sems = r.sp_send.at[stream], r.sp_recv.at[stream, step]
        return remote(ref, ref, *sems, {"dp": partner})

    def ahead_of(way, step):
        return turns - step if way == 0 else turns + step

    def push(way, step, stream):
        sems = r.s_send.at[stream], r.s_recv.at[stream, step]
        if step == 0:
            src = pairs[stream].at[turns, pl.ds(way * half, half)]
            return remote(src, ends[stream].at[way], *sems, {"dp": targets[way]})
        src = pairs[stream].at[ahead_of(way, step)]
        return remote(src, recvs[stream].at[way, step - 1], *sems, {"dp": targets[way]})

    def both_pushes(step, stream):
        ref = ends[stream] if step == 0 else recvs[stream].at[:, step - 1]
        return remote(ref, ref, r.s_send.at[stream], r.s_recv.at[stream, step], {"dp": right})

    def pair_sum(ahead, stream):
        own = grads[stream][block(ahead, core), :].astype(f32)
        return own + pairs[stream][ahead].astype(f32)

    def scatter_ops(stream, finish):
        def gives():
            order = [turns] + [turns + sign * d for d in range(1, turns) for sign in (-1, 1)] + [0]
            for ahead in order:
                give(ahead, stream).start()

        def start():
            given(0, stream).wait_recv()
            pairs[stream][turns] = pair_sum(turns, stream).astype(bf16)
            for way in range(2):
                push(way, 0, stream).start()

        def middle(step):
            if step == 1:
                given(1, stream).wait_recv()
            both_pushes(step - 1, stream).wait_recv()
            for way in range(2):
                ahead = ahead_of(way, step)
                total = pair_sum(ahead, stream)
                if step == 1:
                    near = ends[stream][way].astype(f32)
                    parts = [total[:half], total[half:]]
                    parts[way] = parts[way] + near
                    total = jnp.concatenate(parts, axis=0)
                else:
                    total = total + recvs[stream][way, step - 2].astype(f32)
                pairs[stream][ahead] = total.astype(bf16)
                push(way, step, stream).start()

        def last():
            both_pushes(turns - 1, stream).wait_recv()
            total = pair_sum(0, stream)
            for way in range(2):
                total = total + recvs[stream][way, turns - 2].astype(f32)
            finish(total)

        steps = [functools.partial(middle, step) for step in range(1, turns)]
        return [gives, start] + steps + [last]

    def scatter_drain(stream):
        ref = fulls[stream].at[sent_rows(stream)]
        sems = r.s_send.at[stream], r.s_recv.at[stream, 0]
        remote(ref, ref, *sems, {"dp": right}).wait_send()
        ref = fulls[stream].at[pl.ds(0, count * rows)]
        sems = r.sp_send.at[stream], r.sp_recv.at[stream, 0]
        remote(ref, ref, *sems, {"dp": partner}).wait_send()


    own = pl.ds(0, own_rows)
    far = pl.ds(own_rows, own_rows)
    exchanged = [
        (r.seg_own, r.seg_other),
        (r.tokens, r.tok_other),
        (r.cot, r.cot_all.at[far]),
        (r.out_send, r.out_recv),
        (r.n2.at[own], r.n2.at[far]),
        (r.down_send, r.down_recv),
        (r.dn2_send, r.dn2_recv),
        (r.dres.at[own], r.dres.at[far]),
        (r.dn1_send, r.dn1_recv),
        (r.gain_part, r.gain_recv),
    ]
    by_lanes, by_rows = (3, 5, 6, 8), (4, 7)
    chunks = model // (2 * LANES)
    chunk_rows = own_rows // chunks

    def swap(index, part=0):
        src, dst = exchanged[index]
        if index in by_lanes:
            lanes = pl.ds(pl.multiple_of(part * 2 * LANES, 2 * LANES), 2 * LANES)
            src, dst = src.at[:, lanes], dst.at[:, lanes]
        elif index in by_rows:
            here = pl.ds(pl.multiple_of(part * chunk_rows, chunk_rows), chunk_rows)
            src, dst = src.at[here], dst.at[here]
        return remote(src, dst, r.y_send.at[index], r.y_recv.at[index], {"seq": other})

    def whole_swap(index):
        src, dst = exchanged[index]
        return remote(src, dst, r.y_send.at[index], r.y_recv.at[index], {"seq": other})

    def arrived(index):
        whole_swap(index).wait_recv()

    def swap_drain(index):
        whole_swap(index).wait_send()


    def normed(values):
        center = values - jnp.mean(values, axis=-1, keepdims=True)
        inv_std = lax.rsqrt(jnp.mean(center * center, axis=-1, keepdims=True) + EPS)
        return center * inv_std, inv_std

    def to_columns(src, dst):
        def body(index, lanes):
            dst[lanes, :] = src[:, lanes].astype(f32).T.astype(bf16)

        tiles(model, LANES, body)

    def partial_sums(terms, own_ref, send_ref, exchange):
        def body(index, lanes):
            total = sum(nt(left[...], right[lanes, :]) for left, right in terms)
            own_ref[:, lanes] = total[:own_rows]
            send_ref[:, lanes] = total[own_rows:].astype(bf16)
            swap(exchange, index).start()

        tiles(model, 2 * LANES, body)

    def weight_grad(columns, right, out):
        size = right.shape[1]

        def body(index, lanes):
            out[:, lanes] = nn(columns[...], right[:, lanes]).astype(bf16)

        whole = size // (2 * LANES) * 2 * LANES
        tiles(whole, 2 * LANES, body)
        if whole < size:
            body(0, pl.ds(whole, size - whole))

    blocks = width // LANES
    hidden_blocks = hidden // LANES
    lane = lax.broadcasted_iota(jnp.int32, (total_rows, LANES), 1)
    low_half = lane % (2 * HEAD_HALF) < HEAD_HALF
    first = lane < 2 * HEAD_HALF

    def setup():
        r.cos[own, :] = r.cos_table[pl.ds(pl.multiple_of(mine * own_rows, own_rows), own_rows), :]
        r.cos[far, :] = r.cos_table[pl.ds(pl.multiple_of(other * own_rows, own_rows), own_rows), :]
        r.sin[own, :] = r.sin_table[pl.ds(pl.multiple_of(mine * own_rows, own_rows), own_rows), :]
        r.sin[far, :] = r.sin_table[pl.ds(pl.multiple_of(other * own_rows, own_rows), own_rows), :]

    def position(dim):
        index = lax.broadcasted_iota(jnp.int32, (total_rows, total_rows), dim)
        return jnp.where(index < own_rows, index + mine * own_rows, index - mine * own_rows)

    def make_bias():
        seg_row = jnp.concatenate([r.seg_own[0:1, :], r.seg_other[0:1, :]], axis=1).astype(f32)
        across = jnp.broadcast_to(seg_row, (total_rows, total_rows))
        allowed = (jnp.abs(position(0) - position(1)) <= HALO) & (across == across.T)
        r.bias[...] = jnp.where(allowed, 0.0, NEG_FILL)

    def expand_special():
        spot = lax.broadcasted_iota(jnp.int32, (2 * LANES, LANES), 1)
        keep = spot < rest

        def body(index, here):
            part = fulls[6][here, :].astype(f32)
            r.gains[:, here] = part.T[3 * rest : 3 * rest + 8]
            r.sp_in[here, :LANES] = jnp.where(keep, part, 0.0).astype(bf16)
            r.sp_in[here, LANES:] = jnp.where(
                keep, pltpu.roll(part, LANES - rest, 1), 0.0
            ).astype(bf16)
            r.sp_down[here, :] = jnp.where(
                keep, pltpu.roll(part, LANES - 2 * rest, 1), 0.0
            ).astype(bf16)

        tiles(model, 2 * LANES, body)

    def attn_gain():
        return r.gains[0:1, :] + r.gains[1:2, :]

    def mlp_gain():
        return r.gains[2:3, :] + r.gains[3:4, :]

    def norm_one():
        for src, place_of in ((r.tokens, 0), (r.tok_other, own_rows)):
            def body(index, here):
                unit_rows, _ = normed(src[here, :].astype(f32))
                at = pl.ds(pl.multiple_of(index * 32 + place_of, 32), 32)
                r.n1[at, :] = (unit_rows * attn_gain()).astype(bf16)

            tiles(own_rows, 32, body)

    def values_of():
        def body(index, lanes):
            r.v[:, lanes] = nn(r.n1[...], fulls[1][:, lanes]).astype(bf16)

        tiles(width, 2 * LANES, body)

    def attend(index, wide, lanes):
        cos_table, sin_table = r.cos[...], r.sin[...]
        proj = nn(r.n1[...], fulls[0][:, wide])
        queries = turn(proj[:, :LANES], cos_table, sin_table, low_half)
        keys = turn(proj[:, LANES:], cos_table, sin_table, low_half).astype(bf16)
        r.qk[:, wide] = jnp.concatenate([queries.astype(bf16), keys], axis=1)
        values = r.v[:, lanes].astype(f32)
        mixed = jnp.zeros((total_rows, LANES), f32)
        for head in range(2):
            here = first if head == 0 else ~first
            scores = nt(jnp.where(here, queries, 0.0).astype(bf16), keys) * scale + r.bias[...]
            top_score = jnp.max(scores, axis=-1, keepdims=True)
            total = jnp.sum(jnp.exp(scores - top_score), axis=-1, keepdims=True)
            probs = jnp.exp(scores - (top_score + jnp.log(total)))
            r.probs[index * 2 + head] = probs
            mixed = mixed + nn(probs.astype(bf16), jnp.where(here, values, 0.0).astype(bf16))
        r.mixed[:, lanes] = mixed.astype(bf16)

    def attend_back(index, wide, lanes):
        cos_table, sin_table = r.cos[...], -r.sin[...]
        both = r.qk[:, wide]
        queries = both[:, :LANES].astype(f32)
        keys = both[:, LANES:].astype(f32)
        values = r.v[:, lanes]
        dmixed = r.dmixed[:, lanes].astype(f32)
        products = dmixed * r.mixed[:, lanes].astype(f32)
        dquery = jnp.zeros((total_rows, LANES), f32)
        dkey = jnp.zeros((total_rows, LANES), f32)
        dvalue = jnp.zeros((total_rows, LANES), f32)
        for head in range(2):
            here = first if head == 0 else ~first
            head_queries = jnp.where(here, queries, 0.0).astype(bf16)
            head_keys = jnp.where(here, keys, 0.0).astype(bf16)
            head_dmixed = jnp.where(here, dmixed, 0.0).astype(bf16)
            delta = jnp.sum(jnp.where(here, products, 0.0), axis=-1, keepdims=True)
            probs = r.probs[index * 2 + head]
            dprobs = nt(head_dmixed, values)
            dscores = (probs * (dprobs - delta) * scale).astype(bf16)
            dvalue = dvalue + lax.dot_general(
                probs.astype(bf16), head_dmixed, OVER_ROWS, preferred_element_type=f32
            )
            dkey = dkey + lax.dot_general(
                dscores, head_queries, OVER_ROWS, preferred_element_type=f32
            )
            dquery = dquery + nn(dscores, head_keys)
        dquery = turn(dquery, cos_table, sin_table, low_half)
        dkey = turn(dkey, cos_table, sin_table, low_half)
        r.dqk[:, wide] = jnp.concatenate([dquery, dkey], axis=1).astype(bf16)
        r.dv[:, lanes] = dvalue.astype(bf16)

    def over_heads(body, start, stop):
        def step(index, carry):
            body(
                index,
                pl.ds(pl.multiple_of(index * 2 * LANES, 2 * LANES), 2 * LANES),
                pl.ds(pl.multiple_of(index * LANES, LANES), LANES),
            )
            return carry

        lax.fori_loop(start, stop, step, 0)

    def norm_two():
        def body(index, here):
            residual = (
                r.tokens[here, :].astype(f32)
                + r.acc[here, :]
                + r.out_recv[here, :].astype(f32)
            )
            r.residual[here, :] = residual
            unit_rows, _ = normed(residual)
            r.n2[here, :] = (unit_rows * mlp_gain()).astype(bf16)
            swap(4, index).start()

        tiles(own_rows, chunk_rows, body)

    def expand_tile(weight, at):
        both = nn(r.n2[...], weight)
        gate, linear = both[:, :LANES], both[:, LANES:]
        erf_part = 0.5 * (1.0 + lax.erf(gate * 0.7071067811865476))
        active = gate * erf_part
        slope = erf_part + gate * jnp.exp(-0.5 * gate * gate) * 0.3989422804014327
        r.mid[:, at] = (active * linear).astype(bf16)
        r.act[:, at] = active
        r.slope[:, at] = linear * slope

    def expand_stream(stream, offset):
        def body(index, lanes):
            at = pl.ds(pl.multiple_of((index + offset) * LANES, LANES), LANES)
            expand_tile(fulls[stream][:, lanes], at)

        tiles(fulls[stream].shape[1], 2 * LANES, body)

    spare = pl.ds(hidden, LANES)

    def dexpand(weight, at, to):
        dmiddle = nn(r.cot_all[...], weight)
        dgate = (dmiddle * r.slope[:, at]).astype(bf16)
        dlinear = (dmiddle * r.act[:, at]).astype(bf16)
        parts = []
        for start in range(0, dmiddle.shape[1], LANES):
            parts += [dgate[:, start : start + LANES], dlinear[:, start : start + LANES]]
        r.dexp[:, to] = jnp.concatenate(parts, axis=1)

    def dexpand_stream(stream, offset):
        def body(index, lanes):
            at = pl.ds(pl.multiple_of(offset * LANES + index * LANES, LANES), LANES)
            to = pl.ds(
                pl.multiple_of(offset * 2 * LANES + index * 2 * LANES, 2 * LANES), 2 * LANES
            )
            dexpand(fulls[stream][:, lanes], at, to)

        tiles(fulls[stream].shape[1], LANES, body)

    split = fulls[3].shape[1]
    mid_parts = [
        r.mid.at[:, pl.ds(0, split // 2)],
        r.mid.at[:, pl.ds(split // 2, hidden - split // 2)],
    ]
    dexp_parts = [
        r.dexp.at[:, pl.ds(0, split)],
        r.dexp.at[:, pl.ds(split, 2 * hidden - split)],
        r.dexp.at[:, pl.ds(2 * hidden, 2 * LANES)],
    ]

    def special_grad():
        spot = lax.broadcasted_iota(jnp.int32, (2 * LANES, LANES), 1)

        def body(index, here):
            both = nn(r.n2_col[here, :], dexp_parts[2][...])
            down = nn(r.cot_col[here, :], r.mid[:, spare])
            value = jnp.where(
                spot < rest,
                both[:, :LANES],
                jnp.where(
                    spot < 2 * rest,
                    pltpu.roll(both[:, LANES:], rest, 1),
                    jnp.where(spot < 3 * rest, pltpu.roll(down, 2 * rest, 1), 0.0),
                ),
            )
            grads[6][here, :] = value.astype(bf16)

        tiles(model, 2 * LANES, body)

    def back_through_norm(grad_rows, gain, values):
        unit_rows, inv_std = normed(values)
        scaled = grad_rows * gain
        inner = (
            scaled
            - jnp.mean(scaled, axis=-1, keepdims=True)
            - unit_rows * jnp.mean(scaled * unit_rows, axis=-1, keepdims=True)
        )
        return inner * inv_std, jnp.sum(grad_rows * unit_rows, axis=0, keepdims=True)

    def norm_two_back():
        r.gain_part[...] = jnp.zeros_like(r.gain_part)

        def body(index, here):
            grad_rows = r.acc[here, :] + r.dn2_recv[here, :].astype(f32)
            part, gain_sum = back_through_norm(grad_rows, mlp_gain(), r.residual[here, :])
            dresidual = r.cot[here, :].astype(f32) + part
            r.dres_own[here, :] = dresidual
            r.dres[here, :] = dresidual.astype(bf16)
            r.gain_part[1:2, :] += gain_sum
            swap(7, index).start()

        tiles(own_rows, chunk_rows, body)

    def norm_one_back():
        def body(index, here):
            grad_rows = r.acc[here, :] + r.dn1_recv[here, :].astype(f32)
            part, gain_sum = back_through_norm(
                grad_rows, attn_gain(), r.tokens[here, :].astype(f32)
            )
            r.tokens_grad[0, here, :] = (r.dres_own[here, :] + part).astype(bf16)
            r.gain_part[0:1, :] += gain_sum

        tiles(own_rows, 32, body)

    def layer_out():
        def body(index, here):
            r.layer_out[0, here, :] = (
                r.residual[here, :]
                + r.down_acc[here, :]
                + r.down_recv[here, :].astype(f32)
            ).astype(bf16)

        tiles(own_rows, 32, body)

    def gain_columns():
        spot = lax.broadcasted_iota(jnp.int32, (LANES, 2 * LANES), 0)

        def body(index, here):
            sums = r.gain_part[:, here] + r.gain_recv[:, here]
            value = jnp.where(
                spot == 3 * rest, sums[0:1], jnp.where(spot == 3 * rest + 1, sums[1:2], 0.0)
            ).T
            old = grads[6][here, :].astype(f32)
            grads[6][here, :] = (old + value).astype(bf16)

        tiles(model, 2 * LANES, body)

    def dmixed_of():
        def body(index, lanes):
            r.dmixed[:, lanes] = nn(r.dres[...], fulls[2][:, lanes]).astype(bf16)

        tiles(width, 2 * LANES, body)


    def pack_keys():
        for at in range(0, width, LANES):
            for which in range(2):
                to = 2 * at + which * LANES
                fulls[0][my_rows, to : to + LANES] = r.raw_qkv[which, :, at : at + LANES]
        fulls[1][my_rows, :] = r.raw_qkv[2]

    def pack_special():
        spot = lax.broadcasted_iota(jnp.int32, (LANES, rows), 0)
        gain_parts = []
        for gain in (r.attn_gain[...], r.mlp_gain[...]):
            spread = gain * 65537.0
            high = spread - (spread - gain)
            gain_parts += [high, gain - high]
        gains = jnp.zeros((LANES, rows), f32)
        for index, part in enumerate(gain_parts):
            gains = jnp.where(spot == 3 * rest + index, part, gains)
        special = gains.T
        if rest:
            parts = [
                r.raw_in[:, 0, hidden:].astype(f32),
                r.raw_in[:, 1, hidden:].astype(f32),
                r.raw_down[:, hidden:].astype(f32),
                jnp.zeros((rows, LANES - 3 * rest), f32),
            ]
            special = special + jnp.concatenate(parts, axis=1)
        fulls[6][my_rows, :] = special.astype(bf16)

    def pack_rest():
        fulls[2][my_rows, :] = r.raw_out[...]
        for at in range(0, hidden, LANES):
            stream, to = (3, 2 * at) if 2 * at < split else (4, 2 * at - split)
            for which in range(2):
                start = to + which * LANES
                fulls[stream][my_rows, start : start + LANES] = r.raw_in[:, which, at : at + LANES]
        fulls[5][my_rows, :] = r.raw_down[:, : split // 2]
        fulls[7][my_rows, :] = r.raw_down[:, split // 2 : hidden]


    def finish_keys(total):
        for at in range(0, width, LANES):
            for which in range(2):
                to = 2 * at + which * LANES
                r.qkv_grad[which, :, at : at + LANES] = total[:, to : to + LANES]

    def finish_values(total):
        r.qkv_grad[2] = total

    def finish_out(total):
        r.out_grad[...] = total

    def finish_special(total):
        turned = total.T
        r.attn_gain_grad[...] = turned[3 * rest : 3 * rest + 1]
        r.mlp_gain_grad[...] = turned[3 * rest + 1 : 3 * rest + 2]
        if rest:
            r.in_grad[:, 0, hidden:] = total[:, :rest]
            r.in_grad[:, 1, hidden:] = total[:, rest : 2 * rest]
            r.down_grad[:, hidden:] = total[:, 2 * rest : 3 * rest]

    def finish_in(start):
        def finish(total):
            for at in range(0, total.shape[1], 2 * LANES):
                to = start + at // 2
                r.in_grad[:, 0, to : to + LANES] = total[:, at : at + LANES]
                r.in_grad[:, 1, to : to + LANES] = total[:, at + LANES : at + 2 * LANES]

        return finish

    def finish_down(start):
        def finish(total):
            r.down_grad[:, start : start + total.shape[1]] = total

        return finish

    gathers = [gather_ops(stream) for stream in range(streams)]
    finishes = [finish_keys, finish_values, finish_out, finish_in(0), finish_in(split // 2)]
    finishes += [finish_down(0), finish_special, finish_down(split // 2)]
    scatters = [scatter_ops(stream, finishes[stream]) for stream in range(streams)]

    def go(ops, *chosen):
        for stream in chosen:
            if ops[stream]:
                ops[stream].pop(0)()

    def end(ops, *chosen):
        while any(ops[stream] for stream in chosen):
            go(ops, *chosen)

    stores = [
        pltpu.make_async_copy(r.layer_out, r.to_layer_out, r.own_sem.at[11]),
        pltpu.make_async_copy(r.tokens_grad, r.to_tokens_grad, r.own_sem.at[12]),
    ]


    barrier = pltpu.get_barrier_semaphore()
    for device in (right, left, partner):
        pl.semaphore_signal(barrier, inc=1, device_id={"dp": device}, device_id_type=MESH)
    pl.semaphore_signal(barrier, inc=1, device_id={"seq": other}, device_id_type=MESH)
    loads = [
        pltpu.make_async_copy(src, dst, r.own_sem.at[index])
        for index, (src, dst) in enumerate(
            [
                (r.in_qkv, r.raw_qkv),
                (r.in_in, r.raw_in),
                (r.in_down, r.raw_down),
                (r.in_attn_gain, r.attn_gain),
                (r.in_mlp_gain, r.mlp_gain),
                (r.in_seg, r.seg),
                (r.in_tokens.at[0], r.tokens),
                (r.in_cot.at[0], r.cot),
                (r.in_out, r.raw_out),
                (r.in_cos, r.cos_table),
                (r.in_sin, r.sin_table),
            ]
        )
    ]
    for load in loads:
        load.start()
    loads[0].wait()
    pack_keys()
    pl.semaphore_wait(barrier, 4)
    go(gathers, 0)
    for load in loads[1:8]:
        load.wait()
    pack_special()
    r.seg_own[...] = jnp.broadcast_to(r.seg[...], r.seg_own.shape)
    for index in range(3):
        swap(index).start()
    loads[8].wait()
    pack_rest()
    r.cot_all[own, :] = r.cot[...]
    go(gathers, 1)
    for load in loads[9:]:
        load.wait()
    setup()
    to_columns(r.cot_all.at[own], r.cot_col.at[:, own])
    go(gathers, 6)
    arrived(0)
    make_bias()
    go(gathers, 2, 0, 1, 6)
    go(gathers, 2, 0, 1, 6)
    go(gathers, 2, 3, 0, 1, 6)
    go(gathers, 2, 5, 3, 0, 1, 6)
    go(gathers, 2)
    arrived(1)
    arrived(2)
    gather_arrived(6)
    expand_special()
    norm_one()
    go(gathers, 5)
    gather_arrived(1)
    values_of()
    go(gathers, 4)
    gather_arrived(0)
    over_heads(attend, blocks * 0 // 4, blocks * 1 // 4)
    over_heads(attend, blocks * 1 // 4, blocks * 2 // 4)
    go(gathers, 3)
    over_heads(attend, blocks * 2 // 4, blocks * 3 // 4)
    over_heads(attend, blocks * 3 // 4, blocks * 4 // 4)
    go(gathers, 5)
    gather_arrived(2)
    partial_sums([(r.mixed, fulls[2])], r.acc, r.out_send, 3)
    to_columns(r.n1, r.n1_col)
    to_columns(r.cot_all.at[far], r.cot_col.at[:, far])
    go(gathers, 4, 3)
    arrived(3)
    norm_two()
    go(gathers, 5, 7, 4, 3)
    go(gathers, 5)
    arrived(4)
    gather_arrived(3)
    expand_stream(3, 0)
    go(gathers, 7)
    weight_grad(r.cot_col, mid_parts[0], grads[5])
    go(scatters, 5)
    to_columns(r.n2, r.n2_col)
    go(scatters, 5)
    go(gathers, 4)
    expand_tile(r.sp_in[...], spare)
    gather_arrived(5)
    dexpand_stream(5, 0)
    go(gathers, 7)
    dexpand(r.sp_down[...], spare, pl.ds(2 * hidden, 2 * LANES))
    go(scatters, 5)
    weight_grad(r.n2_col, dexp_parts[0], grads[3])
    go(gathers, 4)
    go(scatters, 3)
    go(gathers, 7)
    go(scatters, 3)
    gather_arrived(4)
    expand_stream(4, split // (2 * LANES))
    go(gathers, 7)
    go(scatters, 5)
    weight_grad(r.cot_col, mid_parts[1], grads[7])
    go(scatters, 7)
    gather_arrived(7)
    dexpand_stream(7, split // (2 * LANES))
    go(scatters, 7, 3)
    partial_sums(
        [(dexp_parts[0], fulls[3]), (dexp_parts[1], fulls[4]), (dexp_parts[2], r.sp_in)],
        r.acc,
        r.dn2_send,
        6,
    )
    go(scatters, 7, 5)
    weight_grad(r.n2_col, dexp_parts[1], grads[4])
    go(scatters, 4)
    go(scatters, 4, 3, 7)
    arrived(6)
    norm_two_back()
    go(scatters, 5)
    special_grad()
    partial_sums(
        [(mid_parts[0], fulls[5]), (mid_parts[1], fulls[7]), (r.mid.at[:, spare], r.sp_down)],
        r.down_acc,
        r.down_send,
        5,
    )
    go(scatters, 4, 3)
    arrived(7)
    dmixed_of()
    go(scatters, 7)
    over_heads(attend_back, blocks * 0 // 4, blocks * 1 // 4)
    over_heads(attend_back, blocks * 1 // 4, blocks * 2 // 4)
    over_heads(attend_back, blocks * 2 // 4, blocks * 3 // 4)
    go(scatters, 4)
    over_heads(attend_back, blocks * 3 // 4, blocks * 4 // 4)
    partial_sums([(r.dqk, fulls[0]), (r.dv, fulls[1])], r.acc, r.dn1_send, 8)
    go(scatters, 3)
    weight_grad(r.n1_col, r.dv, grads[1])
    go(scatters, 1)
    weight_grad(r.n1_col, r.dqk, grads[0])
    go(scatters, 7, 1, 0)
    to_columns(r.dres, r.dres_col)
    go(scatters, 0)
    weight_grad(r.dres_col, r.mixed, grads[2])
    go(scatters, 2, 4, 1)
    go(scatters, 2)
    arrived(8)
    norm_one_back()
    swap(9).start()
    stores[1].start()
    go(scatters, 0)
    arrived(5)
    layer_out()
    stores[0].start()
    arrived(9)
    gain_columns()
    go(scatters, 6, 4)
    go(scatters, 6, 1, 2)
    go(scatters, 6, 0, 1, 2)
    go(scatters, 6, 0, 1, 2)
    go(scatters, 6, 0, 2)
    go(scatters, 6)
    end(scatters, *range(streams))

    for stream in range(streams):
        gather_drain(stream)
        scatter_drain(stream)
    for index in range(len(exchanged)):
        swap_drain(index)
    for store in stores:
        store.wait()


def fused_call(inputs, devices, widths):
    names, arrays = zip(*inputs.items())
    whole = dict(inputs)
    count = devices // 2
    own_rows, model = whole["in_tokens"].shape[1:]
    total = 2 * own_rows
    _, rows, width = whole["in_qkv"].shape
    local_hidden = whole["in_in"].shape[2]
    rest = local_hidden % LANES
    hidden = local_hidden - rest
    half = rows // 2
    turns = count // 2
    f32, bf16 = jnp.float32, jnp.bfloat16
    streams = len(widths)
    heads = width // (2 * HEAD_HALF)
    outs = dict(
        to_layer_out=((1, own_rows, model), bf16),
        to_tokens_grad=((1, own_rows, model), bf16),
        qkv_grad=((3, rows, width), f32),
        out_grad=((rows, width), f32),
        in_grad=((rows, 2, local_hidden), f32),
        down_grad=((rows, local_hidden), f32),
        attn_gain_grad=((1, rows), f32),
        mlp_gain_grad=((1, rows), f32),
    )
    shapes = dict(
        tokens=((own_rows, model), bf16),
        cot=((own_rows, model), bf16),
        seg=((1, own_rows), jnp.int32),
        attn_gain=((1, rows), f32),
        mlp_gain=((1, rows), f32),
        cos_table=((total, LANES), f32),
        sin_table=((total, LANES), f32),
        seg_own=((8, own_rows), jnp.int32),
        seg_other=((8, own_rows), jnp.int32),
        layer_out=((1, own_rows, model), bf16),
        tokens_grad=((1, own_rows, model), bf16),
        raw_qkv=((3, rows, width), bf16),
        raw_out=((rows, width), bf16),
        raw_in=((rows, 2, local_hidden), bf16),
        raw_down=((rows, local_hidden), bf16),
        tok_other=((own_rows, model), bf16),
        cot_all=((total, model), bf16),
        cot_col=((model, total), bf16),
        n1=((total, model), bf16),
        n1_col=((model, total), bf16),
        gains=((8, model), f32),
        cos=((total, LANES), f32),
        sin=((total, LANES), f32),
        bias=((total, total), f32),
        sp_in=((model, 2 * LANES), bf16),
        sp_down=((model, LANES), bf16),
        v=((total, width), bf16),
        qk=((total, 2 * width), bf16),
        probs=((heads, total, total), f32),
        mixed=((total, width), bf16),
        acc=((own_rows, model), f32),
        down_acc=((own_rows, model), f32),
        out_send=((own_rows, model), bf16),
        out_recv=((own_rows, model), bf16),
        down_send=((own_rows, model), bf16),
        down_recv=((own_rows, model), bf16),
        dn2_send=((own_rows, model), bf16),
        dn2_recv=((own_rows, model), bf16),
        dn1_send=((own_rows, model), bf16),
        dn1_recv=((own_rows, model), bf16),
        residual=((own_rows, model), f32),
        n2=((total, model), bf16),
        n2_col=((model, total), bf16),
        mid=((total, hidden + LANES), bf16),
        act=((total, hidden + LANES), f32),
        slope=((total, hidden + LANES), f32),
        dexp=((total, 2 * hidden + 2 * LANES), bf16),
        dres_own=((own_rows, model), f32),
        dres=((total, model), bf16),
        dres_col=((model, total), bf16),
        dmixed=((total, width), bf16),
        dqk=((total, 2 * width), bf16),
        dv=((total, width), bf16),
        gain_part=((8, model), f32),
        gain_recv=((8, model), f32),
    )
    for i, w in enumerate(widths):
        shapes["full%d" % i] = ((model, w), bf16)
        shapes["grad%d" % i] = ((model, w), bf16)
        shapes["pair%d" % i] = ((count, rows, w), bf16)
        shapes["end%d" % i] = ((2, half, w), bf16)
        shapes["recv%d" % i] = ((2, turns - 1, rows, w), bf16)
    scratch = {name: pltpu.VMEM(shape, dtype) for name, (shape, dtype) in shapes.items()}
    semaphores = dict(
        own_sem=(13,),
        g_send=(streams,),
        g_recv=(streams, turns),
        gp_send=(streams,),
        gp_recv=(streams,),
        s_send=(streams,),
        s_recv=(streams, turns),
        sp_send=(streams,),
        sp_recv=(streams, 2),
        y_send=(10,),
        y_recv=(10,),
    )
    for name, shape in semaphores.items():
        scratch[name] = pltpu.SemaphoreType.DMA(shape)
    vmem = pl.BlockSpec(memory_space=pltpu.VMEM)
    anywhere = pl.BlockSpec(memory_space=pl.ANY)
    sizes = (count, own_rows, width, hidden, rest, 1.0 / math.sqrt(2 * HEAD_HALF))
    layout = list(names) + list(outs) + list(scratch)
    return pl.pallas_call(
        functools.partial(fused_kernel, sizes, layout),
        out_shape=[jax.ShapeDtypeStruct(shape, dtype) for shape, dtype in outs.values()],
        in_specs=[anywhere] * len(names),
        out_specs=[anywhere] * 2 + [vmem] * (len(outs) - 2),
        scratch_shapes=list(scratch.values()),
        compiler_params=pltpu.CompilerParams(
            collective_id=2, has_side_effects=True, vmem_limit_bytes=FUSED_LIMIT
        ),
        name="fused_layer",
    )(*arrays)


def copy_kernel(count, *refs):
    sources, targets, buffers = refs[:count], refs[count : 2 * count], refs[2 * count : 3 * count]
    sems = refs[3 * count]
    ins, outs = [], []
    for index in range(count):
        rows = sources[index].shape[0]
        cuts = 2 if rows % 32 == 0 else 1
        for part in range(cuts):
            here = pl.ds(part * (rows // cuts), rows // cuts)
            source, buffer, target = (
                ref.at[here] for ref in (sources[index], buffers[index], targets[index])
            )
            ins.append(pltpu.make_async_copy(source, buffer, sems.at[0, index, part]))
            outs.append(pltpu.make_async_copy(buffer, target, sems.at[1, index, part]))
    for copy in ins:
        copy.start()
    for arrive, leave in zip(ins, outs):
        arrive.wait()
        leave.start()
    for copy in outs:
        copy.wait()


def finish_call(arrays):
    anywhere = pl.BlockSpec(memory_space=pl.ANY)
    count = len(arrays)
    return pl.pallas_call(
        functools.partial(copy_kernel, count),
        out_shape=[jax.ShapeDtypeStruct(array.shape, array.dtype) for array in arrays],
        in_specs=[anywhere] * count,
        out_specs=[anywhere] * count,
        scratch_shapes=[pltpu.VMEM(array.shape, array.dtype) for array in arrays]
        + [pltpu.SemaphoreType.DMA((2, count, 2))],
        name="finish",
    )(*arrays)


FUSED_LIMIT = 63 * 1024 * 1024


def position_tables(total, head_size):
    half_size = head_size // 2
    freqs = THETA ** (-(2.0 / head_size) * np.arange(half_size))
    angles = np.arange(total)[:, None] * freqs[None, :]
    cos_table = np.cos(angles).astype(np.float32)
    sin_table = np.sin(angles).astype(np.float32)
    return (
        jnp.asarray(np.concatenate([cos_table] * 4, axis=1)),
        jnp.asarray(np.concatenate([-sin_table, sin_table] * 2, axis=1)),
    )


def fused_device(
    devices,
    tokens,
    segments,
    cotangent,
    qkv_weight,
    out_weight,
    in_weight,
    down_weight,
    attn_gain,
    mlp_gain,
):
    own_rows = tokens.shape[1]
    width = qkv_weight.shape[2]
    blocks = in_weight.shape[2] // LANES
    first = blocks // 2 * 2 * LANES
    second = 2 * blocks * LANES - first
    widths = [2 * width, width, width, first, second, first // 2, LANES, second // 2]
    cos_table, sin_table = position_tables(2 * own_rows, 2 * HEAD_HALF)
    inputs = dict(
        in_qkv=jnp.transpose(qkv_weight, (1, 0, 2)),
        in_out=out_weight.T,
        in_in=in_weight,
        in_down=down_weight.T,
        in_tokens=tokens,
        in_cot=cotangent,
        in_seg=segments,
        in_attn_gain=attn_gain[None],
        in_mlp_gain=mlp_gain[None],
        in_cos=cos_table,
        in_sin=sin_table,
    )
    results = finish_call(fused_call(inputs, devices, widths))
    layer_out, tokens_grad, qkv, out, in_grad, down, attn_grad, mlp_grad = results
    return (
        layer_out,
        tokens_grad,
        jnp.transpose(qkv, (1, 0, 2)),
        out.T,
        in_grad,
        down.T,
        attn_grad[0],
        mlp_grad[0],
    )


def per_device(
    devices,
    seq_size,
    tokens,
    segments,
    cotangent,
    qkv_weight,
    out_weight,
    in_weight,
    down_weight,
    attn_gain,
    mlp_gain,
):
    args = (
        tokens,
        segments,
        cotangent,
        qkv_weight,
        out_weight,
        in_weight,
        down_weight,
        attn_gain,
        mlp_gain,
    )
    own_rows, model = tokens.shape[1:]
    sizes = (own_rows, model, qkv_weight.shape[2], in_weight.shape[2])
    if fits_fused(devices, seq_size, *sizes) and tokens.shape[0] == 1:
        return fused_device(devices, *args)
    return general_device(devices, seq_size, *args)


def solution(mesh):
    return jax.shard_map(
        functools.partial(per_device, mesh.shape["dp"], mesh.shape["seq"]),
        mesh=mesh,
        in_specs=(
            P("dp", "seq", None),
            P("dp", "seq"),
            P("dp", "seq", None),
            P("dp", None, "seq"),
            P("seq", "dp"),
            P("dp", None, "seq"),
            P("seq", "dp"),
            P("dp"),
            P("dp"),
        ),
        out_specs=(
            P("dp", "seq", None),
            P("dp", "seq", None),
            P("dp", None, "seq"),
            P("seq", "dp"),
            P("dp", None, "seq"),
            P("seq", "dp"),
            P("dp"),
            P("dp"),
        ),
        check_vma=False,
    )
```
